32 devices in a mesh: dp: 8 (over y, x, core), seq: 4 (over z).
Axes of the slice: x: 2, y: 2, z: 4, core: 2. Of those that a mesh axis runs over, the one named last changes fastest.
Arguments:
- inputs: float32 [8, 2048, 1472], P('dp', 'seq'), may hold values from -6 to 6
- layer3_rows: bfloat16 [12288, 1472], P(('dp', 'seq')), may hold values from -2 to 2
- layer4_rows: bfloat16 [12288, 1472], P(('dp', 'seq')), may hold values from -2 to 2
- norm_gains: float32 [4, 1472], replicated, may hold values from 0.25 to 1.75
- gate_weight: float32 [1472], replicated, may hold values from -0.15625 to 0.15625
- rel_bias: float32 [32, 6], replicated, may hold values from -4 to 4
- segment_ids: int32 [8, 2048], P('dp'), may hold values from 0 to 7, never falling along the last dimension, each value on 1 to 800 neighbouring positions
- cotangent: float32 [8, 2048, 1472], P('dp', 'seq'), may hold values from -24 to 24
Outputs:
- output: float32 [8, 2048, 1472], P('dp', 'seq')
- gate_mask: float32 [8, 2048], P('dp', 'seq')
- input_grad: float32 [8, 2048, 1472], P('dp', 'seq')
- layer3_grad: float32 [12288, 1472], P(('dp', 'seq'))
- layer4_grad: float32 [12288, 1472], P(('dp', 'seq'))
- norm_gains_grad: float32 [4, 1472], replicated
- gate_weight_grad: float32 [1472], replicated
- rel_bias_grad: float32 [32, 6], replicated
The draws below stay inside these ranges and needn't reach their ends.
Inputs may be any that keep to these rules, and one draw needn't show every extreme that they name: `segment_ids`: segment numbers never fall along a sequence; a document holds at most 800 tokens, and some document holds exactly that many.
All inputs are finite; a program needn't handle non-finite values.
Results may differ from the reference program's by a relative error of at most 0.03.
Values may be sent and summed in bfloat16 or wider, within the bound.
No kernel may reach another device: no remote copies, remote signals or barrier semaphores. Data moves between devices by JAX's collectives and lax.ppermute only.
A program may use at most 512 MiB of HBM per device.

```python
import math
import jax
import jax.numpy as jnp
import numpy as np
from jax import lax

D = 1472
HEADS = 6
HEAD_DIM = 64
FF = 3584
BUCKETS = 32
LENGTH = 2048
INNER = 384
SEQS = 8
DOC_MOST = 800


def layer_rows_sample(key):
    total_rows = 4 * INNER + 3 * FF
    row_index = jnp.arange(total_rows)[:, None]
    row_scale = jnp.where(row_index < 2 * INNER, 0.5 * D ** (-0.5), jnp.where(row_index < 3 * INNER, D ** (-0.5), jnp.where(row_index < 4 * INNER, INNER ** (-0.5), jnp.where(row_index < 4 * INNER + 2 * FF, 1.25 * D ** (-0.5), FF ** (-0.5)))))
    sample = jnp.clip(jax.random.normal(key, (total_rows, D), jnp.float32), -4.0, 4.0)
    return (sample * row_scale).astype(jnp.bfloat16)


def draw_layer3_rows(key, part):
    return layer_rows_sample(jax.random.fold_in(key, 3))


def draw_layer4_rows(key, part):
    return layer_rows_sample(jax.random.fold_in(key, 4))


def draw_cotangent(key, part):
    full_shape = (SEQS, LENGTH, D)
    seq_rise = jnp.exp(jnp.log(3.0) * jnp.arange(SEQS, dtype=jnp.float32) / max(SEQS - 1, 1))
    pos_rise = 1.0 + jnp.arange(LENGTH, dtype=jnp.float32) / LENGTH
    inner_key = jax.random.fold_in(key, 7)
    sample = jnp.clip(jax.random.normal(inner_key, full_shape, jnp.float32), -4.0, 4.0)
    return sample * seq_rise[:, None, None] * pos_rise[None, :, None]


def level_of(key, shape, split, low, largest):
    loudness = 1.0
    for axis_at, shards_of in split:
        heights = jax.random.uniform(jax.random.fold_in(jax.random.fold_in(key, 6), axis_at), (shards_of,), jnp.float32, low / len(split), largest / len(split))
        loudness = loudness * jnp.repeat(jnp.exp(heights), shape[axis_at] // shards_of).reshape((-1,) + (1,) * (len(shape) - 1 - axis_at))
    return loudness


def length_profile(count, total, reach, slope):
    weights = [(1 << 20) // math.isqrt(rank ** slope) + 1 for rank in range(2, count + 1)]
    rest, holding = total - reach - (count - 1), [1] * (count - 1)
    while rest > 0:
        candidates = [i for i in range(count - 1) if holding[i] < reach]
        pool, remaining = sum([weights[i] for i in candidates]), rest
        for i in candidates:
            addition = min(reach - holding[i], max(1, remaining * weights[i] // pool), rest)
            holding[i] = holding[i] + addition
            rest = rest - addition
    return np.array([reach] + holding)


def ragged_sizes(stream_key, amount, total, most, lean):
    if amount == 2:
        one = jax.random.randint(stream_key, (), max(1, total - most), min(most, total - 1) + 1)
        return jnp.stack([one, total - one])
    sizes = jnp.asarray(length_profile(amount, total, most, lean), jnp.int32)
    pairs = (amount - 1) // 2
    source_of, sink = sizes[1:1 + 2 * pairs:2], sizes[2:2 + 2 * pairs:2]
    slack = jnp.minimum(source_of - 1, most - sink)
    passed = jax.random.randint(jax.random.fold_in(stream_key, 1), (pairs,), 0, 1 << 20) % (slack + 1)
    sizes = sizes.at[1:1 + 2 * pairs:2].set(source_of - passed).at[2:2 + 2 * pairs:2].set(sink + passed)
    return sizes[jax.random.permutation(jax.random.fold_in(stream_key, 2), amount)]


def centred(own_key, extent, spread, most, shards=(), held_as=jnp.bfloat16):
    entries = jax.random.normal(own_key, extent, jnp.float32) * spread
    if len(shards) > 0:
        entries = level_of(own_key, extent, shards, -0.22, 0.18) * entries
    return jnp.clip(entries, min=-most, max=most).astype(held_as)


def setup_inputs(seed: int = 0) -> dict:
    key_list = jax.random.split(jax.random.key(seed), 9)
    inputs = centred(key_list[0], (SEQS, LENGTH, D), 1.0, 6.0, ((0, 8), (1, 4)), jnp.float32)
    layer3_rows = draw_layer3_rows(jax.random.fold_in(key_list[8], 71), 0)
    layer4_rows = draw_layer4_rows(jax.random.fold_in(key_list[8], 71), 0)
    norm_gains = jnp.clip(1.0 + 0.15 * jax.random.normal(key_list[3], (4, D), jnp.float32), 0.25, 1.75)
    gate_weight = centred(key_list[4], (D,), D ** -0.5, 0.15625, (), jnp.float32)
    rel_bias = centred(key_list[5], (BUCKETS, HEADS), 1.0, 4.0, (), jnp.float32)
    segment_ids = jax.vmap(lambda own: jnp.searchsorted(jnp.cumsum(ragged_sizes(own, 8, LENGTH, DOC_MOST, 0)), jnp.arange(LENGTH), side="right"))(jax.random.split(key_list[6], SEQS)).reshape((SEQS, LENGTH)).astype(jnp.int32)
    cotangent = draw_cotangent(jax.random.fold_in(key_list[8], 71), 0)
    return {"inputs": inputs, "layer3_rows": layer3_rows, "layer4_rows": layer4_rows, "norm_gains": norm_gains, "gate_weight": gate_weight, "rel_bias": rel_bias, "segment_ids": segment_ids, "cotangent": cotangent}


@jax.custom_vjp
def low(v):
    return lax.optimization_barrier(v.astype(jnp.bfloat16)).astype(jnp.float32)

@jax.custom_vjp
def low_back(v):
    return v

def low_keep(v):
    return (low(v), None)

def low_pass(kept, grad):
    return (grad,)

def back_keep(v):
    return (v, None)

def back_low(kept, grad):
    return (low(grad),)
low.defvjp(low_keep, low_pass)
low_back.defvjp(back_keep, back_low)
epsilon = 1e-06
gate_scale = -30.0
gate_offset = -3.5
masked_out = -1e+30
limits = (12, 16, 23, 32, 46, 64, 91)
highest = lax.Precision.HIGHEST

def bucket_table(queries, first_pos, keys_count):
    relative = jnp.arange(keys_count, dtype=jnp.int32)[None, :] - (first_pos + jnp.arange(queries, dtype=jnp.int32))[:, None]
    magnitude = jnp.abs(relative)
    beyond = jnp.zeros_like(magnitude)
    for bound_value in limits:
        beyond = beyond + (magnitude >= bound_value).astype(jnp.int32)
    inside = jnp.where(magnitude < 8, magnitude, 8 + beyond)
    return inside + 16 * (relative > 0).astype(jnp.int32)

def plain_norm(stream):
    return stream * lax.rsqrt(lax.optimization_barrier(jnp.mean(stream * stream, axis=-1, keepdims=True)) + epsilon)

def rms_norm(stream, gain_row):
    return plain_norm(stream) * gain_row

def gelu_tanh(values):
    return 0.5 * values * (1.0 + jnp.tanh(0.7978845608028654 * (values + 0.044715 * values ** 3)))

def product(left_side, right_side):
    return jnp.dot(left_side, right_side, precision=highest)

def encoder_layer(stream, weights, gain_one, gain_two, rel_bias, buckets, allowed, shift):
    w_query = weights[0:INNER]
    w_key = weights[INNER:2 * INNER]
    w_value = weights[2 * INNER:3 * INNER]
    w_out = weights[3 * INNER:4 * INNER]
    w_gelu = weights[4 * INNER:4 * INNER + FF]
    w_linear = weights[4 * INNER + FF:4 * INNER + 2 * FF]
    w_down = weights[4 * INNER + 2 * FF:]
    length_here = stream.shape[0]
    normed = low(rms_norm(stream, gain_one))
    queries = low_back(low(product(normed, w_query.T)))
    keys_all = low_back(low(product(normed, w_key.T)))
    values_all = low_back(low(product(normed, w_value.T)))

    def split_heads(values):
        return values.reshape(length_here, HEADS, HEAD_DIM).transpose(1, 0, 2)

    def one_head(head_items):
        head_query, head_key, head_value, column = head_items
        scores = low_back(product(head_query, head_key.T)) + column[buckets] + shift[None, :]
        scores = jnp.where(allowed, scores, masked_out)
        row_peak = lax.optimization_barrier(jnp.max(scores, axis=-1, keepdims=True))
        exponent = jnp.exp(scores - row_peak)
        softmax_weights = exponent / lax.optimization_barrier(jnp.sum(exponent, axis=-1, keepdims=True))
        return product(low(softmax_weights), head_value)
    mixed_heads = lax.map(jax.checkpoint(one_head), (split_heads(queries), split_heads(keys_all), split_heads(values_all), rel_bias.T))
    attended = low_back(low(mixed_heads.transpose(1, 0, 2).reshape(length_here, INNER)))
    middle = stream + low_back(product(attended, w_out))
    normed_two = low(rms_norm(middle, gain_two))
    up_gelu = low_back(product(normed_two, w_gelu.T))
    up_linear = low_back(product(normed_two, w_linear.T))
    hidden = low(gelu_tanh(up_gelu) * up_linear)
    return middle + low_back(product(hidden, w_down))

def encode(params, stream, allowed, buckets):
    rows_three, rows_four, norm_gains, gate_weight, rel_bias = params
    zero_shift = jnp.zeros((stream.shape[0],), stream.dtype)
    after_three = encoder_layer(stream, rows_three, norm_gains[0], norm_gains[1], rel_bias, buckets, allowed, zero_shift)
    gate_logit = lax.optimization_barrier(jnp.sum(plain_norm(after_three) * gate_weight, axis=-1)) + gate_offset
    gate_mask = gate_scale / (1.0 + jnp.exp(-gate_logit))
    after_four = encoder_layer(after_three, rows_four, norm_gains[2], norm_gains[3], rel_bias, buckets, allowed, low(gate_mask))
    return (after_four, gate_mask)

def reference(inputs, layer3_rows, layer4_rows, norm_gains, gate_weight, rel_bias, segment_ids, cotangent):
    params = (layer3_rows.astype(jnp.float32), layer4_rows.astype(jnp.float32), norm_gains, gate_weight, rel_bias)
    buckets = bucket_table(LENGTH, 0, LENGTH)

    def per_sequence(running, sequence_items):
        stream, sequence_segments, sequence_cotangent = sequence_items
        allowed = sequence_segments[:, None] == sequence_segments[None, :]

        def forward(param_tree, stream_in):
            return encode(param_tree, stream_in, allowed, buckets)
        (result, gate_mask), pullback = jax.vjp(forward, params, stream)
        grad_params, grad_stream = pullback((sequence_cotangent, jnp.zeros_like(gate_mask)))
        running = jax.tree.map(jnp.add, running, grad_params)
        return (running, (result, gate_mask, grad_stream))
    zeros_tree = jax.tree.map(jnp.zeros_like, params)
    grad_sums, (result, gate_mask, grad_input) = lax.scan(per_sequence, zeros_tree, (inputs, segment_ids, cotangent))
    return (result, gate_mask, grad_input, grad_sums[0], grad_sums[1], grad_sums[2], grad_sums[3], grad_sums[4])
```

```python
import functools

import jax
import jax.numpy as jnp
from jax import lax
from jax.experimental import pallas as pl
from jax.experimental.pallas import tpu as pltpu
from jax.sharding import PartitionSpec as P

HEADS = 6
PAIRS = 3
BLOCK = 128
WIDE = 2 * BLOCK
INNER = 384
BUCKETS = 32
OFFSETS = 5
masked_out = -1e30
limits = (12, 16, 23, 32, 46, 64, 91)
both_last = (((1,), (1,)), ((), ()))


def bucket_of(relative):
    magnitude = jnp.abs(relative)
    beyond = jnp.zeros_like(magnitude)
    for bound_value in limits:
        beyond = beyond + (magnitude >= bound_value).astype(jnp.int32)
    inside = jnp.where(magnitude < 8, magnitude, 8 + beyond)
    return inside + 16 * (relative > 0).astype(jnp.int32)


def near_buckets(offset):
    if offset < 0:
        return range(1, 16)
    if offset > 0:
        return range(17, 32)
    return range(0, 32)


def tile_buckets(offset, width):
    key_at = lax.broadcasted_iota(jnp.int32, (BLOCK, width), 0)
    query_at = lax.broadcasted_iota(jnp.int32, (BLOCK, width), 1) % BLOCK
    return bucket_of(offset * BLOCK + key_at - query_at)


def bias_body(table_ref, tiles_ref):
    head = pl.program_id(0)
    tiles_ref[0, 0] = jnp.full((BLOCK, BLOCK), table_ref[15, head], jnp.float32)
    tiles_ref[0, 4] = jnp.full((BLOCK, BLOCK), table_ref[31, head], jnp.float32)
    for offset in (-1, 0, 1):
        buckets = tile_buckets(offset, BLOCK)
        tile = jnp.zeros((BLOCK, BLOCK), jnp.float32)
        for bucket in near_buckets(offset):
            tile = jnp.where(buckets == bucket, table_ref[bucket, head], tile)
        tiles_ref[0, offset + 2] = tile


def bias_tiles(rel_bias):
    return pl.pallas_call(
        bias_body,
        grid=(HEADS,),
        in_specs=[pl.BlockSpec(memory_space=pltpu.SMEM)],
        out_specs=pl.BlockSpec((1, OFFSETS, BLOCK, BLOCK), lambda h: (h, 0, 0, 0)),
        out_shape=jax.ShapeDtypeStruct((HEADS, OFFSETS, BLOCK, BLOCK), jnp.float32),
        name="bias_tiles",
    )(rel_bias)


def lane_masks():
    lane = lax.broadcasted_iota(jnp.int32, (BLOCK, BLOCK), 1)
    low = jnp.where(lane < 64, 1.0, 0.0).astype(jnp.bfloat16)
    high = jnp.where(lane < 64, 0.0, 1.0).astype(jnp.bfloat16)
    return low, high


def stacked(block, masks):
    low, high = masks
    return jnp.concatenate([block * low, block * high], axis=0)


def pair_cols(pair):
    return slice(pair * BLOCK, (pair + 1) * BLOCK)


def value_cols(pair):
    return slice(INNER + pair * BLOCK, INNER + (pair + 1) * BLOCK)


def block_rows(block):
    return pl.ds(pl.multiple_of(block * BLOCK, BLOCK), BLOCK)


def fold(values):
    return values.reshape(BLOCK // 8, 8, WIDE)


def shift_tile(gated, rows, own_segment, segment_ref, shared_ref):
    same = segment_ref[rows, :] == own_segment
    inside = shared_ref[rows, 2 * INNER :].astype(jnp.float32) if gated else 0.0
    shift = jnp.where(same, inside, masked_out)
    return jnp.concatenate([shift, shift], axis=1)


def bias_pair(bias_ref, pair, offset):
    return jnp.concatenate([bias_ref[2 * pair, offset], bias_ref[2 * pair + 1, offset]], axis=1)


def pick_heads(wide):
    return jnp.concatenate([wide[:64, :BLOCK], wide[64:, BLOCK:]], axis=0)


def forward_body(gated, low_ref, high_ref, base_ref, *refs):
    query_ref, shared_ref, own_ref, segment_ref, bias_ref = refs[:5]
    mixed_ref, total_ref, turned_ref, score_ref = refs[5:]
    step = pl.program_id(0)
    key_blocks = shared_ref.shape[0] // BLOCK

    @pl.when(step == 0)
    def _():
        @pl.loop(0, key_blocks)
        def _(block):
            rows = block_rows(block)
            turned_ref[:, rows] = shared_ref[rows, INNER : 2 * INNER].T

    first, last = low_ref[step], high_ref[step]
    own_block = base_ref[0] + step
    own_segment = own_ref[0]
    masks = lane_masks()
    queries = [stacked(query_ref[:, pair_cols(pair)], masks) for pair in range(PAIRS)]

    def scores(block, peaks):
        rows = block_rows(block)
        shift = shift_tile(gated, rows, own_segment, segment_ref, shared_ref)
        offset = jnp.clip(block - own_block, -2, 2) + 2
        new_peaks = []
        for pair in range(PAIRS):
            score = lax.dot_general(
                shared_ref[rows, pair_cols(pair)],
                queries[pair],
                both_last,
                preferred_element_type=jnp.float32,
            )
            score = score + bias_pair(bias_ref, pair, offset) + shift
            score_ref[pair, block] = score
            new_peaks.append(jnp.maximum(peaks[pair], jnp.max(fold(score), axis=0)))
        return tuple(new_peaks)

    start = jnp.full((8, WIDE), -3e38, jnp.float32)
    peaks = lax.fori_loop(first, last, scores, (start,) * PAIRS)
    for pair in range(PAIRS):
        peak = jnp.max(peaks[pair], axis=0, keepdims=True)

        def mix(block, carry, pair=pair, peak=peak):
            total, mixed = carry
            weight = jnp.exp(score_ref[pair, block] - peak)
            total = total + jnp.sum(fold(weight), axis=0)
            mixed = mixed + jnp.dot(
                turned_ref[pair_cols(pair), block_rows(block)],
                weight.astype(jnp.bfloat16),
                preferred_element_type=jnp.float32,
            )
            return total, mixed

        zero = (jnp.zeros((8, WIDE), jnp.float32), jnp.zeros((BLOCK, WIDE), jnp.float32))
        total, mixed = lax.fori_loop(first, last, mix, zero)
        row_total = jnp.sum(total, axis=0, keepdims=True)
        mixed = pick_heads(mixed * (1.0 / row_total))
        mixed_ref[:, pair_cols(pair)] = mixed.T.astype(jnp.bfloat16)
        total_ref[0, pair : pair + 1, :] = peak + jnp.log(row_total)


def whole(shape):
    return pl.BlockSpec(shape, lambda i, *_: (0,) * len(shape), pipeline_mode=pl.Buffered(1))


def rows_spec(width):
    return pl.BlockSpec((BLOCK, width), lambda i, *_: (i, 0))


def attend_forward(queries, shared, context):
    lows, highs, base, own_rows, segment_wide, tiles = context
    tokens, (length, width) = queries.shape[0], shared.shape
    steps, key_blocks = tokens // BLOCK, length // BLOCK
    return pl.pallas_call(
        functools.partial(forward_body, width > 2 * INNER),
        grid_spec=pltpu.PrefetchScalarGridSpec(
            num_scalar_prefetch=3,
            grid=(steps,),
            in_specs=[
                rows_spec(INNER),
                whole((length, width)),
                pl.BlockSpec((1, 1, BLOCK), lambda i, *_: (i, 0, 0)),
                whole((length, BLOCK)),
                whole(tiles.shape),
            ],
            out_specs=[
                rows_spec(INNER),
                pl.BlockSpec((1, 8, WIDE), lambda i, *_: (i, 0, 0)),
            ],
            scratch_shapes=[
                pltpu.VMEM((INNER, length), jnp.bfloat16),
                pltpu.VMEM((PAIRS, key_blocks, BLOCK, WIDE), jnp.float32),
            ],
        ),
        out_shape=[
            jax.ShapeDtypeStruct((tokens, INNER), jnp.bfloat16),
            jax.ShapeDtypeStruct((steps, 8, WIDE), jnp.float32),
        ],
        compiler_params=pltpu.CompilerParams(vmem_limit_bytes=40 << 20),
        cost_estimate=pl.CostEstimate(
            flops=tokens * length * INNER * 4,
            bytes_accessed=8 << 20,
            transcendentals=tokens * length * 3,
        ),
        name="attend_forward",
    )(lows, highs, base, queries, shared, own_rows, segment_wide, tiles)


def backward_body(gated, low_ref, high_ref, base_ref, *refs):
    query_ref, grad_ref, shared_ref, own_ref, segment_ref, bias_ref, total_ref = refs[:7]
    grad_query_ref, grad_shared_ref, bucket_ref = refs[7:10]
    turned_ref, prob_ref, pull_ref, sum_ref, bias_sum_ref, turn_sum_ref = refs[10:]
    step = pl.program_id(0)
    key_blocks = shared_ref.shape[0] // BLOCK

    @pl.when(step == 0)
    def _():
        bias_sum_ref[...] = jnp.zeros_like(bias_sum_ref)

        @pl.loop(0, key_blocks)
        def _(block):
            rows = block_rows(block)
            turned_ref[:, rows] = shared_ref[rows, :INNER].T
            sum_ref[rows, :] = jnp.zeros((BLOCK, sum_ref.shape[1]), jnp.float32)

    first, last = low_ref[step], high_ref[step]
    own_block = base_ref[0] + step
    own_segment = own_ref[0]
    masks = lane_masks()
    queries = [stacked(query_ref[:, pair_cols(pair)], masks) for pair in range(PAIRS)]
    grads = [stacked(grad_ref[:, pair_cols(pair)], masks) for pair in range(PAIRS)]
    totals = [total_ref[0, pair : pair + 1, :] for pair in range(PAIRS)]

    def weights(block, deltas):
        rows = block_rows(block)
        shift = shift_tile(gated, rows, own_segment, segment_ref, shared_ref)
        offset = jnp.clip(block - own_block, -2, 2) + 2
        new_deltas = []
        for pair in range(PAIRS):
            cols = pair_cols(pair)
            score = lax.dot_general(
                shared_ref[rows, cols], queries[pair], both_last, preferred_element_type=jnp.float32
            )
            pull = lax.dot_general(
                shared_ref[rows, value_cols(pair)],
                grads[pair],
                both_last,
                preferred_element_type=jnp.float32,
            )
            prob = jnp.exp(score + bias_pair(bias_ref, pair, offset) + shift - totals[pair])
            prob_ref[pair, block] = prob
            pull_ref[pair, block] = pull
            sum_ref[rows, value_cols(pair)] += jnp.dot(
                prob.astype(jnp.bfloat16), grads[pair], preferred_element_type=jnp.float32
            )
            new_deltas.append(deltas[pair] + jnp.sum(fold(prob * pull), axis=0))
        return tuple(new_deltas)

    start = jnp.zeros((8, WIDE), jnp.float32)
    deltas = lax.fori_loop(first, last, weights, (start,) * PAIRS)
    deltas = [jnp.sum(delta, axis=0, keepdims=True) for delta in deltas]
    turn_sum_ref[...] = jnp.zeros_like(turn_sum_ref)

    @pl.loop(first, last)
    def _(block):
        rows = block_rows(block)
        offset = jnp.clip(block - own_block, -2, 2) + 2
        gate_part = jnp.zeros((BLOCK, BLOCK), jnp.float32)
        for pair in range(PAIRS):
            cols = pair_cols(pair)
            grad_score = prob_ref[pair, block] * (pull_ref[pair, block] - deltas[pair])
            bias_sum_ref[pair, offset] += grad_score
            if gated:
                gate_part = gate_part + (grad_score[:, :BLOCK] + grad_score[:, BLOCK:])
            score_low = grad_score.astype(jnp.bfloat16)
            sum_ref[rows, cols] += jnp.dot(
                score_low, queries[pair], preferred_element_type=jnp.float32
            )
            turn_sum_ref[pair] += jnp.dot(
                turned_ref[cols, rows], score_low, preferred_element_type=jnp.float32
            )
        if gated:
            sum_ref[rows, 2 * INNER :] += gate_part

    for pair in range(PAIRS):
        grad_query_ref[:, pair_cols(pair)] = pick_heads(turn_sum_ref[pair]).T.astype(jnp.bfloat16)

    @pl.when(step == pl.num_programs(0) - 1)
    def _():
        @pl.loop(0, key_blocks)
        def _(block):
            rows = block_rows(block)
            both = slice(0, 2 * INNER)
            grad_shared_ref[rows, both] = sum_ref[rows, both].astype(jnp.bfloat16)
            if gated:
                gate_total = jnp.sum(sum_ref[rows, 2 * INNER :], axis=1, keepdims=True)
                grad_shared_ref[rows, 2 * INNER :] = jnp.broadcast_to(
                    gate_total, (BLOCK, BLOCK)
                ).astype(jnp.bfloat16)

        tables = {offset: tile_buckets(offset, WIDE) for offset in (-1, 0, 1)}

        @pl.loop(0, PAIRS)
        def _(pair):
            for bucket in range(BUCKETS):
                part = jnp.zeros((8, WIDE), jnp.float32)
                for offset in (-1, 0, 1):
                    if bucket in near_buckets(offset):
                        chosen = jnp.where(
                            tables[offset] == bucket, bias_sum_ref[pair, offset + 2], 0.0
                        )
                        part = part + jnp.sum(fold(chosen), axis=0)
                if bucket == 15:
                    part = part + jnp.sum(fold(bias_sum_ref[pair, 0]), axis=0)
                if bucket == 31:
                    part = part + jnp.sum(fold(bias_sum_ref[pair, 4]), axis=0)
                bucket_ref[pair, bucket : bucket + 1, :] = jnp.sum(part, axis=0, keepdims=True)


def attend_backward(queries, grad_mixed, shared, log_total, context):
    lows, highs, base, own_rows, segment_wide, tiles = context
    tokens, (length, width) = queries.shape[0], shared.shape
    steps, key_blocks = tokens // BLOCK, length // BLOCK
    grad_query, grad_shared, bucket_sums = pl.pallas_call(
        functools.partial(backward_body, width > 2 * INNER),
        grid_spec=pltpu.PrefetchScalarGridSpec(
            num_scalar_prefetch=3,
            grid=(steps,),
            in_specs=[
                rows_spec(INNER),
                rows_spec(INNER),
                whole((length, width)),
                pl.BlockSpec((1, 1, BLOCK), lambda i, *_: (i, 0, 0)),
                whole((length, BLOCK)),
                whole(tiles.shape),
                pl.BlockSpec((1, 8, WIDE), lambda i, *_: (i, 0, 0)),
            ],
            out_specs=[
                rows_spec(INNER),
                whole((length, width)),
                whole((PAIRS, BUCKETS, WIDE)),
            ],
            scratch_shapes=[
                pltpu.VMEM((INNER, length), jnp.bfloat16),
                pltpu.VMEM((PAIRS, key_blocks, BLOCK, WIDE), jnp.float32),
                pltpu.VMEM((PAIRS, key_blocks, BLOCK, WIDE), jnp.float32),
                pltpu.VMEM((length, width), jnp.float32),
                pltpu.VMEM((PAIRS, OFFSETS, BLOCK, WIDE), jnp.float32),
                pltpu.VMEM((PAIRS, BLOCK, WIDE), jnp.float32),
            ],
        ),
        out_shape=[
            jax.ShapeDtypeStruct((tokens, INNER), jnp.bfloat16),
            jax.ShapeDtypeStruct((length, width), jnp.bfloat16),
            jax.ShapeDtypeStruct((PAIRS, BUCKETS, WIDE), jnp.float32),
        ],
        compiler_params=pltpu.CompilerParams(vmem_limit_bytes=48 << 20),
        cost_estimate=pl.CostEstimate(
            flops=tokens * length * INNER * 10,
            bytes_accessed=12 << 20,
            transcendentals=tokens * length * 3,
        ),
        name="attend_backward",
    )(lows, highs, base, queries, grad_mixed, shared, own_rows, segment_wide, tiles, log_total)
    table = jnp.sum(bucket_sums.reshape(PAIRS, BUCKETS, 2, BLOCK), axis=3)
    return grad_query, grad_shared, table.transpose(1, 0, 2).reshape(BUCKETS, HEADS)


def attention_context(segment_row, first_pos, tokens, rel_bias):
    length = segment_row.shape[0]
    steps = tokens // BLOCK
    own = lax.dynamic_slice_in_dim(segment_row, first_pos, tokens, 0).reshape(steps, 1, BLOCK)
    lows = jnp.sum(segment_row[None, :] < own[:, 0, :1], axis=1, dtype=jnp.int32) // BLOCK
    ends = jnp.sum(segment_row[None, :] <= own[:, 0, BLOCK - 1 :], axis=1, dtype=jnp.int32)
    highs = (ends + BLOCK - 1) // BLOCK
    base = (first_pos // BLOCK).astype(jnp.int32).reshape(1)
    segment_wide = jnp.broadcast_to(segment_row[:, None], (length, BLOCK))
    return lows, highs, base, own, segment_wide, bias_tiles(rel_bias)

HEAD_DIM = 64
FF = 3584
epsilon = 1e-06
gate_scale = -30.0
gate_offset = -3.5

def rms_forward(stream, gain_row):
    inverse = lax.rsqrt(jnp.mean(stream * stream, axis=1, keepdims=True) + epsilon)
    return (stream * inverse * gain_row, inverse)


def stream_backward(stream, inverse, scaled):
    return inverse * scaled - stream * inverse**3 * jnp.mean(scaled * stream, axis=1, keepdims=True)


def rms_backward(stream, inverse, gain_row, grad_normed):
    grad_gain = jnp.sum(grad_normed * stream * inverse, axis=0)
    return (stream_backward(stream, inverse, gain_row * grad_normed), grad_gain)


def gelu_tanh(values):
    return 0.5 * values * (1.0 + jnp.tanh(0.7978845608028654 * (values + 0.044715 * values**3)))


def times_rows(left_side, weight):
    return lax.dot_general(
        left_side, weight, (((1,), (1,)), ((), ())), preferred_element_type=jnp.float32
    )


def times_plain(left_side, weight):
    return jnp.dot(left_side, weight, preferred_element_type=jnp.float32)


def outer_sum(left_side, right_side):
    return lax.dot_general(
        left_side, right_side, (((0,), (0,)), ((), ())), preferred_element_type=jnp.float32
    )


def fetch_rows(local_rows):
    return lax.all_gather(local_rows, ("dp", "seq"), axis=0, tiled=True)


def reduce_rows(grad_rows):
    summed = lax.psum_scatter(grad_rows, ("dp", "seq"), scatter_dimension=0, tiled=True)
    return summed.astype(jnp.float32)


def share_keys(projected, gate_low):
    parts = [projected[:, INNER:]]
    if gate_low is not None:
        parts.append(jnp.broadcast_to(gate_low[:, None], (gate_low.shape[0], BLOCK)))
    return lax.all_gather(jnp.concatenate(parts, axis=1), "seq", axis=0, tiled=True)


def layer_forward(stream, gathered, gain_one, gain_two, gate_low, context):
    normed, inverse_one = rms_forward(stream, gain_one)
    normed_low = normed.astype(jnp.bfloat16)
    projected = times_rows(normed_low, gathered[: 3 * INNER]).astype(jnp.bfloat16)
    queries = projected[:, :INNER]
    shared = share_keys(projected, gate_low)
    attended, log_total = attend_forward(queries, shared, context)
    middle = stream + times_plain(attended, gathered[3 * INNER : 4 * INNER])
    normed_two, inverse_two = rms_forward(middle, gain_two)
    normed_two_low = normed_two.astype(jnp.bfloat16)
    up_both = times_rows(normed_two_low, gathered[4 * INNER : 4 * INNER + 2 * FF])
    up_gelu = up_both[:, :FF]
    up_linear = up_both[:, FF:]
    hidden = (gelu_tanh(up_gelu) * up_linear).astype(jnp.bfloat16)
    result = middle + times_plain(hidden, gathered[4 * INNER + 2 * FF :])
    kept = (
        stream,
        inverse_one,
        normed_low,
        queries,
        shared,
        attended,
        log_total,
        middle,
        inverse_two,
        normed_two_low,
        up_gelu,
        up_linear,
        hidden,
    )
    return (result, kept)


def layer_backward(grad_out, kept, gathered, gain_one, gain_two, context):
    (
        stream,
        inverse_one,
        normed_low,
        queries,
        shared,
        attended,
        log_total,
        middle,
        inverse_two,
        normed_two_low,
        up_gelu,
        up_linear,
        hidden,
    ) = kept
    w_down = gathered[4 * INNER + 2 * FF :]
    branch_low = grad_out.astype(jnp.bfloat16)
    grad_down = outer_sum(hidden, branch_low).astype(jnp.bfloat16)
    grad_hidden = times_rows(branch_low, w_down)
    activated, gelu_pullback = jax.vjp(gelu_tanh, up_gelu)
    grad_gelu = gelu_pullback(grad_hidden * up_linear)[0]
    grad_ffn_low = jnp.concatenate([grad_gelu, grad_hidden * activated], axis=1).astype(
        jnp.bfloat16
    )
    grad_ffn = outer_sum(grad_ffn_low, normed_two_low).astype(jnp.bfloat16)
    grad_normed_two = times_plain(grad_ffn_low, gathered[4 * INNER : 4 * INNER + 2 * FF])
    grad_middle, grad_gain_two = rms_backward(middle, inverse_two, gain_two, grad_normed_two)
    grad_middle = grad_out + grad_middle
    middle_low = grad_middle.astype(jnp.bfloat16)
    grad_attn_out = outer_sum(attended, middle_low).astype(jnp.bfloat16)
    grad_mixed = times_rows(middle_low, gathered[3 * INNER : 4 * INNER]).astype(jnp.bfloat16)
    grad_query, grad_shared, grad_table = attend_backward(
        queries, grad_mixed, shared, log_total, context
    )
    grad_own = lax.psum_scatter(grad_shared, "seq", scatter_dimension=0, tiled=True)
    grad_input_low = jnp.concatenate([grad_query, grad_own[:, : 2 * INNER]], axis=1)
    grad_gate = grad_own[:, 2 * INNER :].astype(jnp.float32)
    grad_input_rows = outer_sum(grad_input_low, normed_low).astype(jnp.bfloat16)
    grad_normed = times_plain(grad_input_low, gathered[: 3 * INNER])
    grad_stream, grad_gain_one = rms_backward(stream, inverse_one, gain_one, grad_normed)
    grad_rows = jnp.concatenate([grad_input_rows, grad_attn_out, grad_ffn, grad_down], axis=0)
    return (
        grad_middle + grad_stream,
        grad_rows,
        grad_table,
        grad_gate,
        grad_gain_one,
        grad_gain_two,
    )


def per_device(
    inputs, layer3_rows, layer4_rows, norm_gains, gate_weight, rel_bias, segment_ids, cotangent
):
    seqs_here, tokens_here, width = inputs.shape
    first_pos = lax.axis_index("seq") * tokens_here
    context = attention_context(segment_ids[0], first_pos, tokens_here, rel_bias)
    stream = inputs.reshape(tokens_here, width)
    gathered_three = fetch_rows(layer3_rows)
    after_three, kept_three = layer_forward(
        stream, gathered_three, norm_gains[0], norm_gains[1], None, context
    )
    gate_inverse = lax.rsqrt(jnp.mean(after_three * after_three, axis=1, keepdims=True) + epsilon)
    gate_normed = after_three * gate_inverse
    gate_logit = jnp.sum(gate_normed * gate_weight, axis=1) + gate_offset
    sigmoid_value = 1.0 / (1.0 + jnp.exp(-gate_logit))
    gate_mask = gate_scale * sigmoid_value
    gate_low = gate_mask.astype(jnp.bfloat16)
    gathered_four = fetch_rows(layer4_rows)
    after_four, kept_four = layer_forward(
        after_three, gathered_four, norm_gains[2], norm_gains[3], gate_low, context
    )
    grad_three_out, rows_four, table_four, grad_gate, gain_four_one, gain_four_two = layer_backward(
        cotangent.reshape(tokens_here, width),
        kept_four,
        gathered_four,
        norm_gains[2],
        norm_gains[3],
        context,
    )
    local_four = reduce_rows(rows_four)
    grad_logit = grad_gate[:, 0] * gate_scale * sigmoid_value * (1.0 - sigmoid_value)
    grad_gate_weight = jnp.sum(grad_logit[:, None] * gate_normed, axis=0)
    gate_stream = stream_backward(after_three, gate_inverse, grad_logit[:, None] * gate_weight)
    grad_three_out = grad_three_out + gate_stream
    grad_input, rows_three, table_three, unused, gain_three_one, gain_three_two = layer_backward(
        grad_three_out,
        kept_three,
        gathered_three,
        norm_gains[0],
        norm_gains[1],
        context,
    )
    local_three = reduce_rows(rows_three)
    gains_grad = jnp.stack([gain_three_one, gain_three_two, gain_four_one, gain_four_two])
    summed = lax.psum((gains_grad, grad_gate_weight, table_three + table_four), ("dp", "seq"))
    return (
        after_four.reshape(inputs.shape),
        gate_mask.reshape(seqs_here, tokens_here),
        grad_input.reshape(inputs.shape),
        local_three,
        local_four,
        summed[0],
        summed[1],
        summed[2],
    )


def solution(mesh):
    placed = (
        P("dp", "seq", None),
        P(("dp", "seq"), None),
        P(("dp", "seq"), None),
        P(),
        P(),
        P(),
        P("dp", None),
        P("dp", "seq", None),
    )
    return jax.shard_map(
        per_device,
        mesh=mesh,
        in_specs=placed,
        out_specs=(
            P("dp", "seq", None),
            P("dp", "seq"),
            P("dp", "seq", None),
            P(("dp", "seq"), None),
            P(("dp", "seq"), None),
            P(),
            P(),
            P(),
        ),
        check_vma=False,
    )
```

```python
import functools

import jax
import jax.numpy as jnp
from jax import lax
from jax.experimental import pallas as pl
from jax.experimental.pallas import tpu as pltpu
from jax.sharding import Mesh
from jax.sharding import PartitionSpec as P

HEADS = 6
PAIRS = 3
BLOCK = 128
WIDE = 2 * BLOCK
INNER = 384
BUCKETS = 32
FF = 3584
REACH = 799
HALO = 896
TILE = 256
ATTENTION_TILES = 4 * INNER // TILE
OFFSETS = 5
CHUNK = 384
CUTS = (0, 384, 768, 1152, 1472)
DEVICES = ("y", "x", "c", "z")
epsilon = 1e-06
gate_scale = -30.0
gate_offset = -3.5
masked_out = -1e30
limits = (12, 16, 23, 32, 46, 64, 91)
both_last = (((1,), (1,)), ((), ()))


def bucket_of(relative):
    magnitude = jnp.abs(relative)
    beyond = jnp.zeros_like(magnitude)
    for bound_value in limits:
        beyond = beyond + (magnitude >= bound_value).astype(jnp.int32)
    inside = jnp.where(magnitude < 8, magnitude, 8 + beyond)
    return inside + 16 * (relative > 0).astype(jnp.int32)


def near_buckets(offset):
    if offset < 0:
        return range(1, 16)
    if offset > 0:
        return range(17, 32)
    return range(0, 32)


def tile_buckets(offset, width):
    key_at = lax.broadcasted_iota(jnp.int32, (BLOCK, width), 0)
    query_at = lax.broadcasted_iota(jnp.int32, (BLOCK, width), 1) % BLOCK
    return bucket_of(offset * BLOCK + key_at - query_at)


def bias_body(table_ref, tiles_ref):
    head = pl.program_id(0)
    tiles_ref[0, 0] = jnp.full((BLOCK, BLOCK), table_ref[15, head], jnp.float32)
    tiles_ref[0, 4] = jnp.full((BLOCK, BLOCK), table_ref[31, head], jnp.float32)
    for offset in (-1, 0, 1):
        buckets = tile_buckets(offset, BLOCK)
        tile = jnp.zeros((BLOCK, BLOCK), jnp.float32)
        for bucket in near_buckets(offset):
            tile = jnp.where(buckets == bucket, table_ref[bucket, head], tile)
        tiles_ref[0, offset + 2] = tile


def bias_tiles(rel_bias):
    return pl.pallas_call(
        bias_body,
        grid=(HEADS,),
        in_specs=[pl.BlockSpec(memory_space=pltpu.SMEM)],
        out_specs=pl.BlockSpec((1, OFFSETS, BLOCK, BLOCK), lambda h: (h, 0, 0, 0)),
        out_shape=jax.ShapeDtypeStruct((HEADS, OFFSETS, BLOCK, BLOCK), jnp.float32),
        name="bias_tiles",
    )(rel_bias)


def lane_masks():
    lane = lax.broadcasted_iota(jnp.int32, (BLOCK, BLOCK), 1)
    low = jnp.where(lane < 64, 1.0, 0.0).astype(jnp.bfloat16)
    high = jnp.where(lane < 64, 0.0, 1.0).astype(jnp.bfloat16)
    return low, high


def stacked(block, masks):
    low, high = masks
    return jnp.concatenate([block * low, block * high], axis=0)


def pair_cols(pair):
    return slice(pair * BLOCK, (pair + 1) * BLOCK)


def value_cols(pair):
    return slice(INNER + pair * BLOCK, INNER + (pair + 1) * BLOCK)


def block_rows(block):
    return pl.ds(pl.multiple_of(block * BLOCK, BLOCK), BLOCK)


def fold(values):
    return values.reshape(BLOCK // 8, 8, WIDE)


def shift_tile(gated, rows, own_segment, segment_ref, shared_ref):
    same = segment_ref[rows, :] == own_segment
    inside = shared_ref[rows, 2 * INNER :].astype(jnp.float32) if gated else 0.0
    shift = jnp.where(same, inside, masked_out)
    return jnp.concatenate([shift, shift], axis=1)


def bias_pair(bias_ref, pair, offset):
    return jnp.concatenate([bias_ref[2 * pair, offset], bias_ref[2 * pair + 1, offset]], axis=1)


def pick_heads(wide):
    return jnp.concatenate([wide[:64, :BLOCK], wide[64:, BLOCK:]], axis=0)


def forward_body(gated, low_ref, high_ref, *refs):
    query_ref, shared_ref, own_ref, segment_ref, bias_ref = refs[:5]
    mixed_ref, total_ref, turned_ref, score_ref = refs[5:]
    step = pl.program_id(0)
    key_blocks = shared_ref.shape[0] // BLOCK

    @pl.when(step == 0)
    def _():
        @pl.loop(0, key_blocks)
        def _(block):
            rows = block_rows(block)
            turned_ref[:, rows] = shared_ref[rows, INNER : 2 * INNER].T

    first, last = low_ref[step], high_ref[step]
    own_block = HALO // BLOCK + step
    own_segment = own_ref[0]
    masks = lane_masks()
    queries = [stacked(query_ref[:, pair_cols(pair)], masks) for pair in range(PAIRS)]

    def scores(block, peaks):
        rows = block_rows(block)
        shift = shift_tile(gated, rows, own_segment, segment_ref, shared_ref)
        offset = jnp.clip(block - own_block, -2, 2) + 2
        new_peaks = []
        for pair in range(PAIRS):
            score = lax.dot_general(
                shared_ref[rows, pair_cols(pair)],
                queries[pair],
                both_last,
                preferred_element_type=jnp.float32,
            )
            score = score + bias_pair(bias_ref, pair, offset) + shift
            score_ref[pair, block] = score
            new_peaks.append(jnp.maximum(peaks[pair], jnp.max(fold(score), axis=0)))
        return tuple(new_peaks)

    start = jnp.full((8, WIDE), -3e38, jnp.float32)
    peaks = lax.fori_loop(first, last, scores, (start,) * PAIRS)
    for pair in range(PAIRS):
        peak = jnp.max(peaks[pair], axis=0, keepdims=True)

        def mix(block, carry, pair=pair, peak=peak):
            total, mixed = carry
            weight = jnp.exp(score_ref[pair, block] - peak)
            total = total + jnp.sum(fold(weight), axis=0)
            mixed = mixed + jnp.dot(
                turned_ref[pair_cols(pair), block_rows(block)],
                weight.astype(jnp.bfloat16),
                preferred_element_type=jnp.float32,
            )
            return total, mixed

        zero = (jnp.zeros((8, WIDE), jnp.float32), jnp.zeros((BLOCK, WIDE), jnp.float32))
        total, mixed = lax.fori_loop(first, last, mix, zero)
        row_total = jnp.sum(total, axis=0, keepdims=True)
        mixed = pick_heads(mixed * (1.0 / row_total))
        mixed_ref[:, pair_cols(pair)] = mixed.T.astype(jnp.bfloat16)
        total_ref[0, pair : pair + 1, :] = peak + jnp.log(row_total)


def whole(shape):
    return pl.BlockSpec(shape, lambda i, *_: (0,) * len(shape), pipeline_mode=pl.Buffered(1))


def rows_spec(width):
    return pl.BlockSpec((BLOCK, width), lambda i, *_: (i, 0))


def attend_forward(queries, shared, context):
    lows, highs, own_rows, segment_wide, tiles = context
    tokens, (length, width) = queries.shape[0], shared.shape
    steps, key_blocks = tokens // BLOCK, length // BLOCK
    return pl.pallas_call(
        functools.partial(forward_body, width > 2 * INNER),
        grid_spec=pltpu.PrefetchScalarGridSpec(
            num_scalar_prefetch=2,
            grid=(steps,),
            in_specs=[
                rows_spec(INNER),
                whole((length, width)),
                pl.BlockSpec((1, 1, BLOCK), lambda i, *_: (i, 0, 0)),
                whole((length, BLOCK)),
                whole(tiles.shape),
            ],
            out_specs=[
                rows_spec(INNER),
                pl.BlockSpec((1, 8, WIDE), lambda i, *_: (i, 0, 0)),
            ],
            scratch_shapes=[
                pltpu.VMEM((INNER, length), jnp.bfloat16),
                pltpu.VMEM((PAIRS, key_blocks, BLOCK, WIDE), jnp.float32),
            ],
        ),
        out_shape=[
            jax.ShapeDtypeStruct((tokens, INNER), jnp.bfloat16),
            jax.ShapeDtypeStruct((steps, 8, WIDE), jnp.float32),
        ],
        compiler_params=pltpu.CompilerParams(vmem_limit_bytes=40 << 20),
        cost_estimate=pl.CostEstimate(
            flops=tokens * length * INNER * 4,
            bytes_accessed=8 << 20,
            transcendentals=tokens * length * 3,
        ),
        name="attend_forward",
    )(lows, highs, queries, shared, own_rows, segment_wide, tiles)


def backward_body(gated, low_ref, high_ref, *refs):
    query_ref, grad_ref, shared_ref, own_ref, segment_ref, bias_ref, total_ref = refs[:7]
    grad_query_ref, grad_shared_ref, bucket_ref = refs[7:10]
    turned_ref, prob_ref, pull_ref, sum_ref, bias_sum_ref, turn_sum_ref = refs[10:]
    step = pl.program_id(0)
    key_blocks = shared_ref.shape[0] // BLOCK

    @pl.when(step == 0)
    def _():
        bias_sum_ref[...] = jnp.zeros_like(bias_sum_ref)

        @pl.loop(0, key_blocks)
        def _(block):
            rows = block_rows(block)
            turned_ref[:, rows] = shared_ref[rows, :INNER].T
            sum_ref[rows, :] = jnp.zeros((BLOCK, sum_ref.shape[1]), jnp.float32)

    first, last = low_ref[step], high_ref[step]
    own_block = HALO // BLOCK + step
    own_segment = own_ref[0]
    masks = lane_masks()
    queries = [stacked(query_ref[:, pair_cols(pair)], masks) for pair in range(PAIRS)]
    grads = [stacked(grad_ref[:, pair_cols(pair)], masks) for pair in range(PAIRS)]
    totals = [total_ref[0, pair : pair + 1, :] for pair in range(PAIRS)]

    def weights(block, deltas):
        rows = block_rows(block)
        shift = shift_tile(gated, rows, own_segment, segment_ref, shared_ref)
        offset = jnp.clip(block - own_block, -2, 2) + 2
        new_deltas = []
        for pair in range(PAIRS):
            cols = pair_cols(pair)
            score = lax.dot_general(
                shared_ref[rows, cols], queries[pair], both_last, preferred_element_type=jnp.float32
            )
            pull = lax.dot_general(
                shared_ref[rows, value_cols(pair)],
                grads[pair],
                both_last,
                preferred_element_type=jnp.float32,
            )
            prob = jnp.exp(score + bias_pair(bias_ref, pair, offset) + shift - totals[pair])
            prob_ref[pair, block] = prob
            pull_ref[pair, block] = pull
            sum_ref[rows, value_cols(pair)] += jnp.dot(
                prob.astype(jnp.bfloat16), grads[pair], preferred_element_type=jnp.float32
            )
            new_deltas.append(deltas[pair] + jnp.sum(fold(prob * pull), axis=0))
        return tuple(new_deltas)

    start = jnp.zeros((8, WIDE), jnp.float32)
    deltas = lax.fori_loop(first, last, weights, (start,) * PAIRS)
    deltas = [jnp.sum(delta, axis=0, keepdims=True) for delta in deltas]
    turn_sum_ref[...] = jnp.zeros_like(turn_sum_ref)

    @pl.loop(first, last)
    def _(block):
        rows = block_rows(block)
        offset = jnp.clip(block - own_block, -2, 2) + 2
        gate_part = jnp.zeros((BLOCK, BLOCK), jnp.float32)
        for pair in range(PAIRS):
            cols = pair_cols(pair)
            grad_score = prob_ref[pair, block] * (pull_ref[pair, block] - deltas[pair])
            bias_sum_ref[pair, offset] += grad_score
            if gated:
                gate_part = gate_part + (grad_score[:, :BLOCK] + grad_score[:, BLOCK:])
            score_low = grad_score.astype(jnp.bfloat16)
            sum_ref[rows, cols] += jnp.dot(
                score_low, queries[pair], preferred_element_type=jnp.float32
            )
            turn_sum_ref[pair] += jnp.dot(
                turned_ref[cols, rows], score_low, preferred_element_type=jnp.float32
            )
        if gated:
            sum_ref[rows, 2 * INNER :] += gate_part

    for pair in range(PAIRS):
        grad_query_ref[:, pair_cols(pair)] = pick_heads(turn_sum_ref[pair]).T.astype(jnp.bfloat16)

    @pl.when(step == pl.num_programs(0) - 1)
    def _():
        @pl.loop(0, key_blocks)
        def _(block):
            rows = block_rows(block)
            both = slice(0, 2 * INNER)
            grad_shared_ref[rows, both] = sum_ref[rows, both].astype(jnp.bfloat16)
            if gated:
                gate_total = jnp.sum(sum_ref[rows, 2 * INNER :], axis=1, keepdims=True)
                grad_shared_ref[rows, 2 * INNER :] = jnp.broadcast_to(
                    gate_total, (BLOCK, BLOCK)
                ).astype(jnp.bfloat16)

        tables = {offset: tile_buckets(offset, WIDE) for offset in (-1, 0, 1)}

        @pl.loop(0, PAIRS)
        def _(pair):
            for bucket in range(BUCKETS):
                part = jnp.zeros((8, WIDE), jnp.float32)
                for offset in (-1, 0, 1):
                    if bucket in near_buckets(offset):
                        chosen = jnp.where(
                            tables[offset] == bucket, bias_sum_ref[pair, offset + 2], 0.0
                        )
                        part = part + jnp.sum(fold(chosen), axis=0)
                if bucket == 15:
                    part = part + jnp.sum(fold(bias_sum_ref[pair, 0]), axis=0)
                if bucket == 31:
                    part = part + jnp.sum(fold(bias_sum_ref[pair, 4]), axis=0)
                bucket_ref[pair, bucket : bucket + 1, :] = jnp.sum(part, axis=0, keepdims=True)


def attend_backward(queries, grad_mixed, shared, log_total, context):
    lows, highs, own_rows, segment_wide, tiles = context
    tokens, (length, width) = queries.shape[0], shared.shape
    steps, key_blocks = tokens // BLOCK, length // BLOCK
    grad_query, grad_shared, bucket_sums = pl.pallas_call(
        functools.partial(backward_body, width > 2 * INNER),
        grid_spec=pltpu.PrefetchScalarGridSpec(
            num_scalar_prefetch=2,
            grid=(steps,),
            in_specs=[
                rows_spec(INNER),
                rows_spec(INNER),
                whole((length, width)),
                pl.BlockSpec((1, 1, BLOCK), lambda i, *_: (i, 0, 0)),
                whole((length, BLOCK)),
                whole(tiles.shape),
                pl.BlockSpec((1, 8, WIDE), lambda i, *_: (i, 0, 0)),
            ],
            out_specs=[
                rows_spec(INNER),
                whole((length, width)),
                whole((PAIRS, BUCKETS, WIDE)),
            ],
            scratch_shapes=[
                pltpu.VMEM((INNER, length), jnp.bfloat16),
                pltpu.VMEM((PAIRS, key_blocks, BLOCK, WIDE), jnp.float32),
                pltpu.VMEM((PAIRS, key_blocks, BLOCK, WIDE), jnp.float32),
                pltpu.VMEM((length, width), jnp.float32),
                pltpu.VMEM((PAIRS, OFFSETS, BLOCK, WIDE), jnp.float32),
                pltpu.VMEM((PAIRS, BLOCK, WIDE), jnp.float32),
            ],
        ),
        out_shape=[
            jax.ShapeDtypeStruct((tokens, INNER), jnp.bfloat16),
            jax.ShapeDtypeStruct((length, width), jnp.bfloat16),
            jax.ShapeDtypeStruct((PAIRS, BUCKETS, WIDE), jnp.float32),
        ],
        compiler_params=pltpu.CompilerParams(vmem_limit_bytes=48 << 20),
        cost_estimate=pl.CostEstimate(
            flops=tokens * length * INNER * 10,
            bytes_accessed=12 << 20,
            transcendentals=tokens * length * 3,
        ),
        name="attend_backward",
    )(lows, highs, queries, grad_mixed, shared, own_rows, segment_wide, tiles, log_total)
    table = jnp.sum(bucket_sums.reshape(PAIRS, BUCKETS, 2, BLOCK), axis=3)
    return grad_query, grad_shared, table.transpose(1, 0, 2).reshape(BUCKETS, HEADS)


def attention_context(segment_row, first_pos, tokens, rel_bias):
    steps = tokens // BLOCK
    padded = jnp.pad(segment_row, (HALO, 0), constant_values=-1)
    padded = jnp.pad(padded, (0, HALO), constant_values=1000)
    window = lax.dynamic_slice_in_dim(padded, first_pos, tokens + 2 * HALO, 0)
    own = window[HALO : HALO + tokens].reshape(steps, 1, BLOCK)
    lows = jnp.sum(window[None, :] < own[:, 0, :1], axis=1, dtype=jnp.int32) // BLOCK
    ends = jnp.sum(window[None, :] <= own[:, 0, BLOCK - 1 :], axis=1, dtype=jnp.int32)
    highs = (ends + BLOCK - 1) // BLOCK
    segment_wide = jnp.broadcast_to(window[:, None], (window.shape[0], BLOCK))
    return lows, highs, own, segment_wide, bias_tiles(rel_bias)


def rms_forward(stream, gain_row):
    inverse = lax.rsqrt(jnp.mean(stream * stream, axis=1, keepdims=True) + epsilon)
    return (stream * inverse * gain_row, inverse)


def stream_backward(stream, inverse, scaled):
    return inverse * scaled - stream * inverse**3 * jnp.mean(scaled * stream, axis=1, keepdims=True)


def rms_backward(stream, inverse, gain_row, grad_normed):
    grad_gain = jnp.sum(grad_normed * stream * inverse, axis=0)
    return (stream_backward(stream, inverse, gain_row * grad_normed), grad_gain)


def gelu_tanh(values):
    return 0.5 * values * (1.0 + jnp.tanh(0.7978845608028654 * (values + 0.044715 * values**3)))


def times_rows(left_side, weight):
    return lax.dot_general(
        left_side, weight, (((1,), (1,)), ((), ())), preferred_element_type=jnp.float32
    )


def times_plain(left_side, weight):
    return jnp.dot(left_side, weight, preferred_element_type=jnp.float32)


def outer_sum(left_side, right_side):
    return lax.dot_general(
        left_side, right_side, (((0,), (0,)), ((), ())), preferred_element_type=jnp.float32
    )


def shift(value, axis, amount):
    count = lax.axis_size(axis)
    return lax.ppermute(value, axis, [(i, (i + amount) % count) for i in range(count)])


def slide(value, amount):
    count = lax.axis_size("z")
    pairs = [(i, i + amount) for i in range(count) if 0 <= i + amount < count]
    return lax.ppermute(value, "z", pairs)


def halo_pieces(tokens):
    pieces = []
    distance, covered = 1, 0
    while covered < HALO:
        span = min(tokens, HALO - covered)
        needed = min(span, -(-(REACH - covered) // 16) * 16)
        pieces.append((distance, span, needed))
        distance, covered = distance + 1, covered + span
    return pieces


def with_neighbours(own):
    tokens = own.shape[0]
    before, after = [], []
    for distance, span, needed in halo_pieces(tokens):
        if distance < lax.axis_size("z"):
            left = slide(own[tokens - needed :], distance)
            right = slide(own[:needed], -distance)
            before.append(jnp.pad(left, ((span - needed, 0), (0, 0))))
            after.append(jnp.pad(right, ((0, span - needed), (0, 0))))
        else:
            empty = jnp.zeros((span, own.shape[1]), own.dtype)
            before.append(empty)
            after.append(empty)
    return jnp.concatenate(before[::-1] + [own] + after, axis=0)


def from_neighbours(window, tokens):
    total = window[HALO : HALO + tokens].astype(jnp.float32)
    covered = 0
    for distance, span, needed in halo_pieces(tokens):
        if distance < lax.axis_size("z"):
            left_end = HALO - covered
            right_start = HALO + tokens + covered
            back = slide(window[left_end - needed : left_end], -distance)
            ahead = slide(window[right_start : right_start + needed], distance)
            total = total + jnp.pad(
                back.astype(jnp.float32), ((tokens - needed, 0), (0, 0))
            )
            total = total + jnp.pad(ahead.astype(jnp.float32), ((0, tokens - needed), (0, 0)))
        covered += span
    return total


def sum_everywhere(value):
    for axis in ("c", "x", "y", "z"):
        count = lax.axis_size(axis)
        bit = 1
        while bit < count:
            value = value + lax.ppermute(value, axis, [(i, i ^ bit) for i in range(count)])
            bit *= 2
    return value


def pick(value, index, axis):
    return lax.dynamic_index_in_dim(value, index, axis, keepdims=False)


def stage_sends(value, axis_name, axis):
    count, here = lax.axis_size(axis_name), lax.axis_index(axis_name)
    return [pick(value, (here + k) % count, axis) for k in range(1, count)]


def stage_moves(sends, axis_name):
    return [shift(sent, axis_name, k + 1) for k, sent in enumerate(sends)]


def grad_tiles_body(phase, attended, core_ref, *refs):
    up_ref, hidden_ref, normed_ref, branch_ref = refs[:4]
    outs = refs[-4:]
    tile = source_tile(phase, pl.program_id(0), core_ref)

    def put(*products):
        turned = [(left[...].T, right) for left, right in products]
        for out, start, end in zip(outs, CUTS[:-1], CUTS[1:]):
            total = jnp.zeros((TILE, end - start), jnp.float32)
            for left, right in turned:
                total = total + jnp.dot(
                    left, right[:, start:end], preferred_element_type=jnp.float32
                )
            out[:, : end - start] = total.astype(jnp.bfloat16)
            if end - start < CHUNK:
                out[:, end - start :] = jnp.zeros((TILE, CHUNK - end + start), jnp.bfloat16)

    @pl.when(tile < ATTENTION_TILES)
    def _():
        if attended:
            first_ref, second_ref, first_side_ref, second_side_ref = refs[4:8]
            put((first_ref, first_side_ref), (second_ref, second_side_ref))
        else:
            put()

    @pl.when((tile >= ATTENTION_TILES) & (tile < ATTENTION_TILES + 2 * FF // TILE))
    def _():
        put((up_ref, normed_ref))

    @pl.when(tile >= ATTENTION_TILES + 2 * FF // TILE)
    def _():
        put((hidden_ref, branch_ref))


def source_tile(phase, step, core_ref):
    core = core_ref[0] if phase else 1 - core_ref[0]
    unit = core_ref[1]
    return (step // unit) * 2 * unit + core * unit + step % unit


def grad_tiles(phase, up_grads, hidden, normed_two, branch, attention):
    tokens, width = normed_two.shape
    rows = 4 * INNER + 3 * FF
    steps = rows // TILE // 2
    unit = steps // (lax.axis_size("y") * lax.axis_size("x"))
    core = jnp.stack([lax.axis_index("c").astype(jnp.int32), jnp.int32(unit)])
    up_tiles = 2 * FF // TILE

    def up_map(step, core_ref):
        tile = source_tile(phase, step, core_ref)
        return 0, jnp.clip(tile - ATTENTION_TILES, 0, up_tiles - 1)

    def hidden_map(step, core_ref):
        tile = source_tile(phase, step, core_ref)
        return 0, jnp.clip(tile - ATTENTION_TILES - up_tiles, 0, FF // TILE - 1)

    def attention_map(step, core_ref):
        return 0, jnp.minimum(source_tile(phase, step, core_ref), ATTENTION_TILES - 1)

    side = pl.BlockSpec((tokens, width), lambda *_: (0, 0), pipeline_mode=pl.Buffered(1))
    column = (tokens, TILE)
    operands = [up_grads, hidden, normed_two, branch]
    in_specs = [pl.BlockSpec(column, up_map), pl.BlockSpec(column, hidden_map), side, side]
    if attention is not None:
        operands += attention
        in_specs += [
            pl.BlockSpec(column, attention_map),
            pl.BlockSpec(column, attention_map),
            side,
            side,
        ]
    results = pl.pallas_call(
        functools.partial(grad_tiles_body, phase, attention is not None),
        grid_spec=pltpu.PrefetchScalarGridSpec(
            num_scalar_prefetch=1,
            grid=(steps,),
            in_specs=in_specs,
            out_specs=[pl.BlockSpec((TILE, CHUNK), lambda i, *_: (i, 0))] * 4,
        ),
        out_shape=[jax.ShapeDtypeStruct((rows // 2, CHUNK), jnp.bfloat16)] * 4,
        compiler_params=pltpu.CompilerParams(vmem_limit_bytes=40 << 20),
        cost_estimate=pl.CostEstimate(
            flops=tokens * rows * width,
            bytes_accessed=2 * rows * width,
            transcendentals=0,
        ),
        name="grad_tiles",
    )(core, *operands)
    return list(results)


def split_body(place_ref, kept_ref, moved_ref, left_ref, left_send_ref, right_ref, right_send_ref):
    i, j = pl.program_id(0), pl.program_id(1)
    both = kept_ref[0, 0].astype(jnp.float32) + moved_ref[0, 0].astype(jnp.float32)
    both = both.astype(jnp.bfloat16)
    left, right = both[:, 0], both[:, 1]

    @pl.when(i < pl.num_programs(0) - 1)
    def _():
        left_send_ref[0, 0] = left

    @pl.when(i == pl.num_programs(0) - 1)
    def _():
        left_ref[0] = left

    @pl.when(j < pl.num_programs(1) - 1)
    def _():
        right_send_ref[0, 0] = right

    @pl.when(j == pl.num_programs(1) - 1)
    def _():
        right_ref[0] = right


def split_sums(kept, moved):
    size_y, size_x, size_z = (lax.axis_size(axis) for axis in ("y", "x", "z"))
    chunk = kept.shape[-1]
    shape = (size_y, size_x, size_z, 2, kept.size // (2 * size_y * size_x * size_z * chunk), chunk)
    piece = shape[2:3] + shape[4:]
    place = jnp.stack([lax.axis_index("y"), lax.axis_index("x")]).astype(jnp.int32)
    zeros = (0, 0, 0)

    def row_of(i, place_ref):
        return (place_ref[0] + 1 + i) % size_y

    def column_of(j, place_ref):
        return (place_ref[1] + 1 + j) % size_x

    def in_map(i, j, place_ref):
        return (row_of(i, place_ref), column_of(j, place_ref), 0) + zeros

    def left_map(i, j, place_ref):
        return (jnp.where(i == size_y - 1, column_of(j, place_ref), column_of(0, place_ref)),) + zeros

    def left_send_map(i, j, place_ref):
        column = jnp.where(i < size_y - 1, column_of(j, place_ref), place_ref[1])
        return (jnp.minimum(i, size_y - 2), column) + zeros

    def right_map(i, j, place_ref):
        return (row_of(i, place_ref),) + zeros

    def right_send_map(i, j, place_ref):
        return (jnp.minimum(j, size_x - 2), row_of(i, place_ref)) + zeros

    block = pl.BlockSpec((1, 1) + shape[2:], in_map)
    left, left_sends, right, right_sends = pl.pallas_call(
        split_body,
        grid_spec=pltpu.PrefetchScalarGridSpec(
            num_scalar_prefetch=1,
            grid=(size_y, size_x),
            in_specs=[block, block],
            out_specs=[
                pl.BlockSpec((1,) + piece, left_map),
                pl.BlockSpec((1, 1) + piece, left_send_map),
                pl.BlockSpec((1,) + piece, right_map),
                pl.BlockSpec((1, 1) + piece, right_send_map),
            ],
        ),
        out_shape=[
            jax.ShapeDtypeStruct((size_x,) + piece, jnp.bfloat16),
            jax.ShapeDtypeStruct((size_y - 1, size_x) + piece, jnp.bfloat16),
            jax.ShapeDtypeStruct((size_y,) + piece, jnp.bfloat16),
            jax.ShapeDtypeStruct((size_x - 1, size_y) + piece, jnp.bfloat16),
        ],
        compiler_params=pltpu.CompilerParams(vmem_limit_bytes=32 << 20),
        cost_estimate=pl.CostEstimate(
            flops=kept.size, bytes_accessed=6 * kept.size, transcendentals=0
        ),
        name="split_sums",
    )(place, kept.reshape(shape), moved.reshape(shape))
    return (
        left,
        [left_sends[k] for k in range(size_y - 1)],
        right,
        [right_sends[k] for k in range(size_x - 1)],
    )


def tied(first, second):
    return lax.optimization_barrier((first, second))


class Scatter:
    def __init__(self):
        self.waiting, self.flying, self.results = [], [], {}

    def push(self, name, kept, moved):
        self.waiting.append((name, kept, moved))

    def busy(self):
        return bool(self.waiting or self.flying)

    def step(self, values, enter=1):
        flying = [item[2:] for item in self.flying]
        entering, self.waiting = self.waiting[:enter], self.waiting[enter:]
        flying, values = tied(flying, values)
        moves = []
        for (name, stage, *_), (left, left_moved, right, right_moved) in zip(self.flying, flying):
            if stage == 1:
                left = total_of(left, left_moved)
                right = total_of(right, right_moved)
                left_sends, right_sends = stage_sends(left, "x", 0), stage_sends(right, "y", 0)
                left = pick(left, lax.axis_index("x"), 0)
                right = pick(right, lax.axis_index("y"), 0)
                moves.append((name, 2, left, left_sends, right, right_sends))
            elif stage == 2:
                left = total_of(left, left_moved)
                right = total_of(right, right_moved)
                sends = [
                    jnp.concatenate(pair, axis=0)
                    for pair in zip(stage_sends(left, "z", 0), stage_sends(right, "z", 0))
                ]
                here = lax.axis_index("z")
                own = jnp.concatenate([pick(left, here, 0), pick(right, here, 0)], axis=0)
                moves.append((name, 3, own, sends, own[:0], []))
            else:
                total = left.astype(jnp.float32)
                for part in left_moved:
                    total = total + part.astype(jnp.float32)
                self.results[name] = total
        for name, kept, moved in entering:
            left, left_sends, right, right_sends = split_sums(kept, moved)
            moves.append((name, 1, left, left_sends, right, right_sends))
        arrays, values = tied([item[2:] for item in moves], values)
        self.flying = []
        for (name, stage, *_), (left, left_sends, right, right_sends) in zip(moves, arrays):
            first, second = {1: ("y", "x"), 2: ("x", "y"), 3: ("z", "z")}[stage]
            left_moved = stage_moves(left_sends, first)
            right_moved = stage_moves(right_sends, second)
            self.flying.append((name, stage, left, left_moved, right, right_moved))
        return values


def total_of(value, moved):
    total = value.astype(jnp.float32)
    for part in moved:
        total = total + part.astype(jnp.float32)
    return total.astype(jnp.bfloat16)


def fetch_rows(local_rows):
    return lax.all_gather(local_rows, DEVICES, axis=0, tiled=True)


def share_keys(projected, gate_low):
    parts = [projected[:, INNER:]]
    if gate_low is not None:
        parts.append(jnp.broadcast_to(gate_low[:, None], (gate_low.shape[0], BLOCK)))
    return with_neighbours(jnp.concatenate(parts, axis=1))


def layer_forward(stream, gathered, gain_one, gain_two, gate_low, context):
    normed, inverse_one = rms_forward(stream, gain_one)
    normed_low = normed.astype(jnp.bfloat16)
    projected = times_rows(normed_low, gathered[: 3 * INNER]).astype(jnp.bfloat16)
    queries = projected[:, :INNER]
    shared = share_keys(projected, gate_low)
    attended, log_total = attend_forward(queries, shared, context)
    middle = stream + times_plain(attended, gathered[3 * INNER : 4 * INNER])
    normed_two, inverse_two = rms_forward(middle, gain_two)
    normed_two_low = normed_two.astype(jnp.bfloat16)
    up_both = times_rows(normed_two_low, gathered[4 * INNER : 4 * INNER + 2 * FF])
    up_gelu = up_both[:, :FF]
    up_linear = up_both[:, FF:]
    hidden = (gelu_tanh(up_gelu) * up_linear).astype(jnp.bfloat16)
    result = middle + times_plain(hidden, gathered[4 * INNER + 2 * FF :])
    kept = (
        stream,
        inverse_one,
        normed_low,
        queries,
        shared,
        attended,
        log_total,
        middle,
        inverse_two,
        normed_two_low,
        up_gelu,
        up_linear,
        hidden,
    )
    return (result, kept)


def layer_backward(
    grad_out, kept, gathered, gain_one, gain_two, context, waiting, scatter, name, before_tiles
):
    (
        stream,
        inverse_one,
        normed_low,
        queries,
        shared,
        attended,
        log_total,
        middle,
        inverse_two,
        normed_two_low,
        up_gelu,
        up_linear,
        hidden,
    ) = kept
    w_down = gathered[4 * INNER + 2 * FF :]
    branch_low = grad_out.astype(jnp.bfloat16)
    grad_hidden = times_rows(branch_low, w_down)
    activated, gelu_pullback = jax.vjp(gelu_tanh, up_gelu)
    grad_gelu = gelu_pullback(grad_hidden * up_linear)[0]
    grad_ffn_low = jnp.concatenate([grad_gelu, grad_hidden * activated], axis=1).astype(
        jnp.bfloat16
    )
    if before_tiles:
        grad_ffn_low, branch_low = scatter.step((grad_ffn_low, branch_low))
    sent = grad_tiles(0, grad_ffn_low, hidden, normed_two_low, branch_low, waiting)
    moved = [shift(part, "c", 1) for part in sent]
    grad_ffn_low, branch_low, sent = lax.optimization_barrier((grad_ffn_low, branch_low, sent))
    own = grad_tiles(1, grad_ffn_low, hidden, normed_two_low, branch_low, waiting)
    for k in range(4):
        scatter.push((name, k), own[k], moved[k])
    grad_ffn_low, grad_out = scatter.step((grad_ffn_low, grad_out))
    grad_normed_two = times_plain(grad_ffn_low, gathered[4 * INNER : 4 * INNER + 2 * FF])
    grad_middle, grad_gain_two = rms_backward(middle, inverse_two, gain_two, grad_normed_two)
    grad_middle = grad_out + grad_middle
    middle_low = grad_middle.astype(jnp.bfloat16)
    grad_mixed = times_rows(middle_low, gathered[3 * INNER : 4 * INNER]).astype(jnp.bfloat16)
    grad_mixed, grad_middle, middle_low = scatter.step((grad_mixed, grad_middle, middle_low))
    grad_query, grad_shared, grad_table = attend_backward(
        queries, grad_mixed, shared, log_total, context
    )
    grad_query, grad_shared, grad_table = scatter.step((grad_query, grad_shared, grad_table))
    grad_own = from_neighbours(grad_shared, queries.shape[0])
    grad_gate = grad_own[:, 2 * INNER :]
    grad_input_low = jnp.concatenate(
        [grad_query, grad_own[:, : 2 * INNER].astype(jnp.bfloat16)], axis=1
    )
    grad_normed = times_plain(grad_input_low, gathered[: 3 * INNER])
    grad_stream, grad_gain_one = rms_backward(stream, inverse_one, gain_one, grad_normed)
    grad_stream = grad_middle + grad_stream
    attention = [
        jnp.pad(grad_input_low, ((0, 0), (0, INNER))),
        jnp.pad(attended, ((0, 0), (3 * INNER, 0))),
        normed_low,
        middle_low,
    ]
    grad_stream, attention = scatter.step((grad_stream, attention))
    return (
        grad_stream,
        grad_table,
        grad_gate,
        grad_gain_one,
        grad_gain_two,
        attention,
    )


def push_last_attention(attention, scatter):
    first, second, first_side, second_side = attention
    rows = outer_sum(first, first_side) + outer_sum(second, second_side)
    size_y, size_x, size_z = (lax.axis_size(axis) for axis in ("y", "x", "z"))
    core = lax.axis_index("c")
    width = rows.shape[1]
    owners, part = owner_parts()
    rows = rows.astype(jnp.bfloat16).reshape(owners, size_z, size_y, size_x, 2, -1, width)
    rows = rows.transpose(2, 3, 4, 1, 0, 5, 6).reshape(size_y, size_x, 2, size_z, part, width)
    kept, sent = pick(rows, core, 2), pick(rows, 1 - core, 2)
    scatter.push("late", kept, shift(sent, "c", 1))


def owner_parts():
    size_y, size_x, size_z = (lax.axis_size(axis) for axis in ("y", "x", "z"))
    block = (4 * INNER + 3 * FF) // (size_y * size_x * 2 * size_z)
    owners = 4 * INNER // (block * size_z)
    return owners, block * owners // (size_y * size_x * 2)


def bring_to_owners(mine):
    size_y, size_x = lax.axis_size("y"), lax.axis_size("x")
    owners, part = owner_parts()
    width = mine.shape[-1]
    mine = mine.astype(jnp.bfloat16)[None]
    for axis in ("c", "x", "y"):
        count, here = lax.axis_size(axis), lax.axis_index(axis)
        gathered = jnp.zeros((count,) + mine.shape, mine.dtype)
        gathered = lax.dynamic_update_index_in_dim(gathered, mine, here, 0)
        for k in range(1, count):
            gathered = lax.dynamic_update_index_in_dim(
                gathered, shift(mine, axis, k), (here - k) % count, 0
            )
        mine = gathered.reshape((-1,) + mine.shape[1:])
    shape = (size_y, size_x, 2, owners, part // owners, width)
    return mine.reshape(shape).transpose(3, 0, 1, 2, 4, 5).reshape(owners, -1, width)


def per_device(
    inputs, layer3_rows, layer4_rows, norm_gains, gate_weight, rel_bias, segment_ids, cotangent
):
    seqs_here, tokens_here, width = inputs.shape
    first_pos = lax.axis_index("z") * tokens_here
    context = attention_context(segment_ids[0], first_pos, tokens_here, rel_bias)
    stream = inputs.reshape(tokens_here, width)
    gathered_three = fetch_rows(layer3_rows)
    after_three, kept_three = layer_forward(
        stream, gathered_three, norm_gains[0], norm_gains[1], None, context
    )
    gate_inverse = lax.rsqrt(jnp.mean(after_three * after_three, axis=1, keepdims=True) + epsilon)
    gate_normed = after_three * gate_inverse
    gate_logit = jnp.sum(gate_normed * gate_weight, axis=1) + gate_offset
    sigmoid_value = 1.0 / (1.0 + jnp.exp(-gate_logit))
    gate_mask = gate_scale * sigmoid_value
    gate_low = gate_mask.astype(jnp.bfloat16)
    gathered_four = fetch_rows(layer4_rows)
    after_four, kept_four = layer_forward(
        after_three, gathered_four, norm_gains[2], norm_gains[3], gate_low, context
    )
    scatter = Scatter()
    grad_three_out, table_four, grad_gate, gain_four_one, gain_four_two, attention_four = (
        layer_backward(
            cotangent.reshape(tokens_here, width),
            kept_four,
            gathered_four,
            norm_gains[2],
            norm_gains[3],
            context,
            None,
            scatter,
            "four",
            False,
        )
    )
    grad_logit = grad_gate[:, 0] * gate_scale * sigmoid_value * (1.0 - sigmoid_value)
    grad_gate_weight = jnp.sum(grad_logit[:, None] * gate_normed, axis=0)
    gate_stream = stream_backward(after_three, gate_inverse, grad_logit[:, None] * gate_weight)
    grad_three_out = grad_three_out + gate_stream
    grad_input, table_three, unused, gain_three_one, gain_three_two, attention_three = (
        layer_backward(
            grad_three_out,
            kept_three,
            gathered_three,
            norm_gains[0],
            norm_gains[1],
            context,
            attention_four,
            scatter,
            "three",
            True,
        )
    )
    push_last_attention(attention_three, scatter)
    while scatter.busy():
        grad_input = scatter.step(grad_input)
    owner = (
        (lax.axis_index("y") * lax.axis_size("x") + lax.axis_index("x")) * lax.axis_size("c")
    ) + lax.axis_index("c")
    late = bring_to_owners(scatter.results["late"]).astype(jnp.float32)
    owners = late.shape[0]
    mine = pick(late, jnp.minimum(owner, owners - 1), 0)
    local_four, local_three = (
        jnp.concatenate([scatter.results[name, k] for k in range(4)], axis=1)[:, :width]
        for name in ("four", "three")
    )
    local_four = jnp.where(owner < owners, local_three, local_four)
    local_three = jnp.where(owner < owners, mine, local_three)
    table = jnp.pad((table_three + table_four).reshape(1, -1), ((0, 0), (0, width - 6 * BUCKETS)))
    small = jnp.stack(
        [gain_three_one, gain_three_two, gain_four_one, gain_four_two, grad_gate_weight, table[0]]
    )
    summed = sum_everywhere(small)
    return (
        after_four.reshape(inputs.shape),
        gate_mask.reshape(seqs_here, tokens_here),
        grad_input.reshape(inputs.shape),
        local_three,
        local_four,
        summed[:4],
        summed[4],
        summed[5, : 6 * BUCKETS].reshape(BUCKETS, HEADS),
    )


def solution(mesh):
    outer, inner = mesh.devices.shape
    fine = Mesh(mesh.devices.reshape(outer // 4, 2, 2, inner), DEVICES)
    batch = ("y", "x", "c")
    tokens = P(batch, "z", None)
    rows = P(DEVICES, None)
    return jax.shard_map(
        per_device,
        mesh=fine,
        in_specs=(tokens, rows, rows, P(), P(), P(), P(batch, None), tokens),
        out_specs=(tokens, P(batch, "z"), tokens, rows, rows, P(), P(), P()),
        check_vma=False,
    )
```

```python
import functools

import jax
import jax.numpy as jnp
from jax import lax
from jax.experimental import pallas as pl
from jax.experimental.pallas import tpu as pltpu
from jax.sharding import Mesh
from jax.sharding import PartitionSpec as P

HEADS = 6
PAIRS = 3
BLOCK = 128
WIDE = 2 * BLOCK
INNER = 384
BUCKETS = 32
FF = 3584
REACH = 799
HALO = 896
TILE = 256
ATTENTION_TILES = 4 * INNER // TILE
OFFSETS = 5
CHUNK = 384
FORWARD_TILE = 512
CUTS = (0, 384, 768, 1152, 1472)
DEVICES = ("y", "x", "c", "z")
epsilon = 1e-06
gate_scale = -30.0
gate_offset = -3.5
masked_out = -1e30
limits = (12, 16, 23, 32, 46, 64, 91)
both_last = (((1,), (1,)), ((), ()))


def bucket_of(relative):
    magnitude = jnp.abs(relative)
    beyond = jnp.zeros_like(magnitude)
    for bound_value in limits:
        beyond = beyond + (magnitude >= bound_value).astype(jnp.int32)
    inside = jnp.where(magnitude < 8, magnitude, 8 + beyond)
    return inside + 16 * (relative > 0).astype(jnp.int32)


def near_buckets(offset):
    if offset < 0:
        return range(1, 16)
    if offset > 0:
        return range(17, 32)
    return range(0, 32)


def tile_buckets(offset, width):
    key_at = lax.broadcasted_iota(jnp.int32, (BLOCK, width), 0)
    query_at = lax.broadcasted_iota(jnp.int32, (BLOCK, width), 1) % BLOCK
    return bucket_of(offset * BLOCK + key_at - query_at)


def bias_body(table_ref, tiles_ref):
    head = pl.program_id(0)
    tiles_ref[0, 0] = jnp.full((BLOCK, BLOCK), table_ref[15, head], jnp.float32)
    tiles_ref[0, 4] = jnp.full((BLOCK, BLOCK), table_ref[31, head], jnp.float32)
    for offset in (-1, 0, 1):
        buckets = tile_buckets(offset, BLOCK)
        tile = jnp.zeros((BLOCK, BLOCK), jnp.float32)
        for bucket in near_buckets(offset):
            tile = jnp.where(buckets == bucket, table_ref[bucket, head], tile)
        tiles_ref[0, offset + 2] = tile


def bias_tiles(rel_bias):
    return pl.pallas_call(
        bias_body,
        grid=(HEADS,),
        in_specs=[pl.BlockSpec(memory_space=pltpu.SMEM)],
        out_specs=pl.BlockSpec((1, OFFSETS, BLOCK, BLOCK), lambda h: (h, 0, 0, 0)),
        out_shape=jax.ShapeDtypeStruct((HEADS, OFFSETS, BLOCK, BLOCK), jnp.float32),
        name="bias_tiles",
    )(rel_bias)


def lane_masks():
    lane = lax.broadcasted_iota(jnp.int32, (BLOCK, BLOCK), 1)
    low = jnp.where(lane < 64, 1.0, 0.0).astype(jnp.bfloat16)
    high = jnp.where(lane < 64, 0.0, 1.0).astype(jnp.bfloat16)
    return low, high


def stacked(block, masks):
    low, high = masks
    return jnp.concatenate([block * low, block * high], axis=0)


def pair_cols(pair):
    return slice(pair * BLOCK, (pair + 1) * BLOCK)


def value_cols(pair):
    return slice(INNER + pair * BLOCK, INNER + (pair + 1) * BLOCK)


def block_rows(block):
    return pl.ds(pl.multiple_of(block * BLOCK, BLOCK), BLOCK)


def fold(values):
    return values.reshape(BLOCK // 8, 8, WIDE)


def shift_tile(gated, rows, own_segment, segment_ref, shared_ref):
    same = segment_ref[rows, :] == own_segment
    inside = shared_ref[rows, 2 * INNER :].astype(jnp.float32) if gated else 0.0
    shift = jnp.where(same, inside, masked_out)
    return jnp.concatenate([shift, shift], axis=1)


def bias_pair(bias_ref, pair, offset):
    return jnp.concatenate([bias_ref[2 * pair, offset], bias_ref[2 * pair + 1, offset]], axis=1)


def pick_heads(wide):
    return jnp.concatenate([wide[:64, :BLOCK], wide[64:, BLOCK:]], axis=0)


def forward_body(gated, low_ref, high_ref, *refs):
    query_ref, shared_ref, own_ref, segment_ref, bias_ref = refs[:5]
    mixed_ref, total_ref, turned_ref, score_ref = refs[5:]
    step = pl.program_id(0)
    key_blocks = shared_ref.shape[0] // BLOCK

    @pl.when(step == 0)
    def _():
        @pl.loop(0, key_blocks)
        def _(block):
            rows = block_rows(block)
            turned_ref[:, rows] = shared_ref[rows, INNER : 2 * INNER].T

    first, last = low_ref[step], high_ref[step]
    own_block = HALO // BLOCK + step
    own_segment = own_ref[0]
    masks = lane_masks()
    queries = [stacked(query_ref[:, pair_cols(pair)], masks) for pair in range(PAIRS)]

    def scores(block, peaks):
        rows = block_rows(block)
        shift = shift_tile(gated, rows, own_segment, segment_ref, shared_ref)
        offset = jnp.clip(block - own_block, -2, 2) + 2
        new_peaks = []
        for pair in range(PAIRS):
            score = lax.dot_general(
                shared_ref[rows, pair_cols(pair)],
                queries[pair],
                both_last,
                preferred_element_type=jnp.float32,
            )
            score = score + bias_pair(bias_ref, pair, offset) + shift
            score_ref[pair, block] = score
            new_peaks.append(jnp.maximum(peaks[pair], jnp.max(fold(score), axis=0)))
        return tuple(new_peaks)

    start = jnp.full((8, WIDE), -3e38, jnp.float32)
    peaks = lax.fori_loop(first, last, scores, (start,) * PAIRS)
    for pair in range(PAIRS):
        peak = jnp.max(peaks[pair], axis=0, keepdims=True)

        def mix(block, carry, pair=pair, peak=peak):
            total, mixed = carry
            weight = jnp.exp(score_ref[pair, block] - peak)
            total = total + jnp.sum(fold(weight), axis=0)
            mixed = mixed + jnp.dot(
                turned_ref[pair_cols(pair), block_rows(block)],
                weight.astype(jnp.bfloat16),
                preferred_element_type=jnp.float32,
            )
            return total, mixed

        zero = (jnp.zeros((8, WIDE), jnp.float32), jnp.zeros((BLOCK, WIDE), jnp.float32))
        total, mixed = lax.fori_loop(first, last, mix, zero)
        row_total = jnp.sum(total, axis=0, keepdims=True)
        mixed = pick_heads(mixed * (1.0 / row_total))
        mixed_ref[:, pair_cols(pair)] = mixed.T.astype(jnp.bfloat16)
        total_ref[0, pair : pair + 1, :] = peak + jnp.log(row_total)


def whole(shape):
    return pl.BlockSpec(shape, lambda i, *_: (0,) * len(shape), pipeline_mode=pl.Buffered(1))


def rows_spec(width):
    return pl.BlockSpec((BLOCK, width), lambda i, *_: (i, 0))


def attend_forward(queries, shared, context):
    lows, highs, own_rows, segment_wide, tiles = context
    tokens, (length, width) = queries.shape[0], shared.shape
    steps, key_blocks = tokens // BLOCK, length // BLOCK
    return pl.pallas_call(
        functools.partial(forward_body, width > 2 * INNER),
        grid_spec=pltpu.PrefetchScalarGridSpec(
            num_scalar_prefetch=2,
            grid=(steps,),
            in_specs=[
                rows_spec(INNER),
                whole((length, width)),
                pl.BlockSpec((1, 1, BLOCK), lambda i, *_: (i, 0, 0)),
                whole((length, BLOCK)),
                whole(tiles.shape),
            ],
            out_specs=[
                rows_spec(INNER),
                pl.BlockSpec((1, 8, WIDE), lambda i, *_: (i, 0, 0)),
            ],
            scratch_shapes=[
                pltpu.VMEM((INNER, length), jnp.bfloat16),
                pltpu.VMEM((PAIRS, key_blocks, BLOCK, WIDE), jnp.float32),
            ],
        ),
        out_shape=[
            jax.ShapeDtypeStruct((tokens, INNER), jnp.bfloat16),
            jax.ShapeDtypeStruct((steps, 8, WIDE), jnp.float32),
        ],
        compiler_params=pltpu.CompilerParams(vmem_limit_bytes=40 << 20),
        cost_estimate=pl.CostEstimate(
            flops=tokens * length * INNER * 4,
            bytes_accessed=8 << 20,
            transcendentals=tokens * length * 3,
        ),
        name="attend_forward",
    )(lows, highs, queries, shared, own_rows, segment_wide, tiles)


def backward_body(gated, low_ref, high_ref, *refs):
    query_ref, grad_ref, shared_ref, own_ref, segment_ref, bias_ref, total_ref = refs[:7]
    grad_query_ref, grad_shared_ref, bucket_ref = refs[7:10]
    turned_ref, prob_ref, pull_ref, sum_ref, bias_sum_ref, turn_sum_ref = refs[10:]
    step = pl.program_id(0)
    key_blocks = shared_ref.shape[0] // BLOCK

    @pl.when(step == 0)
    def _():
        bias_sum_ref[...] = jnp.zeros_like(bias_sum_ref)

        @pl.loop(0, key_blocks)
        def _(block):
            rows = block_rows(block)
            turned_ref[:, rows] = shared_ref[rows, :INNER].T
            sum_ref[rows, :] = jnp.zeros((BLOCK, sum_ref.shape[1]), jnp.float32)

    first, last = low_ref[step], high_ref[step]
    own_block = HALO // BLOCK + step
    own_segment = own_ref[0]
    masks = lane_masks()
    queries = [stacked(query_ref[:, pair_cols(pair)], masks) for pair in range(PAIRS)]
    grads = [stacked(grad_ref[:, pair_cols(pair)], masks) for pair in range(PAIRS)]
    totals = [total_ref[0, pair : pair + 1, :] for pair in range(PAIRS)]

    def weights(block, deltas):
        rows = block_rows(block)
        shift = shift_tile(gated, rows, own_segment, segment_ref, shared_ref)
        offset = jnp.clip(block - own_block, -2, 2) + 2
        new_deltas = []
        for pair in range(PAIRS):
            cols = pair_cols(pair)
            score = lax.dot_general(
                shared_ref[rows, cols], queries[pair], both_last, preferred_element_type=jnp.float32
            )
            pull = lax.dot_general(
                shared_ref[rows, value_cols(pair)],
                grads[pair],
                both_last,
                preferred_element_type=jnp.float32,
            )
            prob = jnp.exp(score + bias_pair(bias_ref, pair, offset) + shift - totals[pair])
            prob_ref[pair, block] = prob
            pull_ref[pair, block] = pull
            sum_ref[rows, value_cols(pair)] += jnp.dot(
                prob.astype(jnp.bfloat16), grads[pair], preferred_element_type=jnp.float32
            )
            new_deltas.append(deltas[pair] + jnp.sum(fold(prob * pull), axis=0))
        return tuple(new_deltas)

    start = jnp.zeros((8, WIDE), jnp.float32)
    deltas = lax.fori_loop(first, last, weights, (start,) * PAIRS)
    deltas = [jnp.sum(delta, axis=0, keepdims=True) for delta in deltas]
    turn_sum_ref[...] = jnp.zeros_like(turn_sum_ref)

    @pl.loop(first, last)
    def _(block):
        rows = block_rows(block)
        offset = jnp.clip(block - own_block, -2, 2) + 2
        gate_part = jnp.zeros((BLOCK, BLOCK), jnp.float32)
        for pair in range(PAIRS):
            cols = pair_cols(pair)
            grad_score = prob_ref[pair, block] * (pull_ref[pair, block] - deltas[pair])
            bias_sum_ref[pair, offset] += grad_score
            if gated:
                gate_part = gate_part + (grad_score[:, :BLOCK] + grad_score[:, BLOCK:])
            score_low = grad_score.astype(jnp.bfloat16)
            sum_ref[rows, cols] += jnp.dot(
                score_low, queries[pair], preferred_element_type=jnp.float32
            )
            turn_sum_ref[pair] += jnp.dot(
                turned_ref[cols, rows], score_low, preferred_element_type=jnp.float32
            )
        if gated:
            sum_ref[rows, 2 * INNER :] += gate_part

    for pair in range(PAIRS):
        grad_query_ref[:, pair_cols(pair)] = pick_heads(turn_sum_ref[pair]).T.astype(jnp.bfloat16)

    @pl.when(step == pl.num_programs(0) - 1)
    def _():
        @pl.loop(0, key_blocks)
        def _(block):
            rows = block_rows(block)
            both = slice(0, 2 * INNER)
            grad_shared_ref[rows, both] = sum_ref[rows, both].astype(jnp.bfloat16)
            if gated:
                gate_total = jnp.sum(sum_ref[rows, 2 * INNER :], axis=1, keepdims=True)
                grad_shared_ref[rows, 2 * INNER :] = jnp.broadcast_to(
                    gate_total, (BLOCK, BLOCK)
                ).astype(jnp.bfloat16)

        tables = {offset: tile_buckets(offset, WIDE) for offset in (-1, 0, 1)}

        @pl.loop(0, PAIRS)
        def _(pair):
            for bucket in range(BUCKETS):
                part = jnp.zeros((8, WIDE), jnp.float32)
                for offset in (-1, 0, 1):
                    if bucket in near_buckets(offset):
                        chosen = jnp.where(
                            tables[offset] == bucket, bias_sum_ref[pair, offset + 2], 0.0
                        )
                        part = part + jnp.sum(fold(chosen), axis=0)
                if bucket == 15:
                    part = part + jnp.sum(fold(bias_sum_ref[pair, 0]), axis=0)
                if bucket == 31:
                    part = part + jnp.sum(fold(bias_sum_ref[pair, 4]), axis=0)
                bucket_ref[pair, bucket : bucket + 1, :] = jnp.sum(part, axis=0, keepdims=True)


def attend_backward(queries, grad_mixed, shared, log_total, context):
    lows, highs, own_rows, segment_wide, tiles = context
    tokens, (length, width) = queries.shape[0], shared.shape
    steps, key_blocks = tokens // BLOCK, length // BLOCK
    grad_query, grad_shared, bucket_sums = pl.pallas_call(
        functools.partial(backward_body, width > 2 * INNER),
        grid_spec=pltpu.PrefetchScalarGridSpec(
            num_scalar_prefetch=2,
            grid=(steps,),
            in_specs=[
                rows_spec(INNER),
                rows_spec(INNER),
                whole((length, width)),
                pl.BlockSpec((1, 1, BLOCK), lambda i, *_: (i, 0, 0)),
                whole((length, BLOCK)),
                whole(tiles.shape),
                pl.BlockSpec((1, 8, WIDE), lambda i, *_: (i, 0, 0)),
            ],
            out_specs=[
                rows_spec(INNER),
                whole((length, width)),
                whole((PAIRS, BUCKETS, WIDE)),
            ],
            scratch_shapes=[
                pltpu.VMEM((INNER, length), jnp.bfloat16),
                pltpu.VMEM((PAIRS, key_blocks, BLOCK, WIDE), jnp.float32),
                pltpu.VMEM((PAIRS, key_blocks, BLOCK, WIDE), jnp.float32),
                pltpu.VMEM((length, width), jnp.float32),
                pltpu.VMEM((PAIRS, OFFSETS, BLOCK, WIDE), jnp.float32),
                pltpu.VMEM((PAIRS, BLOCK, WIDE), jnp.float32),
            ],
        ),
        out_shape=[
            jax.ShapeDtypeStruct((tokens, INNER), jnp.bfloat16),
            jax.ShapeDtypeStruct((length, width), jnp.bfloat16),
            jax.ShapeDtypeStruct((PAIRS, BUCKETS, WIDE), jnp.float32),
        ],
        compiler_params=pltpu.CompilerParams(vmem_limit_bytes=48 << 20),
        cost_estimate=pl.CostEstimate(
            flops=tokens * length * INNER * 10,
            bytes_accessed=12 << 20,
            transcendentals=tokens * length * 3,
        ),
        name="attend_backward",
    )(lows, highs, queries, grad_mixed, shared, own_rows, segment_wide, tiles, log_total)
    table = jnp.sum(bucket_sums.reshape(PAIRS, BUCKETS, 2, BLOCK), axis=3)
    return grad_query, grad_shared, table.transpose(1, 0, 2).reshape(BUCKETS, HEADS)


def attention_context(segment_row, first_pos, tokens, rel_bias):
    steps = tokens // BLOCK
    padded = jnp.pad(segment_row, (HALO, 0), constant_values=-1)
    padded = jnp.pad(padded, (0, HALO), constant_values=1000)
    window = lax.dynamic_slice_in_dim(padded, first_pos, tokens + 2 * HALO, 0)
    own = window[HALO : HALO + tokens].reshape(steps, 1, BLOCK)
    lows = jnp.sum(window[None, :] < own[:, 0, :1], axis=1, dtype=jnp.int32) // BLOCK
    ends = jnp.sum(window[None, :] <= own[:, 0, BLOCK - 1 :], axis=1, dtype=jnp.int32)
    highs = (ends + BLOCK - 1) // BLOCK
    segment_wide = jnp.broadcast_to(window[:, None], (window.shape[0], BLOCK))
    return lows, highs, own, segment_wide, bias_tiles(rel_bias)


def rms_forward(stream, gain_row):
    inverse = lax.rsqrt(jnp.mean(stream * stream, axis=1, keepdims=True) + epsilon)
    return (stream * inverse * gain_row, inverse)


def stream_backward(stream, inverse, scaled):
    return inverse * scaled - stream * inverse**3 * jnp.mean(scaled * stream, axis=1, keepdims=True)


def rms_backward(stream, inverse, gain_row, grad_normed):
    grad_gain = jnp.sum(grad_normed * stream * inverse, axis=0)
    return (stream_backward(stream, inverse, gain_row * grad_normed), grad_gain)


def gelu_tanh(values):
    return 0.5 * values * (1.0 + jnp.tanh(0.7978845608028654 * (values + 0.044715 * values**3)))


def times_rows(left_side, weight):
    return lax.dot_general(
        left_side, weight, (((1,), (1,)), ((), ())), preferred_element_type=jnp.float32
    )


def times_plain(left_side, weight):
    return jnp.dot(left_side, weight, preferred_element_type=jnp.float32)


def outer_sum(left_side, right_side):
    return lax.dot_general(
        left_side, right_side, (((0,), (0,)), ((), ())), preferred_element_type=jnp.float32
    )


def shift(value, axis, amount):
    count = lax.axis_size(axis)
    return lax.ppermute(value, axis, [(i, (i + amount) % count) for i in range(count)])


def slide(value, amount):
    count = lax.axis_size("z")
    pairs = [(i, i + amount) for i in range(count) if 0 <= i + amount < count]
    return lax.ppermute(value, "z", pairs)


def halo_pieces(tokens):
    pieces = []
    distance, covered = 1, 0
    while covered < HALO:
        span = min(tokens, HALO - covered)
        needed = min(span, -(-(REACH - covered) // 16) * 16)
        pieces.append((distance, span, needed))
        distance, covered = distance + 1, covered + span
    return pieces


def with_neighbours(own):
    tokens = own.shape[0]
    before, after = [], []
    for distance, span, needed in halo_pieces(tokens):
        if distance < lax.axis_size("z"):
            left = slide(own[tokens - needed :], distance)
            right = slide(own[:needed], -distance)
            before.append(jnp.pad(left, ((span - needed, 0), (0, 0))))
            after.append(jnp.pad(right, ((0, span - needed), (0, 0))))
        else:
            empty = jnp.zeros((span, own.shape[1]), own.dtype)
            before.append(empty)
            after.append(empty)
    return jnp.concatenate(before[::-1] + [own] + after, axis=0)


def from_neighbours(window, tokens):
    total = window[HALO : HALO + tokens].astype(jnp.float32)
    covered = 0
    for distance, span, needed in halo_pieces(tokens):
        if distance < lax.axis_size("z"):
            left_end = HALO - covered
            right_start = HALO + tokens + covered
            back = slide(window[left_end - needed : left_end], -distance)
            ahead = slide(window[right_start : right_start + needed], distance)
            total = total + jnp.pad(
                back.astype(jnp.float32), ((tokens - needed, 0), (0, 0))
            )
            total = total + jnp.pad(ahead.astype(jnp.float32), ((0, tokens - needed), (0, 0)))
        covered += span
    return total


def sum_everywhere(value):
    for axis in ("c", "x", "y", "z"):
        count = lax.axis_size(axis)
        bit = 1
        while bit < count:
            value = value + lax.ppermute(value, axis, [(i, i ^ bit) for i in range(count)])
            bit *= 2
    return value


def pick(value, index, axis):
    return lax.dynamic_index_in_dim(value, index, axis, keepdims=False)


def stage_sends(value, axis_name, axis):
    count, here = lax.axis_size(axis_name), lax.axis_index(axis_name)
    return [pick(value, (here + k) % count, axis) for k in range(1, count)]


def stage_moves(sends, axis_name):
    return [shift(sent, axis_name, k + 1) for k, sent in enumerate(sends)]


def gelu_parts(values):
    squared = values * values
    slope = jnp.tanh(0.7978845608028654 * (values + 0.044715 * values * squared))
    active = 0.5 * values * (1.0 + slope)
    inner = 0.7978845608028654 * (1.0 + 3.0 * 0.044715 * squared)
    return active, 0.5 * (1.0 + slope) + 0.5 * values * (1.0 - slope * slope) * inner


def ffn_forward_body(normed_ref, middle_ref, gelu_ref, linear_ref, down_ref, *outs):
    result_ref, up_gelu_ref, up_linear_ref = outs

    @pl.when(pl.program_id(0) == 0)
    def _():
        result_ref[...] = middle_ref[...]

    up_gelu = times_rows(normed_ref[...], gelu_ref[...])
    up_linear = times_rows(normed_ref[...], linear_ref[...])
    up_gelu_ref[...] = up_gelu
    up_linear_ref[...] = up_linear
    hidden = (gelu_tanh(up_gelu) * up_linear).astype(jnp.bfloat16)
    result_ref[...] += times_plain(hidden, down_ref[...])


def resident(shape):
    return pl.BlockSpec(shape, lambda *_: (0,) * len(shape), pipeline_mode=pl.Buffered(1))


def ffn_forward(normed, middle, gathered):
    tokens, width = normed.shape
    steps = FF // FORWARD_TILE
    first = 4 * INNER // FORWARD_TILE

    def weight(kind):
        return pl.BlockSpec((FORWARD_TILE, width), lambda i: (first + kind * steps + i, 0))

    hidden = pl.BlockSpec((tokens, FORWARD_TILE), lambda i: (0, i))
    return pl.pallas_call(
        ffn_forward_body,
        grid=(steps,),
        in_specs=[
            resident((tokens, width)),
            resident((tokens, width)),
            weight(0),
            weight(1),
            weight(2),
        ],
        out_specs=[resident((tokens, width)), hidden, hidden],
        out_shape=[
            jax.ShapeDtypeStruct((tokens, width), jnp.float32),
            jax.ShapeDtypeStruct((tokens, FF), jnp.float32),
            jax.ShapeDtypeStruct((tokens, FF), jnp.float32),
        ],
        compiler_params=pltpu.CompilerParams(vmem_limit_bytes=48 << 20),
        cost_estimate=pl.CostEstimate(
            flops=6 * tokens * FF * width,
            bytes_accessed=6 * FF * width + 8 * tokens * FF,
            transcendentals=tokens * FF,
        ),
        name="ffn_forward",
    )(normed, middle, gathered, gathered, gathered)


def ffn_backward_body(attended, core_ref, *refs):
    branch_ref, normed_ref, up_gelu_ref, up_linear_ref, gelu_ref, linear_ref, down_ref = refs[:7]
    refs = refs[7:]
    if attended:
        first_ref, second_ref, first_side_ref, second_side_ref = refs[:4]
        refs = refs[4:]
    grad_ref, kept_refs, sent_refs = refs[0], refs[1:5], refs[5:9]
    stage_ref, sems = refs[9], refs[10]
    step = pl.program_id(0)
    hidden_steps = FF // TILE
    slot = step % 2
    mine, unit, rows, columns = core_ref[0], core_ref[1], core_ref[2], core_ref[3]

    def places(target):
        unit_at, inside = target // (2 * unit), target % unit
        swapped = (unit_at % columns) * rows + unit_at // columns
        for k in range(4):
            at = (unit_at if k % 2 == 0 else swapped) * unit + inside
            yield k, pl.ds(pl.multiple_of(at * TILE, TILE), TILE)

    def copy(kind, k, place, spot, where):
        source = stage_ref.at[where, kind, :, k * CHUNK : (k + 1) * CHUNK]
        return pltpu.make_async_copy(source, place[k].at[spot, :], sems.at[where, kind, k])

    def wait(kind, where):
        for k in range(4):
            copy(kind, k, kept_refs, pl.ds(0, TILE), where).wait()

    def put(kind, target, left, right):
        product = jnp.dot(left, right, preferred_element_type=jnp.float32)
        stage_ref[slot, kind, :, : CUTS[-1]] = product.astype(jnp.bfloat16)
        own = (target // unit) % 2 == mine
        spots = list(places(target))

        @pl.when(own)
        def _():
            for k, spot in spots:
                copy(kind, k, kept_refs, spot, slot).start()

        @pl.when(jnp.logical_not(own))
        def _():
            for k, spot in spots:
                copy(kind, k, sent_refs, spot, slot).start()

    @pl.when(step == 0)
    def _():
        grad_ref[...] = jnp.zeros_like(grad_ref)
        stage_ref[:, :, :, CUTS[-1] :] = jnp.zeros(
            stage_ref.shape[:3] + (4 * CHUNK - CUTS[-1],), jnp.bfloat16
        )

    @pl.when((step >= 2) & (step < hidden_steps + 2))
    def _():
        for kind in range(3):
            wait(kind, slot)

    if attended:

        @pl.when(step >= hidden_steps + 2)
        def _():
            wait(0, slot)

    @pl.when(step < hidden_steps)
    def _():
        grad_hidden = times_rows(branch_ref[...], down_ref[...])
        active, slope = gelu_parts(up_gelu_ref[...])
        linear = up_linear_ref[...]
        hidden = (active * linear).astype(jnp.bfloat16)
        grad_gelu = (grad_hidden * linear * slope).astype(jnp.bfloat16)
        grad_linear = (grad_hidden * active).astype(jnp.bfloat16)
        grad_ref[...] += times_plain(grad_gelu, gelu_ref[...]) + times_plain(
            grad_linear, linear_ref[...]
        )
        put(0, ATTENTION_TILES + step, grad_gelu.T, normed_ref[...])
        put(1, ATTENTION_TILES + hidden_steps + step, grad_linear.T, normed_ref[...])
        put(2, ATTENTION_TILES + 2 * hidden_steps + step, hidden.T, branch_ref[...])

    if attended:

        @pl.when(step >= hidden_steps)
        def _():
            put(
                0,
                step - hidden_steps,
                jnp.concatenate([first_ref[...], second_ref[...]], axis=0).T,
                jnp.concatenate([first_side_ref[...], second_side_ref[...]], axis=0),
            )

    @pl.when(step == pl.num_programs(0) - 1)
    def _():
        for back in range(2):
            for kind in range(1 if attended else 3):
                wait(kind, back)


def ffn_backward(branch, normed, up_gelu, up_linear, gathered, attention):
    tokens, width = normed.shape
    rows = 4 * INNER + 3 * FF
    hidden_steps = FF // TILE
    size_y, size_x = lax.axis_size("y"), lax.axis_size("x")
    unit = rows // TILE // (2 * size_y * size_x)
    core = jnp.stack(
        [
            lax.axis_index("c").astype(jnp.int32),
            jnp.int32(unit),
            jnp.int32(size_y),
            jnp.int32(size_x),
        ]
    )
    last = hidden_steps - 1

    def weight(kind):
        first = ATTENTION_TILES + kind * hidden_steps
        return pl.BlockSpec((TILE, width), lambda i, *_: (first + jnp.minimum(i, last), 0))

    hidden = pl.BlockSpec((tokens, TILE), lambda i, *_: (0, jnp.minimum(i, last)))
    late = pl.BlockSpec((tokens, TILE), lambda i, *_: (0, jnp.maximum(i - hidden_steps, 0)))
    side = resident((tokens, width))
    operands = [branch, normed, up_gelu, up_linear, gathered, gathered, gathered]
    in_specs = [side, side, hidden, hidden, weight(0), weight(1), weight(2)]
    steps = hidden_steps
    if attention is not None:
        operands += attention
        in_specs += [late, late, side, side]
        steps += ATTENTION_TILES
    anywhere = pl.BlockSpec(memory_space=pl.ANY)
    results = pl.pallas_call(
        functools.partial(ffn_backward_body, attention is not None),
        grid_spec=pltpu.PrefetchScalarGridSpec(
            num_scalar_prefetch=1,
            grid=(steps,),
            in_specs=in_specs,
            out_specs=[side] + [anywhere] * 8,
            scratch_shapes=[
                pltpu.VMEM((2, 3, TILE, 4 * CHUNK), jnp.bfloat16),
                pltpu.SemaphoreType.DMA((2, 3, 4)),
            ],
        ),
        out_shape=[jax.ShapeDtypeStruct((tokens, width), jnp.float32)]
        + [jax.ShapeDtypeStruct((rows // 2, CHUNK), jnp.bfloat16)] * 8,
        compiler_params=pltpu.CompilerParams(vmem_limit_bytes=52 << 20),
        cost_estimate=pl.CostEstimate(
            flops=12 * tokens * FF * width,
            bytes_accessed=12 * FF * width + 8 * tokens * FF,
            transcendentals=tokens * FF,
        ),
        name="ffn_backward",
    )(core, *operands)
    return results[0], list(results[1:5]), list(results[5:9])


def tied(first, second):
    return lax.optimization_barrier((first, second))


class Scatter:
    def __init__(self):
        self.waiting, self.flying, self.results = [], [], {}

    def push(self, name, route, kept, moved):
        shape = tuple(lax.axis_size(axis) for axis in route) + (-1, kept.shape[-1])
        self.waiting.append((name, route, kept.reshape(shape), [moved.reshape(shape)]))

    def busy(self):
        return bool(self.waiting or self.flying)

    def step(self, values, enter=2):
        flying = [item[2:] for item in self.flying]
        flying, values = tied(flying, values)
        entering, self.waiting = self.waiting[:enter], self.waiting[enter:]
        ready = [item[:2] + tuple(arrays) for item, arrays in zip(self.flying, flying)] + entering
        moves = []
        for name, route, kept, moved in ready:
            if not route:
                self.results[name] = kept.astype(jnp.float32) + sum(
                    part.astype(jnp.float32) for part in moved
                )
                continue
            total = total_of(kept, moved)
            sends = stage_sends(total, route[0], 0)
            moves.append((name, route, pick(total, lax.axis_index(route[0]), 0), sends))
        arrays, values = tied([item[2:] for item in moves], values)
        self.flying = [
            (name, route[1:], kept, stage_moves(sends, route[0]))
            for (name, route, *_), (kept, sends) in zip(moves, arrays)
        ]
        return values


def total_of(value, moved):
    total = value.astype(jnp.float32)
    for part in moved:
        total = total + part.astype(jnp.float32)
    return total.astype(jnp.bfloat16)


def fetch_rows(local_rows):
    return lax.all_gather(local_rows, DEVICES, axis=0, tiled=True)


def layer_forward(stream, gathered, gain_one, gain_two, gate_low, context, early):
    tokens = stream.shape[0]
    normed, inverse_one = rms_forward(stream, gain_one)
    normed_low = normed.astype(jnp.bfloat16)
    if early is None:
        projected = times_rows(normed_low, gathered[: 3 * INNER]).astype(jnp.bfloat16)
        queries = projected[:, :INNER]
        wide_gate = jnp.broadcast_to(gate_low[:, None], (tokens, BLOCK))
        shared = with_neighbours(jnp.concatenate([projected[:, INNER:], wide_gate], axis=1))
    else:
        queries = times_rows(normed_low, gathered[:INNER]).astype(jnp.bfloat16)
        shared = times_rows(early, gathered[INNER : 3 * INNER]).astype(jnp.bfloat16)
    attended, log_total = attend_forward(queries, shared, context)
    middle = stream + times_plain(attended, gathered[3 * INNER : 4 * INNER])
    normed_two, inverse_two = rms_forward(middle, gain_two)
    normed_two_low = normed_two.astype(jnp.bfloat16)
    result, up_gelu, up_linear = ffn_forward(normed_two_low, middle, gathered)
    kept = (
        stream,
        inverse_one,
        normed_low,
        queries,
        shared,
        attended,
        log_total,
        middle,
        inverse_two,
        normed_two_low,
        up_gelu,
        up_linear,
    )
    return (result, kept)


def layer_backward(grad_out, kept, gathered, gain_one, gain_two, context, waiting, scatter, name):
    (
        stream,
        inverse_one,
        normed_low,
        queries,
        shared,
        attended,
        log_total,
        middle,
        inverse_two,
        normed_two_low,
        up_gelu,
        up_linear,
    ) = kept
    branch_low = grad_out.astype(jnp.bfloat16)
    grad_normed_two, own, sent = ffn_backward(
        branch_low, normed_two_low, up_gelu, up_linear, gathered, waiting
    )
    moved = [shift(part, "c", 1) for part in sent]
    grad_normed_two, own = lax.optimization_barrier((grad_normed_two, own))
    grad_middle, grad_gain_two = rms_backward(middle, inverse_two, gain_two, grad_normed_two)
    grad_middle = grad_out + grad_middle
    middle_low = grad_middle.astype(jnp.bfloat16)
    grad_mixed = times_rows(middle_low, gathered[3 * INNER : 4 * INNER]).astype(jnp.bfloat16)
    for k in range(4):
        scatter.push((name, k), ("y", "x", "z") if k % 2 == 0 else ("x", "y", "z"), own[k], moved[k])
    grad_mixed, grad_middle, middle_low = scatter.step((grad_mixed, grad_middle, middle_low))
    grad_query, grad_shared, grad_table = attend_backward(
        queries, grad_mixed, shared, log_total, context
    )
    grad_query, grad_shared, grad_table = scatter.step((grad_query, grad_shared, grad_table))
    grad_own = from_neighbours(grad_shared, queries.shape[0])
    grad_gate = grad_own[:, 2 * INNER :]
    grad_input_low = jnp.concatenate(
        [grad_query, grad_own[:, : 2 * INNER].astype(jnp.bfloat16)], axis=1
    )
    grad_input_low, grad_gate = scatter.step((grad_input_low, grad_gate))
    grad_normed = times_plain(grad_input_low, gathered[: 3 * INNER])
    grad_stream, grad_gain_one = rms_backward(stream, inverse_one, gain_one, grad_normed)
    grad_stream = grad_middle + grad_stream
    return (
        grad_stream,
        grad_table,
        grad_gate,
        grad_gain_one,
        grad_gain_two,
        (grad_input_low, attended, normed_low, middle_low),
    )


def padded_attention(attention):
    grad_input_low, attended, normed_low, middle_low = attention
    return [
        jnp.pad(grad_input_low, ((0, 0), (0, INNER))),
        jnp.pad(attended, ((0, 0), (3 * INNER, 0))),
        normed_low,
        middle_low,
    ]


def push_last_attention(attention, scatter):
    grad_input_low, attended, normed_low, middle_low = attention
    size_y, size_x, size_z = (lax.axis_size(axis) for axis in ("y", "x", "z"))
    core = lax.axis_index("c")
    width = normed_low.shape[1]
    owners, part = owner_parts()
    rows = jnp.concatenate(
        [
            outer_sum(grad_input_low, normed_low).astype(jnp.bfloat16),
            outer_sum(attended, middle_low).astype(jnp.bfloat16),
        ],
        axis=0,
    )
    rows = rows.reshape(owners, size_z, size_y, size_x, 2, -1, width)
    rows = rows.transpose(4, 2, 3, 1, 0, 5, 6).reshape(2, -1, width)
    kept, sent = pick(rows, core, 0), pick(rows, 1 - core, 0)
    moved = shift(sent, "c", 1)
    scatter.push("late", ("y", "x", "z"), kept, moved)


def owner_parts():
    size_y, size_x, size_z = (lax.axis_size(axis) for axis in ("y", "x", "z"))
    block = (4 * INNER + 3 * FF) // (size_y * size_x * 2 * size_z)
    owners = 4 * INNER // (block * size_z)
    return owners, block * owners // (size_y * size_x * 2)


def bring_to_owners(mine):
    size_y, size_x = lax.axis_size("y"), lax.axis_size("x")
    owners, part = owner_parts()
    width = mine.shape[-1]
    mine = mine.astype(jnp.bfloat16)[None]
    for axis in ("c", "x", "y"):
        count, here = lax.axis_size(axis), lax.axis_index(axis)
        gathered = jnp.zeros((count,) + mine.shape, mine.dtype)
        gathered = lax.dynamic_update_index_in_dim(gathered, mine, here, 0)
        for k in range(1, count):
            gathered = lax.dynamic_update_index_in_dim(
                gathered, shift(mine, axis, k), (here - k) % count, 0
            )
        mine = gathered.reshape((-1,) + mine.shape[1:])
    shape = (size_y, size_x, 2, owners, part // owners, width)
    return mine.reshape(shape).transpose(3, 0, 1, 2, 4, 5).reshape(owners, -1, width)


def per_device(
    inputs, layer3_rows, layer4_rows, norm_gains, gate_weight, rel_bias, segment_ids, cotangent
):
    seqs_here, tokens_here, width = inputs.shape
    first_pos = lax.axis_index("z") * tokens_here
    context = attention_context(segment_ids[0], first_pos, tokens_here, rel_bias)
    stream = inputs.reshape(tokens_here, width)
    early = with_neighbours(rms_forward(stream, norm_gains[0])[0].astype(jnp.bfloat16))
    gathered_three = fetch_rows(layer3_rows)
    after_three, kept_three = layer_forward(
        stream, gathered_three, norm_gains[0], norm_gains[1], None, context, early
    )
    gate_inverse = lax.rsqrt(jnp.mean(after_three * after_three, axis=1, keepdims=True) + epsilon)
    gate_normed = after_three * gate_inverse
    gate_logit = jnp.sum(gate_normed * gate_weight, axis=1) + gate_offset
    sigmoid_value = 1.0 / (1.0 + jnp.exp(-gate_logit))
    gate_mask = gate_scale * sigmoid_value
    gate_low = gate_mask.astype(jnp.bfloat16)
    gathered_four = fetch_rows(layer4_rows)
    after_four, kept_four = layer_forward(
        after_three, gathered_four, norm_gains[2], norm_gains[3], gate_low, context, None
    )
    scatter = Scatter()
    grad_three_out, table_four, grad_gate, gain_four_one, gain_four_two, attention_four = (
        layer_backward(
            cotangent.reshape(tokens_here, width),
            kept_four,
            gathered_four,
            norm_gains[2],
            norm_gains[3],
            context,
            None,
            scatter,
            "four",
        )
    )
    grad_logit = grad_gate[:, 0] * gate_scale * sigmoid_value * (1.0 - sigmoid_value)
    grad_gate_weight = jnp.sum(grad_logit[:, None] * gate_normed, axis=0)
    gate_stream = stream_backward(after_three, gate_inverse, grad_logit[:, None] * gate_weight)
    grad_three_out = scatter.step(grad_three_out + gate_stream)
    grad_input, table_three, unused, gain_three_one, gain_three_two, attention_three = (
        layer_backward(
            grad_three_out,
            kept_three,
            gathered_three,
            norm_gains[0],
            norm_gains[1],
            context,
            padded_attention(attention_four),
            scatter,
            "three",
        )
    )
    push_last_attention(attention_three, scatter)
    while scatter.busy():
        grad_input = scatter.step(grad_input)
    owner = (
        (lax.axis_index("y") * lax.axis_size("x") + lax.axis_index("x")) * lax.axis_size("c")
    ) + lax.axis_index("c")
    late = bring_to_owners(scatter.results["late"].reshape(-1, width)).astype(jnp.float32)
    owners = late.shape[0]
    mine = pick(late, jnp.minimum(owner, owners - 1), 0)
    local_four, local_three = (
        jnp.concatenate([scatter.results[name, k].reshape(-1, CHUNK) for k in range(4)], axis=1)[:, :width]
        for name in ("four", "three")
    )
    local_four = jnp.where(owner < owners, local_three, local_four)
    local_three = jnp.where(owner < owners, mine, local_three)
    table = jnp.pad((table_three + table_four).reshape(1, -1), ((0, 0), (0, width - 6 * BUCKETS)))
    small = jnp.stack(
        [gain_three_one, gain_three_two, gain_four_one, gain_four_two, grad_gate_weight, table[0]]
    )
    summed = sum_everywhere(small)
    return (
        after_four.reshape(inputs.shape),
        gate_mask.reshape(seqs_here, tokens_here),
        grad_input.reshape(inputs.shape),
        local_three,
        local_four,
        summed[:4],
        summed[4],
        summed[5, : 6 * BUCKETS].reshape(BUCKETS, HEADS),
    )


def solution(mesh):
    outer, inner = mesh.devices.shape
    fine = Mesh(mesh.devices.reshape(outer // 4, 2, 2, inner), DEVICES)
    batch = ("y", "x", "c")
    tokens = P(batch, "z", None)
    rows = P(DEVICES, None)
    return jax.shard_map(
        per_device,
        mesh=fine,
        in_specs=(tokens, rows, rows, P(), P(), P(), P(batch, None), tokens),
        out_specs=(tokens, P(batch, "z"), tokens, rows, rows, P(), P(), P()),
        check_vma=False,
    )
```

```python
import functools

import jax
import jax.numpy as jnp
from jax import lax
from jax.experimental import pallas as pl
from jax.experimental.pallas import tpu as pltpu
from jax.sharding import Mesh
from jax.sharding import PartitionSpec as P

HEADS = 6
PAIRS = 3
BLOCK = 128
WIDE = 2 * BLOCK
INNER = 384
BUCKETS = 32
FF = 3584
REACH = 799
HALO = 896
TILE = 256
ATTENTION_TILES = 4 * INNER // TILE
OFFSETS = 5
CHUNK = 384
FORWARD_TILE = 512
CUTS = (0, 384, 768, 1152, 1472)
DEVICES = ("y", "x", "c", "z")
epsilon = 1e-06
gate_scale = -30.0
gate_offset = -3.5
masked_out = -1e30
limits = (12, 16, 23, 32, 46, 64, 91)
both_last = (((1,), (1,)), ((), ()))


def bucket_of(relative):
    magnitude = jnp.abs(relative)
    beyond = jnp.zeros_like(magnitude)
    for bound_value in limits:
        beyond = beyond + (magnitude >= bound_value).astype(jnp.int32)
    inside = jnp.where(magnitude < 8, magnitude, 8 + beyond)
    return inside + 16 * (relative > 0).astype(jnp.int32)


def near_buckets(offset):
    if offset < 0:
        return range(1, 16)
    if offset > 0:
        return range(17, 32)
    return range(0, 32)


def tile_buckets(offset, width):
    key_at = lax.broadcasted_iota(jnp.int32, (BLOCK, width), 0)
    query_at = lax.broadcasted_iota(jnp.int32, (BLOCK, width), 1) % BLOCK
    return bucket_of(offset * BLOCK + key_at - query_at)


def bias_body(table_ref, tiles_ref):
    head = pl.program_id(0)
    tiles_ref[0, 0] = jnp.full((BLOCK, BLOCK), table_ref[15, head], jnp.float32)
    tiles_ref[0, 4] = jnp.full((BLOCK, BLOCK), table_ref[31, head], jnp.float32)
    for offset in (-1, 0, 1):
        buckets = tile_buckets(offset, BLOCK)
        tile = jnp.zeros((BLOCK, BLOCK), jnp.float32)
        for bucket in near_buckets(offset):
            tile = jnp.where(buckets == bucket, table_ref[bucket, head], tile)
        tiles_ref[0, offset + 2] = tile


def bias_tiles(rel_bias):
    return pl.pallas_call(
        bias_body,
        grid=(HEADS,),
        in_specs=[pl.BlockSpec(memory_space=pltpu.SMEM)],
        out_specs=pl.BlockSpec((1, OFFSETS, BLOCK, BLOCK), lambda h: (h, 0, 0, 0)),
        out_shape=jax.ShapeDtypeStruct((HEADS, OFFSETS, BLOCK, BLOCK), jnp.float32),
        name="bias_tiles",
    )(rel_bias)


def lane_masks():
    lane = lax.broadcasted_iota(jnp.int32, (BLOCK, BLOCK), 1)
    low = jnp.where(lane < 64, 1.0, 0.0).astype(jnp.bfloat16)
    high = jnp.where(lane < 64, 0.0, 1.0).astype(jnp.bfloat16)
    return low, high


def stacked(block, masks):
    low, high = masks
    return jnp.concatenate([block * low, block * high], axis=0)


def pair_cols(pair):
    return slice(pair * BLOCK, (pair + 1) * BLOCK)


def value_cols(pair):
    return slice(INNER + pair * BLOCK, INNER + (pair + 1) * BLOCK)


def block_rows(block):
    return pl.ds(pl.multiple_of(block * BLOCK, BLOCK), BLOCK)


def fold(values):
    return values.reshape(BLOCK // 8, 8, WIDE)


def shift_tile(gated, rows, own_segment, segment_ref, shared_ref):
    same = segment_ref[rows, :] == own_segment
    inside = shared_ref[rows, 2 * INNER :].astype(jnp.float32) if gated else 0.0
    shift = jnp.where(same, inside, masked_out)
    return jnp.concatenate([shift, shift], axis=1)


def bias_pair(bias_ref, pair, offset):
    return jnp.concatenate([bias_ref[2 * pair, offset], bias_ref[2 * pair + 1, offset]], axis=1)


def pick_heads(wide):
    return jnp.concatenate([wide[:64, :BLOCK], wide[64:, BLOCK:]], axis=0)


def forward_body(gated, low_ref, high_ref, *refs):
    query_ref, shared_ref, own_ref, segment_ref, bias_ref = refs[:5]
    mixed_ref, total_ref, turned_ref, score_ref = refs[5:]
    step = pl.program_id(0)
    key_blocks = shared_ref.shape[0] // BLOCK

    @pl.when(step == 0)
    def _():
        @pl.loop(0, key_blocks)
        def _(block):
            rows = block_rows(block)
            turned_ref[:, rows] = shared_ref[rows, INNER : 2 * INNER].T

    first, last = low_ref[step], high_ref[step]
    own_block = HALO // BLOCK + step
    own_segment = own_ref[0]
    masks = lane_masks()
    queries = [stacked(query_ref[:, pair_cols(pair)], masks) for pair in range(PAIRS)]

    def scores(block, peaks):
        rows = block_rows(block)
        shift = shift_tile(gated, rows, own_segment, segment_ref, shared_ref)
        offset = jnp.clip(block - own_block, -2, 2) + 2
        new_peaks = []
        for pair in range(PAIRS):
            score = lax.dot_general(
                shared_ref[rows, pair_cols(pair)],
                queries[pair],
                both_last,
                preferred_element_type=jnp.float32,
            )
            score = score + bias_pair(bias_ref, pair, offset) + shift
            score_ref[pair, block] = score
            new_peaks.append(jnp.maximum(peaks[pair], jnp.max(fold(score), axis=0)))
        return tuple(new_peaks)

    start = jnp.full((8, WIDE), -3e38, jnp.float32)
    peaks = lax.fori_loop(first, last, scores, (start,) * PAIRS)
    for pair in range(PAIRS):
        peak = jnp.max(peaks[pair], axis=0, keepdims=True)

        def mix(block, carry, pair=pair, peak=peak):
            total, mixed = carry
            weight = jnp.exp(score_ref[pair, block] - peak)
            total = total + jnp.sum(fold(weight), axis=0)
            mixed = mixed + jnp.dot(
                turned_ref[pair_cols(pair), block_rows(block)],
                weight.astype(jnp.bfloat16),
                preferred_element_type=jnp.float32,
            )
            return total, mixed

        zero = (jnp.zeros((8, WIDE), jnp.float32), jnp.zeros((BLOCK, WIDE), jnp.float32))
        total, mixed = lax.fori_loop(first, last, mix, zero)
        row_total = jnp.sum(total, axis=0, keepdims=True)
        mixed = pick_heads(mixed * (1.0 / row_total))
        mixed_ref[:, pair_cols(pair)] = mixed.T.astype(jnp.bfloat16)
        total_ref[0, pair : pair + 1, :] = peak + jnp.log(row_total)


def whole(shape):
    return pl.BlockSpec(shape, lambda i, *_: (0,) * len(shape), pipeline_mode=pl.Buffered(1))


def rows_spec(width):
    return pl.BlockSpec((BLOCK, width), lambda i, *_: (i, 0))


def attend_forward(queries, shared, context):
    lows, highs, own_rows, segment_wide, tiles = context
    tokens, (length, width) = queries.shape[0], shared.shape
    steps, key_blocks = tokens // BLOCK, length // BLOCK
    return pl.pallas_call(
        functools.partial(forward_body, width > 2 * INNER),
        grid_spec=pltpu.PrefetchScalarGridSpec(
            num_scalar_prefetch=2,
            grid=(steps,),
            in_specs=[
                rows_spec(INNER),
                whole((length, width)),
                pl.BlockSpec((1, 1, BLOCK), lambda i, *_: (i, 0, 0)),
                whole((length, BLOCK)),
                whole(tiles.shape),
            ],
            out_specs=[
                rows_spec(INNER),
                pl.BlockSpec((1, 8, WIDE), lambda i, *_: (i, 0, 0)),
            ],
            scratch_shapes=[
                pltpu.VMEM((INNER, length), jnp.bfloat16),
                pltpu.VMEM((PAIRS, key_blocks, BLOCK, WIDE), jnp.float32),
            ],
        ),
        out_shape=[
            jax.ShapeDtypeStruct((tokens, INNER), jnp.bfloat16),
            jax.ShapeDtypeStruct((steps, 8, WIDE), jnp.float32),
        ],
        compiler_params=pltpu.CompilerParams(vmem_limit_bytes=40 << 20),
        cost_estimate=pl.CostEstimate(
            flops=tokens * length * INNER * 4,
            bytes_accessed=8 << 20,
            transcendentals=tokens * length * 3,
        ),
        name="attend_forward",
    )(lows, highs, queries, shared, own_rows, segment_wide, tiles)


def backward_body(gated, low_ref, high_ref, *refs):
    query_ref, grad_ref, shared_ref, own_ref, segment_ref, bias_ref, total_ref = refs[:7]
    grad_query_ref, grad_shared_ref, bucket_ref = refs[7:10]
    turned_ref, prob_ref, pull_ref, sum_ref, bias_sum_ref, turn_sum_ref = refs[10:]
    step = pl.program_id(0)
    key_blocks = shared_ref.shape[0] // BLOCK

    @pl.when(step == 0)
    def _():
        bias_sum_ref[...] = jnp.zeros_like(bias_sum_ref)

        @pl.loop(0, key_blocks)
        def _(block):
            rows = block_rows(block)
            turned_ref[:, rows] = shared_ref[rows, :INNER].T
            sum_ref[rows, :] = jnp.zeros((BLOCK, sum_ref.shape[1]), jnp.float32)

    first, last = low_ref[step], high_ref[step]
    own_block = HALO // BLOCK + step
    own_segment = own_ref[0]
    masks = lane_masks()
    queries = [stacked(query_ref[:, pair_cols(pair)], masks) for pair in range(PAIRS)]
    grads = [stacked(grad_ref[:, pair_cols(pair)], masks) for pair in range(PAIRS)]
    totals = [total_ref[0, pair : pair + 1, :] for pair in range(PAIRS)]

    def weights(block, deltas):
        rows = block_rows(block)
        shift = shift_tile(gated, rows, own_segment, segment_ref, shared_ref)
        offset = jnp.clip(block - own_block, -2, 2) + 2
        new_deltas = []
        for pair in range(PAIRS):
            cols = pair_cols(pair)
            score = lax.dot_general(
                shared_ref[rows, cols], queries[pair], both_last, preferred_element_type=jnp.float32
            )
            pull = lax.dot_general(
                shared_ref[rows, value_cols(pair)],
                grads[pair],
                both_last,
                preferred_element_type=jnp.float32,
            )
            prob = jnp.exp(score + bias_pair(bias_ref, pair, offset) + shift - totals[pair])
            prob_ref[pair, block] = prob
            pull_ref[pair, block] = pull
            sum_ref[rows, value_cols(pair)] += jnp.dot(
                prob.astype(jnp.bfloat16), grads[pair], preferred_element_type=jnp.float32
            )
            new_deltas.append(deltas[pair] + jnp.sum(fold(prob * pull), axis=0))
        return tuple(new_deltas)

    start = jnp.zeros((8, WIDE), jnp.float32)
    deltas = lax.fori_loop(first, last, weights, (start,) * PAIRS)
    deltas = [jnp.sum(delta, axis=0, keepdims=True) for delta in deltas]
    turn_sum_ref[...] = jnp.zeros_like(turn_sum_ref)

    @pl.loop(first, last)
    def _(block):
        rows = block_rows(block)
        offset = jnp.clip(block - own_block, -2, 2) + 2
        gate_part = jnp.zeros((BLOCK, BLOCK), jnp.float32)
        for pair in range(PAIRS):
            cols = pair_cols(pair)
            grad_score = prob_ref[pair, block] * (pull_ref[pair, block] - deltas[pair])
            bias_sum_ref[pair, offset] += grad_score
            if gated:
                gate_part = gate_part + (grad_score[:, :BLOCK] + grad_score[:, BLOCK:])
            score_low = grad_score.astype(jnp.bfloat16)
            sum_ref[rows, cols] += jnp.dot(
                score_low, queries[pair], preferred_element_type=jnp.float32
            )
            turn_sum_ref[pair] += jnp.dot(
                turned_ref[cols, rows], score_low, preferred_element_type=jnp.float32
            )
        if gated:
            sum_ref[rows, 2 * INNER :] += gate_part

    for pair in range(PAIRS):
        grad_query_ref[:, pair_cols(pair)] = pick_heads(turn_sum_ref[pair]).T.astype(jnp.bfloat16)

    @pl.when(step == pl.num_programs(0) - 1)
    def _():
        @pl.loop(0, key_blocks)
        def _(block):
            rows = block_rows(block)
            both = slice(0, 2 * INNER)
            grad_shared_ref[rows, both] = sum_ref[rows, both].astype(jnp.bfloat16)
            if gated:
                gate_total = jnp.sum(sum_ref[rows, 2 * INNER :], axis=1, keepdims=True)
                grad_shared_ref[rows, 2 * INNER :] = jnp.broadcast_to(
                    gate_total, (BLOCK, BLOCK)
                ).astype(jnp.bfloat16)

        tables = {offset: tile_buckets(offset, WIDE) for offset in (-1, 0, 1)}

        @pl.loop(0, PAIRS)
        def _(pair):
            for bucket in range(BUCKETS):
                part = jnp.zeros((8, WIDE), jnp.float32)
                for offset in (-1, 0, 1):
                    if bucket in near_buckets(offset):
                        chosen = jnp.where(
                            tables[offset] == bucket, bias_sum_ref[pair, offset + 2], 0.0
                        )
                        part = part + jnp.sum(fold(chosen), axis=0)
                if bucket == 15:
                    part = part + jnp.sum(fold(bias_sum_ref[pair, 0]), axis=0)
                if bucket == 31:
                    part = part + jnp.sum(fold(bias_sum_ref[pair, 4]), axis=0)
                bucket_ref[pair, bucket : bucket + 1, :] = jnp.sum(part, axis=0, keepdims=True)


def attend_backward(queries, grad_mixed, shared, log_total, context):
    lows, highs, own_rows, segment_wide, tiles = context
    tokens, (length, width) = queries.shape[0], shared.shape
    steps, key_blocks = tokens // BLOCK, length // BLOCK
    grad_query, grad_shared, bucket_sums = pl.pallas_call(
        functools.partial(backward_body, width > 2 * INNER),
        grid_spec=pltpu.PrefetchScalarGridSpec(
            num_scalar_prefetch=2,
            grid=(steps,),
            in_specs=[
                rows_spec(INNER),
                rows_spec(INNER),
                whole((length, width)),
                pl.BlockSpec((1, 1, BLOCK), lambda i, *_: (i, 0, 0)),
                whole((length, BLOCK)),
                whole(tiles.shape),
                pl.BlockSpec((1, 8, WIDE), lambda i, *_: (i, 0, 0)),
            ],
            out_specs=[
                rows_spec(INNER),
                whole((length, width)),
                whole((PAIRS, BUCKETS, WIDE)),
            ],
            scratch_shapes=[
                pltpu.VMEM((INNER, length), jnp.bfloat16),
                pltpu.VMEM((PAIRS, key_blocks, BLOCK, WIDE), jnp.float32),
                pltpu.VMEM((PAIRS, key_blocks, BLOCK, WIDE), jnp.float32),
                pltpu.VMEM((length, width), jnp.float32),
                pltpu.VMEM((PAIRS, OFFSETS, BLOCK, WIDE), jnp.float32),
                pltpu.VMEM((PAIRS, BLOCK, WIDE), jnp.float32),
            ],
        ),
        out_shape=[
            jax.ShapeDtypeStruct((tokens, INNER), jnp.bfloat16),
            jax.ShapeDtypeStruct((length, width), jnp.bfloat16),
            jax.ShapeDtypeStruct((PAIRS, BUCKETS, WIDE), jnp.float32),
        ],
        compiler_params=pltpu.CompilerParams(vmem_limit_bytes=48 << 20),
        cost_estimate=pl.CostEstimate(
            flops=tokens * length * INNER * 10,
            bytes_accessed=12 << 20,
            transcendentals=tokens * length * 3,
        ),
        name="attend_backward",
    )(lows, highs, queries, grad_mixed, shared, own_rows, segment_wide, tiles, log_total)
    table = jnp.sum(bucket_sums.reshape(PAIRS, BUCKETS, 2, BLOCK), axis=3)
    return grad_query, grad_shared, table.transpose(1, 0, 2).reshape(BUCKETS, HEADS)


def attention_context(segment_row, first_pos, tokens, rel_bias):
    steps = tokens // BLOCK
    padded = jnp.pad(segment_row, (HALO, 0), constant_values=-1)
    padded = jnp.pad(padded, (0, HALO), constant_values=1000)
    window = lax.dynamic_slice_in_dim(padded, first_pos, tokens + 2 * HALO, 0)
    own = window[HALO : HALO + tokens].reshape(steps, 1, BLOCK)
    lows = jnp.sum(window[None, :] < own[:, 0, :1], axis=1, dtype=jnp.int32) // BLOCK
    ends = jnp.sum(window[None, :] <= own[:, 0, BLOCK - 1 :], axis=1, dtype=jnp.int32)
    highs = (ends + BLOCK - 1) // BLOCK
    segment_wide = jnp.broadcast_to(window[:, None], (window.shape[0], BLOCK))
    return lows, highs, own, segment_wide, bias_tiles(rel_bias)


def rms_forward(stream, gain_row):
    inverse = lax.rsqrt(jnp.mean(stream * stream, axis=1, keepdims=True) + epsilon)
    return (stream * inverse * gain_row, inverse)


def stream_backward(stream, inverse, scaled):
    return inverse * scaled - stream * inverse**3 * jnp.mean(scaled * stream, axis=1, keepdims=True)


def rms_backward(stream, inverse, gain_row, grad_normed):
    grad_gain = jnp.sum(grad_normed * stream * inverse, axis=0)
    return (stream_backward(stream, inverse, gain_row * grad_normed), grad_gain)


def gelu_tanh(values):
    return 0.5 * values * (1.0 + jnp.tanh(0.7978845608028654 * (values + 0.044715 * values**3)))


def times_rows(left_side, weight):
    return lax.dot_general(
        left_side, weight, (((1,), (1,)), ((), ())), preferred_element_type=jnp.float32
    )


def times_plain(left_side, weight):
    return jnp.dot(left_side, weight, preferred_element_type=jnp.float32)


def outer_sum(left_side, right_side):
    return lax.dot_general(
        left_side, right_side, (((0,), (0,)), ((), ())), preferred_element_type=jnp.float32
    )


def shift(value, axis, amount):
    count = lax.axis_size(axis)
    return lax.ppermute(value, axis, [(i, (i + amount) % count) for i in range(count)])


def slide(value, amount):
    count = lax.axis_size("z")
    pairs = [(i, i + amount) for i in range(count) if 0 <= i + amount < count]
    return lax.ppermute(value, "z", pairs)


def halo_pieces(tokens):
    pieces = []
    distance, covered = 1, 0
    while covered < HALO:
        span = min(tokens, HALO - covered)
        needed = min(span, -(-(REACH - covered) // 16) * 16)
        pieces.append((distance, span, needed))
        distance, covered = distance + 1, covered + span
    return pieces


def with_neighbours(own):
    tokens = own.shape[0]
    before, after = [], []
    for distance, span, needed in halo_pieces(tokens):
        if distance < lax.axis_size("z"):
            left = slide(own[tokens - needed :], distance)
            right = slide(own[:needed], -distance)
            before.append(jnp.pad(left, ((span - needed, 0), (0, 0))))
            after.append(jnp.pad(right, ((0, span - needed), (0, 0))))
        else:
            empty = jnp.zeros((span, own.shape[1]), own.dtype)
            before.append(empty)
            after.append(empty)
    return jnp.concatenate(before[::-1] + [own] + after, axis=0)


def start_back(window, tokens):
    moved = []
    covered = 0
    for distance, span, needed in halo_pieces(tokens):
        if distance < lax.axis_size("z"):
            left_end = HALO - covered
            right_start = HALO + tokens + covered
            back = slide(window[left_end - needed : left_end], -distance)
            ahead = slide(window[right_start : right_start + needed], distance)
            moved.append((back, ahead))
        covered += span
    return window[HALO : HALO + tokens], moved


def finish_back(own, moved):
    tokens = own.shape[0]
    total = own.astype(jnp.float32)
    for back, ahead in moved:
        needed = back.shape[0]
        total = total + jnp.pad(back.astype(jnp.float32), ((tokens - needed, 0), (0, 0)))
        total = total + jnp.pad(ahead.astype(jnp.float32), ((0, tokens - needed), (0, 0)))
    return total


def sum_everywhere(value):
    for axis in ("c", "x", "y", "z"):
        count = lax.axis_size(axis)
        bit = 1
        while bit < count:
            value = value + lax.ppermute(value, axis, [(i, i ^ bit) for i in range(count)])
            bit *= 2
    return value


def pick(value, index, axis):
    return lax.dynamic_index_in_dim(value, index, axis, keepdims=False)


def stage_sends(value, axis_name, axis):
    count, here = lax.axis_size(axis_name), lax.axis_index(axis_name)
    return [pick(value, (here + k) % count, axis) for k in range(1, count)]


def stage_moves(sends, axis_name):
    return [shift(sent, axis_name, k + 1) for k, sent in enumerate(sends)]


def gelu_parts(values):
    squared = values * values
    slope = jnp.tanh(0.7978845608028654 * (values + 0.044715 * values * squared))
    active = 0.5 * values * (1.0 + slope)
    inner = 0.7978845608028654 * (1.0 + 3.0 * 0.044715 * squared)
    return active, 0.5 * (1.0 + slope) + 0.5 * values * (1.0 - slope * slope) * inner


def ffn_forward_body(normed_ref, middle_ref, gelu_ref, linear_ref, down_ref, *outs):
    result_ref, up_gelu_ref, up_linear_ref = outs

    @pl.when(pl.program_id(0) == 0)
    def _():
        result_ref[...] = middle_ref[...]

    up_gelu = times_rows(normed_ref[...], gelu_ref[...])
    up_linear = times_rows(normed_ref[...], linear_ref[...])
    up_gelu_ref[...] = up_gelu
    up_linear_ref[...] = up_linear
    hidden = (gelu_tanh(up_gelu) * up_linear).astype(jnp.bfloat16)
    result_ref[...] += times_plain(hidden, down_ref[...])


def resident(shape):
    return pl.BlockSpec(shape, lambda *_: (0,) * len(shape), pipeline_mode=pl.Buffered(1))


def ffn_forward(normed, middle, gathered):
    tokens, width = normed.shape
    steps = FF // FORWARD_TILE
    first = 4 * INNER // FORWARD_TILE

    def weight(kind):
        return pl.BlockSpec((FORWARD_TILE, width), lambda i: (first + kind * steps + i, 0))

    hidden = pl.BlockSpec((tokens, FORWARD_TILE), lambda i: (0, i))
    return pl.pallas_call(
        ffn_forward_body,
        grid=(steps,),
        in_specs=[
            resident((tokens, width)),
            resident((tokens, width)),
            weight(0),
            weight(1),
            weight(2),
        ],
        out_specs=[resident((tokens, width)), hidden, hidden],
        out_shape=[
            jax.ShapeDtypeStruct((tokens, width), jnp.float32),
            jax.ShapeDtypeStruct((tokens, FF), jnp.float32),
            jax.ShapeDtypeStruct((tokens, FF), jnp.float32),
        ],
        compiler_params=pltpu.CompilerParams(vmem_limit_bytes=48 << 20),
        cost_estimate=pl.CostEstimate(
            flops=6 * tokens * FF * width,
            bytes_accessed=6 * FF * width + 8 * tokens * FF,
            transcendentals=tokens * FF,
        ),
        name="ffn_forward",
    )(normed, middle, gathered, gathered, gathered)


def ffn_backward_body(core_ref, *refs):
    branch_ref, normed_ref, up_gelu_ref, up_linear_ref, gelu_ref, linear_ref, down_ref = refs[:7]
    grad_ref, kept_ref, sent_ref, stage_ref, sems = refs[7:]
    step = pl.program_id(0)
    hidden_steps = FF // TILE
    slot = step % 2
    mine, unit = core_ref[0], core_ref[1]

    def copy(kind, place, at, where):
        spot = pl.ds(pl.multiple_of(at * TILE, TILE), TILE)
        return pltpu.make_async_copy(
            stage_ref.at[where, kind], place.at[spot, :], sems.at[where, kind]
        )

    def put(kind, turned):
        target = ATTENTION_TILES + kind * hidden_steps + step
        stage_ref[slot, kind] = turned
        own = (target // unit) % 2 == mine
        at = (target // (2 * unit)) * unit + target % unit

        @pl.when(own)
        def _():
            copy(kind, kept_ref, at, slot).start()

        @pl.when(jnp.logical_not(own))
        def _():
            copy(kind, sent_ref, at, slot).start()

    @pl.when(step == 0)
    def _():
        grad_ref[...] = jnp.zeros_like(grad_ref)

    @pl.when(step >= 2)
    def _():
        for kind in range(3):
            copy(kind, kept_ref, 0, slot).wait()

    grad_hidden = times_rows(branch_ref[...], down_ref[...])
    active, slope = gelu_parts(up_gelu_ref[...])
    linear = up_linear_ref[...]
    grad_gelu = (grad_hidden * linear * slope).astype(jnp.bfloat16)
    grad_linear = (grad_hidden * active).astype(jnp.bfloat16)
    put(2, (active * linear).astype(jnp.bfloat16).T)
    put(0, grad_gelu.T)
    put(1, grad_linear.T)
    grad_ref[...] += times_plain(grad_gelu, gelu_ref[...]) + times_plain(
        grad_linear, linear_ref[...]
    )

    @pl.when(step == hidden_steps - 1)
    def _():
        for back in range(2):
            for kind in range(3):
                copy(kind, kept_ref, 0, back).wait()


def unit_tiles(tile):
    rows = 4 * INNER + 3 * FF
    return rows // tile // (2 * lax.axis_size("y") * lax.axis_size("x"))


def ffn_backward(branch, normed, up_gelu, up_linear, gathered):
    tokens, width = normed.shape
    rows = 4 * INNER + 3 * FF
    steps = FF // TILE
    core = jnp.stack([lax.axis_index("c").astype(jnp.int32), jnp.int32(unit_tiles(TILE))])

    def weight(kind):
        first = ATTENTION_TILES + kind * steps
        return pl.BlockSpec((TILE, width), lambda i, *_: (first + i, 0))

    hidden = pl.BlockSpec((tokens, TILE), lambda i, *_: (0, i))
    side = resident((tokens, width))
    anywhere = pl.BlockSpec(memory_space=pl.ANY)
    return pl.pallas_call(
        ffn_backward_body,
        grid_spec=pltpu.PrefetchScalarGridSpec(
            num_scalar_prefetch=1,
            grid=(steps,),
            in_specs=[side, side, hidden, hidden, weight(0), weight(1), weight(2)],
            out_specs=[side, anywhere, anywhere],
            scratch_shapes=[
                pltpu.VMEM((2, 3, TILE, tokens), jnp.bfloat16),
                pltpu.SemaphoreType.DMA((2, 3)),
            ],
        ),
        out_shape=[jax.ShapeDtypeStruct((tokens, width), jnp.float32)]
        + [jax.ShapeDtypeStruct((rows // 2, tokens), jnp.bfloat16)] * 2,
        compiler_params=pltpu.CompilerParams(vmem_limit_bytes=48 << 20),
        cost_estimate=pl.CostEstimate(
            flops=6 * tokens * FF * width,
            bytes_accessed=6 * FF * width + 14 * tokens * FF,
            transcendentals=tokens * FF,
        ),
        name="ffn_backward",
    )(core, branch, normed, up_gelu, up_linear, gathered, gathered, gathered)


def weight_grads_body(route, tile, place_ref, *refs):
    own_ref, other_ref = refs[:2]
    normed_refs, branch_refs = refs[2:4], refs[4:6]
    outs = refs[6:]
    step = pl.program_id(0)
    count = len(outs) // 2
    per_place = pl.num_programs(0) // count
    source = weight_source(route, tile, step, place_ref)
    unit = place_ref[3]
    at = (source // unit * 2 + place_ref[2]) * unit + source % unit
    first, second = 4 * INNER // tile, (4 * INNER + 2 * FF) // tile

    def put(product_of):
        for turn in range(2):
            chunk = 2 * turn + (0 if route == "y" else 1)
            start, end = CUTS[chunk], CUTS[chunk + 1]
            product = product_of(slice(start, end))
            for k in range(count):

                @pl.when(step // per_place == k)
                def _(k=k, turn=turn, product=product, width=end - start):
                    out = outs[2 * k + turn]
                    out[:, :width] = product.astype(jnp.bfloat16)
                    if width < CHUNK:
                        out[:, width:] = jnp.zeros((tile, CHUNK - width), jnp.bfloat16)

    def both(sides):
        def product_of(columns):
            return jnp.dot(
                own_ref[...], sides[0][:, columns], preferred_element_type=jnp.float32
            ) + jnp.dot(other_ref[...], sides[1][:, columns], preferred_element_type=jnp.float32)

        return product_of

    @pl.when(at < first)
    def _():
        put(lambda columns: jnp.zeros((tile, columns.stop - columns.start), jnp.float32))

    @pl.when((at >= first) & (at < second))
    def _():
        put(both(normed_refs))

    @pl.when(at >= second)
    def _():
        put(both(branch_refs))


def weight_source(route, tile, step, place_ref):
    size_y, size_x, unit = place_ref[4], place_ref[5], place_ref[3]
    if route == "y":
        size, others, here = size_y, size_x, place_ref[0]
    else:
        size, others, here = size_x, size_y, place_ref[1]
    per_place = others * unit
    goal = (here + 1 + step // per_place) % size
    other = step % per_place // unit
    row, column = (goal, other) if route == "y" else (other, goal)
    return (row * size_x + column) * unit + step % unit


def weight_grads(route, own, other, normed, branch):
    rows, tokens = own.shape
    width = normed[0].shape[1]
    size_y, size_x = lax.axis_size("y"), lax.axis_size("x")
    tile = 512 if unit_tiles(256) % 2 == 0 else 256
    size = size_y if route == "y" else size_x
    steps = rows // tile
    per_place = steps // size
    place = jnp.stack(
        [
            lax.axis_index("y").astype(jnp.int32),
            lax.axis_index("x").astype(jnp.int32),
            lax.axis_index("c").astype(jnp.int32),
            jnp.int32(unit_tiles(tile)),
            jnp.int32(size_y),
            jnp.int32(size_x),
        ]
    )
    source = pl.BlockSpec(
        (tile, tokens), lambda i, place_ref: (weight_source(route, tile, i, place_ref), 0)
    )
    side = resident((tokens, width))

    def out_spec(k):
        return pl.BlockSpec(
            (tile, CHUNK), lambda i, *_: (jnp.clip(i - k * per_place, 0, per_place - 1), 0)
        )

    results = pl.pallas_call(
        functools.partial(weight_grads_body, route, tile),
        grid_spec=pltpu.PrefetchScalarGridSpec(
            num_scalar_prefetch=1,
            grid=(steps,),
            in_specs=[source, source, side, side, side, side],
            out_specs=[out_spec(k) for k in range(size) for _ in range(2)],
        ),
        out_shape=[jax.ShapeDtypeStruct((rows // size, CHUNK), jnp.bfloat16)] * (2 * size),
        compiler_params=pltpu.CompilerParams(vmem_limit_bytes=32 << 20),
        cost_estimate=pl.CostEstimate(
            flops=2 * rows * tokens * width,
            bytes_accessed=4 * rows * tokens + rows * width,
            transcendentals=0,
        ),
        name="weight_grads",
    )(place, own, other, *normed, *branch)
    return [[results[2 * k + turn] for k in range(size)] for turn in range(2)]


def with_attention(route, chunk, arrays, rows):
    size = lax.axis_size(route)
    unit_rows = rows.shape[0]
    owners = 4 * INNER // unit_rows
    start, end = CUTS[chunk], CUTS[chunk + 1]
    columns = jnp.pad(rows[:, start:end], ((0, 0), (0, CHUNK - end + start)))
    filled = []
    for k, array in enumerate(arrays):
        here = (lax.axis_index(route) + 1 + k) % size == 0
        here = here & (lax.axis_index("c") < owners)
        filled.append(
            lax.dynamic_update_slice(
                array, jnp.where(here, columns, array[:unit_rows]), (0, 0)
            )
        )
    return filled


def tied(first, second):
    return lax.optimization_barrier((first, second))


class Scatter:
    def __init__(self):
        self.waiting, self.flying, self.results = {}, {}, {}

    def push(self, name, route, kept, sends):
        self.waiting[name] = (route, kept, sends)

    def step(self, values, *names):
        arrays = {name: self.flying[name][1:] for name in names if name in self.flying}
        arrays, values = tied(arrays, values)
        moves = {}
        for name in names:
            if name in self.waiting:
                moves[name] = self.waiting.pop(name)
                continue
            route = self.flying.pop(name)[0]
            kept, moved = arrays[name]
            if not route:
                self.results[name] = kept.astype(jnp.float32) + sum(
                    part.astype(jnp.float32) for part in moved
                )
                continue
            total = total_of(kept, moved)
            total = total.reshape((lax.axis_size(route[0]), -1) + total.shape[-1:])
            sends = stage_sends(total, route[0], 0)
            moves[name] = (route, pick(total, lax.axis_index(route[0]), 0), sends)
        arrays, values = tied({name: move[1:] for name, move in moves.items()}, values)
        for name, (route, *_) in moves.items():
            kept, sends = arrays[name]
            self.flying[name] = (route[1:], kept, stage_moves(sends, route[0]))
        return values


def total_of(value, moved):
    total = value.astype(jnp.float32)
    for part in moved:
        total = total + part.astype(jnp.float32)
    return total.astype(jnp.bfloat16)


def fetch_rows(local_rows):
    return lax.all_gather(local_rows, DEVICES, axis=0, tiled=True)


def layer_forward(stream, gathered, gain_one, gain_two, gate_low, context):
    normed, inverse_one = rms_forward(stream, gain_one)
    normed_low = normed.astype(jnp.bfloat16)
    projected = times_rows(normed_low, gathered[: 3 * INNER]).astype(jnp.bfloat16)
    queries = projected[:, :INNER]
    parts = [projected[:, INNER:]]
    if gate_low is not None:
        parts.append(jnp.broadcast_to(gate_low[:, None], (stream.shape[0], BLOCK)))
    shared = with_neighbours(jnp.concatenate(parts, axis=1))
    attended, log_total = attend_forward(queries, shared, context)
    middle = stream + times_plain(attended, gathered[3 * INNER : 4 * INNER])
    normed_two, inverse_two = rms_forward(middle, gain_two)
    normed_two_low = normed_two.astype(jnp.bfloat16)
    result, up_gelu, up_linear = ffn_forward(normed_two_low, middle, gathered)
    kept = (
        stream,
        inverse_one,
        normed_low,
        queries,
        shared,
        attended,
        log_total,
        middle,
        inverse_two,
        normed_two_low,
        up_gelu,
        up_linear,
    )
    return (result, kept)


def layer_backward(grad_out, kept, gathered, gain_one, gain_two, context, scatter, name, steps):
    (
        stream,
        inverse_one,
        normed_low,
        queries,
        shared,
        attended,
        log_total,
        middle,
        inverse_two,
        normed_two_low,
        up_gelu,
        up_linear,
    ) = kept
    tokens = queries.shape[0]
    branch_low = grad_out.astype(jnp.bfloat16)
    normed_pair = (normed_two_low, shift(normed_two_low, "c", 1))
    branch_pair = (branch_low, shift(branch_low, "c", 1))
    grad_normed_two, own, sent = ffn_backward(
        branch_low, normed_two_low, up_gelu, up_linear, gathered
    )
    other = shift(sent, "c", 1)
    grad_middle, grad_gain_two = rms_backward(middle, inverse_two, gain_two, grad_normed_two)
    grad_middle = grad_out + grad_middle
    middle_low = grad_middle.astype(jnp.bfloat16)
    grad_mixed = times_rows(middle_low, gathered[3 * INNER : 4 * INNER]).astype(jnp.bfloat16)
    grad_mixed, grad_middle, middle_low = steps[0]((grad_mixed, grad_middle, middle_low))
    grad_query, grad_shared, grad_table = attend_backward(
        queries, grad_mixed, shared, log_total, context
    )
    grad_shared, own = lax.optimization_barrier((grad_shared, own))
    moving = start_back(grad_shared, tokens)
    routed = {
        route: weight_grads(route, own, other, normed_pair, branch_pair) for route in ("y", "x")
    }
    output_rows = outer_sum(attended, middle_low).astype(jnp.bfloat16)
    routed, output_rows, moving = steps[1]((routed, output_rows, moving))
    grad_own = finish_back(*moving)
    grad_gate = grad_own[:, 2 * INNER :]
    grad_input_low = jnp.concatenate(
        [grad_query, grad_own[:, : 2 * INNER].astype(jnp.bfloat16)], axis=1
    )
    rows = jnp.concatenate(
        [outer_sum(grad_input_low, normed_low).astype(jnp.bfloat16), output_rows], axis=0
    )
    unit_rows = unit_tiles(TILE) * TILE
    core = lax.axis_index("c")
    most = 4 * INNER // unit_rows - 1
    kept_rows, sent_rows = (
        lax.dynamic_slice_in_dim(rows, jnp.minimum(at, most) * unit_rows, unit_rows, 0)
        for at in (core, 1 - core)
    )
    rows = total_of(kept_rows, [shift(sent_rows, "c", 1)])
    for chunk in range(4):
        route = ("y", "x", "z") if chunk % 2 == 0 else ("x", "y", "z")
        arrays = with_attention(route[0], chunk, routed[route[0]][chunk // 2], rows)
        scatter.push((name, chunk), route, arrays[-1], arrays[:-1])
    grad_input_low, grad_gate = steps[2]((grad_input_low, grad_gate))
    grad_normed = times_plain(grad_input_low, gathered[: 3 * INNER])
    grad_stream, grad_gain_one = rms_backward(stream, inverse_one, gain_one, grad_normed)
    return (grad_middle + grad_stream, grad_table, grad_gate, grad_gain_one, grad_gain_two)


def per_device(
    inputs, layer3_rows, layer4_rows, norm_gains, gate_weight, rel_bias, segment_ids, cotangent
):
    seqs_here, tokens_here, width = inputs.shape
    first_pos = lax.axis_index("z") * tokens_here
    context = attention_context(segment_ids[0], first_pos, tokens_here, rel_bias)
    stream = inputs.reshape(tokens_here, width)
    gathered_three = fetch_rows(layer3_rows)
    after_three, kept_three = layer_forward(
        stream, gathered_three, norm_gains[0], norm_gains[1], None, context
    )
    gate_inverse = lax.rsqrt(jnp.mean(after_three * after_three, axis=1, keepdims=True) + epsilon)
    gate_normed = after_three * gate_inverse
    gate_logit = jnp.sum(gate_normed * gate_weight, axis=1) + gate_offset
    sigmoid_value = 1.0 / (1.0 + jnp.exp(-gate_logit))
    gate_mask = gate_scale * sigmoid_value
    gate_low = gate_mask.astype(jnp.bfloat16)
    gathered_four = fetch_rows(layer4_rows)
    after_four, kept_four = layer_forward(
        after_three, gathered_four, norm_gains[2], norm_gains[3], gate_low, context
    )
    scatter = Scatter()

    def step(*names):
        return lambda values: scatter.step(values, *names)

    four, three = ([(name, chunk) for chunk in range(4)] for name in ("four", "three"))
    grad_three_out, table_four, grad_gate, gain_four_one, gain_four_two = layer_backward(
        cotangent.reshape(tokens_here, width),
        kept_four,
        gathered_four,
        norm_gains[2],
        norm_gains[3],
        context,
        scatter,
        "four",
        [step(), step(), step(*four)],
    )
    grad_logit = grad_gate[:, 0] * gate_scale * sigmoid_value * (1.0 - sigmoid_value)
    grad_gate_weight = jnp.sum(grad_logit[:, None] * gate_normed, axis=0)
    gate_stream = stream_backward(after_three, gate_inverse, grad_logit[:, None] * gate_weight)
    grad_input, table_three, unused, gain_three_one, gain_three_two = layer_backward(
        grad_three_out + gate_stream,
        kept_three,
        gathered_three,
        norm_gains[0],
        norm_gains[1],
        context,
        scatter,
        "three",
        [step(*four[:2]), step(*four[2:]), step(*four[:2], *three[:2])],
    )
    for names in (
        four[2:],
        three[:2] + three[2:],
        four[:2],
        three[:2],
        three[2:],
        four[2:],
        three[2:],
        three[:2],
        three[2:],
    ):
        grad_input = scatter.step(grad_input, *names)
    local_four, local_three = (
        jnp.concatenate([scatter.results[name] for name in names], axis=1)[:, :width]
        for names in (four, three)
    )
    table = jnp.pad((table_three + table_four).reshape(1, -1), ((0, 0), (0, width - 6 * BUCKETS)))
    small = jnp.stack(
        [gain_three_one, gain_three_two, gain_four_one, gain_four_two, grad_gate_weight, table[0]]
    )
    summed = sum_everywhere(small)
    return (
        after_four.reshape(inputs.shape),
        gate_mask.reshape(seqs_here, tokens_here),
        grad_input.reshape(inputs.shape),
        local_three,
        local_four,
        summed[:4],
        summed[4],
        summed[5, : 6 * BUCKETS].reshape(BUCKETS, HEADS),
    )


def solution(mesh):
    outer, inner = mesh.devices.shape
    fine = Mesh(mesh.devices.reshape(outer // 4, 2, 2, inner), DEVICES)
    batch = ("y", "x", "c")
    tokens = P(batch, "z", None)
    rows = P(DEVICES, None)
    return jax.shard_map(
        per_device,
        mesh=fine,
        in_specs=(tokens, rows, rows, P(), P(), P(), P(batch, None), tokens),
        out_specs=(tokens, P(batch, "z"), tokens, rows, rows, P(), P(), P()),
        check_vma=False,
    )
```

```python
import functools

import jax
import jax.numpy as jnp
from jax import lax
from jax.experimental import pallas as pl
from jax.experimental.pallas import tpu as pltpu
from jax.sharding import Mesh
from jax.sharding import PartitionSpec as P

HEADS = 6
PAIRS = 3
BLOCK = 128
WIDE = 2 * BLOCK
INNER = 384
BUCKETS = 32
FF = 3584
REACH = 799
HALO = 896
TILE = 256
ATTENTION_TILES = 4 * INNER // TILE
OFFSETS = 5
CHUNK = 384
PADDED = 1536
FORWARD_TILE = 512
CUTS = (0, 384, 768, 1152, 1472)
DEVICES = ("y", "x", "c", "z")
epsilon = 1e-06
gate_scale = -30.0
gate_offset = -3.5
masked_out = -1e30
limits = (12, 16, 23, 32, 46, 64, 91)
both_last = (((1,), (1,)), ((), ()))


def bucket_of(relative):
    magnitude = jnp.abs(relative)
    beyond = jnp.zeros_like(magnitude)
    for bound_value in limits:
        beyond = beyond + (magnitude >= bound_value).astype(jnp.int32)
    inside = jnp.where(magnitude < 8, magnitude, 8 + beyond)
    return inside + 16 * (relative > 0).astype(jnp.int32)


def near_buckets(offset):
    if offset < 0:
        return range(1, 16)
    if offset > 0:
        return range(17, 32)
    return range(0, 32)


def tile_buckets(offset, width):
    key_at = lax.broadcasted_iota(jnp.int32, (BLOCK, width), 0)
    query_at = lax.broadcasted_iota(jnp.int32, (BLOCK, width), 1) % BLOCK
    return bucket_of(offset * BLOCK + key_at - query_at)


def bias_body(table_ref, tiles_ref):
    head = pl.program_id(0)
    tiles_ref[0, 0] = jnp.full((BLOCK, BLOCK), table_ref[15, head], jnp.float32)
    tiles_ref[0, 4] = jnp.full((BLOCK, BLOCK), table_ref[31, head], jnp.float32)
    for offset in (-1, 0, 1):
        buckets = tile_buckets(offset, BLOCK)
        tile = jnp.zeros((BLOCK, BLOCK), jnp.float32)
        for bucket in near_buckets(offset):
            tile = jnp.where(buckets == bucket, table_ref[bucket, head], tile)
        tiles_ref[0, offset + 2] = tile


def bias_tiles(rel_bias):
    return pl.pallas_call(
        bias_body,
        grid=(HEADS,),
        in_specs=[pl.BlockSpec(memory_space=pltpu.SMEM)],
        out_specs=pl.BlockSpec((1, OFFSETS, BLOCK, BLOCK), lambda h: (h, 0, 0, 0)),
        out_shape=jax.ShapeDtypeStruct((HEADS, OFFSETS, BLOCK, BLOCK), jnp.float32),
        name="bias_tiles",
    )(rel_bias)


def lane_masks():
    lane = lax.broadcasted_iota(jnp.int32, (BLOCK, BLOCK), 1)
    low = jnp.where(lane < 64, 1.0, 0.0).astype(jnp.bfloat16)
    high = jnp.where(lane < 64, 0.0, 1.0).astype(jnp.bfloat16)
    return low, high


def stacked(block, masks):
    low, high = masks
    return jnp.concatenate([block * low, block * high], axis=0)


def pair_cols(pair):
    return slice(pair * BLOCK, (pair + 1) * BLOCK)


def value_cols(pair):
    return slice(INNER + pair * BLOCK, INNER + (pair + 1) * BLOCK)


def block_rows(block):
    return pl.ds(pl.multiple_of(block * BLOCK, BLOCK), BLOCK)


def fold(values):
    return values.reshape(BLOCK // 8, 8, WIDE)


def shift_tile(gated, rows, own_segment, segment_ref, shared_ref):
    same = segment_ref[rows, :] == own_segment
    inside = shared_ref[rows, 2 * INNER :].astype(jnp.float32) if gated else 0.0
    shift = jnp.where(same, inside, masked_out)
    return jnp.concatenate([shift, shift], axis=1)


def bias_pair(bias_ref, pair, offset):
    return jnp.concatenate([bias_ref[2 * pair, offset], bias_ref[2 * pair + 1, offset]], axis=1)


def pick_heads(wide):
    return jnp.concatenate([wide[:64, :BLOCK], wide[64:, BLOCK:]], axis=0)


def forward_body(gated, low_ref, high_ref, *refs):
    query_ref, shared_ref, own_ref, segment_ref, bias_ref = refs[:5]
    mixed_ref, total_ref, turned_ref, score_ref = refs[5:]
    step = pl.program_id(0)
    key_blocks = shared_ref.shape[0] // BLOCK

    @pl.when(step == 0)
    def _():
        @pl.loop(0, key_blocks)
        def _(block):
            rows = block_rows(block)
            turned_ref[:, rows] = shared_ref[rows, INNER : 2 * INNER].T

    first, last = low_ref[step], high_ref[step]
    own_block = HALO // BLOCK + step
    own_segment = own_ref[0]
    masks = lane_masks()
    queries = [stacked(query_ref[:, pair_cols(pair)], masks) for pair in range(PAIRS)]

    def scores(block, peaks):
        rows = block_rows(block)
        shift = shift_tile(gated, rows, own_segment, segment_ref, shared_ref)
        offset = jnp.clip(block - own_block, -2, 2) + 2
        new_peaks = []
        for pair in range(PAIRS):
            score = lax.dot_general(
                shared_ref[rows, pair_cols(pair)],
                queries[pair],
                both_last,
                preferred_element_type=jnp.float32,
            )
            score = score + bias_pair(bias_ref, pair, offset) + shift
            score_ref[pair, block] = score
            new_peaks.append(jnp.maximum(peaks[pair], jnp.max(fold(score), axis=0)))
        return tuple(new_peaks)

    start = jnp.full((8, WIDE), -3e38, jnp.float32)
    peaks = lax.fori_loop(first, last, scores, (start,) * PAIRS)
    for pair in range(PAIRS):
        peak = jnp.max(peaks[pair], axis=0, keepdims=True)

        def mix(block, carry, pair=pair, peak=peak):
            total, mixed = carry
            weight = jnp.exp(score_ref[pair, block] - peak)
            total = total + jnp.sum(fold(weight), axis=0)
            mixed = mixed + jnp.dot(
                turned_ref[pair_cols(pair), block_rows(block)],
                weight.astype(jnp.bfloat16),
                preferred_element_type=jnp.float32,
            )
            return total, mixed

        zero = (jnp.zeros((8, WIDE), jnp.float32), jnp.zeros((BLOCK, WIDE), jnp.float32))
        total, mixed = lax.fori_loop(first, last, mix, zero)
        row_total = jnp.sum(total, axis=0, keepdims=True)
        mixed = pick_heads(mixed * (1.0 / row_total))
        mixed_ref[:, pair_cols(pair)] = mixed.T.astype(jnp.bfloat16)
        total_ref[0, pair : pair + 1, :] = peak + jnp.log(row_total)


def whole(shape):
    return pl.BlockSpec(shape, lambda i, *_: (0,) * len(shape), pipeline_mode=pl.Buffered(1))


def rows_spec(width):
    return pl.BlockSpec((BLOCK, width), lambda i, *_: (i, 0))


def attend_forward(queries, shared, context):
    lows, highs, own_rows, segment_wide, tiles = context
    tokens, (length, width) = queries.shape[0], shared.shape
    steps, key_blocks = tokens // BLOCK, length // BLOCK
    return pl.pallas_call(
        functools.partial(forward_body, width > 2 * INNER),
        grid_spec=pltpu.PrefetchScalarGridSpec(
            num_scalar_prefetch=2,
            grid=(steps,),
            in_specs=[
                rows_spec(INNER),
                whole((length, width)),
                pl.BlockSpec((1, 1, BLOCK), lambda i, *_: (i, 0, 0)),
                whole((length, BLOCK)),
                whole(tiles.shape),
            ],
            out_specs=[
                rows_spec(INNER),
                pl.BlockSpec((1, 8, WIDE), lambda i, *_: (i, 0, 0)),
            ],
            scratch_shapes=[
                pltpu.VMEM((INNER, length), jnp.bfloat16),
                pltpu.VMEM((PAIRS, key_blocks, BLOCK, WIDE), jnp.float32),
            ],
        ),
        out_shape=[
            jax.ShapeDtypeStruct((tokens, INNER), jnp.bfloat16),
            jax.ShapeDtypeStruct((steps, 8, WIDE), jnp.float32),
        ],
        compiler_params=pltpu.CompilerParams(vmem_limit_bytes=40 << 20),
        cost_estimate=pl.CostEstimate(
            flops=tokens * length * INNER * 4,
            bytes_accessed=8 << 20,
            transcendentals=tokens * length * 3,
        ),
        name="attend_forward",
    )(lows, highs, queries, shared, own_rows, segment_wide, tiles)


def backward_body(gated, low_ref, high_ref, *refs):
    query_ref, grad_ref, shared_ref, own_ref, segment_ref, bias_ref, total_ref = refs[:7]
    grad_query_ref, grad_shared_ref, bucket_ref = refs[7:10]
    turned_ref, prob_ref, pull_ref, sum_ref, bias_sum_ref, turn_sum_ref = refs[10:]
    step = pl.program_id(0)
    key_blocks = shared_ref.shape[0] // BLOCK

    @pl.when(step == 0)
    def _():
        bias_sum_ref[...] = jnp.zeros_like(bias_sum_ref)

        @pl.loop(0, key_blocks)
        def _(block):
            rows = block_rows(block)
            turned_ref[:, rows] = shared_ref[rows, :INNER].T
            sum_ref[rows, :] = jnp.zeros((BLOCK, sum_ref.shape[1]), jnp.float32)

    first, last = low_ref[step], high_ref[step]
    own_block = HALO // BLOCK + step
    own_segment = own_ref[0]
    masks = lane_masks()
    queries = [stacked(query_ref[:, pair_cols(pair)], masks) for pair in range(PAIRS)]
    grads = [stacked(grad_ref[:, pair_cols(pair)], masks) for pair in range(PAIRS)]
    totals = [total_ref[0, pair : pair + 1, :] for pair in range(PAIRS)]

    def weights(block, deltas):
        rows = block_rows(block)
        shift = shift_tile(gated, rows, own_segment, segment_ref, shared_ref)
        offset = jnp.clip(block - own_block, -2, 2) + 2
        new_deltas = []
        for pair in range(PAIRS):
            cols = pair_cols(pair)
            score = lax.dot_general(
                shared_ref[rows, cols], queries[pair], both_last, preferred_element_type=jnp.float32
            )
            pull = lax.dot_general(
                shared_ref[rows, value_cols(pair)],
                grads[pair],
                both_last,
                preferred_element_type=jnp.float32,
            )
            prob = jnp.exp(score + bias_pair(bias_ref, pair, offset) + shift - totals[pair])
            prob_ref[pair, block] = prob
            pull_ref[pair, block] = pull
            sum_ref[rows, value_cols(pair)] += jnp.dot(
                prob.astype(jnp.bfloat16), grads[pair], preferred_element_type=jnp.float32
            )
            new_deltas.append(deltas[pair] + jnp.sum(fold(prob * pull), axis=0))
        return tuple(new_deltas)

    start = jnp.zeros((8, WIDE), jnp.float32)
    deltas = lax.fori_loop(first, last, weights, (start,) * PAIRS)
    deltas = [jnp.sum(delta, axis=0, keepdims=True) for delta in deltas]
    turn_sum_ref[...] = jnp.zeros_like(turn_sum_ref)

    @pl.loop(first, last)
    def _(block):
        rows = block_rows(block)
        offset = jnp.clip(block - own_block, -2, 2) + 2
        gate_part = jnp.zeros((BLOCK, BLOCK), jnp.float32)
        for pair in range(PAIRS):
            cols = pair_cols(pair)
            grad_score = prob_ref[pair, block] * (pull_ref[pair, block] - deltas[pair])
            bias_sum_ref[pair, offset] += grad_score
            if gated:
                gate_part = gate_part + (grad_score[:, :BLOCK] + grad_score[:, BLOCK:])
            score_low = grad_score.astype(jnp.bfloat16)
            sum_ref[rows, cols] += jnp.dot(
                score_low, queries[pair], preferred_element_type=jnp.float32
            )
            turn_sum_ref[pair] += jnp.dot(
                turned_ref[cols, rows], score_low, preferred_element_type=jnp.float32
            )
        if gated:
            sum_ref[rows, 2 * INNER :] += gate_part

    for pair in range(PAIRS):
        grad_query_ref[:, pair_cols(pair)] = pick_heads(turn_sum_ref[pair]).T.astype(jnp.bfloat16)

    @pl.when(step == pl.num_programs(0) - 1)
    def _():
        @pl.loop(0, key_blocks)
        def _(block):
            rows = block_rows(block)
            both = slice(0, 2 * INNER)
            grad_shared_ref[rows, both] = sum_ref[rows, both].astype(jnp.bfloat16)
            if gated:
                gate_total = jnp.sum(sum_ref[rows, 2 * INNER :], axis=1, keepdims=True)
                grad_shared_ref[rows, 2 * INNER :] = jnp.broadcast_to(
                    gate_total, (BLOCK, BLOCK)
                ).astype(jnp.bfloat16)

        tables = {offset: tile_buckets(offset, WIDE) for offset in (-1, 0, 1)}

        @pl.loop(0, PAIRS)
        def _(pair):
            for bucket in range(BUCKETS):
                part = jnp.zeros((8, WIDE), jnp.float32)
                for offset in (-1, 0, 1):
                    if bucket in near_buckets(offset):
                        chosen = jnp.where(
                            tables[offset] == bucket, bias_sum_ref[pair, offset + 2], 0.0
                        )
                        part = part + jnp.sum(fold(chosen), axis=0)
                if bucket == 15:
                    part = part + jnp.sum(fold(bias_sum_ref[pair, 0]), axis=0)
                if bucket == 31:
                    part = part + jnp.sum(fold(bias_sum_ref[pair, 4]), axis=0)
                bucket_ref[pair, bucket : bucket + 1, :] = jnp.sum(part, axis=0, keepdims=True)


def attend_backward(queries, grad_mixed, shared, log_total, context):
    lows, highs, own_rows, segment_wide, tiles = context
    tokens, (length, width) = queries.shape[0], shared.shape
    steps, key_blocks = tokens // BLOCK, length // BLOCK
    grad_query, grad_shared, bucket_sums = pl.pallas_call(
        functools.partial(backward_body, width > 2 * INNER),
        grid_spec=pltpu.PrefetchScalarGridSpec(
            num_scalar_prefetch=2,
            grid=(steps,),
            in_specs=[
                rows_spec(INNER),
                rows_spec(INNER),
                whole((length, width)),
                pl.BlockSpec((1, 1, BLOCK), lambda i, *_: (i, 0, 0)),
                whole((length, BLOCK)),
                whole(tiles.shape),
                pl.BlockSpec((1, 8, WIDE), lambda i, *_: (i, 0, 0)),
            ],
            out_specs=[
                rows_spec(INNER),
                whole((length, width)),
                whole((PAIRS, BUCKETS, WIDE)),
            ],
            scratch_shapes=[
                pltpu.VMEM((INNER, length), jnp.bfloat16),
                pltpu.VMEM((PAIRS, key_blocks, BLOCK, WIDE), jnp.float32),
                pltpu.VMEM((PAIRS, key_blocks, BLOCK, WIDE), jnp.float32),
                pltpu.VMEM((length, width), jnp.float32),
                pltpu.VMEM((PAIRS, OFFSETS, BLOCK, WIDE), jnp.float32),
                pltpu.VMEM((PAIRS, BLOCK, WIDE), jnp.float32),
            ],
        ),
        out_shape=[
            jax.ShapeDtypeStruct((tokens, INNER), jnp.bfloat16),
            jax.ShapeDtypeStruct((length, width), jnp.bfloat16),
            jax.ShapeDtypeStruct((PAIRS, BUCKETS, WIDE), jnp.float32),
        ],
        compiler_params=pltpu.CompilerParams(vmem_limit_bytes=48 << 20),
        cost_estimate=pl.CostEstimate(
            flops=tokens * length * INNER * 10,
            bytes_accessed=12 << 20,
            transcendentals=tokens * length * 3,
        ),
        name="attend_backward",
    )(lows, highs, queries, grad_mixed, shared, own_rows, segment_wide, tiles, log_total)
    table = jnp.sum(bucket_sums.reshape(PAIRS, BUCKETS, 2, BLOCK), axis=3)
    return grad_query, grad_shared, table.transpose(1, 0, 2).reshape(BUCKETS, HEADS)


def attention_context(segment_row, first_pos, tokens, rel_bias):
    steps = tokens // BLOCK
    padded = jnp.pad(segment_row, (HALO, 0), constant_values=-1)
    padded = jnp.pad(padded, (0, HALO), constant_values=1000)
    window = lax.dynamic_slice_in_dim(padded, first_pos, tokens + 2 * HALO, 0)
    own = window[HALO : HALO + tokens].reshape(steps, 1, BLOCK)
    lows = jnp.sum(window[None, :] < own[:, 0, :1], axis=1, dtype=jnp.int32) // BLOCK
    ends = jnp.sum(window[None, :] <= own[:, 0, BLOCK - 1 :], axis=1, dtype=jnp.int32)
    highs = (ends + BLOCK - 1) // BLOCK
    segment_wide = jnp.broadcast_to(window[:, None], (window.shape[0], BLOCK))
    return lows, highs, own, segment_wide, bias_tiles(rel_bias)


def rms_forward(stream, gain_row):
    inverse = lax.rsqrt(jnp.mean(stream * stream, axis=1, keepdims=True) + epsilon)
    return (stream * inverse * gain_row, inverse)


def stream_backward(stream, inverse, scaled):
    return inverse * scaled - stream * inverse**3 * jnp.mean(scaled * stream, axis=1, keepdims=True)


def rms_backward(stream, inverse, gain_row, grad_normed):
    grad_gain = jnp.sum(grad_normed * stream * inverse, axis=0)
    return (stream_backward(stream, inverse, gain_row * grad_normed), grad_gain)


def gelu_tanh(values):
    return 0.5 * values * (1.0 + jnp.tanh(0.7978845608028654 * (values + 0.044715 * values**3)))


def times_rows(left_side, weight):
    return lax.dot_general(
        left_side, weight, (((1,), (1,)), ((), ())), preferred_element_type=jnp.float32
    )


def times_plain(left_side, weight):
    return jnp.dot(left_side, weight, preferred_element_type=jnp.float32)


def outer_sum(left_side, right_side):
    return lax.dot_general(
        left_side, right_side, (((0,), (0,)), ((), ())), preferred_element_type=jnp.float32
    )


def shift(value, axis, amount):
    count = lax.axis_size(axis)
    return lax.ppermute(value, axis, [(i, (i + amount) % count) for i in range(count)])


def slide(value, amount):
    count = lax.axis_size("z")
    pairs = [(i, i + amount) for i in range(count) if 0 <= i + amount < count]
    return lax.ppermute(value, "z", pairs)


def far_pair(near_start, near_end, distance):
    count = lax.axis_size("z")
    first_half = lax.axis_index("z") < distance
    sent = jnp.where(first_half, near_end, near_start)
    pairs = [(i, (i + distance) % count) for i in range(count)]
    got = lax.ppermute(sent, "z", pairs)
    return got


def far_split(got, distance):
    first_half = lax.axis_index("z") < distance
    none = jnp.zeros_like(got)
    return jnp.where(first_half, none, got), jnp.where(first_half, got, none)


def halo_pieces(tokens):
    pieces = []
    distance, covered = 1, 0
    while covered < HALO:
        span = min(tokens, HALO - covered)
        needed = min(span, -(-(REACH - covered) // 16) * 16)
        pieces.append((distance, span, needed))
        distance, covered = distance + 1, covered + span
    return pieces


def with_neighbours(own):
    tokens = own.shape[0]
    before, after = [], []
    for distance, span, needed in halo_pieces(tokens):
        if distance < lax.axis_size("z"):
            if 2 * distance == lax.axis_size("z"):
                left, right = far_split(
                    far_pair(own[:needed], own[tokens - needed :], distance), distance
                )
            else:
                left = slide(own[tokens - needed :], distance)
                right = slide(own[:needed], -distance)
            before.append(jnp.pad(left, ((span - needed, 0), (0, 0))))
            after.append(jnp.pad(right, ((0, span - needed), (0, 0))))
        else:
            empty = jnp.zeros((span, own.shape[1]), own.dtype)
            before.append(empty)
            after.append(empty)
    return jnp.concatenate(before[::-1] + [own] + after, axis=0)


def start_back(window, tokens):
    moved = []
    covered = 0
    for distance, span, needed in halo_pieces(tokens):
        if distance < lax.axis_size("z"):
            left_end = HALO - covered
            right_start = HALO + tokens + covered
            left = window[left_end - needed : left_end]
            right = window[right_start : right_start + needed]
            if 2 * distance == lax.axis_size("z"):
                moved.append((far_pair(left, right, distance),))
            else:
                moved.append((slide(left, -distance), slide(right, distance)))
        covered += span
    return window[HALO : HALO + tokens], moved


def finish_back(own, moved):
    tokens = own.shape[0]
    total = own.astype(jnp.float32)
    for distance, pair in enumerate(moved, 1):
        if len(pair) == 1:
            ahead, back = far_split(pair[0], distance)
        else:
            back, ahead = pair
        needed = back.shape[0]
        total = total + jnp.pad(back.astype(jnp.float32), ((tokens - needed, 0), (0, 0)))
        total = total + jnp.pad(ahead.astype(jnp.float32), ((0, tokens - needed), (0, 0)))
    return total


def hop(value, axis, bit=1):
    pairs = [(i, i ^ bit) for i in range(lax.axis_size(axis))]
    return value + lax.ppermute(value, axis, pairs)


def pick(value, index, axis):
    return lax.dynamic_index_in_dim(value, index, axis, keepdims=False)


def stage_sends(value, axis_name, axis):
    count, here = lax.axis_size(axis_name), lax.axis_index(axis_name)
    return [pick(value, (here + k) % count, axis) for k in range(1, count)]


def stage_moves(sends, axis_name):
    return [shift(sent, axis_name, k + 1) for k, sent in enumerate(sends)]


def gelu_parts(values):
    squared = values * values
    slope = jnp.tanh(0.7978845608028654 * (values + 0.044715 * values * squared))
    active = 0.5 * values * (1.0 + slope)
    inner = 0.7978845608028654 * (1.0 + 3.0 * 0.044715 * squared)
    return active, 0.5 * (1.0 + slope) + 0.5 * values * (1.0 - slope * slope) * inner


def ffn_forward_body(normed_ref, middle_ref, gelu_ref, linear_ref, down_ref, *outs):
    result_ref, up_gelu_ref, up_linear_ref = outs

    @pl.when(pl.program_id(0) == 0)
    def _():
        result_ref[...] = middle_ref[...]

    up_gelu = times_rows(normed_ref[...], gelu_ref[...])
    up_linear = times_rows(normed_ref[...], linear_ref[...])
    up_gelu_ref[...] = up_gelu
    up_linear_ref[...] = up_linear
    hidden = (gelu_tanh(up_gelu) * up_linear).astype(jnp.bfloat16)
    result_ref[...] += times_plain(hidden, down_ref[...])


def resident(shape):
    return pl.BlockSpec(shape, lambda *_: (0,) * len(shape), pipeline_mode=pl.Buffered(1))


def ffn_forward(normed, middle, gathered):
    tokens, width = normed.shape
    steps = FF // FORWARD_TILE
    first = 4 * INNER // FORWARD_TILE

    def weight(kind):
        return pl.BlockSpec((FORWARD_TILE, width), lambda i: (first + kind * steps + i, 0))

    hidden = pl.BlockSpec((tokens, FORWARD_TILE), lambda i: (0, i))
    return pl.pallas_call(
        ffn_forward_body,
        grid=(steps,),
        in_specs=[
            resident((tokens, width)),
            resident((tokens, width)),
            weight(0),
            weight(1),
            weight(2),
        ],
        out_specs=[resident((tokens, width)), hidden, hidden],
        out_shape=[
            jax.ShapeDtypeStruct((tokens, width), jnp.float32),
            jax.ShapeDtypeStruct((tokens, FF), jnp.float32),
            jax.ShapeDtypeStruct((tokens, FF), jnp.float32),
        ],
        compiler_params=pltpu.CompilerParams(vmem_limit_bytes=48 << 20),
        cost_estimate=pl.CostEstimate(
            flops=6 * tokens * FF * width,
            bytes_accessed=6 * FF * width + 8 * tokens * FF,
            transcendentals=tokens * FF,
        ),
        name="ffn_forward",
    )(normed, middle, gathered, gathered, gathered)


def ffn_backward_body(core_ref, *refs):
    branch_ref, normed_ref, up_gelu_ref, up_linear_ref, gelu_ref, linear_ref, down_ref = refs[:7]
    grad_ref, kept_ref, sent_ref, stage_ref, sems = refs[7:]
    step = pl.program_id(0)
    hidden_steps = FF // TILE
    slot = step % 2
    mine, unit = core_ref[0], core_ref[1]

    def copy(kind, place, at, where):
        spot = pl.ds(pl.multiple_of(at * TILE, TILE), TILE)
        return pltpu.make_async_copy(
            stage_ref.at[where, kind], place.at[spot, :], sems.at[where, kind]
        )

    def put(kind, turned):
        target = ATTENTION_TILES + kind * hidden_steps + step
        stage_ref[slot, kind] = turned
        own = (target // unit) % 2 == mine
        at = (target // (2 * unit)) * unit + target % unit

        @pl.when(own)
        def _():
            copy(kind, kept_ref, at, slot).start()

        @pl.when(jnp.logical_not(own))
        def _():
            copy(kind, sent_ref, at, slot).start()

    @pl.when(step == 0)
    def _():
        grad_ref[...] = jnp.zeros_like(grad_ref)

    @pl.when(step >= 2)
    def _():
        for kind in range(3):
            copy(kind, kept_ref, 0, slot).wait()

    grad_hidden = times_rows(branch_ref[...], down_ref[...])
    active, slope = gelu_parts(up_gelu_ref[...])
    linear = up_linear_ref[...]
    grad_gelu = (grad_hidden * linear * slope).astype(jnp.bfloat16)
    grad_linear = (grad_hidden * active).astype(jnp.bfloat16)
    put(2, (active * linear).astype(jnp.bfloat16).T)
    put(0, grad_gelu.T)
    put(1, grad_linear.T)
    grad_ref[...] += times_plain(grad_gelu, gelu_ref[...]) + times_plain(
        grad_linear, linear_ref[...]
    )

    @pl.when(step == hidden_steps - 1)
    def _():
        for back in range(2):
            for kind in range(3):
                copy(kind, kept_ref, 0, back).wait()


def unit_tiles(tile):
    rows = 4 * INNER + 3 * FF
    return rows // tile // (2 * lax.axis_size("y") * lax.axis_size("x"))


def ffn_backward(branch, normed, up_gelu, up_linear, gathered):
    tokens, width = normed.shape
    rows = 4 * INNER + 3 * FF
    steps = FF // TILE
    core = jnp.stack([lax.axis_index("c").astype(jnp.int32), jnp.int32(unit_tiles(TILE))])

    def weight(kind):
        first = ATTENTION_TILES + kind * steps
        return pl.BlockSpec((TILE, width), lambda i, *_: (first + i, 0))

    hidden = pl.BlockSpec((tokens, TILE), lambda i, *_: (0, i))
    side = resident((tokens, width))
    anywhere = pl.BlockSpec(memory_space=pl.ANY)
    return pl.pallas_call(
        ffn_backward_body,
        grid_spec=pltpu.PrefetchScalarGridSpec(
            num_scalar_prefetch=1,
            grid=(steps,),
            in_specs=[side, side, hidden, hidden, weight(0), weight(1), weight(2)],
            out_specs=[side, anywhere, anywhere],
            scratch_shapes=[
                pltpu.VMEM((2, 3, TILE, tokens), jnp.bfloat16),
                pltpu.SemaphoreType.DMA((2, 3)),
            ],
        ),
        out_shape=[jax.ShapeDtypeStruct((tokens, width), jnp.float32)]
        + [jax.ShapeDtypeStruct((rows // 2, tokens), jnp.bfloat16)] * 2,
        compiler_params=pltpu.CompilerParams(vmem_limit_bytes=48 << 20),
        cost_estimate=pl.CostEstimate(
            flops=6 * tokens * FF * width,
            bytes_accessed=6 * FF * width + 14 * tokens * FF,
            transcendentals=tokens * FF,
        ),
        name="ffn_backward",
    )(core, branch, normed, up_gelu, up_linear, gathered, gathered, gathered)


def weight_grads_body(route, tile, place_ref, *refs):
    own_ref, other_ref = refs[:2]
    normed_refs, branch_refs = refs[2:4], refs[4:6]
    outs = refs[6:]
    step = pl.program_id(0)
    count = max(len(outs) // 2, 1)
    per_place = pl.num_programs(0) // count
    source = weight_source(route, tile, step, place_ref)
    unit = place_ref[3]
    at = (source // unit * 2 + place_ref[2]) * unit + source % unit
    first, second = 4 * INNER // tile, (4 * INNER + 2 * FF) // tile

    def put(product_of):
        if route == "all":
            outs[0][:, : CUTS[-1]] = product_of(slice(0, CUTS[-1])).astype(jnp.bfloat16)
            outs[0][:, CUTS[-1] :] = jnp.zeros((tile, PADDED - CUTS[-1]), jnp.bfloat16)
            return
        for turn in range(2):
            chunk = 2 * turn + (0 if route == "y" else 1)
            start, end = CUTS[chunk], CUTS[chunk + 1]
            product = product_of(slice(start, end))
            for k in range(count):

                @pl.when(step // per_place == k)
                def _(k=k, turn=turn, product=product, width=end - start):
                    out = outs[2 * k + turn]
                    out[:, :width] = product.astype(jnp.bfloat16)
                    if width < CHUNK:
                        out[:, width:] = jnp.zeros((tile, CHUNK - width), jnp.bfloat16)

    def both(sides):
        def product_of(columns):
            return jnp.dot(
                own_ref[...], sides[0][:, columns], preferred_element_type=jnp.float32
            ) + jnp.dot(other_ref[...], sides[1][:, columns], preferred_element_type=jnp.float32)

        return product_of

    @pl.when(at < first)
    def _():
        put(lambda columns: jnp.zeros((tile, columns.stop - columns.start), jnp.float32))

    @pl.when((at >= first) & (at < second))
    def _():
        put(both(normed_refs))

    @pl.when(at >= second)
    def _():
        put(both(branch_refs))


def weight_source(route, tile, step, place_ref):
    size_y, size_x, unit = place_ref[4], place_ref[5], place_ref[3]
    if route == "all":
        return step
    if route == "y":
        size, others, here = size_y, size_x, place_ref[0]
    else:
        size, others, here = size_x, size_y, place_ref[1]
    per_place = others * unit
    goal = (here + 1 + step // per_place) % size
    other = step % per_place // unit
    row, column = (goal, other) if route == "y" else (other, goal)
    return (row * size_x + column) * unit + step % unit


def weight_grads(route, own, other, sides):
    rows, tokens = own.shape
    width = CUTS[-1]
    size_y, size_x = lax.axis_size("y"), lax.axis_size("x")
    tile = 512 if unit_tiles(256) % 2 == 0 else 256
    size = {"y": size_y, "x": size_x, "all": 1}[route]
    steps = rows // tile
    per_place = steps // size
    place = jnp.stack(
        [
            lax.axis_index("y").astype(jnp.int32),
            lax.axis_index("x").astype(jnp.int32),
            lax.axis_index("c").astype(jnp.int32),
            jnp.int32(unit_tiles(tile)),
            jnp.int32(size_y),
            jnp.int32(size_x),
        ]
    )
    source = pl.BlockSpec(
        (tile, tokens), lambda i, place_ref: (weight_source(route, tile, i, place_ref), 0)
    )
    side = [
        pl.BlockSpec((tokens, PADDED), lambda i, *_, at=at: (at, 0), pipeline_mode=pl.Buffered(1))
        for at in range(2)
    ]

    def out_spec(k):
        return pl.BlockSpec(
            (tile, CHUNK), lambda i, *_: (jnp.clip(i - k * per_place, 0, per_place - 1), 0)
        )

    if route == "all":
        out_specs = [pl.BlockSpec((tile, PADDED), lambda i, *_: (i, 0))]
        out_shape = [jax.ShapeDtypeStruct((rows, PADDED), jnp.bfloat16)]
    else:
        out_specs = [out_spec(k) for k in range(size) for _ in range(2)]
        out_shape = [jax.ShapeDtypeStruct((rows // size, CHUNK), jnp.bfloat16)] * (2 * size)
    results = pl.pallas_call(
        functools.partial(weight_grads_body, route, tile),
        grid_spec=pltpu.PrefetchScalarGridSpec(
            num_scalar_prefetch=1,
            grid=(steps,),
            in_specs=[source, source, side[0], side[0], side[1], side[1]],
            out_specs=out_specs,
        ),
        out_shape=out_shape,
        compiler_params=pltpu.CompilerParams(vmem_limit_bytes=32 << 20),
        cost_estimate=pl.CostEstimate(
            flops=2 * rows * tokens * width,
            bytes_accessed=4 * rows * tokens + rows * width,
            transcendentals=0,
        ),
        name="weight_grads",
    )(place, own, other, *sides, *sides)
    if route == "all":
        return results[0]
    return [[results[2 * k + turn] for k in range(size)] for turn in range(2)]


def attention_rows_body(grad_ref, first_side_ref, second_side_ref, out_ref):
    turned = grad_ref[...].T

    def put(side_ref):
        product = jnp.dot(turned, side_ref[...], preferred_element_type=jnp.float32)
        out_ref[:, : CUTS[-1]] = product.astype(jnp.bfloat16)
        out_ref[:, CUTS[-1] :] = jnp.zeros((BLOCK, PADDED - CUTS[-1]), jnp.bfloat16)

    @pl.when(pl.program_id(0) < 3 * INNER // BLOCK)
    def _():
        put(first_side_ref)

    @pl.when(pl.program_id(0) >= 3 * INNER // BLOCK)
    def _():
        put(second_side_ref)


def attention_rows(grads, first_side, second_side):
    tokens, width = first_side.shape
    return pl.pallas_call(
        attention_rows_body,
        grid=(4 * INNER // BLOCK,),
        in_specs=[
            pl.BlockSpec((tokens, BLOCK), lambda i: (0, i)),
            resident((tokens, width)),
            resident((tokens, width)),
        ],
        out_specs=pl.BlockSpec((BLOCK, PADDED), lambda i: (i, 0)),
        out_shape=jax.ShapeDtypeStruct((4 * INNER, PADDED), jnp.bfloat16),
        cost_estimate=pl.CostEstimate(
            flops=8 * tokens * INNER * width,
            bytes_accessed=8 * INNER * PADDED + 8 * tokens * width,
            transcendentals=0,
        ),
        name="attention_rows",
    )(grads, first_side, second_side)


def with_attention(route, chunk, arrays, rows):
    unit_rows = rows.shape[0]
    if route == "all":
        here = lax.axis_index("c") < 4 * INNER // unit_rows
        filled = jnp.where(here, rows, arrays[0][:unit_rows])
        return [lax.dynamic_update_slice(arrays[0], filled, (0, 0))]
    size = lax.axis_size(route)
    owners = 4 * INNER // unit_rows
    columns = rows[:, chunk * CHUNK : (chunk + 1) * CHUNK]
    filled = []
    for k, array in enumerate(arrays):
        here = (lax.axis_index(route) + 1 + k) % size == 0
        here = here & (lax.axis_index("c") < owners)
        filled.append(
            lax.dynamic_update_slice(
                array, jnp.where(here, columns, array[:unit_rows]), (0, 0)
            )
        )
    return filled


def tied(first, second):
    return lax.optimization_barrier((first, second))


class Scatter:
    def __init__(self):
        self.waiting, self.flying, self.results = {}, {}, {}

    def push(self, name, route, kept, sends):
        self.waiting[name] = (route, kept, sends)

    def step(self, values, *names):
        arrays = {name: self.flying[name][1:] for name in names if name in self.flying}
        arrays, values = tied(arrays, values)
        moves = {}
        for name in names:
            if name in self.waiting:
                moves[name] = self.waiting.pop(name)
                continue
            route = self.flying.pop(name)[0]
            kept, moved = arrays[name]
            if not route:
                self.results[name] = kept.astype(jnp.float32) + sum(
                    part.astype(jnp.float32) for part in moved
                )
                continue
            total = total_of(kept, moved)
            total = total.reshape((lax.axis_size(route[0]), -1) + total.shape[-1:])
            sends = stage_sends(total, route[0], 0)
            moves[name] = (route, pick(total, lax.axis_index(route[0]), 0), sends)
        arrays, values = tied({name: move[1:] for name, move in moves.items()}, values)
        for name, (route, *_) in moves.items():
            kept, sends = arrays[name]
            self.flying[name] = (route[1:], kept, stage_moves(sends, route[0]))
        return values


def total_of(value, moved):
    total = value.astype(jnp.float32)
    for part in moved:
        total = total + part.astype(jnp.float32)
    return total.astype(jnp.bfloat16)


def fetch_rows(local_rows):
    return lax.all_gather(local_rows, DEVICES, axis=0, tiled=True)


def layer_forward(stream, gathered, gain_one, gain_two, gate_low, context):
    normed, inverse_one = rms_forward(stream, gain_one)
    normed_low = normed.astype(jnp.bfloat16)
    projected = times_rows(normed_low, gathered[: 3 * INNER]).astype(jnp.bfloat16)
    queries = projected[:, :INNER]
    parts = [projected[:, INNER:]]
    if gate_low is not None:
        parts.append(jnp.broadcast_to(gate_low[:, None], (stream.shape[0], BLOCK)))
    shared = with_neighbours(jnp.concatenate(parts, axis=1))
    attended, log_total = attend_forward(queries, shared, context)
    middle = stream + times_plain(attended, gathered[3 * INNER : 4 * INNER])
    normed_two, inverse_two = rms_forward(middle, gain_two)
    normed_two_low = normed_two.astype(jnp.bfloat16)
    result, up_gelu, up_linear = ffn_forward(normed_two_low, middle, gathered)
    kept = (
        stream,
        inverse_one,
        normed_low,
        queries,
        shared,
        attended,
        log_total,
        middle,
        inverse_two,
        normed_two_low,
        up_gelu,
        up_linear,
    )
    return (result, kept)


def layer_backward(grad_out, kept, gathered, gain_one, gain_two, context, tail):
    (
        stream,
        inverse_one,
        normed_low,
        queries,
        shared,
        attended,
        log_total,
        middle,
        inverse_two,
        normed_two_low,
        up_gelu,
        up_linear,
    ) = kept
    tokens = queries.shape[0]
    branch_low = grad_out.astype(jnp.bfloat16)
    sides = jnp.concatenate([normed_two_low, branch_low], axis=0)
    sides = jnp.pad(sides, ((0, 0), (0, PADDED - sides.shape[1])))
    sides = (sides, shift(sides, "c", 1))
    grad_normed_two, own, sent = ffn_backward(
        branch_low, normed_two_low, up_gelu, up_linear, gathered
    )
    other = shift(sent, "c", 1)
    grad_middle, grad_gain_two = rms_backward(middle, inverse_two, gain_two, grad_normed_two)
    grad_middle = grad_out + grad_middle
    middle_low = grad_middle.astype(jnp.bfloat16)
    grad_mixed = times_rows(middle_low, gathered[3 * INNER : 4 * INNER]).astype(jnp.bfloat16)
    grad_query, grad_shared, grad_table = attend_backward(
        queries, grad_mixed, shared, log_total, context
    )
    grad_shared, own = lax.optimization_barrier((grad_shared, own))
    moving = start_back(grad_shared, tokens)
    routes = ("y", "x") if tail else ("all",)
    routed = {
        route: weight_grads(route, own, other, sides) for route in routes
    }
    routed, moving = lax.optimization_barrier((routed, moving))
    grad_own = finish_back(*moving)
    grad_gate = grad_own[:, 2 * INNER :]
    grad_input_low = jnp.concatenate(
        [grad_query, grad_own[:, : 2 * INNER].astype(jnp.bfloat16)], axis=1
    )
    rows = attention_rows(
        jnp.concatenate([grad_input_low, attended], axis=1), normed_low, middle_low
    )
    unit_rows = unit_tiles(TILE) * TILE
    core = lax.axis_index("c")
    owners = 4 * INNER // unit_rows
    kept_rows, sent_rows = (
        lax.dynamic_slice_in_dim(rows, jnp.minimum(at, owners - 1) * unit_rows, unit_rows, 0)
        if owners > 1
        else rows
        for at in (core, 1 - core)
    )
    rows = total_of(kept_rows, [shift(sent_rows, "c", 1)])
    if tail:
        scatter = Scatter()
        for chunk in range(4):
            route = ("y", "x", "z") if chunk % 2 == 0 else ("x", "y", "z")
            arrays = with_attention(route[0], chunk, routed[route[0]][chunk // 2], rows)
            scatter.push(chunk, route, arrays[-1], arrays[:-1])
        grad_input_low = scatter.step(grad_input_low, 0, 1, 2, 3)
    else:
        scatter = with_attention("all", 0, [routed["all"]], rows)[0]
        scatter, grad_input_low, grad_gate = lax.optimization_barrier(
            (scatter, grad_input_low, grad_gate)
        )
        scatter = lax.psum_scatter(scatter, ("y", "x", "z"), scatter_dimension=0, tiled=True)
    grad_normed = times_plain(grad_input_low, gathered[: 3 * INNER])
    grad_stream, grad_gain_one = rms_backward(stream, inverse_one, gain_one, grad_normed)
    return (grad_middle + grad_stream, grad_table, grad_gate, grad_gain_one, grad_gain_two, scatter)


def per_device(
    inputs, layer3_rows, layer4_rows, norm_gains, gate_weight, rel_bias, segment_ids, cotangent
):
    seqs_here, tokens_here, width = inputs.shape
    first_pos = lax.axis_index("z") * tokens_here
    context = attention_context(segment_ids[0], first_pos, tokens_here, rel_bias)
    stream = inputs.reshape(tokens_here, width)
    gathered_three = fetch_rows(layer3_rows)
    after_three, kept_three = layer_forward(
        stream, gathered_three, norm_gains[0], norm_gains[1], None, context
    )
    gate_inverse = lax.rsqrt(jnp.mean(after_three * after_three, axis=1, keepdims=True) + epsilon)
    gate_normed = after_three * gate_inverse
    gate_logit = jnp.sum(gate_normed * gate_weight, axis=1) + gate_offset
    sigmoid_value = 1.0 / (1.0 + jnp.exp(-gate_logit))
    gate_mask = gate_scale * sigmoid_value
    gate_low = gate_mask.astype(jnp.bfloat16)
    gathered_four = fetch_rows(layer4_rows)
    after_four, kept_four = layer_forward(
        after_three, gathered_four, norm_gains[2], norm_gains[3], gate_low, context
    )
    grad_three_out, table_four, grad_gate, gain_four_one, gain_four_two, local_four = (
        layer_backward(
            cotangent.reshape(tokens_here, width),
            kept_four,
            gathered_four,
            norm_gains[2],
            norm_gains[3],
            context,
            False,
        )
    )
    grad_logit = grad_gate[:, 0] * gate_scale * sigmoid_value * (1.0 - sigmoid_value)
    grad_gate_weight = jnp.sum(grad_logit[:, None] * gate_normed, axis=0)
    gate_stream = stream_backward(after_three, gate_inverse, grad_logit[:, None] * gate_weight)
    grad_input, table_three, unused, gain_three_one, gain_three_two, scatter = layer_backward(
        grad_three_out + gate_stream,
        kept_three,
        gathered_three,
        norm_gains[0],
        norm_gains[1],
        context,
        True,
    )
    table = jnp.pad((table_three + table_four).reshape(1, -1), ((0, 0), (0, width - 6 * BUCKETS)))
    small_sums = jnp.stack(
        [gain_three_one, gain_three_two, gain_four_one, gain_four_two, grad_gate_weight, table[0]]
    )
    small = hop(small_sums, "c")
    small = scatter.step(small, 0, 1)
    small = hop(small, "z", 1)
    small = scatter.step(small, 2, 3)
    for bit in range(2, lax.axis_size("z")):
        if bit & (bit - 1) == 0:
            small = hop(small, "z", bit)
    small = scatter.step(small, 0, 1)
    small = scatter.step(small, 2, 3)
    small = hop(small, "x")
    for bit in range(1, lax.axis_size("y")):
        if bit & (bit - 1) == 0:
            small = hop(small, "y", bit)
    summed = scatter.step(small, 0, 1)
    summed = scatter.step(summed, 2, 3)
    local_three = jnp.concatenate([scatter.results[chunk] for chunk in range(4)], axis=1)
    local_three, local_four = local_three[:, :width], local_four[:, :width].astype(jnp.float32)
    return (
        after_four.reshape(inputs.shape),
        gate_mask.reshape(seqs_here, tokens_here),
        grad_input.reshape(inputs.shape),
        local_three,
        local_four,
        summed[:4],
        summed[4],
        summed[5, : 6 * BUCKETS].reshape(BUCKETS, HEADS),
    )


def solution(mesh):
    outer, inner = mesh.devices.shape
    fine = Mesh(mesh.devices.reshape(outer // 4, 2, 2, inner), DEVICES)
    batch = ("y", "x", "c")
    tokens = P(batch, "z", None)
    rows = P(DEVICES, None)
    return jax.shard_map(
        per_device,
        mesh=fine,
        in_specs=(tokens, rows, rows, P(), P(), P(), P(batch, None), tokens),
        out_specs=(tokens, P(batch, "z"), tokens, rows, rows, P(), P(), P()),
        check_vma=False,
    )
```

```python
import functools

import jax
import jax.numpy as jnp
from jax import lax
from jax.experimental import pallas as pl
from jax.experimental.pallas import tpu as pltpu
from jax.sharding import Mesh
from jax.sharding import PartitionSpec as P

HEADS = 6
PAIRS = 3
BLOCK = 128
WIDE = 2 * BLOCK
INNER = 384
BUCKETS = 32
FF = 3584
REACH = 799
HALO = 896
TILE = 256
ATTENTION_TILES = 4 * INNER // TILE
OFFSETS = 5
CHUNK = 384
PADDED = 1536
FORWARD_TILE = 512
CUTS = (0, 384, 768, 1152, 1472)
DEVICES = ("y", "x", "c", "z")
epsilon = 1e-06
gate_scale = -30.0
gate_offset = -3.5
masked_out = -1e30
limits = (12, 16, 23, 32, 46, 64, 91)
both_last = (((1,), (1,)), ((), ()))


def bucket_of(relative):
    magnitude = jnp.abs(relative)
    beyond = jnp.zeros_like(magnitude)
    for bound_value in limits:
        beyond = beyond + (magnitude >= bound_value).astype(jnp.int32)
    inside = jnp.where(magnitude < 8, magnitude, 8 + beyond)
    return inside + 16 * (relative > 0).astype(jnp.int32)


def near_buckets(offset):
    if offset < 0:
        return range(1, 16)
    if offset > 0:
        return range(17, 32)
    return range(0, 32)


def tile_buckets(offset, width):
    key_at = lax.broadcasted_iota(jnp.int32, (BLOCK, width), 0)
    query_at = lax.broadcasted_iota(jnp.int32, (BLOCK, width), 1) % BLOCK
    return bucket_of(offset * BLOCK + key_at - query_at)


def bias_body(table_ref, tiles_ref):
    head = pl.program_id(0)
    tiles_ref[0, 0] = jnp.full((BLOCK, BLOCK), table_ref[15, head], jnp.float32)
    tiles_ref[0, 4] = jnp.full((BLOCK, BLOCK), table_ref[31, head], jnp.float32)
    for offset in (-1, 0, 1):
        buckets = tile_buckets(offset, BLOCK)
        tile = jnp.zeros((BLOCK, BLOCK), jnp.float32)
        for bucket in near_buckets(offset):
            tile = jnp.where(buckets == bucket, table_ref[bucket, head], tile)
        tiles_ref[0, offset + 2] = tile


def bias_tiles(rel_bias):
    return pl.pallas_call(
        bias_body,
        grid=(HEADS,),
        in_specs=[pl.BlockSpec(memory_space=pltpu.SMEM)],
        out_specs=pl.BlockSpec((1, OFFSETS, BLOCK, BLOCK), lambda h: (h, 0, 0, 0)),
        out_shape=jax.ShapeDtypeStruct((HEADS, OFFSETS, BLOCK, BLOCK), jnp.float32),
        name="bias_tiles",
    )(rel_bias)


def lane_masks():
    lane = lax.broadcasted_iota(jnp.int32, (BLOCK, BLOCK), 1)
    low = jnp.where(lane < 64, 1.0, 0.0).astype(jnp.bfloat16)
    high = jnp.where(lane < 64, 0.0, 1.0).astype(jnp.bfloat16)
    return low, high


def stacked(block, masks):
    low, high = masks
    return jnp.concatenate([block * low, block * high], axis=0)


def pair_cols(pair):
    return slice(pair * BLOCK, (pair + 1) * BLOCK)


def value_cols(pair):
    return slice(INNER + pair * BLOCK, INNER + (pair + 1) * BLOCK)


def block_rows(block):
    return pl.ds(pl.multiple_of(block * BLOCK, BLOCK), BLOCK)


def fold(values):
    return values.reshape(BLOCK // 8, 8, WIDE)


def shift_tile(gated, rows, own_segment, segment_ref, shared_ref):
    same = segment_ref[rows, :] == own_segment
    inside = shared_ref[rows, 2 * INNER :].astype(jnp.float32) if gated else 0.0
    shift = jnp.where(same, inside, masked_out)
    return jnp.concatenate([shift, shift], axis=1)


def bias_pair(bias_ref, pair, offset):
    return jnp.concatenate([bias_ref[2 * pair, offset], bias_ref[2 * pair + 1, offset]], axis=1)


def pick_heads(wide):
    return jnp.concatenate([wide[:64, :BLOCK], wide[64:, BLOCK:]], axis=0)


def forward_body(gated, low_ref, high_ref, *refs):
    query_ref, shared_ref, own_ref, segment_ref, bias_ref = refs[:5]
    mixed_ref, total_ref, turned_ref, score_ref = refs[5:]
    step = pl.program_id(0)
    key_blocks = shared_ref.shape[0] // BLOCK

    @pl.when(step == 0)
    def _():
        @pl.loop(0, key_blocks)
        def _(block):
            rows = block_rows(block)
            turned_ref[:, rows] = shared_ref[rows, INNER : 2 * INNER].T

    first, last = low_ref[step], high_ref[step]
    own_block = HALO // BLOCK + step
    own_segment = own_ref[0]
    masks = lane_masks()
    queries = [stacked(query_ref[:, pair_cols(pair)], masks) for pair in range(PAIRS)]

    def scores(block, peaks):
        rows = block_rows(block)
        shift = shift_tile(gated, rows, own_segment, segment_ref, shared_ref)
        offset = jnp.clip(block - own_block, -2, 2) + 2
        new_peaks = []
        for pair in range(PAIRS):
            score = lax.dot_general(
                shared_ref[rows, pair_cols(pair)],
                queries[pair],
                both_last,
                preferred_element_type=jnp.float32,
            )
            score = score + bias_pair(bias_ref, pair, offset) + shift
            score_ref[pair, block] = score
            new_peaks.append(jnp.maximum(peaks[pair], jnp.max(fold(score), axis=0)))
        return tuple(new_peaks)

    start = jnp.full((8, WIDE), -3e38, jnp.float32)
    peaks = lax.fori_loop(first, last, scores, (start,) * PAIRS)
    for pair in range(PAIRS):
        peak = jnp.max(peaks[pair], axis=0, keepdims=True)

        def mix(block, carry, pair=pair, peak=peak):
            total, mixed = carry
            weight = jnp.exp(score_ref[pair, block] - peak)
            total = total + jnp.sum(fold(weight), axis=0)
            mixed = mixed + jnp.dot(
                turned_ref[pair_cols(pair), block_rows(block)],
                weight.astype(jnp.bfloat16),
                preferred_element_type=jnp.float32,
            )
            return total, mixed

        zero = (jnp.zeros((8, WIDE), jnp.float32), jnp.zeros((BLOCK, WIDE), jnp.float32))
        total, mixed = lax.fori_loop(first, last, mix, zero)
        row_total = jnp.sum(total, axis=0, keepdims=True)
        mixed = pick_heads(mixed * (1.0 / row_total))
        mixed_ref[:, pair_cols(pair)] = mixed.T.astype(jnp.bfloat16)
        total_ref[0, pair : pair + 1, :] = peak + jnp.log(row_total)


def whole(shape):
    return pl.BlockSpec(shape, lambda i, *_: (0,) * len(shape), pipeline_mode=pl.Buffered(1))


def rows_spec(width):
    return pl.BlockSpec((BLOCK, width), lambda i, *_: (i, 0))


def attend_forward(queries, shared, context):
    lows, highs, own_rows, segment_wide, tiles = context
    tokens, (length, width) = queries.shape[0], shared.shape
    steps, key_blocks = tokens // BLOCK, length // BLOCK
    return pl.pallas_call(
        functools.partial(forward_body, width > 2 * INNER),
        grid_spec=pltpu.PrefetchScalarGridSpec(
            num_scalar_prefetch=2,
            grid=(steps,),
            in_specs=[
                rows_spec(INNER),
                whole((length, width)),
                pl.BlockSpec((1, 1, BLOCK), lambda i, *_: (i, 0, 0)),
                whole((length, BLOCK)),
                whole(tiles.shape),
            ],
            out_specs=[
                rows_spec(INNER),
                pl.BlockSpec((1, 8, WIDE), lambda i, *_: (i, 0, 0)),
            ],
            scratch_shapes=[
                pltpu.VMEM((INNER, length), jnp.bfloat16),
                pltpu.VMEM((PAIRS, key_blocks, BLOCK, WIDE), jnp.float32),
            ],
        ),
        out_shape=[
            jax.ShapeDtypeStruct((tokens, INNER), jnp.bfloat16),
            jax.ShapeDtypeStruct((steps, 8, WIDE), jnp.float32),
        ],
        compiler_params=pltpu.CompilerParams(vmem_limit_bytes=40 << 20),
        cost_estimate=pl.CostEstimate(
            flops=tokens * length * INNER * 4,
            bytes_accessed=8 << 20,
            transcendentals=tokens * length * 3,
        ),
        name="attend_forward",
    )(lows, highs, queries, shared, own_rows, segment_wide, tiles)


def backward_body(gated, low_ref, high_ref, *refs):
    query_ref, grad_ref, shared_ref, own_ref, segment_ref, bias_ref, total_ref = refs[:7]
    grad_query_ref, grad_shared_ref, bucket_ref = refs[7:10]
    turned_ref, prob_ref, pull_ref, sum_ref, bias_sum_ref, turn_sum_ref = refs[10:]
    step = pl.program_id(0)
    key_blocks = shared_ref.shape[0] // BLOCK

    @pl.when(step == 0)
    def _():
        bias_sum_ref[...] = jnp.zeros_like(bias_sum_ref)

        @pl.loop(0, key_blocks)
        def _(block):
            rows = block_rows(block)
            turned_ref[:, rows] = shared_ref[rows, :INNER].T
            sum_ref[rows, :] = jnp.zeros((BLOCK, sum_ref.shape[1]), jnp.float32)

    first, last = low_ref[step], high_ref[step]
    own_block = HALO // BLOCK + step
    own_segment = own_ref[0]
    masks = lane_masks()
    queries = [stacked(query_ref[:, pair_cols(pair)], masks) for pair in range(PAIRS)]
    grads = [stacked(grad_ref[:, pair_cols(pair)], masks) for pair in range(PAIRS)]
    totals = [total_ref[0, pair : pair + 1, :] for pair in range(PAIRS)]

    def weights(block, deltas):
        rows = block_rows(block)
        shift = shift_tile(gated, rows, own_segment, segment_ref, shared_ref)
        offset = jnp.clip(block - own_block, -2, 2) + 2
        new_deltas = []
        for pair in range(PAIRS):
            cols = pair_cols(pair)
            score = lax.dot_general(
                shared_ref[rows, cols], queries[pair], both_last, preferred_element_type=jnp.float32
            )
            pull = lax.dot_general(
                shared_ref[rows, value_cols(pair)],
                grads[pair],
                both_last,
                preferred_element_type=jnp.float32,
            )
            prob = jnp.exp(score + bias_pair(bias_ref, pair, offset) + shift - totals[pair])
            prob_ref[pair, block] = prob
            pull_ref[pair, block] = pull
            sum_ref[rows, value_cols(pair)] += jnp.dot(
                prob.astype(jnp.bfloat16), grads[pair], preferred_element_type=jnp.float32
            )
            new_deltas.append(deltas[pair] + jnp.sum(fold(prob * pull), axis=0))
        return tuple(new_deltas)

    start = jnp.zeros((8, WIDE), jnp.float32)
    deltas = lax.fori_loop(first, last, weights, (start,) * PAIRS)
    deltas = [jnp.sum(delta, axis=0, keepdims=True) for delta in deltas]
    turn_sum_ref[...] = jnp.zeros_like(turn_sum_ref)

    @pl.loop(first, last)
    def _(block):
        rows = block_rows(block)
        offset = jnp.clip(block - own_block, -2, 2) + 2
        gate_part = jnp.zeros((BLOCK, BLOCK), jnp.float32)
        for pair in range(PAIRS):
            cols = pair_cols(pair)
            grad_score = prob_ref[pair, block] * (pull_ref[pair, block] - deltas[pair])
            bias_sum_ref[pair, offset] += grad_score
            if gated:
                gate_part = gate_part + (grad_score[:, :BLOCK] + grad_score[:, BLOCK:])
            score_low = grad_score.astype(jnp.bfloat16)
            sum_ref[rows, cols] += jnp.dot(
                score_low, queries[pair], preferred_element_type=jnp.float32
            )
            turn_sum_ref[pair] += jnp.dot(
                turned_ref[cols, rows], score_low, preferred_element_type=jnp.float32
            )
        if gated:
            sum_ref[rows, 2 * INNER :] += gate_part

    for pair in range(PAIRS):
        grad_query_ref[:, pair_cols(pair)] = pick_heads(turn_sum_ref[pair]).T.astype(jnp.bfloat16)

    @pl.when(step == pl.num_programs(0) - 1)
    def _():
        @pl.loop(0, key_blocks)
        def _(block):
            rows = block_rows(block)
            both = slice(0, 2 * INNER)
            grad_shared_ref[rows, both] = sum_ref[rows, both].astype(jnp.bfloat16)
            if gated:
                gate_total = jnp.sum(sum_ref[rows, 2 * INNER :], axis=1, keepdims=True)
                grad_shared_ref[rows, 2 * INNER :] = jnp.broadcast_to(
                    gate_total, (BLOCK, BLOCK)
                ).astype(jnp.bfloat16)

        tables = {offset: tile_buckets(offset, WIDE) for offset in (-1, 0, 1)}

        @pl.loop(0, PAIRS)
        def _(pair):
            for bucket in range(BUCKETS):
                part = jnp.zeros((8, WIDE), jnp.float32)
                for offset in (-1, 0, 1):
                    if bucket in near_buckets(offset):
                        chosen = jnp.where(
                            tables[offset] == bucket, bias_sum_ref[pair, offset + 2], 0.0
                        )
                        part = part + jnp.sum(fold(chosen), axis=0)
                if bucket == 15:
                    part = part + jnp.sum(fold(bias_sum_ref[pair, 0]), axis=0)
                if bucket == 31:
                    part = part + jnp.sum(fold(bias_sum_ref[pair, 4]), axis=0)
                bucket_ref[pair, bucket : bucket + 1, :] = jnp.sum(part, axis=0, keepdims=True)


def attend_backward(queries, grad_mixed, shared, log_total, context):
    lows, highs, own_rows, segment_wide, tiles = context
    tokens, (length, width) = queries.shape[0], shared.shape
    steps, key_blocks = tokens // BLOCK, length // BLOCK
    grad_query, grad_shared, bucket_sums = pl.pallas_call(
        functools.partial(backward_body, width > 2 * INNER),
        grid_spec=pltpu.PrefetchScalarGridSpec(
            num_scalar_prefetch=2,
            grid=(steps,),
            in_specs=[
                rows_spec(INNER),
                rows_spec(INNER),
                whole((length, width)),
                pl.BlockSpec((1, 1, BLOCK), lambda i, *_: (i, 0, 0)),
                whole((length, BLOCK)),
                whole(tiles.shape),
                pl.BlockSpec((1, 8, WIDE), lambda i, *_: (i, 0, 0)),
            ],
            out_specs=[
                rows_spec(INNER),
                whole((length, width)),
                whole((PAIRS, BUCKETS, WIDE)),
            ],
            scratch_shapes=[
                pltpu.VMEM((INNER, length), jnp.bfloat16),
                pltpu.VMEM((PAIRS, key_blocks, BLOCK, WIDE), jnp.float32),
                pltpu.VMEM((PAIRS, key_blocks, BLOCK, WIDE), jnp.float32),
                pltpu.VMEM((length, width), jnp.float32),
                pltpu.VMEM((PAIRS, OFFSETS, BLOCK, WIDE), jnp.float32),
                pltpu.VMEM((PAIRS, BLOCK, WIDE), jnp.float32),
            ],
        ),
        out_shape=[
            jax.ShapeDtypeStruct((tokens, INNER), jnp.bfloat16),
            jax.ShapeDtypeStruct((length, width), jnp.bfloat16),
            jax.ShapeDtypeStruct((PAIRS, BUCKETS, WIDE), jnp.float32),
        ],
        compiler_params=pltpu.CompilerParams(vmem_limit_bytes=48 << 20),
        cost_estimate=pl.CostEstimate(
            flops=tokens * length * INNER * 10,
            bytes_accessed=12 << 20,
            transcendentals=tokens * length * 3,
        ),
        name="attend_backward",
    )(lows, highs, queries, grad_mixed, shared, own_rows, segment_wide, tiles, log_total)
    table = jnp.sum(bucket_sums.reshape(PAIRS, BUCKETS, 2, BLOCK), axis=3)
    return grad_query, grad_shared, table.transpose(1, 0, 2).reshape(BUCKETS, HEADS)


def attention_context(segment_row, first_pos, tokens, rel_bias):
    steps = tokens // BLOCK
    padded = jnp.pad(segment_row, (HALO, 0), constant_values=-1)
    padded = jnp.pad(padded, (0, HALO), constant_values=1000)
    window = lax.dynamic_slice_in_dim(padded, first_pos, tokens + 2 * HALO, 0)
    own = window[HALO : HALO + tokens].reshape(steps, 1, BLOCK)
    lows = jnp.sum(window[None, :] < own[:, 0, :1], axis=1, dtype=jnp.int32) // BLOCK
    ends = jnp.sum(window[None, :] <= own[:, 0, BLOCK - 1 :], axis=1, dtype=jnp.int32)
    highs = (ends + BLOCK - 1) // BLOCK
    segment_wide = jnp.broadcast_to(window[:, None], (window.shape[0], BLOCK))
    return lows, highs, own, segment_wide, bias_tiles(rel_bias)


def rms_forward(stream, gain_row):
    inverse = lax.rsqrt(jnp.mean(stream * stream, axis=1, keepdims=True) + epsilon)
    return (stream * inverse * gain_row, inverse)


def stream_backward(stream, inverse, scaled):
    return inverse * scaled - stream * inverse**3 * jnp.mean(scaled * stream, axis=1, keepdims=True)


def rms_backward(stream, inverse, gain_row, grad_normed):
    grad_gain = jnp.sum(grad_normed * stream * inverse, axis=0)
    return (stream_backward(stream, inverse, gain_row * grad_normed), grad_gain)


def gelu_tanh(values):
    return 0.5 * values * (1.0 + jnp.tanh(0.7978845608028654 * (values + 0.044715 * values**3)))


def times_rows(left_side, weight):
    return lax.dot_general(
        left_side, weight, (((1,), (1,)), ((), ())), preferred_element_type=jnp.float32
    )


def times_plain(left_side, weight):
    return jnp.dot(left_side, weight, preferred_element_type=jnp.float32)


def outer_sum(left_side, right_side):
    return lax.dot_general(
        left_side, right_side, (((0,), (0,)), ((), ())), preferred_element_type=jnp.float32
    )


def shift(value, axis, amount):
    count = lax.axis_size(axis)
    return lax.ppermute(value, axis, [(i, (i + amount) % count) for i in range(count)])


def slide(value, amount):
    count = lax.axis_size("z")
    pairs = [(i, i + amount) for i in range(count) if 0 <= i + amount < count]
    return lax.ppermute(value, "z", pairs)


def far_pair(near_start, near_end, distance):
    count = lax.axis_size("z")
    first_half = lax.axis_index("z") < distance
    sent = jnp.where(first_half, near_end, near_start)
    pairs = [(i, (i + distance) % count) for i in range(count)]
    got = lax.ppermute(sent, "z", pairs)
    return got


def far_split(got, distance):
    first_half = lax.axis_index("z") < distance
    none = jnp.zeros_like(got)
    return jnp.where(first_half, none, got), jnp.where(first_half, got, none)


def halo_pieces(tokens):
    pieces = []
    distance, covered = 1, 0
    while covered < HALO:
        span = min(tokens, HALO - covered)
        needed = min(span, -(-(REACH - covered) // 16) * 16)
        pieces.append((distance, span, needed))
        distance, covered = distance + 1, covered + span
    return pieces


def with_neighbours(own):
    tokens = own.shape[0]
    before, after = [], []
    for distance, span, needed in halo_pieces(tokens):
        if distance < lax.axis_size("z"):
            if 2 * distance == lax.axis_size("z"):
                left, right = far_split(
                    far_pair(own[:needed], own[tokens - needed :], distance), distance
                )
            else:
                left = slide(own[tokens - needed :], distance)
                right = slide(own[:needed], -distance)
            before.append(jnp.pad(left, ((span - needed, 0), (0, 0))))
            after.append(jnp.pad(right, ((0, span - needed), (0, 0))))
        else:
            empty = jnp.zeros((span, own.shape[1]), own.dtype)
            before.append(empty)
            after.append(empty)
    return jnp.concatenate(before[::-1] + [own] + after, axis=0)


def start_back(window, tokens):
    moved = []
    covered = 0
    for distance, span, needed in halo_pieces(tokens):
        if distance < lax.axis_size("z"):
            left_end = HALO - covered
            right_start = HALO + tokens + covered
            left = window[left_end - needed : left_end]
            right = window[right_start : right_start + needed]
            if 2 * distance == lax.axis_size("z"):
                moved.append((far_pair(left, right, distance),))
            else:
                moved.append((slide(left, -distance), slide(right, distance)))
        covered += span
    return window[HALO : HALO + tokens], moved


def finish_back(own, moved):
    tokens = own.shape[0]
    total = own.astype(jnp.float32)
    for distance, pair in enumerate(moved, 1):
        if len(pair) == 1:
            ahead, back = far_split(pair[0], distance)
        else:
            back, ahead = pair
        needed = back.shape[0]
        total = total + jnp.pad(back.astype(jnp.float32), ((tokens - needed, 0), (0, 0)))
        total = total + jnp.pad(ahead.astype(jnp.float32), ((0, tokens - needed), (0, 0)))
    return total


def hop(value, axis, bit=1):
    pairs = [(i, i ^ bit) for i in range(lax.axis_size(axis))]
    return value + lax.ppermute(value, axis, pairs)


def pick(value, index, axis):
    return lax.dynamic_index_in_dim(value, index, axis, keepdims=False)


def stage_sends(value, axis_name, axis):
    count, here = lax.axis_size(axis_name), lax.axis_index(axis_name)
    return [pick(value, (here + k) % count, axis) for k in range(1, count)]


def stage_moves(sends, axis_name):
    return [shift(sent, axis_name, k + 1) for k, sent in enumerate(sends)]


def gelu_parts(values):
    squared = values * values
    slope = jnp.tanh(0.7978845608028654 * (values + 0.044715 * values * squared))
    active = 0.5 * values * (1.0 + slope)
    inner = 0.7978845608028654 * (1.0 + 3.0 * 0.044715 * squared)
    return active, 0.5 * (1.0 + slope) + 0.5 * values * (1.0 - slope * slope) * inner


def ffn_forward_body(normed_ref, middle_ref, gelu_ref, linear_ref, down_ref, *outs):
    result_ref, up_gelu_ref, up_linear_ref = outs

    @pl.when(pl.program_id(0) == 0)
    def _():
        result_ref[...] = middle_ref[...]

    up_gelu = times_rows(normed_ref[...], gelu_ref[...])
    up_linear = times_rows(normed_ref[...], linear_ref[...])
    up_gelu_ref[...] = up_gelu
    up_linear_ref[...] = up_linear
    hidden = (gelu_tanh(up_gelu) * up_linear).astype(jnp.bfloat16)
    result_ref[...] += times_plain(hidden, down_ref[...])


def resident(shape):
    return pl.BlockSpec(shape, lambda *_: (0,) * len(shape), pipeline_mode=pl.Buffered(1))


def ffn_forward(normed, middle, gathered):
    tokens, width = normed.shape
    steps = FF // FORWARD_TILE
    first = 4 * INNER // FORWARD_TILE

    def weight(kind):
        return pl.BlockSpec((FORWARD_TILE, width), lambda i: (first + kind * steps + i, 0))

    hidden = pl.BlockSpec((tokens, FORWARD_TILE), lambda i: (0, i))
    return pl.pallas_call(
        ffn_forward_body,
        grid=(steps,),
        in_specs=[
            resident((tokens, width)),
            resident((tokens, width)),
            weight(0),
            weight(1),
            weight(2),
        ],
        out_specs=[resident((tokens, width)), hidden, hidden],
        out_shape=[
            jax.ShapeDtypeStruct((tokens, width), jnp.float32),
            jax.ShapeDtypeStruct((tokens, FF), jnp.float32),
            jax.ShapeDtypeStruct((tokens, FF), jnp.float32),
        ],
        compiler_params=pltpu.CompilerParams(vmem_limit_bytes=48 << 20),
        cost_estimate=pl.CostEstimate(
            flops=6 * tokens * FF * width,
            bytes_accessed=6 * FF * width + 8 * tokens * FF,
            transcendentals=tokens * FF,
        ),
        name="ffn_forward",
    )(normed, middle, gathered, gathered, gathered)


def ffn_backward_body(core_ref, *refs):
    branch_ref, normed_ref, up_gelu_ref, up_linear_ref, gelu_ref, linear_ref, down_ref = refs[:7]
    grad_ref, kept_ref, sent_ref, stage_ref, sems = refs[7:]
    step = pl.program_id(0)
    slot = step % 2
    mine, unit = core_ref[0], core_ref[1]
    parts = FORWARD_TILE // TILE

    def copy(kind, part, place, at, where):
        spot = pl.ds(pl.multiple_of(at * TILE, TILE), TILE)
        source = stage_ref.at[where, kind, part * TILE : (part + 1) * TILE, :]
        return pltpu.make_async_copy(source, place.at[spot, :], sems.at[where, kind, part])

    def wait(where):
        for kind in range(3):
            for part in range(parts):
                copy(kind, part, kept_ref, 0, where).wait()

    def put(kind, turned):
        stage_ref[slot, kind] = turned
        for part in range(parts):
            target = ATTENTION_TILES + kind * (FF // TILE) + step * parts + part
            own = (target // unit) % 2 == mine
            at = (target // (2 * unit)) * unit + target % unit

            @pl.when(own)
            def _(part=part, at=at):
                copy(kind, part, kept_ref, at, slot).start()

            @pl.when(jnp.logical_not(own))
            def _(part=part, at=at):
                copy(kind, part, sent_ref, at, slot).start()

    @pl.when(step == 0)
    def _():
        grad_ref[...] = jnp.zeros_like(grad_ref)

    @pl.when(step >= 2)
    def _():
        wait(slot)

    grad_hidden = times_rows(branch_ref[...], down_ref[...])
    active, slope = gelu_parts(up_gelu_ref[...])
    linear = up_linear_ref[...]
    grad_gelu = (grad_hidden * linear * slope).astype(jnp.bfloat16)
    grad_linear = (grad_hidden * active).astype(jnp.bfloat16)
    put(2, (active * linear).astype(jnp.bfloat16).T)
    put(0, grad_gelu.T)
    put(1, grad_linear.T)
    grad_ref[...] += times_plain(grad_gelu, gelu_ref[...]) + times_plain(
        grad_linear, linear_ref[...]
    )

    @pl.when(step == pl.num_programs(0) - 1)
    def _():
        wait(0)
        wait(1)


def unit_tiles(tile):
    rows = 4 * INNER + 3 * FF
    return rows // tile // (2 * lax.axis_size("y") * lax.axis_size("x"))


def ffn_backward(branch, normed, up_gelu, up_linear, gathered):
    tokens, width = normed.shape
    rows = 4 * INNER + 3 * FF
    steps = FF // FORWARD_TILE
    core = jnp.stack([lax.axis_index("c").astype(jnp.int32), jnp.int32(unit_tiles(TILE))])

    def weight(kind):
        first = 4 * INNER // FORWARD_TILE + kind * steps
        return pl.BlockSpec((FORWARD_TILE, width), lambda i, *_: (first + i, 0))

    hidden = pl.BlockSpec((tokens, FORWARD_TILE), lambda i, *_: (0, i))
    side = resident((tokens, width))
    anywhere = pl.BlockSpec(memory_space=pl.ANY)
    return pl.pallas_call(
        ffn_backward_body,
        grid_spec=pltpu.PrefetchScalarGridSpec(
            num_scalar_prefetch=1,
            grid=(steps,),
            in_specs=[side, side, hidden, hidden, weight(0), weight(1), weight(2)],
            out_specs=[side, anywhere, anywhere],
            scratch_shapes=[
                pltpu.VMEM((2, 3, FORWARD_TILE, tokens), jnp.bfloat16),
                pltpu.SemaphoreType.DMA((2, 3, FORWARD_TILE // TILE)),
            ],
        ),
        out_shape=[jax.ShapeDtypeStruct((tokens, width), jnp.float32)]
        + [jax.ShapeDtypeStruct((rows // 2, tokens), jnp.bfloat16)] * 2,
        compiler_params=pltpu.CompilerParams(vmem_limit_bytes=56 << 20),
        cost_estimate=pl.CostEstimate(
            flops=6 * tokens * FF * width,
            bytes_accessed=6 * FF * width + 14 * tokens * FF,
            transcendentals=tokens * FF,
        ),
        name="ffn_backward",
    )(core, branch, normed, up_gelu, up_linear, gathered, gathered, gathered)


def spots_of(unit_at, place_ref):
    here_y, here_x, size_y, size_x = place_ref[0], place_ref[1], place_ref[4], place_ref[5]
    row, column = unit_at // size_x, unit_at % size_x
    return (
        ((row + 2 * size_y - here_y - 1) % size_y, column),
        ((column + 2 * size_x - here_x - 1) % size_x, row),
    )


def weight_grads_body(tail, tile, place_ref, *refs):
    own_ref, other_ref, normed_ref, branch_ref, other_normed_ref, other_branch_ref = refs[:6]
    refs = refs[6:]
    step = pl.program_id(0)
    unit = place_ref[3]
    at = (step // unit * 2 + place_ref[2]) * unit + step % unit
    first, second = 4 * INNER // tile, (4 * INNER + 2 * FF) // tile
    slot = step % 2
    if tail:
        stage_ref, sems = refs[-2:]
        places = split_places(refs[:-2])

    def copy(chunk, place, row, where):
        source = stage_ref.at[where, :, chunk * CHUNK : (chunk + 1) * CHUNK]
        spot = pl.ds(pl.multiple_of(row * tile, tile), tile)
        return pltpu.make_async_copy(source, place.at[spot, :], sems.at[where, chunk])

    def wait(where):
        for chunk in range(4):
            copy(chunk, places[chunk % 2][0][chunk // 2], 0, where).wait()

    def put(product):
        if not tail:
            refs[0][:, : CUTS[-1]] = product.astype(jnp.bfloat16)
            refs[0][:, CUTS[-1] :] = jnp.zeros((tile, PADDED - CUTS[-1]), jnp.bfloat16)
            return
        stage_ref[slot, :, : CUTS[-1]] = product.astype(jnp.bfloat16)
        spots = spots_of(step // unit, place_ref)
        for chunk in range(4):
            which, position = spots[chunk % 2]
            for k, pair in enumerate(places[chunk % 2]):

                @pl.when(which == k)
                def _(chunk=chunk, place=pair[chunk // 2], row=position * unit + step % unit):
                    copy(chunk, place, row, slot).start()

    def both(side_ref, other_side_ref):
        return jnp.dot(
            own_ref[...], side_ref[:, : CUTS[-1]], preferred_element_type=jnp.float32
        ) + jnp.dot(
            other_ref[...], other_side_ref[:, : CUTS[-1]], preferred_element_type=jnp.float32
        )

    if tail:

        @pl.when(step < 2)
        def _():
            stage_ref[slot, :, CUTS[-1] :] = jnp.zeros((tile, PADDED - CUTS[-1]), jnp.bfloat16)

        @pl.when(step >= 2)
        def _():
            wait(slot)

    @pl.when(at < first)
    def _():
        put(jnp.zeros((tile, CUTS[-1]), jnp.float32))

    @pl.when((at >= first) & (at < second))
    def _():
        put(both(normed_ref, other_normed_ref))

    @pl.when(at >= second)
    def _():
        put(both(branch_ref, other_branch_ref))

    if tail:

        @pl.when(step == pl.num_programs(0) - 1)
        def _():
            wait(0)
            wait(1)


def split_places(refs):
    size_y, size_x = lax.axis_size("y"), lax.axis_size("x")
    along_y = [refs[2 * k : 2 * k + 2] for k in range(size_y)]
    along_x = [refs[2 * size_y + 2 * k : 2 * size_y + 2 * k + 2] for k in range(size_x)]
    return along_y, along_x


def place_of(tile):
    return jnp.stack(
        [
            lax.axis_index("y").astype(jnp.int32),
            lax.axis_index("x").astype(jnp.int32),
            lax.axis_index("c").astype(jnp.int32),
            jnp.int32(unit_tiles(tile)),
            jnp.int32(lax.axis_size("y")),
            jnp.int32(lax.axis_size("x")),
        ]
    )


def half_side(tokens, at):
    return pl.BlockSpec(
        (tokens, PADDED), lambda i, *_: (at, 0), pipeline_mode=pl.Buffered(1)
    )


def weight_grads(tail, own, other, sides):
    rows, tokens = own.shape
    tile = 512 if unit_tiles(256) % 2 == 0 else 256
    steps = rows // tile
    source = pl.BlockSpec((tile, tokens), lambda i, *_: (i, 0))
    halves = [half_side(tokens, 0), half_side(tokens, 1)]
    scratch = []
    if tail:
        sizes = [lax.axis_size("y")] * 2 * lax.axis_size("y")
        sizes += [lax.axis_size("x")] * 2 * lax.axis_size("x")
        out_specs = [pl.BlockSpec(memory_space=pl.ANY)] * len(sizes)
        out_shape = [jax.ShapeDtypeStruct((rows // n, CHUNK), jnp.bfloat16) for n in sizes]
        scratch = [pltpu.VMEM((2, tile, PADDED), jnp.bfloat16), pltpu.SemaphoreType.DMA((2, 4))]
    else:
        out_specs = [pl.BlockSpec((tile, PADDED), lambda i, *_: (i, 0))]
        out_shape = [jax.ShapeDtypeStruct((rows, PADDED), jnp.bfloat16)]
    return pl.pallas_call(
        functools.partial(weight_grads_body, tail, tile),
        grid_spec=pltpu.PrefetchScalarGridSpec(
            num_scalar_prefetch=1,
            grid=(steps,),
            in_specs=[source, source] + halves * 2,
            out_specs=out_specs,
            scratch_shapes=scratch,
        ),
        out_shape=out_shape,
        compiler_params=pltpu.CompilerParams(vmem_limit_bytes=40 << 20),
        cost_estimate=pl.CostEstimate(
            flops=4 * rows * tokens * CUTS[-1],
            bytes_accessed=4 * rows * tokens + 2 * rows * PADDED,
            transcendentals=0,
        ),
        name="weight_grads",
    )(place_of(tile), own, other, sides[0], sides[0], sides[1], sides[1])


def attention_fill_body(tail, owners, place_ref, *refs):
    own_ref, other_ref, first_ref, second_ref, other_first_ref, other_second_ref = refs[:6]
    outs = refs[6 + (len(refs) - 8) // 2 : -2]
    stage_ref, sems = refs[-2:]
    step = pl.program_id(0)
    slot = step % 2
    tile = jnp.minimum(place_ref[2], owners - 1) * pl.num_programs(0) + step

    def copy(chunk, place, row, where):
        width = CHUNK if tail else PADDED
        source = stage_ref.at[where, :, chunk * width : (chunk + 1) * width]
        spot = pl.ds(pl.multiple_of(row * INNER, INNER), INNER)
        return pltpu.make_async_copy(source, place.at[spot, :], sems.at[where, chunk])

    places = split_places(outs) if tail else None

    def wait(where):
        for chunk in range(4 if tail else 1):
            place = places[chunk % 2][0][chunk // 2] if tail else outs[0]
            copy(chunk, place, 0, where).wait()

    def put(side_ref, other_side_ref):
        product = jnp.dot(
            own_ref[...].T, side_ref[:, : CUTS[-1]], preferred_element_type=jnp.float32
        ) + jnp.dot(
            other_ref[...].T, other_side_ref[:, : CUTS[-1]], preferred_element_type=jnp.float32
        )
        stage_ref[slot, :, : CUTS[-1]] = product.astype(jnp.bfloat16)
        stage_ref[slot, :, CUTS[-1] :] = jnp.zeros((INNER, PADDED - CUTS[-1]), jnp.bfloat16)
        if not tail:
            copy(0, outs[0], step, slot).start()
            return
        spots = spots_of(0, place_ref)
        for chunk in range(4):
            which, _ = spots[chunk % 2]
            for k, pair in enumerate(places[chunk % 2]):

                @pl.when(which == k)
                def _(chunk=chunk, place=pair[chunk // 2]):
                    copy(chunk, place, step, slot).start()

    @pl.when(place_ref[2] < owners)
    def _():
        @pl.when(step >= 2)
        def _():
            wait(slot)

        @pl.when(tile < 3)
        def _():
            put(first_ref, other_first_ref)

        @pl.when(tile >= 3)
        def _():
            put(second_ref, other_second_ref)

        @pl.when(step == pl.num_programs(0) - 1)
        def _():
            wait(0)
            wait(1)


def attention_fill(tail, arrays, own, other, sides):
    tokens = own.shape[0]
    unit_rows = unit_tiles(TILE) * TILE
    owners = 4 * INNER // unit_rows
    steps = unit_rows // INNER

    def column(i, place_ref):
        return 0, jnp.minimum(place_ref[2], owners - 1) * steps + i

    halves = [half_side(tokens, 0), half_side(tokens, 1)]
    anywhere = pl.BlockSpec(memory_space=pl.ANY)
    return pl.pallas_call(
        functools.partial(attention_fill_body, tail, owners),
        grid_spec=pltpu.PrefetchScalarGridSpec(
            num_scalar_prefetch=1,
            grid=(steps,),
            in_specs=[pl.BlockSpec((tokens, INNER), column)] * 2
            + halves * 2
            + [anywhere] * len(arrays),
            out_specs=[anywhere] * len(arrays),
            scratch_shapes=[
                pltpu.VMEM((2, INNER, PADDED), jnp.bfloat16),
                pltpu.SemaphoreType.DMA((2, 4)),
            ],
        ),
        out_shape=[jax.ShapeDtypeStruct(array.shape, array.dtype) for array in arrays],
        input_output_aliases={7 + k: k for k in range(len(arrays))},
        compiler_params=pltpu.CompilerParams(vmem_limit_bytes=32 << 20),
        cost_estimate=pl.CostEstimate(
            flops=4 * unit_rows * tokens * CUTS[-1],
            bytes_accessed=4 * unit_rows * tokens + 2 * unit_rows * PADDED,
            transcendentals=0,
        ),
        name="attention_fill",
    )(place_of(TILE), own, other, sides[0], sides[0], sides[1], sides[1], *arrays)


def tied(first, second):
    return lax.optimization_barrier((first, second))


class Scatter:
    def __init__(self):
        self.waiting, self.flying, self.results = {}, {}, {}

    def push(self, name, route, kept, sends):
        self.waiting[name] = (route, kept, sends)

    def step(self, values, *names):
        arrays = {name: self.flying[name][1:] for name in names if name in self.flying}
        arrays, values = tied(arrays, values)
        moves = {}
        for name in names:
            if name in self.waiting:
                moves[name] = self.waiting.pop(name)
                continue
            route = self.flying.pop(name)[0]
            kept, moved = arrays[name]
            if not route:
                self.results[name] = kept.astype(jnp.float32) + sum(
                    part.astype(jnp.float32) for part in moved
                )
                continue
            total = total_of(kept, moved)
            total = total.reshape((lax.axis_size(route[0]), -1) + total.shape[-1:])
            sends = stage_sends(total, route[0], 0)
            moves[name] = (route, pick(total, lax.axis_index(route[0]), 0), sends)
        arrays, values = tied({name: move[1:] for name, move in moves.items()}, values)
        for name, (route, *_) in moves.items():
            kept, sends = arrays[name]
            self.flying[name] = (route[1:], kept, stage_moves(sends, route[0]))
        return values


def total_of(value, moved):
    total = value.astype(jnp.float32)
    for part in moved:
        total = total + part.astype(jnp.float32)
    return total.astype(jnp.bfloat16)


def fetch_rows(local_rows):
    return lax.all_gather(local_rows, DEVICES, axis=0, tiled=True)


def layer_forward(stream, gathered, gain_one, gain_two, gate_low, context):
    normed, inverse_one = rms_forward(stream, gain_one)
    normed_low = normed.astype(jnp.bfloat16)
    projected = times_rows(normed_low, gathered[: 3 * INNER]).astype(jnp.bfloat16)
    queries = projected[:, :INNER]
    parts = [projected[:, INNER:]]
    if gate_low is not None:
        parts.append(jnp.broadcast_to(gate_low[:, None], (stream.shape[0], BLOCK)))
    shared = with_neighbours(jnp.concatenate(parts, axis=1))
    attended, log_total = attend_forward(queries, shared, context)
    middle = stream + times_plain(attended, gathered[3 * INNER : 4 * INNER])
    normed_two, inverse_two = rms_forward(middle, gain_two)
    normed_two_low = normed_two.astype(jnp.bfloat16)
    result, up_gelu, up_linear = ffn_forward(normed_two_low, middle, gathered)
    kept = (
        stream,
        inverse_one,
        normed_low,
        queries,
        shared,
        attended,
        log_total,
        middle,
        inverse_two,
        normed_two_low,
        up_gelu,
        up_linear,
    )
    return (result, kept)


def layer_backward(grad_out, kept, gathered, gain_one, gain_two, context, tail):
    (
        stream,
        inverse_one,
        normed_low,
        queries,
        shared,
        attended,
        log_total,
        middle,
        inverse_two,
        normed_two_low,
        up_gelu,
        up_linear,
    ) = kept
    tokens = queries.shape[0]
    branch_low = grad_out.astype(jnp.bfloat16)
    sides = jnp.concatenate([normed_two_low, branch_low], axis=0)
    sides = jnp.pad(sides, ((0, 0), (0, PADDED - sides.shape[1])))
    sides = (sides, shift(sides, "c", 1))
    grad_normed_two, own, sent = ffn_backward(
        branch_low, normed_two_low, up_gelu, up_linear, gathered
    )
    other = shift(sent, "c", 1)
    grad_middle, grad_gain_two = rms_backward(middle, inverse_two, gain_two, grad_normed_two)
    grad_middle = grad_out + grad_middle
    middle_low = grad_middle.astype(jnp.bfloat16)
    late_sides = jnp.concatenate([normed_low, middle_low], axis=0)
    late_sides = jnp.pad(late_sides, ((0, 0), (0, PADDED - late_sides.shape[1])))
    late_sides = (late_sides, shift(late_sides, "c", 1))
    grad_mixed = times_rows(middle_low, gathered[3 * INNER : 4 * INNER]).astype(jnp.bfloat16)
    grad_query, grad_shared, grad_table = attend_backward(
        queries, grad_mixed, shared, log_total, context
    )
    grad_shared, own = lax.optimization_barrier((grad_shared, own))
    moving = start_back(grad_shared, tokens)
    arrays = weight_grads(tail, own, other, sides)
    arrays, moving = lax.optimization_barrier((arrays, moving))
    grad_own = finish_back(*moving)
    grad_gate = grad_own[:, 2 * INNER :]
    grad_input_low = jnp.concatenate(
        [grad_query, grad_own[:, : 2 * INNER].astype(jnp.bfloat16)], axis=1
    )
    late = jnp.concatenate([grad_input_low, attended], axis=1)
    arrays = attention_fill(tail, arrays, late, shift(late, "c", 1), late_sides)
    if tail:
        scatter = Scatter()
        for chunk in range(4):
            route = ("y", "x", "z") if chunk % 2 == 0 else ("x", "y", "z")
            ordered = [pair[chunk // 2] for pair in split_places(arrays)[chunk % 2]]
            scatter.push(chunk, route, ordered[-1], ordered[:-1])
        grad_input_low = scatter.step(grad_input_low, 0, 1)
    else:
        arrays, grad_input_low, grad_gate = lax.optimization_barrier(
            (arrays, grad_input_low, grad_gate)
        )
        scatter = lax.psum_scatter(arrays[0], ("y", "x", "z"), scatter_dimension=0, tiled=True)
    grad_normed = times_plain(grad_input_low, gathered[: 3 * INNER])
    grad_stream, grad_gain_one = rms_backward(stream, inverse_one, gain_one, grad_normed)
    return (grad_middle + grad_stream, grad_table, grad_gate, grad_gain_one, grad_gain_two, scatter)


def per_device(
    inputs, layer3_rows, layer4_rows, norm_gains, gate_weight, rel_bias, segment_ids, cotangent
):
    seqs_here, tokens_here, width = inputs.shape
    first_pos = lax.axis_index("z") * tokens_here
    context = attention_context(segment_ids[0], first_pos, tokens_here, rel_bias)
    stream = inputs.reshape(tokens_here, width)
    gathered_three = fetch_rows(layer3_rows)
    after_three, kept_three = layer_forward(
        stream, gathered_three, norm_gains[0], norm_gains[1], None, context
    )
    gate_inverse = lax.rsqrt(jnp.mean(after_three * after_three, axis=1, keepdims=True) + epsilon)
    gate_normed = after_three * gate_inverse
    gate_logit = jnp.sum(gate_normed * gate_weight, axis=1) + gate_offset
    sigmoid_value = 1.0 / (1.0 + jnp.exp(-gate_logit))
    gate_mask = gate_scale * sigmoid_value
    gate_low = gate_mask.astype(jnp.bfloat16)
    gathered_four = fetch_rows(layer4_rows)
    after_four, kept_four = layer_forward(
        after_three, gathered_four, norm_gains[2], norm_gains[3], gate_low, context
    )
    grad_three_out, table_four, grad_gate, gain_four_one, gain_four_two, local_four = (
        layer_backward(
            cotangent.reshape(tokens_here, width),
            kept_four,
            gathered_four,
            norm_gains[2],
            norm_gains[3],
            context,
            False,
        )
    )
    grad_logit = grad_gate[:, 0] * gate_scale * sigmoid_value * (1.0 - sigmoid_value)
    grad_gate_weight = jnp.sum(grad_logit[:, None] * gate_normed, axis=0)
    gate_stream = stream_backward(after_three, gate_inverse, grad_logit[:, None] * gate_weight)
    grad_input, table_three, unused, gain_three_one, gain_three_two, scatter = layer_backward(
        grad_three_out + gate_stream,
        kept_three,
        gathered_three,
        norm_gains[0],
        norm_gains[1],
        context,
        True,
    )
    table = jnp.pad((table_three + table_four).reshape(1, -1), ((0, 0), (0, width - 6 * BUCKETS)))
    small_sums = jnp.stack(
        [gain_three_one, gain_three_two, gain_four_one, gain_four_two, grad_gate_weight, table[0]]
    )
    small = hop(small_sums, "c")
    small = scatter.step(small, 0, 1)
    small = scatter.step(small, 2, 3)
    small = hop(small, "z", 1)
    small = scatter.step(small, 0, 1)
    for bit in range(2, lax.axis_size("z")):
        if bit & (bit - 1) == 0:
            small = hop(small, "z", bit)
    small = scatter.step(small, 2, 3)
    small = scatter.step(small, 2, 3)
    small = hop(small, "x")
    for bit in range(1, lax.axis_size("y")):
        if bit & (bit - 1) == 0:
            small = hop(small, "y", bit)
    summed = scatter.step(small, 0, 1)
    summed = scatter.step(summed, 2, 3)
    local_three = jnp.concatenate([scatter.results[chunk] for chunk in range(4)], axis=1)
    local_three, local_four = local_three[:, :width], local_four[:, :width].astype(jnp.float32)
    return (
        after_four.reshape(inputs.shape),
        gate_mask.reshape(seqs_here, tokens_here),
        grad_input.reshape(inputs.shape),
        local_three,
        local_four,
        summed[:4],
        summed[4],
        summed[5, : 6 * BUCKETS].reshape(BUCKETS, HEADS),
    )


def solution(mesh):
    outer, inner = mesh.devices.shape
    fine = Mesh(mesh.devices.reshape(outer // 4, 2, 2, inner), DEVICES)
    batch = ("y", "x", "c")
    tokens = P(batch, "z", None)
    rows = P(DEVICES, None)
    return jax.shard_map(
        per_device,
        mesh=fine,
        in_specs=(tokens, rows, rows, P(), P(), P(), P(batch, None), tokens),
        out_specs=(tokens, P(batch, "z"), tokens, rows, rows, P(), P(), P()),
        check_vma=False,
    )
```

```python
import functools

import jax
import jax.numpy as jnp
from jax import lax
from jax.experimental import pallas as pl
from jax.experimental.pallas import tpu as pltpu
from jax.sharding import Mesh
from jax.sharding import PartitionSpec as P

HEADS = 6
PAIRS = 3
BLOCK = 128
WIDE = 2 * BLOCK
INNER = 384
BUCKETS = 32
FF = 3584
REACH = 799
HALO = 896
TILE = 256
ATTENTION_TILES = 4 * INNER // TILE
OFFSETS = 5
CHUNK = 384
PADDED = 1536
FORWARD_TILE = 512
CUTS = (0, 384, 768, 1152, 1472)
DEVICES = ("y", "x", "c", "z")
epsilon = 1e-06
gate_scale = -30.0
gate_offset = -3.5
masked_out = -1e30
limits = (12, 16, 23, 32, 46, 64, 91)
both_last = (((1,), (1,)), ((), ()))


def bucket_of(relative):
    magnitude = jnp.abs(relative)
    beyond = jnp.zeros_like(magnitude)
    for bound_value in limits:
        beyond = beyond + (magnitude >= bound_value).astype(jnp.int32)
    inside = jnp.where(magnitude < 8, magnitude, 8 + beyond)
    return inside + 16 * (relative > 0).astype(jnp.int32)


def near_buckets(offset):
    if offset < 0:
        return range(1, 16)
    if offset > 0:
        return range(17, 32)
    return range(0, 32)


def tile_buckets(offset, width):
    key_at = lax.broadcasted_iota(jnp.int32, (BLOCK, width), 0)
    query_at = lax.broadcasted_iota(jnp.int32, (BLOCK, width), 1) % BLOCK
    return bucket_of(offset * BLOCK + key_at - query_at)


def bias_body(table_ref, tiles_ref):
    head = pl.program_id(0)
    tiles_ref[0, 0] = jnp.full((BLOCK, BLOCK), table_ref[15, head], jnp.float32)
    tiles_ref[0, 4] = jnp.full((BLOCK, BLOCK), table_ref[31, head], jnp.float32)
    for offset in (-1, 0, 1):
        buckets = tile_buckets(offset, BLOCK)
        tile = jnp.zeros((BLOCK, BLOCK), jnp.float32)
        for bucket in near_buckets(offset):
            tile = jnp.where(buckets == bucket, table_ref[bucket, head], tile)
        tiles_ref[0, offset + 2] = tile


def bias_tiles(rel_bias):
    return pl.pallas_call(
        bias_body,
        grid=(HEADS,),
        in_specs=[pl.BlockSpec(memory_space=pltpu.SMEM)],
        out_specs=pl.BlockSpec((1, OFFSETS, BLOCK, BLOCK), lambda h: (h, 0, 0, 0)),
        out_shape=jax.ShapeDtypeStruct((HEADS, OFFSETS, BLOCK, BLOCK), jnp.float32),
        name="bias_tiles",
    )(rel_bias)


def lane_masks():
    lane = lax.broadcasted_iota(jnp.int32, (BLOCK, BLOCK), 1)
    low = jnp.where(lane < 64, 1.0, 0.0).astype(jnp.bfloat16)
    high = jnp.where(lane < 64, 0.0, 1.0).astype(jnp.bfloat16)
    return low, high


def stacked(block, masks):
    low, high = masks
    return jnp.concatenate([block * low, block * high], axis=0)


def pair_cols(pair):
    return slice(pair * BLOCK, (pair + 1) * BLOCK)


def value_cols(pair):
    return slice(INNER + pair * BLOCK, INNER + (pair + 1) * BLOCK)


def block_rows(block):
    return pl.ds(pl.multiple_of(block * BLOCK, BLOCK), BLOCK)


def fold(values):
    return values.reshape(BLOCK // 8, 8, WIDE)


def shift_tile(gated, rows, own_segment, segment_ref, shared_ref):
    same = segment_ref[rows, :] == own_segment
    inside = shared_ref[rows, 2 * INNER :].astype(jnp.float32) if gated else 0.0
    shift = jnp.where(same, inside, masked_out)
    return jnp.concatenate([shift, shift], axis=1)


def bias_pair(bias_ref, pair, offset):
    return jnp.concatenate([bias_ref[2 * pair, offset], bias_ref[2 * pair + 1, offset]], axis=1)


def pick_heads(wide):
    return jnp.concatenate([wide[:64, :BLOCK], wide[64:, BLOCK:]], axis=0)


def forward_body(gated, low_ref, high_ref, *refs):
    query_ref, shared_ref, own_ref, segment_ref, bias_ref = refs[:5]
    mixed_ref, total_ref, turned_ref, score_ref = refs[5:]
    step = pl.program_id(0)
    key_blocks = shared_ref.shape[0] // BLOCK

    @pl.when(step == 0)
    def _():
        @pl.loop(0, key_blocks)
        def _(block):
            rows = block_rows(block)
            turned_ref[:, rows] = shared_ref[rows, INNER : 2 * INNER].T

    first, last = low_ref[step], high_ref[step]
    own_block = HALO // BLOCK + step
    own_segment = own_ref[0]
    masks = lane_masks()
    queries = [stacked(query_ref[:, pair_cols(pair)], masks) for pair in range(PAIRS)]

    def scores(block, peaks):
        rows = block_rows(block)
        shift = shift_tile(gated, rows, own_segment, segment_ref, shared_ref)
        offset = jnp.clip(block - own_block, -2, 2) + 2
        new_peaks = []
        for pair in range(PAIRS):
            score = lax.dot_general(
                shared_ref[rows, pair_cols(pair)],
                queries[pair],
                both_last,
                preferred_element_type=jnp.float32,
            )
            score = score + bias_pair(bias_ref, pair, offset) + shift
            score_ref[pair, block] = score
            new_peaks.append(jnp.maximum(peaks[pair], jnp.max(fold(score), axis=0)))
        return tuple(new_peaks)

    start = jnp.full((8, WIDE), -3e38, jnp.float32)
    peaks = lax.fori_loop(first, last, scores, (start,) * PAIRS)
    for pair in range(PAIRS):
        peak = jnp.max(peaks[pair], axis=0, keepdims=True)

        def mix(block, carry, pair=pair, peak=peak):
            total, mixed = carry
            weight = jnp.exp(score_ref[pair, block] - peak)
            total = total + jnp.sum(fold(weight), axis=0)
            mixed = mixed + jnp.dot(
                turned_ref[pair_cols(pair), block_rows(block)],
                weight.astype(jnp.bfloat16),
                preferred_element_type=jnp.float32,
            )
            return total, mixed

        zero = (jnp.zeros((8, WIDE), jnp.float32), jnp.zeros((BLOCK, WIDE), jnp.float32))
        total, mixed = lax.fori_loop(first, last, mix, zero)
        row_total = jnp.sum(total, axis=0, keepdims=True)
        mixed = pick_heads(mixed * (1.0 / row_total))
        mixed_ref[:, pair_cols(pair)] = mixed.T.astype(jnp.bfloat16)
        total_ref[0, pair : pair + 1, :] = peak + jnp.log(row_total)


def whole(shape):
    return pl.BlockSpec(shape, lambda i, *_: (0,) * len(shape), pipeline_mode=pl.Buffered(1))


def rows_spec(width):
    return pl.BlockSpec((BLOCK, width), lambda i, *_: (i, 0))


def attend_forward(queries, shared, context):
    lows, highs, own_rows, segment_wide, tiles = context
    tokens, (length, width) = queries.shape[0], shared.shape
    steps, key_blocks = tokens // BLOCK, length // BLOCK
    return pl.pallas_call(
        functools.partial(forward_body, width > 2 * INNER),
        grid_spec=pltpu.PrefetchScalarGridSpec(
            num_scalar_prefetch=2,
            grid=(steps,),
            in_specs=[
                rows_spec(INNER),
                whole((length, width)),
                pl.BlockSpec((1, 1, BLOCK), lambda i, *_: (i, 0, 0)),
                whole((length, BLOCK)),
                whole(tiles.shape),
            ],
            out_specs=[
                rows_spec(INNER),
                pl.BlockSpec((1, 8, WIDE), lambda i, *_: (i, 0, 0)),
            ],
            scratch_shapes=[
                pltpu.VMEM((INNER, length), jnp.bfloat16),
                pltpu.VMEM((PAIRS, key_blocks, BLOCK, WIDE), jnp.float32),
            ],
        ),
        out_shape=[
            jax.ShapeDtypeStruct((tokens, INNER), jnp.bfloat16),
            jax.ShapeDtypeStruct((steps, 8, WIDE), jnp.float32),
        ],
        compiler_params=pltpu.CompilerParams(vmem_limit_bytes=40 << 20),
        cost_estimate=pl.CostEstimate(
            flops=tokens * length * INNER * 4,
            bytes_accessed=8 << 20,
            transcendentals=tokens * length * 3,
        ),
        name="attend_forward",
    )(lows, highs, queries, shared, own_rows, segment_wide, tiles)


def backward_body(gated, low_ref, high_ref, *refs):
    query_ref, grad_ref, shared_ref, own_ref, segment_ref, bias_ref, total_ref = refs[:7]
    grad_query_ref, grad_shared_ref, bucket_ref = refs[7:10]
    turned_ref, prob_ref, pull_ref, sum_ref, bias_sum_ref, turn_sum_ref = refs[10:]
    step = pl.program_id(0)
    key_blocks = shared_ref.shape[0] // BLOCK

    @pl.when(step == 0)
    def _():
        bias_sum_ref[...] = jnp.zeros_like(bias_sum_ref)

        @pl.loop(0, key_blocks)
        def _(block):
            rows = block_rows(block)
            turned_ref[:, rows] = shared_ref[rows, :INNER].T
            sum_ref[rows, :] = jnp.zeros((BLOCK, sum_ref.shape[1]), jnp.float32)

    first, last = low_ref[step], high_ref[step]
    own_block = HALO // BLOCK + step
    own_segment = own_ref[0]
    masks = lane_masks()
    queries = [stacked(query_ref[:, pair_cols(pair)], masks) for pair in range(PAIRS)]
    grads = [stacked(grad_ref[:, pair_cols(pair)], masks) for pair in range(PAIRS)]
    totals = [total_ref[0, pair : pair + 1, :] for pair in range(PAIRS)]

    def weights(block, deltas):
        rows = block_rows(block)
        shift = shift_tile(gated, rows, own_segment, segment_ref, shared_ref)
        offset = jnp.clip(block - own_block, -2, 2) + 2
        new_deltas = []
        for pair in range(PAIRS):
            cols = pair_cols(pair)
            score = lax.dot_general(
                shared_ref[rows, cols], queries[pair], both_last, preferred_element_type=jnp.float32
            )
            pull = lax.dot_general(
                shared_ref[rows, value_cols(pair)],
                grads[pair],
                both_last,
                preferred_element_type=jnp.float32,
            )
            prob = jnp.exp(score + bias_pair(bias_ref, pair, offset) + shift - totals[pair])
            prob_ref[pair, block] = prob
            pull_ref[pair, block] = pull
            sum_ref[rows, value_cols(pair)] += jnp.dot(
                prob.astype(jnp.bfloat16), grads[pair], preferred_element_type=jnp.float32
            )
            new_deltas.append(deltas[pair] + jnp.sum(fold(prob * pull), axis=0))
        return tuple(new_deltas)

    start = jnp.zeros((8, WIDE), jnp.float32)
    deltas = lax.fori_loop(first, last, weights, (start,) * PAIRS)
    deltas = [jnp.sum(delta, axis=0, keepdims=True) for delta in deltas]
    turn_sum_ref[...] = jnp.zeros_like(turn_sum_ref)

    @pl.loop(first, last)
    def _(block):
        rows = block_rows(block)
        offset = jnp.clip(block - own_block, -2, 2) + 2
        gate_part = jnp.zeros((BLOCK, BLOCK), jnp.float32)
        for pair in range(PAIRS):
            cols = pair_cols(pair)
            grad_score = prob_ref[pair, block] * (pull_ref[pair, block] - deltas[pair])
            bias_sum_ref[pair, offset] += grad_score
            if gated:
                gate_part = gate_part + (grad_score[:, :BLOCK] + grad_score[:, BLOCK:])
            score_low = grad_score.astype(jnp.bfloat16)
            sum_ref[rows, cols] += jnp.dot(
                score_low, queries[pair], preferred_element_type=jnp.float32
            )
            turn_sum_ref[pair] += jnp.dot(
                turned_ref[cols, rows], score_low, preferred_element_type=jnp.float32
            )
        if gated:
            sum_ref[rows, 2 * INNER :] += gate_part

    for pair in range(PAIRS):
        grad_query_ref[:, pair_cols(pair)] = pick_heads(turn_sum_ref[pair]).T.astype(jnp.bfloat16)

    @pl.when(step == pl.num_programs(0) - 1)
    def _():
        @pl.loop(0, key_blocks)
        def _(block):
            rows = block_rows(block)
            both = slice(0, 2 * INNER)
            grad_shared_ref[rows, both] = sum_ref[rows, both].astype(jnp.bfloat16)
            if gated:
                gate_total = jnp.sum(sum_ref[rows, 2 * INNER :], axis=1, keepdims=True)
                grad_shared_ref[rows, 2 * INNER :] = jnp.broadcast_to(
                    gate_total, (BLOCK, BLOCK)
                ).astype(jnp.bfloat16)

        tables = {offset: tile_buckets(offset, WIDE) for offset in (-1, 0, 1)}

        @pl.loop(0, PAIRS)
        def _(pair):
            for bucket in range(BUCKETS):
                part = jnp.zeros((8, WIDE), jnp.float32)
                for offset in (-1, 0, 1):
                    if bucket in near_buckets(offset):
                        chosen = jnp.where(
                            tables[offset] == bucket, bias_sum_ref[pair, offset + 2], 0.0
                        )
                        part = part + jnp.sum(fold(chosen), axis=0)
                if bucket == 15:
                    part = part + jnp.sum(fold(bias_sum_ref[pair, 0]), axis=0)
                if bucket == 31:
                    part = part + jnp.sum(fold(bias_sum_ref[pair, 4]), axis=0)
                bucket_ref[pair, bucket : bucket + 1, :] = jnp.sum(part, axis=0, keepdims=True)


def attend_backward(queries, grad_mixed, shared, log_total, context):
    lows, highs, own_rows, segment_wide, tiles = context
    tokens, (length, width) = queries.shape[0], shared.shape
    steps, key_blocks = tokens // BLOCK, length // BLOCK
    grad_query, grad_shared, bucket_sums = pl.pallas_call(
        functools.partial(backward_body, width > 2 * INNER),
        grid_spec=pltpu.PrefetchScalarGridSpec(
            num_scalar_prefetch=2,
            grid=(steps,),
            in_specs=[
                rows_spec(INNER),
                rows_spec(INNER),
                whole((length, width)),
                pl.BlockSpec((1, 1, BLOCK), lambda i, *_: (i, 0, 0)),
                whole((length, BLOCK)),
                whole(tiles.shape),
                pl.BlockSpec((1, 8, WIDE), lambda i, *_: (i, 0, 0)),
            ],
            out_specs=[
                rows_spec(INNER),
                whole((length, width)),
                whole((PAIRS, BUCKETS, WIDE)),
            ],
            scratch_shapes=[
                pltpu.VMEM((INNER, length), jnp.bfloat16),
                pltpu.VMEM((PAIRS, key_blocks, BLOCK, WIDE), jnp.float32),
                pltpu.VMEM((PAIRS, key_blocks, BLOCK, WIDE), jnp.float32),
                pltpu.VMEM((length, width), jnp.float32),
                pltpu.VMEM((PAIRS, OFFSETS, BLOCK, WIDE), jnp.float32),
                pltpu.VMEM((PAIRS, BLOCK, WIDE), jnp.float32),
            ],
        ),
        out_shape=[
            jax.ShapeDtypeStruct((tokens, INNER), jnp.bfloat16),
            jax.ShapeDtypeStruct((length, width), jnp.bfloat16),
            jax.ShapeDtypeStruct((PAIRS, BUCKETS, WIDE), jnp.float32),
        ],
        compiler_params=pltpu.CompilerParams(vmem_limit_bytes=48 << 20),
        cost_estimate=pl.CostEstimate(
            flops=tokens * length * INNER * 10,
            bytes_accessed=12 << 20,
            transcendentals=tokens * length * 3,
        ),
        name="attend_backward",
    )(lows, highs, queries, grad_mixed, shared, own_rows, segment_wide, tiles, log_total)
    table = jnp.sum(bucket_sums.reshape(PAIRS, BUCKETS, 2, BLOCK), axis=3)
    return grad_query, grad_shared, table.transpose(1, 0, 2).reshape(BUCKETS, HEADS)


def attention_context(segment_row, first_pos, tokens, rel_bias):
    steps = tokens // BLOCK
    padded = jnp.pad(segment_row, (HALO, 0), constant_values=-1)
    padded = jnp.pad(padded, (0, HALO), constant_values=1000)
    window = lax.dynamic_slice_in_dim(padded, first_pos, tokens + 2 * HALO, 0)
    own = window[HALO : HALO + tokens].reshape(steps, 1, BLOCK)
    lows = jnp.sum(window[None, :] < own[:, 0, :1], axis=1, dtype=jnp.int32) // BLOCK
    ends = jnp.sum(window[None, :] <= own[:, 0, BLOCK - 1 :], axis=1, dtype=jnp.int32)
    highs = (ends + BLOCK - 1) // BLOCK
    segment_wide = jnp.broadcast_to(window[:, None], (window.shape[0], BLOCK))
    return lows, highs, own, segment_wide, bias_tiles(rel_bias)


def rms_forward(stream, gain_row):
    inverse = lax.rsqrt(jnp.mean(stream * stream, axis=1, keepdims=True) + epsilon)
    return (stream * inverse * gain_row, inverse)


def stream_backward(stream, inverse, scaled):
    return inverse * scaled - stream * inverse**3 * jnp.mean(scaled * stream, axis=1, keepdims=True)


def rms_backward(stream, inverse, gain_row, grad_normed):
    grad_gain = jnp.sum(grad_normed * stream * inverse, axis=0)
    return (stream_backward(stream, inverse, gain_row * grad_normed), grad_gain)


def gelu_tanh(values):
    return 0.5 * values * (1.0 + jnp.tanh(0.7978845608028654 * (values + 0.044715 * values**3)))


def times_rows(left_side, weight):
    return lax.dot_general(
        left_side, weight, (((1,), (1,)), ((), ())), preferred_element_type=jnp.float32
    )


def times_plain(left_side, weight):
    return jnp.dot(left_side, weight, preferred_element_type=jnp.float32)


def outer_sum(left_side, right_side):
    return lax.dot_general(
        left_side, right_side, (((0,), (0,)), ((), ())), preferred_element_type=jnp.float32
    )


def shift(value, axis, amount):
    count = lax.axis_size(axis)
    return lax.ppermute(value, axis, [(i, (i + amount) % count) for i in range(count)])


def slide(value, amount):
    count = lax.axis_size("z")
    pairs = [(i, i + amount) for i in range(count) if 0 <= i + amount < count]
    return lax.ppermute(value, "z", pairs)


def far_pair(near_start, near_end, distance):
    count = lax.axis_size("z")
    first_half = lax.axis_index("z") < distance
    sent = jnp.where(first_half, near_end, near_start)
    pairs = [(i, (i + distance) % count) for i in range(count)]
    got = lax.ppermute(sent, "z", pairs)
    return got


def far_split(got, distance):
    first_half = lax.axis_index("z") < distance
    none = jnp.zeros_like(got)
    return jnp.where(first_half, none, got), jnp.where(first_half, got, none)


def halo_pieces(tokens):
    pieces = []
    distance, covered = 1, 0
    while covered < HALO:
        span = min(tokens, HALO - covered)
        needed = min(span, -(-(REACH - covered) // 16) * 16)
        pieces.append((distance, span, needed))
        distance, covered = distance + 1, covered + span
    return pieces


def with_neighbours(own):
    tokens = own.shape[0]
    before, after = [], []
    for distance, span, needed in halo_pieces(tokens):
        if distance < lax.axis_size("z"):
            if 2 * distance == lax.axis_size("z"):
                left, right = far_split(
                    far_pair(own[:needed], own[tokens - needed :], distance), distance
                )
            else:
                left = slide(own[tokens - needed :], distance)
                right = slide(own[:needed], -distance)
            before.append(jnp.pad(left, ((span - needed, 0), (0, 0))))
            after.append(jnp.pad(right, ((0, span - needed), (0, 0))))
        else:
            empty = jnp.zeros((span, own.shape[1]), own.dtype)
            before.append(empty)
            after.append(empty)
    return jnp.concatenate(before[::-1] + [own] + after, axis=0)


def start_back(window, tokens):
    moved = []
    covered = 0
    for distance, span, needed in halo_pieces(tokens):
        if distance < lax.axis_size("z"):
            left_end = HALO - covered
            right_start = HALO + tokens + covered
            left = window[left_end - needed : left_end]
            right = window[right_start : right_start + needed]
            if 2 * distance == lax.axis_size("z"):
                moved.append((far_pair(left, right, distance),))
            else:
                moved.append((slide(left, -distance), slide(right, distance)))
        covered += span
    return window[HALO : HALO + tokens], moved


def finish_back(own, moved):
    tokens = own.shape[0]
    total = own.astype(jnp.float32)
    for distance, pair in enumerate(moved, 1):
        if len(pair) == 1:
            ahead, back = far_split(pair[0], distance)
        else:
            back, ahead = pair
        needed = back.shape[0]
        total = total + jnp.pad(back.astype(jnp.float32), ((tokens - needed, 0), (0, 0)))
        total = total + jnp.pad(ahead.astype(jnp.float32), ((0, tokens - needed), (0, 0)))
    return total


def hop(value, axis, bit=1):
    pairs = [(i, i ^ bit) for i in range(lax.axis_size(axis))]
    return value + lax.ppermute(value, axis, pairs)


def pick(value, index, axis):
    return lax.dynamic_index_in_dim(value, index, axis, keepdims=False)


def stage_sends(value, axis_name, axis):
    count, here = lax.axis_size(axis_name), lax.axis_index(axis_name)
    return [pick(value, (here + k) % count, axis) for k in range(1, count)]


def stage_moves(sends, axis_name):
    return [shift(sent, axis_name, k + 1) for k, sent in enumerate(sends)]


def gelu_parts(values):
    squared = values * values
    slope = jnp.tanh(0.7978845608028654 * (values + 0.044715 * values * squared))
    active = 0.5 * values * (1.0 + slope)
    inner = 0.7978845608028654 * (1.0 + 3.0 * 0.044715 * squared)
    return active, 0.5 * (1.0 + slope) + 0.5 * values * (1.0 - slope * slope) * inner


def ffn_forward_body(normed_ref, middle_ref, gelu_ref, linear_ref, down_ref, *outs):
    result_ref, up_gelu_ref, up_linear_ref = outs

    @pl.when(pl.program_id(0) == 0)
    def _():
        result_ref[...] = middle_ref[...]

    up_gelu = times_rows(normed_ref[...], gelu_ref[...])
    up_linear = times_rows(normed_ref[...], linear_ref[...])
    up_gelu_ref[...] = up_gelu
    up_linear_ref[...] = up_linear
    hidden = (gelu_tanh(up_gelu) * up_linear).astype(jnp.bfloat16)
    result_ref[...] += times_plain(hidden, down_ref[...])


def resident(shape):
    return pl.BlockSpec(shape, lambda *_: (0,) * len(shape), pipeline_mode=pl.Buffered(1))


def ffn_forward(normed, middle, gathered):
    tokens, width = normed.shape
    steps = FF // FORWARD_TILE
    first = 4 * INNER // FORWARD_TILE

    def weight(kind):
        return pl.BlockSpec((FORWARD_TILE, width), lambda i: (first + kind * steps + i, 0))

    hidden = pl.BlockSpec((tokens, FORWARD_TILE), lambda i: (0, i))
    return pl.pallas_call(
        ffn_forward_body,
        grid=(steps,),
        in_specs=[
            resident((tokens, width)),
            resident((tokens, width)),
            weight(0),
            weight(1),
            weight(2),
        ],
        out_specs=[resident((tokens, width)), hidden, hidden],
        out_shape=[
            jax.ShapeDtypeStruct((tokens, width), jnp.float32),
            jax.ShapeDtypeStruct((tokens, FF), jnp.float32),
            jax.ShapeDtypeStruct((tokens, FF), jnp.float32),
        ],
        compiler_params=pltpu.CompilerParams(vmem_limit_bytes=48 << 20),
        cost_estimate=pl.CostEstimate(
            flops=6 * tokens * FF * width,
            bytes_accessed=6 * FF * width + 8 * tokens * FF,
            transcendentals=tokens * FF,
        ),
        name="ffn_forward",
    )(normed, middle, gathered, gathered, gathered)


def ffn_backward_body(core_ref, *refs):
    branch_ref, normed_ref, up_gelu_ref, up_linear_ref, gelu_ref, linear_ref, down_ref = refs[:7]
    grad_ref, kept_ref, sent_ref, stage_ref, sems = refs[7:]
    step = pl.program_id(0)
    slot = step % 2
    mine, unit = core_ref[0], core_ref[1]
    parts = FORWARD_TILE // TILE

    def copy(kind, part, place, at, where):
        spot = pl.ds(pl.multiple_of(at * TILE, TILE), TILE)
        source = stage_ref.at[where, kind, part * TILE : (part + 1) * TILE, :]
        return pltpu.make_async_copy(source, place.at[spot, :], sems.at[where, kind, part])

    def wait(where):
        for kind in range(3):
            for part in range(parts):
                copy(kind, part, kept_ref, 0, where).wait()

    def put(kind, turned):
        stage_ref[slot, kind] = turned
        for part in range(parts):
            target = ATTENTION_TILES + kind * (FF // TILE) + step * parts + part
            own = (target // unit) % 2 == mine
            at = (target // (2 * unit)) * unit + target % unit

            @pl.when(own)
            def _(part=part, at=at):
                copy(kind, part, kept_ref, at, slot).start()

            @pl.when(jnp.logical_not(own))
            def _(part=part, at=at):
                copy(kind, part, sent_ref, at, slot).start()

    @pl.when(step == 0)
    def _():
        grad_ref[...] = jnp.zeros_like(grad_ref)

    @pl.when(step >= 2)
    def _():
        wait(slot)

    grad_hidden = times_rows(branch_ref[...], down_ref[...])
    active, slope = gelu_parts(up_gelu_ref[...])
    linear = up_linear_ref[...]
    grad_gelu = (grad_hidden * linear * slope).astype(jnp.bfloat16)
    grad_linear = (grad_hidden * active).astype(jnp.bfloat16)
    put(2, (active * linear).astype(jnp.bfloat16).T)
    put(0, grad_gelu.T)
    put(1, grad_linear.T)
    grad_ref[...] += times_plain(grad_gelu, gelu_ref[...]) + times_plain(
        grad_linear, linear_ref[...]
    )

    @pl.when(step == pl.num_programs(0) - 1)
    def _():
        wait(0)
        wait(1)


def unit_tiles(tile):
    rows = 4 * INNER + 3 * FF
    return rows // tile // (2 * lax.axis_size("y") * lax.axis_size("x"))


def ffn_backward(branch, normed, up_gelu, up_linear, gathered):
    tokens, width = normed.shape
    rows = 4 * INNER + 3 * FF
    steps = FF // FORWARD_TILE
    core = jnp.stack([lax.axis_index("c").astype(jnp.int32), jnp.int32(unit_tiles(TILE))])

    def weight(kind):
        first = 4 * INNER // FORWARD_TILE + kind * steps
        return pl.BlockSpec((FORWARD_TILE, width), lambda i, *_: (first + i, 0))

    hidden = pl.BlockSpec((tokens, FORWARD_TILE), lambda i, *_: (0, i))
    side = resident((tokens, width))
    anywhere = pl.BlockSpec(memory_space=pl.ANY)
    return pl.pallas_call(
        ffn_backward_body,
        grid_spec=pltpu.PrefetchScalarGridSpec(
            num_scalar_prefetch=1,
            grid=(steps,),
            in_specs=[side, side, hidden, hidden, weight(0), weight(1), weight(2)],
            out_specs=[side, anywhere, anywhere],
            scratch_shapes=[
                pltpu.VMEM((2, 3, FORWARD_TILE, tokens), jnp.bfloat16),
                pltpu.SemaphoreType.DMA((2, 3, FORWARD_TILE // TILE)),
            ],
        ),
        out_shape=[jax.ShapeDtypeStruct((tokens, width), jnp.float32)]
        + [jax.ShapeDtypeStruct((rows // 2, tokens), jnp.bfloat16)] * 2,
        compiler_params=pltpu.CompilerParams(vmem_limit_bytes=56 << 20),
        cost_estimate=pl.CostEstimate(
            flops=6 * tokens * FF * width,
            bytes_accessed=6 * FF * width + 14 * tokens * FF,
            transcendentals=tokens * FF,
        ),
        name="ffn_backward",
    )(core, branch, normed, up_gelu, up_linear, gathered, gathered, gathered)


def spots_of(unit_at, place_ref):
    here_y, here_x, size_y, size_x = place_ref[0], place_ref[1], place_ref[4], place_ref[5]
    row, column = unit_at // size_x, unit_at % size_x
    return (
        ((row + 2 * size_y - here_y - 1) % size_y, column),
        ((column + 2 * size_x - here_x - 1) % size_x, row),
    )


def weight_grads_body(tail, tile, place_ref, *refs):
    own_ref, other_ref, normed_ref, branch_ref, other_normed_ref, other_branch_ref = refs[:6]
    refs = refs[6:]
    step = pl.program_id(0)
    unit = place_ref[3]
    at = (step // unit * 2 + place_ref[2]) * unit + step % unit
    first, second = 4 * INNER // tile, (4 * INNER + 2 * FF) // tile
    slot = step % 2
    if tail:
        stage_ref, sems = refs[-2:]
        places = split_places(refs[:-2])

    def copy(chunk, place, row, where):
        source = stage_ref.at[where, :, chunk * CHUNK : (chunk + 1) * CHUNK]
        spot = pl.ds(pl.multiple_of(row * tile, tile), tile)
        return pltpu.make_async_copy(source, place.at[spot, :], sems.at[where, chunk])

    def wait(where):
        for chunk in range(4):
            copy(chunk, places[chunk % 2][0][chunk // 2], 0, where).wait()

    def put(product):
        if not tail:
            refs[0][:, : CUTS[-1]] = product.astype(jnp.bfloat16)
            refs[0][:, CUTS[-1] :] = jnp.zeros((tile, PADDED - CUTS[-1]), jnp.bfloat16)
            return
        stage_ref[slot, :, : CUTS[-1]] = product.astype(jnp.bfloat16)
        spots = spots_of(step // unit, place_ref)
        for chunk in range(4):
            which, position = spots[chunk % 2]
            for k, pair in enumerate(places[chunk % 2]):

                @pl.when(which == k)
                def _(chunk=chunk, place=pair[chunk // 2], row=position * unit + step % unit):
                    copy(chunk, place, row, slot).start()

    def both(side_ref, other_side_ref):
        return jnp.dot(
            own_ref[...], side_ref[:, : CUTS[-1]], preferred_element_type=jnp.float32
        ) + jnp.dot(
            other_ref[...], other_side_ref[:, : CUTS[-1]], preferred_element_type=jnp.float32
        )

    if tail:

        @pl.when(step < 2)
        def _():
            stage_ref[slot, :, CUTS[-1] :] = jnp.zeros((tile, PADDED - CUTS[-1]), jnp.bfloat16)

        @pl.when(step >= 2)
        def _():
            wait(slot)

    @pl.when(at < first)
    def _():
        put(jnp.zeros((tile, CUTS[-1]), jnp.float32))

    @pl.when((at >= first) & (at < second))
    def _():
        put(both(normed_ref, other_normed_ref))

    @pl.when(at >= second)
    def _():
        put(both(branch_ref, other_branch_ref))

    if tail:

        @pl.when(step == pl.num_programs(0) - 1)
        def _():
            wait(0)
            wait(1)


def split_places(refs):
    size_y, size_x = lax.axis_size("y"), lax.axis_size("x")
    along_y = [refs[2 * k : 2 * k + 2] for k in range(size_y)]
    along_x = [refs[2 * size_y + 2 * k : 2 * size_y + 2 * k + 2] for k in range(size_x)]
    return along_y, along_x


def place_of(tile):
    return jnp.stack(
        [
            lax.axis_index("y").astype(jnp.int32),
            lax.axis_index("x").astype(jnp.int32),
            lax.axis_index("c").astype(jnp.int32),
            jnp.int32(unit_tiles(tile)),
            jnp.int32(lax.axis_size("y")),
            jnp.int32(lax.axis_size("x")),
        ]
    )


def half_side(tokens, at):
    return pl.BlockSpec(
        (tokens, PADDED), lambda i, *_: (at, 0), pipeline_mode=pl.Buffered(1)
    )


def weight_grads(tail, own, other, sides):
    rows, tokens = own.shape
    tile = 512 if unit_tiles(256) % 2 == 0 else 256
    steps = rows // tile
    source = pl.BlockSpec((tile, tokens), lambda i, *_: (i, 0))
    halves = [half_side(tokens, 0), half_side(tokens, 1)]
    scratch = []
    if tail:
        sizes = [lax.axis_size("y")] * 2 * lax.axis_size("y")
        sizes += [lax.axis_size("x")] * 2 * lax.axis_size("x")
        out_specs = [pl.BlockSpec(memory_space=pl.ANY)] * len(sizes)
        out_shape = [jax.ShapeDtypeStruct((rows // n, CHUNK), jnp.bfloat16) for n in sizes]
        scratch = [pltpu.VMEM((2, tile, PADDED), jnp.bfloat16), pltpu.SemaphoreType.DMA((2, 4))]
    else:
        out_specs = [pl.BlockSpec((tile, PADDED), lambda i, *_: (i, 0))]
        out_shape = [jax.ShapeDtypeStruct((rows, PADDED), jnp.bfloat16)]
    return pl.pallas_call(
        functools.partial(weight_grads_body, tail, tile),
        grid_spec=pltpu.PrefetchScalarGridSpec(
            num_scalar_prefetch=1,
            grid=(steps,),
            in_specs=[source, source] + halves * 2,
            out_specs=out_specs,
            scratch_shapes=scratch,
        ),
        out_shape=out_shape,
        compiler_params=pltpu.CompilerParams(vmem_limit_bytes=40 << 20),
        cost_estimate=pl.CostEstimate(
            flops=4 * rows * tokens * CUTS[-1],
            bytes_accessed=4 * rows * tokens + 2 * rows * PADDED,
            transcendentals=0,
        ),
        name="weight_grads",
    )(place_of(tile), own, other, sides[0], sides[0], sides[1], sides[1])


def attention_fill_body(tail, owners, place_ref, *refs):
    own_ref, other_ref, first_ref, second_ref, other_first_ref, other_second_ref = refs[:6]
    outs = refs[6 + (len(refs) - 8) // 2 : -2]
    stage_ref, sems = refs[-2:]
    step = pl.program_id(0)
    slot = step % 2
    tile = jnp.minimum(place_ref[2], owners - 1) * pl.num_programs(0) + step

    def copy(chunk, place, row, where):
        width = CHUNK if tail else PADDED
        source = stage_ref.at[where, :, chunk * width : (chunk + 1) * width]
        spot = pl.ds(pl.multiple_of(row * INNER, INNER), INNER)
        return pltpu.make_async_copy(source, place.at[spot, :], sems.at[where, chunk])

    places = split_places(outs) if tail else None

    def wait(where):
        for chunk in range(4 if tail else 1):
            place = places[chunk % 2][0][chunk // 2] if tail else outs[0]
            copy(chunk, place, 0, where).wait()

    def put(side_ref, other_side_ref):
        product = jnp.dot(
            own_ref[...].T, side_ref[:, : CUTS[-1]], preferred_element_type=jnp.float32
        ) + jnp.dot(
            other_ref[...].T, other_side_ref[:, : CUTS[-1]], preferred_element_type=jnp.float32
        )
        stage_ref[slot, :, : CUTS[-1]] = product.astype(jnp.bfloat16)
        stage_ref[slot, :, CUTS[-1] :] = jnp.zeros((INNER, PADDED - CUTS[-1]), jnp.bfloat16)
        if not tail:
            copy(0, outs[0], step, slot).start()
            return
        spots = spots_of(0, place_ref)
        for chunk in range(4):
            which, _ = spots[chunk % 2]
            for k, pair in enumerate(places[chunk % 2]):

                @pl.when(which == k)
                def _(chunk=chunk, place=pair[chunk // 2]):
                    copy(chunk, place, step, slot).start()

    @pl.when(place_ref[2] < owners)
    def _():
        @pl.when(step >= 2)
        def _():
            wait(slot)

        @pl.when(tile < 3)
        def _():
            put(first_ref, other_first_ref)

        @pl.when(tile >= 3)
        def _():
            put(second_ref, other_second_ref)

        @pl.when(step == pl.num_programs(0) - 1)
        def _():
            wait(0)
            wait(1)


def attention_fill(tail, arrays, own, other, sides):
    tokens = own.shape[0]
    unit_rows = unit_tiles(TILE) * TILE
    owners = 4 * INNER // unit_rows
    steps = unit_rows // INNER

    def column(i, place_ref):
        return 0, jnp.minimum(place_ref[2], owners - 1) * steps + i

    halves = [half_side(tokens, 0), half_side(tokens, 1)]
    anywhere = pl.BlockSpec(memory_space=pl.ANY)
    return pl.pallas_call(
        functools.partial(attention_fill_body, tail, owners),
        grid_spec=pltpu.PrefetchScalarGridSpec(
            num_scalar_prefetch=1,
            grid=(steps,),
            in_specs=[pl.BlockSpec((tokens, INNER), column)] * 2
            + halves * 2
            + [anywhere] * len(arrays),
            out_specs=[anywhere] * len(arrays),
            scratch_shapes=[
                pltpu.VMEM((2, INNER, PADDED), jnp.bfloat16),
                pltpu.SemaphoreType.DMA((2, 4)),
            ],
        ),
        out_shape=[jax.ShapeDtypeStruct(array.shape, array.dtype) for array in arrays],
        input_output_aliases={7 + k: k for k in range(len(arrays))},
        compiler_params=pltpu.CompilerParams(vmem_limit_bytes=32 << 20),
        cost_estimate=pl.CostEstimate(
            flops=4 * unit_rows * tokens * CUTS[-1],
            bytes_accessed=4 * unit_rows * tokens + 2 * unit_rows * PADDED,
            transcendentals=0,
        ),
        name="attention_fill",
    )(place_of(TILE), own, other, sides[0], sides[0], sides[1], sides[1], *arrays)


def tied(first, second):
    return lax.optimization_barrier((first, second))


class Scatter:
    def __init__(self):
        self.waiting, self.flying, self.results = {}, {}, {}

    def push(self, name, route, kept, sends):
        self.waiting[name] = (route, kept, sends)

    def step(self, values, *names):
        arrays = {name: self.flying[name][1:] for name in names if name in self.flying}
        arrays, values = tied(arrays, values)
        moves = {}
        for name in names:
            if name in self.waiting:
                moves[name] = self.waiting.pop(name)
                continue
            route = self.flying.pop(name)[0]
            kept, moved = arrays[name]
            if not route:
                self.results[name] = kept.astype(jnp.float32) + sum(
                    part.astype(jnp.float32) for part in moved
                )
                continue
            total = total_of(kept, moved)
            total = total.reshape((lax.axis_size(route[0]), -1) + total.shape[-1:])
            sends = stage_sends(total, route[0], 0)
            moves[name] = (route, pick(total, lax.axis_index(route[0]), 0), sends)
        if moves and all(move[0] == ("z",) for move in moves.values()):
            kept = jnp.concatenate([move[1] for move in moves.values()], axis=-1)
            sends = [
                jnp.concatenate(parts, axis=-1) for parts in zip(*(m[2] for m in moves.values()))
            ]
            moves = {tuple(moves): (("z",), kept, sends)}
        arrays, values = tied({name: move[1:] for name, move in moves.items()}, values)
        for name, (route, *_) in moves.items():
            kept, sends = arrays[name]
            self.flying[name] = (route[1:], kept, stage_moves(sends, route[0]))
        return values


def total_of(value, moved):
    total = value.astype(jnp.float32)
    for part in moved:
        total = total + part.astype(jnp.float32)
    return total.astype(jnp.bfloat16)


def fetch_rows(local_rows):
    return lax.all_gather(local_rows, DEVICES, axis=0, tiled=True)


def from_first(value, axis):
    result = value
    here = lax.axis_index(axis)
    for k in range(1, lax.axis_size(axis)):
        result = jnp.where(here == k, lax.ppermute(value, axis, [(0, k)]), result)
    return result


def placed(own, axis, order):
    here, count = lax.axis_index(axis), lax.axis_size(axis)
    whole_axis = jnp.zeros(own.shape[:order] + (count,) + own.shape[order:], own.dtype)
    whole_axis = lax.dynamic_update_index_in_dim(whole_axis, own, here, order)
    for k in range(1, count):
        moved = shift(own, axis, k)
        whole_axis = lax.dynamic_update_index_in_dim(whole_axis, moved, (here - k) % count, order)
    return whole_axis


def attention_weights(local_rows):
    block, width = local_rows.shape
    owners = 4 * INNER // (block * lax.axis_size("z"))
    if owners == 1:
        halves = local_rows.reshape(2, block // 2, width)
        own = jnp.where(
            lax.axis_index("c") == 0, halves[0], lax.ppermute(halves[1], "c", [(0, 1)])
        )
    else:
        own = local_rows
    own = from_first(from_first(own, "x"), "y")
    return placed(placed(own, "z", 0), "c", 1 if owners == 1 else 0).reshape(4 * INNER, width)


def layer_forward(stream, gathered, attention, gain_one, gain_two, gate_low, context):
    normed, inverse_one = rms_forward(stream, gain_one)
    normed_low = normed.astype(jnp.bfloat16)
    projected = times_rows(normed_low, attention[: 3 * INNER]).astype(jnp.bfloat16)
    queries = projected[:, :INNER]
    parts = [projected[:, INNER:]]
    if gate_low is not None:
        parts.append(jnp.broadcast_to(gate_low[:, None], (stream.shape[0], BLOCK)))
    shared = with_neighbours(jnp.concatenate(parts, axis=1))
    attended, log_total = attend_forward(queries, shared, context)
    middle = stream + times_plain(attended, attention[3 * INNER :])
    normed_two, inverse_two = rms_forward(middle, gain_two)
    normed_two_low = normed_two.astype(jnp.bfloat16)
    result, up_gelu, up_linear = ffn_forward(normed_two_low, middle, gathered)
    kept = (
        stream,
        inverse_one,
        normed_low,
        queries,
        shared,
        attended,
        log_total,
        middle,
        inverse_two,
        normed_two_low,
        up_gelu,
        up_linear,
    )
    return (result, kept)


def layer_backward(grad_out, kept, gathered, gain_one, gain_two, context, tail):
    (
        stream,
        inverse_one,
        normed_low,
        queries,
        shared,
        attended,
        log_total,
        middle,
        inverse_two,
        normed_two_low,
        up_gelu,
        up_linear,
    ) = kept
    tokens = queries.shape[0]
    branch_low = grad_out.astype(jnp.bfloat16)
    sides = jnp.concatenate([normed_two_low, branch_low], axis=0)
    sides = jnp.pad(sides, ((0, 0), (0, PADDED - sides.shape[1])))
    sides = (sides, shift(sides, "c", 1))
    grad_normed_two, own, sent = ffn_backward(
        branch_low, normed_two_low, up_gelu, up_linear, gathered
    )
    other = shift(sent, "c", 1)
    grad_middle, grad_gain_two = rms_backward(middle, inverse_two, gain_two, grad_normed_two)
    grad_middle = grad_out + grad_middle
    middle_low = grad_middle.astype(jnp.bfloat16)
    late_sides = jnp.concatenate([normed_low, middle_low], axis=0)
    late_sides = jnp.pad(late_sides, ((0, 0), (0, PADDED - late_sides.shape[1])))
    late_sides = (late_sides, shift(late_sides, "c", 1))
    grad_mixed = times_rows(middle_low, gathered[3 * INNER : 4 * INNER]).astype(jnp.bfloat16)
    grad_query, grad_shared, grad_table = attend_backward(
        queries, grad_mixed, shared, log_total, context
    )
    grad_shared, own = lax.optimization_barrier((grad_shared, own))
    moving = start_back(grad_shared, tokens)
    arrays = weight_grads(tail, own, other, sides)
    arrays, moving = lax.optimization_barrier((arrays, moving))
    grad_own = finish_back(*moving)
    grad_gate = grad_own[:, 2 * INNER :]
    grad_input_low = jnp.concatenate(
        [grad_query, grad_own[:, : 2 * INNER].astype(jnp.bfloat16)], axis=1
    )
    late = jnp.concatenate([grad_input_low, attended], axis=1)
    arrays = attention_fill(tail, arrays, late, shift(late, "c", 1), late_sides)
    if tail:
        scatter = Scatter()
        for chunk in range(4):
            route = ("y", "x", "z") if chunk % 2 == 0 else ("x", "y", "z")
            ordered = [pair[chunk // 2] for pair in split_places(arrays)[chunk % 2]]
            scatter.push(chunk, route, ordered[-1], ordered[:-1])
        grad_input_low = scatter.step(grad_input_low, 0, 1)
    else:
        arrays, grad_input_low, grad_gate = lax.optimization_barrier(
            (arrays, grad_input_low, grad_gate)
        )
        scatter = lax.psum_scatter(arrays[0], ("y", "x", "z"), scatter_dimension=0, tiled=True)
    grad_normed = times_plain(grad_input_low, gathered[: 3 * INNER])
    grad_stream, grad_gain_one = rms_backward(stream, inverse_one, gain_one, grad_normed)
    return (grad_middle + grad_stream, grad_table, grad_gate, grad_gain_one, grad_gain_two, scatter)


def per_device(
    inputs, layer3_rows, layer4_rows, norm_gains, gate_weight, rel_bias, segment_ids, cotangent
):
    seqs_here, tokens_here, width = inputs.shape
    first_pos = lax.axis_index("z") * tokens_here
    context = attention_context(segment_ids[0], first_pos, tokens_here, rel_bias)
    stream = inputs.reshape(tokens_here, width)
    gathered_three = fetch_rows(layer3_rows)
    attention_four = attention_weights(layer4_rows)
    stream, attention_four = tied(stream, attention_four)
    after_three, kept_three = layer_forward(
        stream,
        gathered_three,
        gathered_three[: 4 * INNER],
        norm_gains[0],
        norm_gains[1],
        None,
        context,
    )
    gate_inverse = lax.rsqrt(jnp.mean(after_three * after_three, axis=1, keepdims=True) + epsilon)
    gate_normed = after_three * gate_inverse
    gate_logit = jnp.sum(gate_normed * gate_weight, axis=1) + gate_offset
    sigmoid_value = 1.0 / (1.0 + jnp.exp(-gate_logit))
    gate_mask = gate_scale * sigmoid_value
    gate_low = gate_mask.astype(jnp.bfloat16)
    gathered_four = fetch_rows(layer4_rows)
    after_four, kept_four = layer_forward(
        after_three,
        gathered_four,
        attention_four,
        norm_gains[2],
        norm_gains[3],
        gate_low,
        context,
    )
    grad_three_out, table_four, grad_gate, gain_four_one, gain_four_two, local_four = (
        layer_backward(
            cotangent.reshape(tokens_here, width),
            kept_four,
            gathered_four,
            norm_gains[2],
            norm_gains[3],
            context,
            False,
        )
    )
    grad_logit = grad_gate[:, 0] * gate_scale * sigmoid_value * (1.0 - sigmoid_value)
    grad_gate_weight = jnp.sum(grad_logit[:, None] * gate_normed, axis=0)
    gate_stream = stream_backward(after_three, gate_inverse, grad_logit[:, None] * gate_weight)
    grad_input, table_three, unused, gain_three_one, gain_three_two, scatter = layer_backward(
        grad_three_out + gate_stream,
        kept_three,
        gathered_three,
        norm_gains[0],
        norm_gains[1],
        context,
        True,
    )
    table = jnp.pad((table_three + table_four).reshape(1, -1), ((0, 0), (0, width - 6 * BUCKETS)))
    small_sums = jnp.stack(
        [gain_three_one, gain_three_two, gain_four_one, gain_four_two, grad_gate_weight, table[0]]
    )
    small = hop(small_sums, "c")
    small = scatter.step(small, 0, 1)
    small = scatter.step(small, 2, 3)
    small = hop(small, "z", 1)
    small = scatter.step(small, 0, 1)
    for bit in range(2, lax.axis_size("z")):
        if bit & (bit - 1) == 0:
            small = hop(small, "z", bit)
    small = scatter.step(small, (0, 1))
    small = scatter.step(small, 2, 3)
    small = scatter.step(small, 2, 3)
    small = hop(small, "x")
    for bit in range(1, lax.axis_size("y")):
        if bit & (bit - 1) == 0:
            small = hop(small, "y", bit)
    summed = scatter.step(small, (2, 3))
    local_three = jnp.concatenate([scatter.results[pair] for pair in ((0, 1), (2, 3))], axis=1)
    local_three, local_four = local_three[:, :width], local_four[:, :width].astype(jnp.float32)
    return (
        after_four.reshape(inputs.shape),
        gate_mask.reshape(seqs_here, tokens_here),
        grad_input.reshape(inputs.shape),
        local_three,
        local_four,
        summed[:4],
        summed[4],
        summed[5, : 6 * BUCKETS].reshape(BUCKETS, HEADS),
    )


def solution(mesh):
    outer, inner = mesh.devices.shape
    fine = Mesh(mesh.devices.reshape(outer // 4, 2, 2, inner), DEVICES)
    batch = ("y", "x", "c")
    tokens = P(batch, "z", None)
    rows = P(DEVICES, None)
    return jax.shard_map(
        per_device,
        mesh=fine,
        in_specs=(tokens, rows, rows, P(), P(), P(), P(batch, None), tokens),
        out_specs=(tokens, P(batch, "z"), tokens, rows, rows, P(), P(), P()),
        check_vma=False,
    )
```

```python
import functools

import jax
import jax.numpy as jnp
from jax import lax
from jax.experimental import pallas as pl
from jax.experimental.pallas import tpu as pltpu
from jax.sharding import Mesh
from jax.sharding import PartitionSpec as P

HEADS = 6
PAIRS = 3
BLOCK = 128
WIDE = 2 * BLOCK
INNER = 384
BUCKETS = 32
FF = 3584
REACH = 799
HALO = 896
TILE = 256
ATTENTION_TILES = 4 * INNER // TILE
OFFSETS = 5
CHUNK = 384
PADDED = 1536
FORWARD_TILE = 512
CUTS = (0, 384, 768, 1152, 1472)
DEVICES = ("y", "x", "c", "z")
epsilon = 1e-06
gate_scale = -30.0
gate_offset = -3.5
masked_out = -1e30
limits = (12, 16, 23, 32, 46, 64, 91)
both_last = (((1,), (1,)), ((), ()))


def bucket_of(relative):
    magnitude = jnp.abs(relative)
    beyond = jnp.zeros_like(magnitude)
    for bound_value in limits:
        beyond = beyond + (magnitude >= bound_value).astype(jnp.int32)
    inside = jnp.where(magnitude < 8, magnitude, 8 + beyond)
    return inside + 16 * (relative > 0).astype(jnp.int32)


def near_buckets(offset):
    if offset < 0:
        return range(1, 16)
    if offset > 0:
        return range(17, 32)
    return range(0, 32)


def tile_buckets(offset, width):
    key_at = lax.broadcasted_iota(jnp.int32, (BLOCK, width), 0)
    query_at = lax.broadcasted_iota(jnp.int32, (BLOCK, width), 1) % BLOCK
    return bucket_of(offset * BLOCK + key_at - query_at)


def bias_body(table_ref, tiles_ref):
    head = pl.program_id(0)
    tiles_ref[0, 0] = jnp.full((BLOCK, BLOCK), table_ref[15, head], jnp.float32)
    tiles_ref[0, 4] = jnp.full((BLOCK, BLOCK), table_ref[31, head], jnp.float32)
    for offset in (-1, 0, 1):
        buckets = tile_buckets(offset, BLOCK)
        tile = jnp.zeros((BLOCK, BLOCK), jnp.float32)
        for bucket in near_buckets(offset):
            tile = jnp.where(buckets == bucket, table_ref[bucket, head], tile)
        tiles_ref[0, offset + 2] = tile


def bias_tiles(rel_bias):
    return pl.pallas_call(
        bias_body,
        grid=(HEADS,),
        in_specs=[pl.BlockSpec(memory_space=pltpu.SMEM)],
        out_specs=pl.BlockSpec((1, OFFSETS, BLOCK, BLOCK), lambda h: (h, 0, 0, 0)),
        out_shape=jax.ShapeDtypeStruct((HEADS, OFFSETS, BLOCK, BLOCK), jnp.float32),
        name="bias_tiles",
    )(rel_bias)


def lane_masks():
    lane = lax.broadcasted_iota(jnp.int32, (BLOCK, BLOCK), 1)
    low = jnp.where(lane < 64, 1.0, 0.0).astype(jnp.bfloat16)
    high = jnp.where(lane < 64, 0.0, 1.0).astype(jnp.bfloat16)
    return low, high


def stacked(block, masks):
    low, high = masks
    return jnp.concatenate([block * low, block * high], axis=0)


def pair_cols(pair):
    return slice(pair * BLOCK, (pair + 1) * BLOCK)


def value_cols(pair):
    return slice(INNER + pair * BLOCK, INNER + (pair + 1) * BLOCK)


def block_rows(block):
    return pl.ds(pl.multiple_of(block * BLOCK, BLOCK), BLOCK)


def wide_rows(block):
    return pl.ds(pl.multiple_of(block * WIDE, WIDE), WIDE)


def fold(values):
    return values.reshape(values.shape[0] // 8, 8, WIDE)


def shift_tile(gated, rows, own_segment, segment_ref, shared_ref):
    same = segment_ref[rows, :] == own_segment
    inside = shared_ref[rows, 2 * INNER :].astype(jnp.float32) if gated else 0.0
    shift = jnp.where(same, inside, masked_out)
    return jnp.concatenate([shift, shift], axis=1)


def used_blocks(low_ref, high_ref):
    last = pl.num_programs(0) - 1
    return low_ref[0] // 2 * 2, (high_ref[last] + 1) // 2 * 2


def tile_offsets(block, own_block):
    return [jnp.clip(2 * block + k - own_block, -2, 2) + 2 for k in range(2)]


def bias_pair(bias_ref, pair, offsets):
    halves = [
        jnp.concatenate([bias_ref[2 * pair, at], bias_ref[2 * pair + 1, at]], axis=1)
        for at in offsets
    ]
    return jnp.concatenate(halves, axis=0)


def pick_heads(wide):
    return jnp.concatenate([wide[:64, :BLOCK], wide[64:, BLOCK:]], axis=0)


def forward_body(gated, low_ref, high_ref, *refs):
    query_ref, shared_ref, own_ref, segment_ref, bias_ref = refs[:5]
    mixed_ref, total_ref, turned_ref, score_ref, sum_ref = refs[5:]
    step = pl.program_id(0)

    @pl.when(step == 0)
    def _():
        @pl.loop(*used_blocks(low_ref, high_ref))
        def _(block):
            rows = block_rows(block)
            turned_ref[:, rows] = shared_ref[rows, INNER : 2 * INNER].T

    first, last = low_ref[step] // 2, (high_ref[step] + 1) // 2
    own_block = HALO // BLOCK + step
    own_segment = own_ref[0]
    masks = lane_masks()
    queries = [stacked(query_ref[:, pair_cols(pair)], masks) for pair in range(PAIRS)]

    def scores(block, peaks):
        rows = wide_rows(block)
        shift = shift_tile(gated, rows, own_segment, segment_ref, shared_ref)
        offsets = tile_offsets(block, own_block)
        new_peaks = []
        for pair in range(PAIRS):
            score = lax.dot_general(
                shared_ref[rows, pair_cols(pair)],
                queries[pair],
                both_last,
                preferred_element_type=jnp.float32,
            )
            score = score + bias_pair(bias_ref, pair, offsets) + shift
            score_ref[pair, block] = score
            new_peaks.append(jnp.maximum(peaks[pair], jnp.max(fold(score), axis=0)))
        return tuple(new_peaks)

    start = jnp.full((8, WIDE), -3e38, jnp.float32)
    peaks = lax.fori_loop(first, last, scores, (start,) * PAIRS)
    peaks = [jnp.max(peak, axis=0, keepdims=True) for peak in peaks]
    sum_ref[...] = jnp.zeros_like(sum_ref)

    def mix(block, totals):
        new_totals = []
        for pair in range(PAIRS):
            weight = jnp.exp(score_ref[pair, block] - peaks[pair])
            new_totals.append(totals[pair] + jnp.sum(fold(weight), axis=0))
            sum_ref[pair] += jnp.dot(
                turned_ref[pair_cols(pair), wide_rows(block)],
                weight.astype(jnp.bfloat16),
                preferred_element_type=jnp.float32,
            )
        return tuple(new_totals)

    totals = lax.fori_loop(first, last, mix, (jnp.zeros((8, WIDE), jnp.float32),) * PAIRS)
    for pair in range(PAIRS):
        row_total = jnp.sum(totals[pair], axis=0, keepdims=True)
        mixed = pick_heads(sum_ref[pair] * (1.0 / row_total))
        mixed_ref[:, pair_cols(pair)] = mixed.T.astype(jnp.bfloat16)
        total_ref[0, pair : pair + 1, :] = peaks[pair] + jnp.log(row_total)


def whole(shape):
    return pl.BlockSpec(shape, lambda i, *_: (0,) * len(shape), pipeline_mode=pl.Buffered(1))


def rows_spec(width):
    return pl.BlockSpec((BLOCK, width), lambda i, *_: (i, 0))


def attend_forward(queries, shared, context):
    lows, highs, own_rows, segment_wide, tiles = context
    tokens, (length, width) = queries.shape[0], shared.shape
    steps, key_blocks = tokens // BLOCK, length // BLOCK
    return pl.pallas_call(
        functools.partial(forward_body, width > 2 * INNER),
        grid_spec=pltpu.PrefetchScalarGridSpec(
            num_scalar_prefetch=2,
            grid=(steps,),
            in_specs=[
                rows_spec(INNER),
                whole((length, width)),
                pl.BlockSpec((1, 1, BLOCK), lambda i, *_: (i, 0, 0)),
                whole((length, BLOCK)),
                whole(tiles.shape),
            ],
            out_specs=[
                rows_spec(INNER),
                pl.BlockSpec((1, 8, WIDE), lambda i, *_: (i, 0, 0)),
            ],
            scratch_shapes=[
                pltpu.VMEM((INNER, length), jnp.bfloat16),
                pltpu.VMEM((PAIRS, key_blocks // 2, WIDE, WIDE), jnp.float32),
                pltpu.VMEM((PAIRS, BLOCK, WIDE), jnp.float32),
            ],
        ),
        out_shape=[
            jax.ShapeDtypeStruct((tokens, INNER), jnp.bfloat16),
            jax.ShapeDtypeStruct((steps, 8, WIDE), jnp.float32),
        ],
        compiler_params=pltpu.CompilerParams(vmem_limit_bytes=40 << 20),
        cost_estimate=pl.CostEstimate(
            flops=tokens * length * INNER * 4,
            bytes_accessed=8 << 20,
            transcendentals=tokens * length * 3,
        ),
        name="attend_forward",
    )(lows, highs, queries, shared, own_rows, segment_wide, tiles)


def backward_body(gated, low_ref, high_ref, *refs):
    query_ref, grad_ref, shared_ref, own_ref, segment_ref, bias_ref, total_ref = refs[:7]
    grad_query_ref, grad_shared_ref, bucket_ref = refs[7:10]
    turned_ref, prob_ref, pull_ref, sum_ref, bias_sum_ref, turn_sum_ref = refs[10:]
    step = pl.program_id(0)

    @pl.when(step == 0)
    def _():
        bias_sum_ref[...] = jnp.zeros_like(bias_sum_ref)

        @pl.loop(*used_blocks(low_ref, high_ref))
        def _(block):
            rows = block_rows(block)
            turned_ref[:, rows] = shared_ref[rows, :INNER].T
            sum_ref[rows, :] = jnp.zeros((BLOCK, sum_ref.shape[1]), jnp.float32)

    first, last = low_ref[step] // 2, (high_ref[step] + 1) // 2
    own_block = HALO // BLOCK + step
    own_segment = own_ref[0]
    masks = lane_masks()
    queries = [stacked(query_ref[:, pair_cols(pair)], masks) for pair in range(PAIRS)]
    grads = [stacked(grad_ref[:, pair_cols(pair)], masks) for pair in range(PAIRS)]
    totals = [total_ref[0, pair : pair + 1, :] for pair in range(PAIRS)]

    def weights(block, deltas):
        rows = wide_rows(block)
        shift = shift_tile(gated, rows, own_segment, segment_ref, shared_ref)
        offsets = tile_offsets(block, own_block)
        new_deltas = []
        for pair in range(PAIRS):
            cols = pair_cols(pair)
            score = lax.dot_general(
                shared_ref[rows, cols], queries[pair], both_last, preferred_element_type=jnp.float32
            )
            pull = lax.dot_general(
                shared_ref[rows, value_cols(pair)],
                grads[pair],
                both_last,
                preferred_element_type=jnp.float32,
            )
            prob = jnp.exp(score + bias_pair(bias_ref, pair, offsets) + shift - totals[pair])
            prob_ref[pair, block] = prob
            pull_ref[pair, block] = pull
            sum_ref[rows, value_cols(pair)] += jnp.dot(
                prob.astype(jnp.bfloat16), grads[pair], preferred_element_type=jnp.float32
            )
            new_deltas.append(deltas[pair] + jnp.sum(fold(prob * pull), axis=0))
        return tuple(new_deltas)

    start = jnp.zeros((8, WIDE), jnp.float32)
    deltas = lax.fori_loop(first, last, weights, (start,) * PAIRS)
    deltas = [jnp.sum(delta, axis=0, keepdims=True) for delta in deltas]
    turn_sum_ref[...] = jnp.zeros_like(turn_sum_ref)

    @pl.loop(first, last)
    def _(block):
        rows = wide_rows(block)
        offsets = tile_offsets(block, own_block)
        gate_part = jnp.zeros((WIDE, BLOCK), jnp.float32)
        for pair in range(PAIRS):
            cols = pair_cols(pair)
            grad_score = prob_ref[pair, block] * (pull_ref[pair, block] - deltas[pair])
            bias_sum_ref[pair, offsets[0]] += grad_score[:BLOCK]
            bias_sum_ref[pair, offsets[1]] += grad_score[BLOCK:]
            if gated:
                gate_part = gate_part + (grad_score[:, :BLOCK] + grad_score[:, BLOCK:])
            score_low = grad_score.astype(jnp.bfloat16)
            sum_ref[rows, cols] += jnp.dot(
                score_low, queries[pair], preferred_element_type=jnp.float32
            )
            turn_sum_ref[pair] += jnp.dot(
                turned_ref[cols, rows], score_low, preferred_element_type=jnp.float32
            )
        if gated:
            sum_ref[rows, 2 * INNER :] += gate_part

    for pair in range(PAIRS):
        grad_query_ref[:, pair_cols(pair)] = pick_heads(turn_sum_ref[pair]).T.astype(jnp.bfloat16)

    @pl.when(step == pl.num_programs(0) - 1)
    def _():
        grad_shared_ref[...] = jnp.zeros_like(grad_shared_ref)

        @pl.loop(*used_blocks(low_ref, high_ref))
        def _(block):
            rows = block_rows(block)
            both = slice(0, 2 * INNER)
            grad_shared_ref[rows, both] = sum_ref[rows, both].astype(jnp.bfloat16)
            if gated:
                gate_total = jnp.sum(sum_ref[rows, 2 * INNER :], axis=1, keepdims=True)
                grad_shared_ref[rows, 2 * INNER :] = jnp.broadcast_to(
                    gate_total, (BLOCK, BLOCK)
                ).astype(jnp.bfloat16)

        tables = {offset: tile_buckets(offset, WIDE) for offset in (-1, 0, 1)}

        @pl.loop(0, PAIRS)
        def _(pair):
            for bucket in range(BUCKETS):
                part = jnp.zeros((8, WIDE), jnp.float32)
                for offset in (-1, 0, 1):
                    if bucket in near_buckets(offset):
                        chosen = jnp.where(
                            tables[offset] == bucket, bias_sum_ref[pair, offset + 2], 0.0
                        )
                        part = part + jnp.sum(fold(chosen), axis=0)
                if bucket == 15:
                    part = part + jnp.sum(fold(bias_sum_ref[pair, 0]), axis=0)
                if bucket == 31:
                    part = part + jnp.sum(fold(bias_sum_ref[pair, 4]), axis=0)
                bucket_ref[pair, bucket : bucket + 1, :] = jnp.sum(part, axis=0, keepdims=True)


def attend_backward(queries, grad_mixed, shared, log_total, context):
    lows, highs, own_rows, segment_wide, tiles = context
    tokens, (length, width) = queries.shape[0], shared.shape
    steps, key_blocks = tokens // BLOCK, length // BLOCK
    grad_query, grad_shared, bucket_sums = pl.pallas_call(
        functools.partial(backward_body, width > 2 * INNER),
        grid_spec=pltpu.PrefetchScalarGridSpec(
            num_scalar_prefetch=2,
            grid=(steps,),
            in_specs=[
                rows_spec(INNER),
                rows_spec(INNER),
                whole((length, width)),
                pl.BlockSpec((1, 1, BLOCK), lambda i, *_: (i, 0, 0)),
                whole((length, BLOCK)),
                whole(tiles.shape),
                pl.BlockSpec((1, 8, WIDE), lambda i, *_: (i, 0, 0)),
            ],
            out_specs=[
                rows_spec(INNER),
                whole((length, width)),
                whole((PAIRS, BUCKETS, WIDE)),
            ],
            scratch_shapes=[
                pltpu.VMEM((INNER, length), jnp.bfloat16),
                pltpu.VMEM((PAIRS, key_blocks // 2, WIDE, WIDE), jnp.float32),
                pltpu.VMEM((PAIRS, key_blocks // 2, WIDE, WIDE), jnp.float32),
                pltpu.VMEM((length, width), jnp.float32),
                pltpu.VMEM((PAIRS, OFFSETS, BLOCK, WIDE), jnp.float32),
                pltpu.VMEM((PAIRS, BLOCK, WIDE), jnp.float32),
            ],
        ),
        out_shape=[
            jax.ShapeDtypeStruct((tokens, INNER), jnp.bfloat16),
            jax.ShapeDtypeStruct((length, width), jnp.bfloat16),
            jax.ShapeDtypeStruct((PAIRS, BUCKETS, WIDE), jnp.float32),
        ],
        compiler_params=pltpu.CompilerParams(vmem_limit_bytes=48 << 20),
        cost_estimate=pl.CostEstimate(
            flops=tokens * length * INNER * 10,
            bytes_accessed=12 << 20,
            transcendentals=tokens * length * 3,
        ),
        name="attend_backward",
    )(lows, highs, queries, grad_mixed, shared, own_rows, segment_wide, tiles, log_total)
    table = jnp.sum(bucket_sums.reshape(PAIRS, BUCKETS, 2, BLOCK), axis=3)
    return grad_query, grad_shared, table.transpose(1, 0, 2).reshape(BUCKETS, HEADS)


def attention_context(segment_row, first_pos, tokens, rel_bias):
    steps = tokens // BLOCK
    padded = jnp.pad(segment_row, (HALO, 0), constant_values=-1)
    padded = jnp.pad(padded, (0, HALO), constant_values=1000)
    window = lax.dynamic_slice_in_dim(padded, first_pos, tokens + 2 * HALO, 0)
    own = window[HALO : HALO + tokens].reshape(steps, 1, BLOCK)
    lows = jnp.sum(window[None, :] < own[:, 0, :1], axis=1, dtype=jnp.int32) // BLOCK
    ends = jnp.sum(window[None, :] <= own[:, 0, BLOCK - 1 :], axis=1, dtype=jnp.int32)
    highs = (ends + BLOCK - 1) // BLOCK
    segment_wide = jnp.broadcast_to(window[:, None], (window.shape[0], BLOCK))
    return lows, highs, own, segment_wide, bias_tiles(rel_bias)


def rms_forward(stream, gain_row):
    inverse = lax.rsqrt(jnp.mean(stream * stream, axis=1, keepdims=True) + epsilon)
    return (stream * inverse * gain_row, inverse)


def stream_backward(stream, inverse, scaled):
    return inverse * scaled - stream * inverse**3 * jnp.mean(scaled * stream, axis=1, keepdims=True)


def rms_backward(stream, inverse, gain_row, grad_normed):
    grad_gain = jnp.sum(grad_normed * stream * inverse, axis=0)
    return (stream_backward(stream, inverse, gain_row * grad_normed), grad_gain)


def gelu_tanh(values):
    return 0.5 * values * (1.0 + jnp.tanh(0.7978845608028654 * (values + 0.044715 * values**3)))


def times_rows(left_side, weight):
    return lax.dot_general(
        left_side, weight, (((1,), (1,)), ((), ())), preferred_element_type=jnp.float32
    )


def times_plain(left_side, weight):
    return jnp.dot(left_side, weight, preferred_element_type=jnp.float32)


def outer_sum(left_side, right_side):
    return lax.dot_general(
        left_side, right_side, (((0,), (0,)), ((), ())), preferred_element_type=jnp.float32
    )


def shift(value, axis, amount):
    count = lax.axis_size(axis)
    return lax.ppermute(value, axis, [(i, (i + amount) % count) for i in range(count)])


def slide(value, amount):
    count = lax.axis_size("z")
    pairs = [(i, i + amount) for i in range(count) if 0 <= i + amount < count]
    return lax.ppermute(value, "z", pairs)


def far_pair(near_start, near_end, distance):
    count = lax.axis_size("z")
    first_half = lax.axis_index("z") < distance
    sent = jnp.where(first_half, near_end, near_start)
    pairs = [(i, (i + distance) % count) for i in range(count)]
    got = lax.ppermute(sent, "z", pairs)
    return got


def far_split(got, distance):
    first_half = lax.axis_index("z") < distance
    none = jnp.zeros_like(got)
    return jnp.where(first_half, none, got), jnp.where(first_half, got, none)


def halo_pieces(tokens):
    pieces = []
    distance, covered = 1, 0
    while covered < HALO:
        span = min(tokens, HALO - covered)
        needed = min(span, -(-(REACH - covered) // 16) * 16)
        pieces.append((distance, span, needed))
        distance, covered = distance + 1, covered + span
    return pieces


def with_neighbours(own):
    tokens = own.shape[0]
    before, after = [], []
    for distance, span, needed in halo_pieces(tokens):
        if distance < lax.axis_size("z"):
            if 2 * distance == lax.axis_size("z"):
                left, right = far_split(
                    far_pair(own[:needed], own[tokens - needed :], distance), distance
                )
            else:
                left = slide(own[tokens - needed :], distance)
                right = slide(own[:needed], -distance)
            before.append(jnp.pad(left, ((span - needed, 0), (0, 0))))
            after.append(jnp.pad(right, ((0, span - needed), (0, 0))))
        else:
            empty = jnp.zeros((span, own.shape[1]), own.dtype)
            before.append(empty)
            after.append(empty)
    return jnp.concatenate(before[::-1] + [own] + after, axis=0)


def start_back(window, tokens):
    moved = []
    covered = 0
    for distance, span, needed in halo_pieces(tokens):
        if distance < lax.axis_size("z"):
            left_end = HALO - covered
            right_start = HALO + tokens + covered
            left = window[left_end - needed : left_end]
            right = window[right_start : right_start + needed]
            if 2 * distance == lax.axis_size("z"):
                moved.append((far_pair(left, right, distance),))
            else:
                moved.append((slide(left, -distance), slide(right, distance)))
        covered += span
    return window[HALO : HALO + tokens], moved


def finish_back(own, moved):
    tokens = own.shape[0]
    total = own.astype(jnp.float32)
    for distance, pair in enumerate(moved, 1):
        if len(pair) == 1:
            ahead, back = far_split(pair[0], distance)
        else:
            back, ahead = pair
        needed = back.shape[0]
        total = total + jnp.pad(back.astype(jnp.float32), ((tokens - needed, 0), (0, 0)))
        total = total + jnp.pad(ahead.astype(jnp.float32), ((0, tokens - needed), (0, 0)))
    return total


def hop(value, axis, bit=1):
    pairs = [(i, i ^ bit) for i in range(lax.axis_size(axis))]
    return value + lax.ppermute(value, axis, pairs)


def pick(value, index, axis):
    return lax.dynamic_index_in_dim(value, index, axis, keepdims=False)


def stage_sends(value, axis_name, axis):
    count, here = lax.axis_size(axis_name), lax.axis_index(axis_name)
    return [pick(value, (here + k) % count, axis) for k in range(1, count)]


def stage_moves(sends, axis_name):
    return [shift(sent, axis_name, k + 1) for k, sent in enumerate(sends)]


def gelu_parts(values):
    squared = values * values
    slope = jnp.tanh(0.7978845608028654 * (values + 0.044715 * values * squared))
    active = 0.5 * values * (1.0 + slope)
    inner = 0.7978845608028654 * (1.0 + 3.0 * 0.044715 * squared)
    return active, 0.5 * (1.0 + slope) + 0.5 * values * (1.0 - slope * slope) * inner


def ffn_forward_body(normed_ref, middle_ref, gelu_ref, linear_ref, down_ref, *outs):
    result_ref, up_gelu_ref, up_linear_ref = outs

    @pl.when(pl.program_id(0) == 0)
    def _():
        result_ref[...] = middle_ref[...]

    up_gelu = times_rows(normed_ref[...], gelu_ref[...])
    up_linear = times_rows(normed_ref[...], linear_ref[...])
    up_gelu_ref[...] = up_gelu
    up_linear_ref[...] = up_linear
    hidden = (gelu_tanh(up_gelu) * up_linear).astype(jnp.bfloat16)
    result_ref[...] += times_plain(hidden, down_ref[...])


def resident(shape):
    return pl.BlockSpec(shape, lambda *_: (0,) * len(shape), pipeline_mode=pl.Buffered(1))


def ffn_forward(normed, middle, gathered):
    tokens, width = normed.shape
    steps = FF // FORWARD_TILE
    first = 4 * INNER // FORWARD_TILE

    def weight(kind):
        return pl.BlockSpec((FORWARD_TILE, width), lambda i: (first + kind * steps + i, 0))

    hidden = pl.BlockSpec((tokens, FORWARD_TILE), lambda i: (0, i))
    return pl.pallas_call(
        ffn_forward_body,
        grid=(steps,),
        in_specs=[
            resident((tokens, width)),
            resident((tokens, width)),
            weight(0),
            weight(1),
            weight(2),
        ],
        out_specs=[resident((tokens, width)), hidden, hidden],
        out_shape=[
            jax.ShapeDtypeStruct((tokens, width), jnp.float32),
            jax.ShapeDtypeStruct((tokens, FF), jnp.float32),
            jax.ShapeDtypeStruct((tokens, FF), jnp.float32),
        ],
        compiler_params=pltpu.CompilerParams(vmem_limit_bytes=48 << 20),
        cost_estimate=pl.CostEstimate(
            flops=6 * tokens * FF * width,
            bytes_accessed=6 * FF * width + 8 * tokens * FF,
            transcendentals=tokens * FF,
        ),
        name="ffn_forward",
    )(normed, middle, gathered, gathered, gathered)


def ffn_backward_body(core_ref, *refs):
    branch_ref, normed_ref, up_gelu_ref, up_linear_ref, gelu_ref, linear_ref, down_ref = refs[:7]
    grad_ref, kept_ref, sent_ref, stage_ref, sems = refs[7:]
    step = pl.program_id(0)
    slot = step % 2
    mine, unit = core_ref[0], core_ref[1]
    parts = FORWARD_TILE // TILE

    def copy(kind, part, place, at, where):
        spot = pl.ds(pl.multiple_of(at * TILE, TILE), TILE)
        source = stage_ref.at[where, kind, part * TILE : (part + 1) * TILE, :]
        return pltpu.make_async_copy(source, place.at[spot, :], sems.at[where, kind, part])

    def wait(where):
        for kind in range(3):
            for part in range(parts):
                copy(kind, part, kept_ref, 0, where).wait()

    def put(kind, turned):
        stage_ref[slot, kind] = turned
        for part in range(parts):
            target = ATTENTION_TILES + kind * (FF // TILE) + step * parts + part
            own = (target // unit) % 2 == mine
            at = (target // (2 * unit)) * unit + target % unit

            @pl.when(own)
            def _(part=part, at=at):
                copy(kind, part, kept_ref, at, slot).start()

            @pl.when(jnp.logical_not(own))
            def _(part=part, at=at):
                copy(kind, part, sent_ref, at, slot).start()

    @pl.when(step == 0)
    def _():
        grad_ref[...] = jnp.zeros_like(grad_ref)

    @pl.when(step >= 2)
    def _():
        wait(slot)

    grad_hidden = times_rows(branch_ref[...], down_ref[...])
    active, slope = gelu_parts(up_gelu_ref[...])
    linear = up_linear_ref[...]
    grad_gelu = (grad_hidden * linear * slope).astype(jnp.bfloat16)
    grad_linear = (grad_hidden * active).astype(jnp.bfloat16)
    put(2, (active * linear).astype(jnp.bfloat16).T)
    put(0, grad_gelu.T)
    put(1, grad_linear.T)
    grad_ref[...] += times_plain(grad_gelu, gelu_ref[...]) + times_plain(
        grad_linear, linear_ref[...]
    )

    @pl.when(step == pl.num_programs(0) - 1)
    def _():
        wait(0)
        wait(1)


def unit_tiles(tile):
    rows = 4 * INNER + 3 * FF
    return rows // tile // (2 * lax.axis_size("y") * lax.axis_size("x"))


def ffn_backward(branch, normed, up_gelu, up_linear, gathered):
    tokens, width = normed.shape
    rows = 4 * INNER + 3 * FF
    steps = FF // FORWARD_TILE
    core = jnp.stack([lax.axis_index("c").astype(jnp.int32), jnp.int32(unit_tiles(TILE))])

    def weight(kind):
        first = 4 * INNER // FORWARD_TILE + kind * steps
        return pl.BlockSpec((FORWARD_TILE, width), lambda i, *_: (first + i, 0))

    hidden = pl.BlockSpec((tokens, FORWARD_TILE), lambda i, *_: (0, i))
    side = resident((tokens, width))
    anywhere = pl.BlockSpec(memory_space=pl.ANY)
    return pl.pallas_call(
        ffn_backward_body,
        grid_spec=pltpu.PrefetchScalarGridSpec(
            num_scalar_prefetch=1,
            grid=(steps,),
            in_specs=[side, side, hidden, hidden, weight(0), weight(1), weight(2)],
            out_specs=[side, anywhere, anywhere],
            scratch_shapes=[
                pltpu.VMEM((2, 3, FORWARD_TILE, tokens), jnp.bfloat16),
                pltpu.SemaphoreType.DMA((2, 3, FORWARD_TILE // TILE)),
            ],
        ),
        out_shape=[jax.ShapeDtypeStruct((tokens, width), jnp.float32)]
        + [jax.ShapeDtypeStruct((rows // 2, tokens), jnp.bfloat16)] * 2,
        compiler_params=pltpu.CompilerParams(vmem_limit_bytes=56 << 20),
        cost_estimate=pl.CostEstimate(
            flops=6 * tokens * FF * width,
            bytes_accessed=6 * FF * width + 14 * tokens * FF,
            transcendentals=tokens * FF,
        ),
        name="ffn_backward",
    )(core, branch, normed, up_gelu, up_linear, gathered, gathered, gathered)


def spots_of(unit_at, place_ref):
    here_y, here_x, size_y, size_x = place_ref[0], place_ref[1], place_ref[4], place_ref[5]
    row, column = unit_at // size_x, unit_at % size_x
    return (
        ((row + 2 * size_y - here_y - 1) % size_y, column),
        ((column + 2 * size_x - here_x - 1) % size_x, row),
    )


def weight_grads_body(tail, tile, place_ref, *refs):
    own_ref, other_ref, normed_ref, branch_ref, other_normed_ref, other_branch_ref = refs[:6]
    refs = refs[6:]
    step = pl.program_id(0)
    unit = place_ref[3]
    at = (step // unit * 2 + place_ref[2]) * unit + step % unit
    first, second = 4 * INNER // tile, (4 * INNER + 2 * FF) // tile
    slot = step % 2
    if tail:
        stage_ref, sems = refs[-2:]
        places = split_places(refs[:-2])

    def copy(chunk, place, row, where):
        source = stage_ref.at[where, :, chunk * CHUNK : (chunk + 1) * CHUNK]
        spot = pl.ds(pl.multiple_of(row * tile, tile), tile)
        return pltpu.make_async_copy(source, place.at[spot, :], sems.at[where, chunk])

    def wait(where):
        for chunk in range(4):
            copy(chunk, places[chunk % 2][0][chunk // 2], 0, where).wait()

    def put(product):
        if not tail:
            refs[0][:, : CUTS[-1]] = product.astype(jnp.bfloat16)
            refs[0][:, CUTS[-1] :] = jnp.zeros((tile, PADDED - CUTS[-1]), jnp.bfloat16)
            return
        stage_ref[slot, :, : CUTS[-1]] = product.astype(jnp.bfloat16)
        spots = spots_of(step // unit, place_ref)
        for chunk in range(4):
            which, position = spots[chunk % 2]
            for k, pair in enumerate(places[chunk % 2]):

                @pl.when(which == k)
                def _(chunk=chunk, place=pair[chunk // 2], row=position * unit + step % unit):
                    copy(chunk, place, row, slot).start()

    def both(side_ref, other_side_ref):
        return jnp.dot(
            own_ref[...], side_ref[:, : CUTS[-1]], preferred_element_type=jnp.float32
        ) + jnp.dot(
            other_ref[...], other_side_ref[:, : CUTS[-1]], preferred_element_type=jnp.float32
        )

    if tail:

        @pl.when(step < 2)
        def _():
            stage_ref[slot, :, CUTS[-1] :] = jnp.zeros((tile, PADDED - CUTS[-1]), jnp.bfloat16)

        @pl.when(step >= 2)
        def _():
            wait(slot)

    @pl.when(at < first)
    def _():
        put(jnp.zeros((tile, CUTS[-1]), jnp.float32))

    @pl.when((at >= first) & (at < second))
    def _():
        put(both(normed_ref, other_normed_ref))

    @pl.when(at >= second)
    def _():
        put(both(branch_ref, other_branch_ref))

    if tail:

        @pl.when(step == pl.num_programs(0) - 1)
        def _():
            wait(0)
            wait(1)


def split_places(refs):
    size_y, size_x = lax.axis_size("y"), lax.axis_size("x")
    along_y = [refs[2 * k : 2 * k + 2] for k in range(size_y)]
    along_x = [refs[2 * size_y + 2 * k : 2 * size_y + 2 * k + 2] for k in range(size_x)]
    return along_y, along_x


def place_of(tile):
    return jnp.stack(
        [
            lax.axis_index("y").astype(jnp.int32),
            lax.axis_index("x").astype(jnp.int32),
            lax.axis_index("c").astype(jnp.int32),
            jnp.int32(unit_tiles(tile)),
            jnp.int32(lax.axis_size("y")),
            jnp.int32(lax.axis_size("x")),
        ]
    )


def half_side(tokens, at):
    return pl.BlockSpec(
        (tokens, PADDED), lambda i, *_: (at, 0), pipeline_mode=pl.Buffered(1)
    )


def weight_grads(tail, own, other, sides):
    rows, tokens = own.shape
    tile = 512 if unit_tiles(256) % 2 == 0 else 256
    steps = rows // tile
    source = pl.BlockSpec((tile, tokens), lambda i, *_: (i, 0))
    halves = [half_side(tokens, 0), half_side(tokens, 1)]
    scratch = []
    if tail:
        sizes = [lax.axis_size("y")] * 2 * lax.axis_size("y")
        sizes += [lax.axis_size("x")] * 2 * lax.axis_size("x")
        out_specs = [pl.BlockSpec(memory_space=pl.ANY)] * len(sizes)
        out_shape = [jax.ShapeDtypeStruct((rows // n, CHUNK), jnp.bfloat16) for n in sizes]
        scratch = [pltpu.VMEM((2, tile, PADDED), jnp.bfloat16), pltpu.SemaphoreType.DMA((2, 4))]
    else:
        out_specs = [pl.BlockSpec((tile, PADDED), lambda i, *_: (i, 0))]
        out_shape = [jax.ShapeDtypeStruct((rows, PADDED), jnp.bfloat16)]
    return pl.pallas_call(
        functools.partial(weight_grads_body, tail, tile),
        grid_spec=pltpu.PrefetchScalarGridSpec(
            num_scalar_prefetch=1,
            grid=(steps,),
            in_specs=[source, source] + halves * 2,
            out_specs=out_specs,
            scratch_shapes=scratch,
        ),
        out_shape=out_shape,
        compiler_params=pltpu.CompilerParams(vmem_limit_bytes=40 << 20),
        cost_estimate=pl.CostEstimate(
            flops=4 * rows * tokens * CUTS[-1],
            bytes_accessed=4 * rows * tokens + 2 * rows * PADDED,
            transcendentals=0,
        ),
        name="weight_grads",
    )(place_of(tile), own, other, sides[0], sides[0], sides[1], sides[1])


def attention_fill_body(tail, owners, place_ref, *refs):
    own_ref, other_ref, first_ref, second_ref, other_first_ref, other_second_ref = refs[:6]
    outs = refs[6 + (len(refs) - 8) // 2 : -2]
    stage_ref, sems = refs[-2:]
    step = pl.program_id(0)
    slot = step % 2
    tile = jnp.minimum(place_ref[2], owners - 1) * pl.num_programs(0) + step

    def copy(chunk, place, row, where):
        width = CHUNK if tail else PADDED
        source = stage_ref.at[where, :, chunk * width : (chunk + 1) * width]
        spot = pl.ds(pl.multiple_of(row * INNER, INNER), INNER)
        return pltpu.make_async_copy(source, place.at[spot, :], sems.at[where, chunk])

    places = split_places(outs) if tail else None

    def wait(where):
        for chunk in range(4 if tail else 1):
            place = places[chunk % 2][0][chunk // 2] if tail else outs[0]
            copy(chunk, place, 0, where).wait()

    def put(side_ref, other_side_ref):
        product = jnp.dot(
            own_ref[...].T, side_ref[:, : CUTS[-1]], preferred_element_type=jnp.float32
        ) + jnp.dot(
            other_ref[...].T, other_side_ref[:, : CUTS[-1]], preferred_element_type=jnp.float32
        )
        stage_ref[slot, :, : CUTS[-1]] = product.astype(jnp.bfloat16)
        stage_ref[slot, :, CUTS[-1] :] = jnp.zeros((INNER, PADDED - CUTS[-1]), jnp.bfloat16)
        if not tail:
            copy(0, outs[0], step, slot).start()
            return
        spots = spots_of(0, place_ref)
        for chunk in range(4):
            which, _ = spots[chunk % 2]
            for k, pair in enumerate(places[chunk % 2]):

                @pl.when(which == k)
                def _(chunk=chunk, place=pair[chunk // 2]):
                    copy(chunk, place, step, slot).start()

    @pl.when(place_ref[2] < owners)
    def _():
        @pl.when(step >= 2)
        def _():
            wait(slot)

        @pl.when(tile < 3)
        def _():
            put(first_ref, other_first_ref)

        @pl.when(tile >= 3)
        def _():
            put(second_ref, other_second_ref)

        @pl.when(step == pl.num_programs(0) - 1)
        def _():
            wait(0)
            wait(1)


def attention_fill(tail, arrays, own, other, sides):
    tokens = own.shape[0]
    unit_rows = unit_tiles(TILE) * TILE
    owners = 4 * INNER // unit_rows
    steps = unit_rows // INNER

    def column(i, place_ref):
        return 0, jnp.minimum(place_ref[2], owners - 1) * steps + i

    halves = [half_side(tokens, 0), half_side(tokens, 1)]
    anywhere = pl.BlockSpec(memory_space=pl.ANY)
    return pl.pallas_call(
        functools.partial(attention_fill_body, tail, owners),
        grid_spec=pltpu.PrefetchScalarGridSpec(
            num_scalar_prefetch=1,
            grid=(steps,),
            in_specs=[pl.BlockSpec((tokens, INNER), column)] * 2
            + halves * 2
            + [anywhere] * len(arrays),
            out_specs=[anywhere] * len(arrays),
            scratch_shapes=[
                pltpu.VMEM((2, INNER, PADDED), jnp.bfloat16),
                pltpu.SemaphoreType.DMA((2, 4)),
            ],
        ),
        out_shape=[jax.ShapeDtypeStruct(array.shape, array.dtype) for array in arrays],
        input_output_aliases={7 + k: k for k in range(len(arrays))},
        compiler_params=pltpu.CompilerParams(vmem_limit_bytes=32 << 20),
        cost_estimate=pl.CostEstimate(
            flops=4 * unit_rows * tokens * CUTS[-1],
            bytes_accessed=4 * unit_rows * tokens + 2 * unit_rows * PADDED,
            transcendentals=0,
        ),
        name="attention_fill",
    )(place_of(TILE), own, other, sides[0], sides[0], sides[1], sides[1], *arrays)


def tied(first, second):
    return lax.optimization_barrier((first, second))


class Scatter:
    def __init__(self):
        self.waiting, self.flying, self.results = {}, {}, {}

    def push(self, name, route, kept, sends):
        self.waiting[name] = (route, kept, sends)

    def step(self, values, *names):
        arrays = {name: self.flying[name][1:] for name in names if name in self.flying}
        arrays, values = tied(arrays, values)
        moves = {}
        for name in names:
            if name in self.waiting:
                moves[name] = self.waiting.pop(name)
                continue
            route = self.flying.pop(name)[0]
            kept, moved = arrays[name]
            if not route:
                self.results[name] = kept.astype(jnp.float32) + sum(
                    part.astype(jnp.float32) for part in moved
                )
                continue
            total = total_of(kept, moved)
            total = total.reshape((lax.axis_size(route[0]), -1) + total.shape[-1:])
            sends = stage_sends(total, route[0], 0)
            moves[name] = (route, pick(total, lax.axis_index(route[0]), 0), sends)
        if moves and all(move[0] == ("z",) for move in moves.values()):
            kept = jnp.concatenate([move[1] for move in moves.values()], axis=-1)
            sends = [
                jnp.concatenate(parts, axis=-1) for parts in zip(*(m[2] for m in moves.values()))
            ]
            moves = {tuple(moves): (("z",), kept, sends)}
        arrays, values = tied({name: move[1:] for name, move in moves.items()}, values)
        for name, (route, *_) in moves.items():
            kept, sends = arrays[name]
            self.flying[name] = (route[1:], kept, stage_moves(sends, route[0]))
        return values


def total_of(value, moved):
    total = value.astype(jnp.float32)
    for part in moved:
        total = total + part.astype(jnp.float32)
    return total.astype(jnp.bfloat16)


def fetch_rows(local_rows):
    return lax.all_gather(local_rows, DEVICES, axis=0, tiled=True)


def layer_forward(stream, gathered, gain_one, gain_two, gate_low, context):
    normed, inverse_one = rms_forward(stream, gain_one)
    normed_low = normed.astype(jnp.bfloat16)
    projected = times_rows(normed_low, gathered[: 3 * INNER]).astype(jnp.bfloat16)
    queries = projected[:, :INNER]
    parts = [projected[:, INNER:]]
    if gate_low is not None:
        parts.append(jnp.broadcast_to(gate_low[:, None], (stream.shape[0], BLOCK)))
    shared = with_neighbours(jnp.concatenate(parts, axis=1))
    attended, log_total = attend_forward(queries, shared, context)
    middle = stream + times_plain(attended, gathered[3 * INNER : 4 * INNER])
    normed_two, inverse_two = rms_forward(middle, gain_two)
    normed_two_low = normed_two.astype(jnp.bfloat16)
    result, up_gelu, up_linear = ffn_forward(normed_two_low, middle, gathered)
    kept = (
        stream,
        inverse_one,
        normed_low,
        queries,
        shared,
        attended,
        log_total,
        middle,
        inverse_two,
        normed_two_low,
        up_gelu,
        up_linear,
    )
    return (result, kept)


def layer_backward(grad_out, kept, gathered, gain_one, gain_two, context, tail):
    (
        stream,
        inverse_one,
        normed_low,
        queries,
        shared,
        attended,
        log_total,
        middle,
        inverse_two,
        normed_two_low,
        up_gelu,
        up_linear,
    ) = kept
    tokens = queries.shape[0]
    branch_low = grad_out.astype(jnp.bfloat16)
    sides = jnp.concatenate([normed_two_low, branch_low], axis=0)
    sides = jnp.pad(sides, ((0, 0), (0, PADDED - sides.shape[1])))
    sides = (sides, shift(sides, "c", 1))
    grad_normed_two, own, sent = ffn_backward(
        branch_low, normed_two_low, up_gelu, up_linear, gathered
    )
    other = shift(sent, "c", 1)
    grad_middle, grad_gain_two = rms_backward(middle, inverse_two, gain_two, grad_normed_two)
    grad_middle = grad_out + grad_middle
    middle_low = grad_middle.astype(jnp.bfloat16)
    late_sides = jnp.concatenate([normed_low, middle_low], axis=0)
    late_sides = jnp.pad(late_sides, ((0, 0), (0, PADDED - late_sides.shape[1])))
    late_sides = (late_sides, shift(late_sides, "c", 1))
    grad_mixed = times_rows(middle_low, gathered[3 * INNER : 4 * INNER]).astype(jnp.bfloat16)
    grad_query, grad_shared, grad_table = attend_backward(
        queries, grad_mixed, shared, log_total, context
    )
    grad_shared, own = lax.optimization_barrier((grad_shared, own))
    moving = start_back(grad_shared, tokens)
    arrays = weight_grads(tail, own, other, sides)
    arrays, moving = lax.optimization_barrier((arrays, moving))
    grad_own = finish_back(*moving)
    grad_gate = grad_own[:, 2 * INNER :]
    grad_input_low = jnp.concatenate(
        [grad_query, grad_own[:, : 2 * INNER].astype(jnp.bfloat16)], axis=1
    )
    late = jnp.concatenate([grad_input_low, attended], axis=1)
    arrays = attention_fill(tail, arrays, late, shift(late, "c", 1), late_sides)
    if tail:
        scatter = Scatter()
        for chunk in range(4):
            route = ("y", "x", "z") if chunk % 2 == 0 else ("x", "y", "z")
            ordered = [pair[chunk // 2] for pair in split_places(arrays)[chunk % 2]]
            scatter.push(chunk, route, ordered[-1], ordered[:-1])
        grad_input_low = scatter.step(grad_input_low, 0, 1)
    else:
        arrays, grad_input_low, grad_gate = lax.optimization_barrier(
            (arrays, grad_input_low, grad_gate)
        )
        scatter = lax.psum_scatter(arrays[0], ("y", "x", "z"), scatter_dimension=0, tiled=True)
    grad_normed = times_plain(grad_input_low, gathered[: 3 * INNER])
    grad_stream, grad_gain_one = rms_backward(stream, inverse_one, gain_one, grad_normed)
    return (grad_middle + grad_stream, grad_table, grad_gate, grad_gain_one, grad_gain_two, scatter)


def per_device(
    inputs, layer3_rows, layer4_rows, norm_gains, gate_weight, rel_bias, segment_ids, cotangent
):
    seqs_here, tokens_here, width = inputs.shape
    first_pos = lax.axis_index("z") * tokens_here
    context = attention_context(segment_ids[0], first_pos, tokens_here, rel_bias)
    stream = inputs.reshape(tokens_here, width)
    gathered_three = fetch_rows(layer3_rows)
    after_three, kept_three = layer_forward(
        stream, gathered_three, norm_gains[0], norm_gains[1], None, context
    )
    gate_inverse = lax.rsqrt(jnp.mean(after_three * after_three, axis=1, keepdims=True) + epsilon)
    gate_normed = after_three * gate_inverse
    gate_logit = jnp.sum(gate_normed * gate_weight, axis=1) + gate_offset
    sigmoid_value = 1.0 / (1.0 + jnp.exp(-gate_logit))
    gate_mask = gate_scale * sigmoid_value
    gate_low = gate_mask.astype(jnp.bfloat16)
    gathered_four = fetch_rows(layer4_rows)
    after_four, kept_four = layer_forward(
        after_three, gathered_four, norm_gains[2], norm_gains[3], gate_low, context
    )
    grad_three_out, table_four, grad_gate, gain_four_one, gain_four_two, local_four = (
        layer_backward(
            cotangent.reshape(tokens_here, width),
            kept_four,
            gathered_four,
            norm_gains[2],
            norm_gains[3],
            context,
            False,
        )
    )
    grad_logit = grad_gate[:, 0] * gate_scale * sigmoid_value * (1.0 - sigmoid_value)
    grad_gate_weight = jnp.sum(grad_logit[:, None] * gate_normed, axis=0)
    gate_stream = stream_backward(after_three, gate_inverse, grad_logit[:, None] * gate_weight)
    grad_input, table_three, unused, gain_three_one, gain_three_two, scatter = layer_backward(
        grad_three_out + gate_stream,
        kept_three,
        gathered_three,
        norm_gains[0],
        norm_gains[1],
        context,
        True,
    )
    table = jnp.pad((table_three + table_four).reshape(1, -1), ((0, 0), (0, width - 6 * BUCKETS)))
    small_sums = jnp.stack(
        [gain_three_one, gain_three_two, gain_four_one, gain_four_two, grad_gate_weight, table[0]]
    )
    small = hop(small_sums, "c")
    small = scatter.step(small, 0, 1)
    small = scatter.step(small, 2, 3)
    small = hop(small, "z", 1)
    small = scatter.step(small, 0, 1)
    for bit in range(2, lax.axis_size("z")):
        if bit & (bit - 1) == 0:
            small = hop(small, "z", bit)
    small = scatter.step(small, (0, 1))
    small = scatter.step(small, 2, 3)
    small = scatter.step(small, 2, 3)
    small = hop(small, "x")
    for bit in range(1, lax.axis_size("y")):
        if bit & (bit - 1) == 0:
            small = hop(small, "y", bit)
    summed = scatter.step(small, (2, 3))
    local_three = jnp.concatenate([scatter.results[pair] for pair in ((0, 1), (2, 3))], axis=1)
    local_three, local_four = local_three[:, :width], local_four[:, :width].astype(jnp.float32)
    return (
        after_four.reshape(inputs.shape),
        gate_mask.reshape(seqs_here, tokens_here),
        grad_input.reshape(inputs.shape),
        local_three,
        local_four,
        summed[:4],
        summed[4],
        summed[5, : 6 * BUCKETS].reshape(BUCKETS, HEADS),
    )


def solution(mesh):
    outer, inner = mesh.devices.shape
    fine = Mesh(mesh.devices.reshape(outer // 4, 2, 2, inner), DEVICES)
    batch = ("y", "x", "c")
    tokens = P(batch, "z", None)
    rows = P(DEVICES, None)
    return jax.shard_map(
        per_device,
        mesh=fine,
        in_specs=(tokens, rows, rows, P(), P(), P(), P(batch, None), tokens),
        out_specs=(tokens, P(batch, "z"), tokens, rows, rows, P(), P(), P()),
        check_vma=False,
    )
```

```python
import functools

import jax
import jax.numpy as jnp
from jax import lax
from jax.experimental import pallas as pl
from jax.experimental.pallas import tpu as pltpu
from jax.sharding import Mesh
from jax.sharding import PartitionSpec as P

HEADS = 6
PAIRS = 3
BLOCK = 128
WIDE = 2 * BLOCK
INNER = 384
BUCKETS = 32
FF = 3584
REACH = 799
HALO = 896
TILE = 256
ATTENTION_TILES = 4 * INNER // TILE
OFFSETS = 5
CHUNK = 384
PADDED = 1536
FORWARD_TILE = 512
CUTS = (0, 384, 768, 1152, 1472)
DEVICES = ("y", "x", "c", "z")
epsilon = 1e-06
gate_scale = -30.0
gate_offset = -3.5
masked_out = -1e30
limits = (12, 16, 23, 32, 46, 64, 91)
both_last = (((1,), (1,)), ((), ()))


def bucket_of(relative):
    magnitude = jnp.abs(relative)
    beyond = jnp.zeros_like(magnitude)
    for bound_value in limits:
        beyond = beyond + (magnitude >= bound_value).astype(jnp.int32)
    inside = jnp.where(magnitude < 8, magnitude, 8 + beyond)
    return inside + 16 * (relative > 0).astype(jnp.int32)


def near_buckets(offset):
    if offset < 0:
        return range(1, 16)
    if offset > 0:
        return range(17, 32)
    return range(0, 32)


def tile_buckets(offset, width):
    key_at = lax.broadcasted_iota(jnp.int32, (BLOCK, width), 0)
    query_at = lax.broadcasted_iota(jnp.int32, (BLOCK, width), 1) % BLOCK
    return bucket_of(offset * BLOCK + key_at - query_at)


def bias_body(table_ref, tiles_ref):
    head = pl.program_id(0)
    tiles_ref[0, 0] = jnp.full((BLOCK, BLOCK), table_ref[15, head], jnp.float32)
    tiles_ref[0, 4] = jnp.full((BLOCK, BLOCK), table_ref[31, head], jnp.float32)
    for offset in (-1, 0, 1):
        buckets = tile_buckets(offset, BLOCK)
        tile = jnp.zeros((BLOCK, BLOCK), jnp.float32)
        for bucket in near_buckets(offset):
            tile = jnp.where(buckets == bucket, table_ref[bucket, head], tile)
        tiles_ref[0, offset + 2] = tile


def bias_tiles(rel_bias):
    return pl.pallas_call(
        bias_body,
        grid=(HEADS,),
        in_specs=[pl.BlockSpec(memory_space=pltpu.SMEM)],
        out_specs=pl.BlockSpec((1, OFFSETS, BLOCK, BLOCK), lambda h: (h, 0, 0, 0)),
        out_shape=jax.ShapeDtypeStruct((HEADS, OFFSETS, BLOCK, BLOCK), jnp.float32),
        name="bias_tiles",
    )(rel_bias)


def lane_masks():
    lane = lax.broadcasted_iota(jnp.int32, (BLOCK, BLOCK), 1)
    low = jnp.where(lane < 64, 1.0, 0.0).astype(jnp.bfloat16)
    high = jnp.where(lane < 64, 0.0, 1.0).astype(jnp.bfloat16)
    return low, high


def stacked(block, masks):
    low, high = masks
    return jnp.concatenate([block * low, block * high], axis=0)


def pair_cols(pair):
    return slice(pair * BLOCK, (pair + 1) * BLOCK)


def value_cols(pair):
    return slice(INNER + pair * BLOCK, INNER + (pair + 1) * BLOCK)


def block_rows(block):
    return pl.ds(pl.multiple_of(block * BLOCK, BLOCK), BLOCK)


def wide_rows(block):
    return pl.ds(pl.multiple_of(block * WIDE, WIDE), WIDE)


def fold(values):
    return values.reshape(values.shape[0] // 8, 8, WIDE)


def shift_tile(gated, rows, own_segment, segment_ref, shared_ref):
    same = segment_ref[rows, :] == own_segment
    inside = shared_ref[rows, 2 * INNER :].astype(jnp.float32) if gated else 0.0
    shift = jnp.where(same, inside, masked_out)
    return jnp.concatenate([shift, shift], axis=1)


def used_blocks(low_ref, high_ref):
    last = pl.num_programs(0) - 1
    return low_ref[0] // 2 * 2, (high_ref[last] + 1) // 2 * 2


def tile_offsets(block, own_block):
    return [jnp.clip(2 * block + k - own_block, -2, 2) + 2 for k in range(2)]


def bias_pair(bias_ref, pair, offsets):
    halves = [
        jnp.concatenate([bias_ref[2 * pair, at], bias_ref[2 * pair + 1, at]], axis=1)
        for at in offsets
    ]
    return jnp.concatenate(halves, axis=0)


def pick_heads(wide):
    return jnp.concatenate([wide[:64, :BLOCK], wide[64:, BLOCK:]], axis=0)


def forward_body(gated, low_ref, high_ref, *refs):
    query_ref, shared_ref, own_ref, segment_ref, bias_ref = refs[:5]
    mixed_ref, total_ref, turned_ref, score_ref, sum_ref = refs[5:]
    step = pl.program_id(0)

    @pl.when(step == 0)
    def _():
        @pl.loop(*used_blocks(low_ref, high_ref))
        def _(block):
            rows = block_rows(block)
            turned_ref[:, rows] = shared_ref[rows, INNER : 2 * INNER].T

    first, last = low_ref[step] // 2, (high_ref[step] + 1) // 2
    own_block = HALO // BLOCK + step
    own_segment = own_ref[0]
    masks = lane_masks()
    queries = [stacked(query_ref[:, pair_cols(pair)], masks) for pair in range(PAIRS)]

    def scores(block, peaks):
        rows = wide_rows(block)
        shift = shift_tile(gated, rows, own_segment, segment_ref, shared_ref)
        offsets = tile_offsets(block, own_block)
        new_peaks = []
        for pair in range(PAIRS):
            score = lax.dot_general(
                shared_ref[rows, pair_cols(pair)],
                queries[pair],
                both_last,
                preferred_element_type=jnp.float32,
            )
            score = score + bias_pair(bias_ref, pair, offsets) + shift
            score_ref[pair, block] = score
            new_peaks.append(jnp.maximum(peaks[pair], jnp.max(fold(score), axis=0)))
        return tuple(new_peaks)

    start = jnp.full((8, WIDE), -3e38, jnp.float32)
    peaks = lax.fori_loop(first, last, scores, (start,) * PAIRS)
    peaks = [jnp.max(peak, axis=0, keepdims=True) for peak in peaks]
    sum_ref[...] = jnp.zeros_like(sum_ref)

    def mix(block, totals):
        new_totals = []
        for pair in range(PAIRS):
            weight = jnp.exp(score_ref[pair, block] - peaks[pair])
            new_totals.append(totals[pair] + jnp.sum(fold(weight), axis=0))
            sum_ref[pair] += jnp.dot(
                turned_ref[pair_cols(pair), wide_rows(block)],
                weight.astype(jnp.bfloat16),
                preferred_element_type=jnp.float32,
            )
        return tuple(new_totals)

    totals = lax.fori_loop(first, last, mix, (jnp.zeros((8, WIDE), jnp.float32),) * PAIRS)
    for pair in range(PAIRS):
        row_total = jnp.sum(totals[pair], axis=0, keepdims=True)
        mixed = pick_heads(sum_ref[pair] * (1.0 / row_total))
        mixed_ref[:, pair_cols(pair)] = mixed.T.astype(jnp.bfloat16)
        total_ref[0, pair : pair + 1, :] = peaks[pair] + jnp.log(row_total)


def whole(shape):
    return pl.BlockSpec(shape, lambda i, *_: (0,) * len(shape), pipeline_mode=pl.Buffered(1))


def rows_spec(width):
    return pl.BlockSpec((BLOCK, width), lambda i, *_: (i, 0))


def attend_forward(queries, shared, context):
    lows, highs, own_rows, segment_wide, tiles = context
    tokens, (length, width) = queries.shape[0], shared.shape
    steps, key_blocks = tokens // BLOCK, length // BLOCK
    return pl.pallas_call(
        functools.partial(forward_body, width > 2 * INNER),
        grid_spec=pltpu.PrefetchScalarGridSpec(
            num_scalar_prefetch=2,
            grid=(steps,),
            in_specs=[
                rows_spec(INNER),
                whole((length, width)),
                pl.BlockSpec((1, 1, BLOCK), lambda i, *_: (i, 0, 0)),
                whole((length, BLOCK)),
                whole(tiles.shape),
            ],
            out_specs=[
                rows_spec(INNER),
                pl.BlockSpec((1, 8, WIDE), lambda i, *_: (i, 0, 0)),
            ],
            scratch_shapes=[
                pltpu.VMEM((INNER, length), jnp.bfloat16),
                pltpu.VMEM((PAIRS, key_blocks // 2, WIDE, WIDE), jnp.float32),
                pltpu.VMEM((PAIRS, BLOCK, WIDE), jnp.float32),
            ],
        ),
        out_shape=[
            jax.ShapeDtypeStruct((tokens, INNER), jnp.bfloat16),
            jax.ShapeDtypeStruct((steps, 8, WIDE), jnp.float32),
        ],
        compiler_params=pltpu.CompilerParams(vmem_limit_bytes=40 << 20),
        cost_estimate=pl.CostEstimate(
            flops=tokens * length * INNER * 4,
            bytes_accessed=8 << 20,
            transcendentals=tokens * length * 3,
        ),
        name="attend_forward",
    )(lows, highs, queries, shared, own_rows, segment_wide, tiles)


def backward_body(gated, low_ref, high_ref, *refs):
    query_ref, grad_ref, shared_ref, own_ref, segment_ref, bias_ref, total_ref = refs[:7]
    grad_query_ref, grad_shared_ref, bucket_ref = refs[7:10]
    turned_ref, prob_ref, pull_ref, sum_ref, bias_sum_ref, turn_sum_ref = refs[10:]
    step = pl.program_id(0)

    @pl.when(step == 0)
    def _():
        bias_sum_ref[...] = jnp.zeros_like(bias_sum_ref)

        @pl.loop(*used_blocks(low_ref, high_ref))
        def _(block):
            rows = block_rows(block)
            turned_ref[:, rows] = shared_ref[rows, :INNER].T
            sum_ref[rows, :] = jnp.zeros((BLOCK, sum_ref.shape[1]), jnp.float32)

    first, last = low_ref[step] // 2, (high_ref[step] + 1) // 2
    own_block = HALO // BLOCK + step
    own_segment = own_ref[0]
    masks = lane_masks()
    queries = [stacked(query_ref[:, pair_cols(pair)], masks) for pair in range(PAIRS)]
    grads = [stacked(grad_ref[:, pair_cols(pair)], masks) for pair in range(PAIRS)]
    totals = [total_ref[0, pair : pair + 1, :] for pair in range(PAIRS)]

    def weights(block, deltas):
        rows = wide_rows(block)
        shift = shift_tile(gated, rows, own_segment, segment_ref, shared_ref)
        offsets = tile_offsets(block, own_block)
        new_deltas = []
        for pair in range(PAIRS):
            cols = pair_cols(pair)
            score = lax.dot_general(
                shared_ref[rows, cols], queries[pair], both_last, preferred_element_type=jnp.float32
            )
            pull = lax.dot_general(
                shared_ref[rows, value_cols(pair)],
                grads[pair],
                both_last,
                preferred_element_type=jnp.float32,
            )
            prob = jnp.exp(score + bias_pair(bias_ref, pair, offsets) + shift - totals[pair])
            prob_ref[pair, block] = prob
            pull_ref[pair, block] = pull
            sum_ref[rows, value_cols(pair)] += jnp.dot(
                prob.astype(jnp.bfloat16), grads[pair], preferred_element_type=jnp.float32
            )
            new_deltas.append(deltas[pair] + jnp.sum(fold(prob * pull), axis=0))
        return tuple(new_deltas)

    start = jnp.zeros((8, WIDE), jnp.float32)
    deltas = lax.fori_loop(first, last, weights, (start,) * PAIRS)
    deltas = [jnp.sum(delta, axis=0, keepdims=True) for delta in deltas]
    turn_sum_ref[...] = jnp.zeros_like(turn_sum_ref)

    @pl.loop(first, last)
    def _(block):
        rows = wide_rows(block)
        offsets = tile_offsets(block, own_block)
        gate_part = jnp.zeros((WIDE, BLOCK), jnp.float32)
        for pair in range(PAIRS):
            cols = pair_cols(pair)
            grad_score = prob_ref[pair, block] * (pull_ref[pair, block] - deltas[pair])
            bias_sum_ref[pair, offsets[0]] += grad_score[:BLOCK]
            bias_sum_ref[pair, offsets[1]] += grad_score[BLOCK:]
            if gated:
                gate_part = gate_part + (grad_score[:, :BLOCK] + grad_score[:, BLOCK:])
            score_low = grad_score.astype(jnp.bfloat16)
            sum_ref[rows, cols] += jnp.dot(
                score_low, queries[pair], preferred_element_type=jnp.float32
            )
            turn_sum_ref[pair] += jnp.dot(
                turned_ref[cols, rows], score_low, preferred_element_type=jnp.float32
            )
        if gated:
            sum_ref[rows, 2 * INNER :] += gate_part

    for pair in range(PAIRS):
        grad_query_ref[:, pair_cols(pair)] = pick_heads(turn_sum_ref[pair]).T.astype(jnp.bfloat16)

    @pl.when(step == pl.num_programs(0) - 1)
    def _():
        grad_shared_ref[...] = jnp.zeros_like(grad_shared_ref)

        @pl.loop(*used_blocks(low_ref, high_ref))
        def _(block):
            rows = block_rows(block)
            both = slice(0, 2 * INNER)
            grad_shared_ref[rows, both] = sum_ref[rows, both].astype(jnp.bfloat16)
            if gated:
                gate_total = jnp.sum(sum_ref[rows, 2 * INNER :], axis=1, keepdims=True)
                grad_shared_ref[rows, 2 * INNER :] = jnp.broadcast_to(
                    gate_total, (BLOCK, BLOCK)
                ).astype(jnp.bfloat16)

        tables = {offset: tile_buckets(offset, WIDE) for offset in (-1, 0, 1)}

        @pl.loop(0, PAIRS)
        def _(pair):
            for bucket in range(BUCKETS):
                part = jnp.zeros((8, WIDE), jnp.float32)
                for offset in (-1, 0, 1):
                    if bucket in near_buckets(offset):
                        chosen = jnp.where(
                            tables[offset] == bucket, bias_sum_ref[pair, offset + 2], 0.0
                        )
                        part = part + jnp.sum(fold(chosen), axis=0)
                if bucket == 15:
                    part = part + jnp.sum(fold(bias_sum_ref[pair, 0]), axis=0)
                if bucket == 31:
                    part = part + jnp.sum(fold(bias_sum_ref[pair, 4]), axis=0)
                bucket_ref[pair, bucket : bucket + 1, :] = jnp.sum(part, axis=0, keepdims=True)


def attend_backward(queries, grad_mixed, shared, log_total, context):
    lows, highs, own_rows, segment_wide, tiles = context
    tokens, (length, width) = queries.shape[0], shared.shape
    steps, key_blocks = tokens // BLOCK, length // BLOCK
    grad_query, grad_shared, bucket_sums = pl.pallas_call(
        functools.partial(backward_body, width > 2 * INNER),
        grid_spec=pltpu.PrefetchScalarGridSpec(
            num_scalar_prefetch=2,
            grid=(steps,),
            in_specs=[
                rows_spec(INNER),
                rows_spec(INNER),
                whole((length, width)),
                pl.BlockSpec((1, 1, BLOCK), lambda i, *_: (i, 0, 0)),
                whole((length, BLOCK)),
                whole(tiles.shape),
                pl.BlockSpec((1, 8, WIDE), lambda i, *_: (i, 0, 0)),
            ],
            out_specs=[
                rows_spec(INNER),
                whole((length, width)),
                whole((PAIRS, BUCKETS, WIDE)),
            ],
            scratch_shapes=[
                pltpu.VMEM((INNER, length), jnp.bfloat16),
                pltpu.VMEM((PAIRS, key_blocks // 2, WIDE, WIDE), jnp.float32),
                pltpu.VMEM((PAIRS, key_blocks // 2, WIDE, WIDE), jnp.float32),
                pltpu.VMEM((length, width), jnp.float32),
                pltpu.VMEM((PAIRS, OFFSETS, BLOCK, WIDE), jnp.float32),
                pltpu.VMEM((PAIRS, BLOCK, WIDE), jnp.float32),
            ],
        ),
        out_shape=[
            jax.ShapeDtypeStruct((tokens, INNER), jnp.bfloat16),
            jax.ShapeDtypeStruct((length, width), jnp.bfloat16),
            jax.ShapeDtypeStruct((PAIRS, BUCKETS, WIDE), jnp.float32),
        ],
        compiler_params=pltpu.CompilerParams(vmem_limit_bytes=48 << 20),
        cost_estimate=pl.CostEstimate(
            flops=tokens * length * INNER * 10,
            bytes_accessed=12 << 20,
            transcendentals=tokens * length * 3,
        ),
        name="attend_backward",
    )(lows, highs, queries, grad_mixed, shared, own_rows, segment_wide, tiles, log_total)
    table = jnp.sum(bucket_sums.reshape(PAIRS, BUCKETS, 2, BLOCK), axis=3)
    return grad_query, grad_shared, table.transpose(1, 0, 2).reshape(BUCKETS, HEADS)


def attention_context(segment_row, first_pos, tokens, rel_bias):
    steps = tokens // BLOCK
    padded = jnp.pad(segment_row, (HALO, 0), constant_values=-1)
    padded = jnp.pad(padded, (0, HALO), constant_values=1000)
    window = lax.dynamic_slice_in_dim(padded, first_pos, tokens + 2 * HALO, 0)
    own = window[HALO : HALO + tokens].reshape(steps, 1, BLOCK)
    lows = jnp.sum(window[None, :] < own[:, 0, :1], axis=1, dtype=jnp.int32) // BLOCK
    ends = jnp.sum(window[None, :] <= own[:, 0, BLOCK - 1 :], axis=1, dtype=jnp.int32)
    highs = (ends + BLOCK - 1) // BLOCK
    segment_wide = jnp.broadcast_to(window[:, None], (window.shape[0], BLOCK))
    return lows, highs, own, segment_wide, bias_tiles(rel_bias)


def rms_forward(stream, gain_row):
    inverse = lax.rsqrt(jnp.mean(stream * stream, axis=1, keepdims=True) + epsilon)
    return (stream * inverse * gain_row, inverse)


def stream_backward(stream, inverse, scaled):
    return inverse * scaled - stream * inverse**3 * jnp.mean(scaled * stream, axis=1, keepdims=True)


def rms_backward(stream, inverse, gain_row, grad_normed):
    grad_gain = jnp.sum(grad_normed * stream * inverse, axis=0)
    return (stream_backward(stream, inverse, gain_row * grad_normed), grad_gain)


def gelu_tanh(values):
    return 0.5 * values * (1.0 + jnp.tanh(0.7978845608028654 * (values + 0.044715 * values**3)))


def times_rows(left_side, weight):
    return lax.dot_general(
        left_side, weight, (((1,), (1,)), ((), ())), preferred_element_type=jnp.float32
    )


def times_plain(left_side, weight):
    return jnp.dot(left_side, weight, preferred_element_type=jnp.float32)


def outer_sum(left_side, right_side):
    return lax.dot_general(
        left_side, right_side, (((0,), (0,)), ((), ())), preferred_element_type=jnp.float32
    )


def shift(value, axis, amount):
    count = lax.axis_size(axis)
    return lax.ppermute(value, axis, [(i, (i + amount) % count) for i in range(count)])


def slide(value, amount):
    count = lax.axis_size("z")
    pairs = [(i, i + amount) for i in range(count) if 0 <= i + amount < count]
    return lax.ppermute(value, "z", pairs)


def far_pair(near_start, near_end, distance):
    count = lax.axis_size("z")
    first_half = lax.axis_index("z") < distance
    sent = jnp.where(first_half, near_end, near_start)
    pairs = [(i, (i + distance) % count) for i in range(count)]
    got = lax.ppermute(sent, "z", pairs)
    return got


def far_split(got, distance):
    first_half = lax.axis_index("z") < distance
    none = jnp.zeros_like(got)
    return jnp.where(first_half, none, got), jnp.where(first_half, got, none)


def halo_pieces(tokens):
    pieces = []
    distance, covered = 1, 0
    while covered < HALO:
        span = min(tokens, HALO - covered)
        needed = min(span, -(-(REACH - covered) // 16) * 16)
        pieces.append((distance, span, needed))
        distance, covered = distance + 1, covered + span
    return pieces


def with_neighbours(own):
    tokens = own.shape[0]
    before, after = [], []
    for distance, span, needed in halo_pieces(tokens):
        if distance < lax.axis_size("z"):
            if 2 * distance == lax.axis_size("z"):
                left, right = far_split(
                    far_pair(own[:needed], own[tokens - needed :], distance), distance
                )
            else:
                left = slide(own[tokens - needed :], distance)
                right = slide(own[:needed], -distance)
            before.append(jnp.pad(left, ((span - needed, 0), (0, 0))))
            after.append(jnp.pad(right, ((0, span - needed), (0, 0))))
        else:
            empty = jnp.zeros((span, own.shape[1]), own.dtype)
            before.append(empty)
            after.append(empty)
    return jnp.concatenate(before[::-1] + [own] + after, axis=0)


def start_back(window, tokens):
    moved = []
    covered = 0
    for distance, span, needed in halo_pieces(tokens):
        if distance < lax.axis_size("z"):
            left_end = HALO - covered
            right_start = HALO + tokens + covered
            left = window[left_end - needed : left_end]
            right = window[right_start : right_start + needed]
            if 2 * distance == lax.axis_size("z"):
                moved.append((far_pair(left, right, distance),))
            else:
                moved.append((slide(left, -distance), slide(right, distance)))
        covered += span
    return window[HALO : HALO + tokens], moved


def finish_back(own, moved):
    tokens = own.shape[0]
    total = own.astype(jnp.float32)
    for distance, pair in enumerate(moved, 1):
        if len(pair) == 1:
            ahead, back = far_split(pair[0], distance)
        else:
            back, ahead = pair
        needed = back.shape[0]
        total = total + jnp.pad(back.astype(jnp.float32), ((tokens - needed, 0), (0, 0)))
        total = total + jnp.pad(ahead.astype(jnp.float32), ((0, tokens - needed), (0, 0)))
    return total


def hop(value, axis, bit=1):
    pairs = [(i, i ^ bit) for i in range(lax.axis_size(axis))]
    return value + lax.ppermute(value, axis, pairs)


def pick(value, index, axis):
    return lax.dynamic_index_in_dim(value, index, axis, keepdims=False)


def stage_sends(value, axis_name, axis):
    count, here = lax.axis_size(axis_name), lax.axis_index(axis_name)
    return [pick(value, (here + k) % count, axis) for k in range(1, count)]


def stage_moves(sends, axis_name):
    return [shift(sent, axis_name, k + 1) for k, sent in enumerate(sends)]


def gelu_parts(values):
    squared = values * values
    slope = jnp.tanh(0.7978845608028654 * (values + 0.044715 * values * squared))
    active = 0.5 * values * (1.0 + slope)
    inner = 0.7978845608028654 * (1.0 + 3.0 * 0.044715 * squared)
    return active, 0.5 * (1.0 + slope) + 0.5 * values * (1.0 - slope * slope) * inner


def ffn_forward_body(normed_ref, middle_ref, gelu_ref, linear_ref, down_ref, *outs):
    result_ref, up_gelu_ref, up_linear_ref = outs

    @pl.when(pl.program_id(0) == 0)
    def _():
        result_ref[...] = middle_ref[...]

    up_gelu = times_rows(normed_ref[...], gelu_ref[...])
    up_linear = times_rows(normed_ref[...], linear_ref[...])
    up_gelu_ref[...] = up_gelu
    up_linear_ref[...] = up_linear
    hidden = (gelu_tanh(up_gelu) * up_linear).astype(jnp.bfloat16)
    result_ref[...] += times_plain(hidden, down_ref[...])


def resident(shape):
    return pl.BlockSpec(shape, lambda *_: (0,) * len(shape), pipeline_mode=pl.Buffered(1))


def ffn_forward(normed, middle, gathered):
    tokens, width = normed.shape
    steps = FF // FORWARD_TILE
    first = 4 * INNER // FORWARD_TILE

    def weight(kind):
        return pl.BlockSpec((FORWARD_TILE, width), lambda i: (first + kind * steps + i, 0))

    hidden = pl.BlockSpec((tokens, FORWARD_TILE), lambda i: (0, i))
    return pl.pallas_call(
        ffn_forward_body,
        grid=(steps,),
        in_specs=[
            resident((tokens, width)),
            resident((tokens, width)),
            weight(0),
            weight(1),
            weight(2),
        ],
        out_specs=[resident((tokens, width)), hidden, hidden],
        out_shape=[
            jax.ShapeDtypeStruct((tokens, width), jnp.float32),
            jax.ShapeDtypeStruct((tokens, FF), jnp.float32),
            jax.ShapeDtypeStruct((tokens, FF), jnp.float32),
        ],
        compiler_params=pltpu.CompilerParams(vmem_limit_bytes=48 << 20),
        cost_estimate=pl.CostEstimate(
            flops=6 * tokens * FF * width,
            bytes_accessed=6 * FF * width + 8 * tokens * FF,
            transcendentals=tokens * FF,
        ),
        name="ffn_forward",
    )(normed, middle, gathered, gathered, gathered)


def ffn_backward_body(core_ref, *refs):
    branch_ref, normed_ref, up_gelu_ref, up_linear_ref, gelu_ref, linear_ref, down_ref = refs[:7]
    grad_ref, kept_ref, sent_ref, stage_ref, sems = refs[7:]
    step = pl.program_id(0)
    slot = step % 2
    mine, unit = core_ref[0], core_ref[1]
    parts = FORWARD_TILE // TILE

    def copy(kind, part, place, at, where):
        spot = pl.ds(pl.multiple_of(at * TILE, TILE), TILE)
        source = stage_ref.at[where, kind, part * TILE : (part + 1) * TILE, :]
        return pltpu.make_async_copy(source, place.at[spot, :], sems.at[where, kind, part])

    def wait(where):
        for kind in range(3):
            for part in range(parts):
                copy(kind, part, kept_ref, 0, where).wait()

    def put(kind, turned):
        stage_ref[slot, kind] = turned
        for part in range(parts):
            target = ATTENTION_TILES + kind * (FF // TILE) + step * parts + part
            own = (target // unit) % 2 == mine
            at = (target // (2 * unit)) * unit + target % unit

            @pl.when(own)
            def _(part=part, at=at):
                copy(kind, part, kept_ref, at, slot).start()

            @pl.when(jnp.logical_not(own))
            def _(part=part, at=at):
                copy(kind, part, sent_ref, at, slot).start()

    @pl.when(step == 0)
    def _():
        grad_ref[...] = jnp.zeros_like(grad_ref)

    @pl.when(step >= 2)
    def _():
        wait(slot)

    grad_hidden = times_rows(branch_ref[...], down_ref[...])
    active, slope = gelu_parts(up_gelu_ref[...])
    linear = up_linear_ref[...]
    grad_gelu = (grad_hidden * linear * slope).astype(jnp.bfloat16)
    grad_linear = (grad_hidden * active).astype(jnp.bfloat16)
    put(2, (active * linear).astype(jnp.bfloat16).T)
    put(0, grad_gelu.T)
    put(1, grad_linear.T)
    grad_ref[...] += times_plain(grad_gelu, gelu_ref[...]) + times_plain(
        grad_linear, linear_ref[...]
    )

    @pl.when(step == pl.num_programs(0) - 1)
    def _():
        wait(0)
        wait(1)


def unit_tiles(tile):
    rows = 4 * INNER + 3 * FF
    return rows // tile // (2 * lax.axis_size("y") * lax.axis_size("x"))


def ffn_backward(branch, normed, up_gelu, up_linear, gathered):
    tokens, width = normed.shape
    rows = 4 * INNER + 3 * FF
    steps = FF // FORWARD_TILE
    core = jnp.stack([lax.axis_index("c").astype(jnp.int32), jnp.int32(unit_tiles(TILE))])

    def weight(kind):
        first = 4 * INNER // FORWARD_TILE + kind * steps
        return pl.BlockSpec((FORWARD_TILE, width), lambda i, *_: (first + i, 0))

    hidden = pl.BlockSpec((tokens, FORWARD_TILE), lambda i, *_: (0, i))
    side = resident((tokens, width))
    anywhere = pl.BlockSpec(memory_space=pl.ANY)
    return pl.pallas_call(
        ffn_backward_body,
        grid_spec=pltpu.PrefetchScalarGridSpec(
            num_scalar_prefetch=1,
            grid=(steps,),
            in_specs=[side, side, hidden, hidden, weight(0), weight(1), weight(2)],
            out_specs=[side, anywhere, anywhere],
            scratch_shapes=[
                pltpu.VMEM((2, 3, FORWARD_TILE, tokens), jnp.bfloat16),
                pltpu.SemaphoreType.DMA((2, 3, FORWARD_TILE // TILE)),
            ],
        ),
        out_shape=[jax.ShapeDtypeStruct((tokens, width), jnp.float32)]
        + [jax.ShapeDtypeStruct((rows // 2, tokens), jnp.bfloat16)] * 2,
        compiler_params=pltpu.CompilerParams(vmem_limit_bytes=56 << 20),
        cost_estimate=pl.CostEstimate(
            flops=6 * tokens * FF * width,
            bytes_accessed=6 * FF * width + 14 * tokens * FF,
            transcendentals=tokens * FF,
        ),
        name="ffn_backward",
    )(core, branch, normed, up_gelu, up_linear, gathered, gathered, gathered)


def spots_of(unit_at, place_ref):
    here_y, here_x, size_y, size_x = place_ref[0], place_ref[1], place_ref[4], place_ref[5]
    row, column = unit_at // size_x, unit_at % size_x
    return (
        ((row + 2 * size_y - here_y - 1) % size_y, column),
        ((column + 2 * size_x - here_x - 1) % size_x, row),
    )


def weight_grads_body(chunks, tile, place_ref, *refs):
    own_ref, other_ref, normed_ref, branch_ref, other_normed_ref, other_branch_ref = refs[:6]
    stage_ref, sems = refs[-2:]
    step = pl.program_id(0)
    unit = place_ref[3]
    at = (step // unit * 2 + place_ref[2]) * unit + step % unit
    first, second = 4 * INNER // tile, (4 * INNER + 2 * FF) // tile
    slot = step % 2
    places = split_places(refs[6:-2], chunks)
    start, wait = place_copies(chunks, stage_ref, sems, places, tile)

    def put(product):
        stage_ref[slot, :, : CUTS[-1]] = product.astype(jnp.bfloat16)
        start(spots_of(step // unit, place_ref), unit, step % unit, step, slot)

    def both(side_ref, other_side_ref):
        return jnp.dot(
            own_ref[...], side_ref[:, : CUTS[-1]], preferred_element_type=jnp.float32
        ) + jnp.dot(
            other_ref[...], other_side_ref[:, : CUTS[-1]], preferred_element_type=jnp.float32
        )

    @pl.when(step < 2)
    def _():
        stage_ref[slot, :, CUTS[-1] :] = jnp.zeros((tile, PADDED - CUTS[-1]), jnp.bfloat16)

    @pl.when(step >= 2)
    def _():
        wait(slot)

    @pl.when(at < first)
    def _():
        put(jnp.zeros((tile, CUTS[-1]), jnp.float32))

    @pl.when((at >= first) & (at < second))
    def _():
        put(both(normed_ref, other_normed_ref))

    @pl.when(at >= second)
    def _():
        put(both(branch_ref, other_branch_ref))

    @pl.when(step == pl.num_programs(0) - 1)
    def _():
        wait(0)
        wait(1)


def split_places(refs, chunks):
    size_y, size_x, per = lax.axis_size("y"), lax.axis_size("x"), chunks // 2
    refs = list(refs)
    along_y = [refs[per * k : per * (k + 1)] for k in range(size_y)]
    refs = refs[per * size_y :]
    along_x = [refs[per * k : per * (k + 1)] for k in range(size_x)]
    return along_y, along_x, refs[per * size_x :]


def array_shapes(chunks, rows):
    shapes = [(rows // lax.axis_size("y"), CHUNK)] * (chunks // 2 * lax.axis_size("y"))
    shapes += [(rows // lax.axis_size("x"), CHUNK)] * (chunks // 2 * lax.axis_size("x"))
    if chunks < 4:
        shapes.append((rows, PADDED - chunks * CHUNK))
    return [jax.ShapeDtypeStruct(shape, jnp.bfloat16) for shape in shapes]


def place_copies(chunks, stage_ref, sems, places, tile):
    along = places[:2]
    rest = places[2]

    def copy(lane, place, row, where):
        start = lane * CHUNK
        end = PADDED if lane == chunks else start + CHUNK
        spot = pl.ds(pl.multiple_of(row * tile, tile), tile)
        return pltpu.make_async_copy(
            stage_ref.at[where, :, start:end], place.at[spot, :], sems.at[where, lane]
        )

    def start(spots, unit, inside, row, where):
        for chunk in range(chunks):
            which, position = spots[chunk % 2]
            for k, group in enumerate(along[chunk % 2]):

                @pl.when(which == k)
                def _(chunk=chunk, place=group[chunk // 2], at=position * unit + inside):
                    copy(chunk, place, at, where).start()

        for place in rest:
            copy(chunks, place, row, where).start()

    def wait(where):
        for chunk in range(chunks):
            copy(chunk, along[chunk % 2][0][chunk // 2], 0, where).wait()
        for place in rest:
            copy(chunks, place, 0, where).wait()

    return start, wait


def place_of(tile):
    return jnp.stack(
        [
            lax.axis_index("y").astype(jnp.int32),
            lax.axis_index("x").astype(jnp.int32),
            lax.axis_index("c").astype(jnp.int32),
            jnp.int32(unit_tiles(tile)),
            jnp.int32(lax.axis_size("y")),
            jnp.int32(lax.axis_size("x")),
        ]
    )


def half_side(tokens, at):
    return pl.BlockSpec(
        (tokens, PADDED), lambda i, *_: (at, 0), pipeline_mode=pl.Buffered(1)
    )


def weight_grads(chunks, own, other, sides):
    rows, tokens = own.shape
    tile = 512 if unit_tiles(256) % 2 == 0 else 256
    source = pl.BlockSpec((tile, tokens), lambda i, *_: (i, 0))
    halves = [half_side(tokens, 0), half_side(tokens, 1)]
    out_shape = array_shapes(chunks, rows)
    return pl.pallas_call(
        functools.partial(weight_grads_body, chunks, tile),
        grid_spec=pltpu.PrefetchScalarGridSpec(
            num_scalar_prefetch=1,
            grid=(rows // tile,),
            in_specs=[source, source] + halves * 2,
            out_specs=[pl.BlockSpec(memory_space=pl.ANY)] * len(out_shape),
            scratch_shapes=[
                pltpu.VMEM((2, tile, PADDED), jnp.bfloat16),
                pltpu.SemaphoreType.DMA((2, 5)),
            ],
        ),
        out_shape=out_shape,
        compiler_params=pltpu.CompilerParams(vmem_limit_bytes=40 << 20),
        cost_estimate=pl.CostEstimate(
            flops=4 * rows * tokens * CUTS[-1],
            bytes_accessed=4 * rows * tokens + 2 * rows * PADDED,
            transcendentals=0,
        ),
        name="weight_grads",
    )(place_of(tile), own, other, sides[0], sides[0], sides[1], sides[1])


def attention_fill_body(chunks, owners, place_ref, *refs):
    own_ref, other_ref, first_ref, second_ref, other_first_ref, other_second_ref = refs[:6]
    outs = refs[6 + (len(refs) - 8) // 2 : -2]
    stage_ref, sems = refs[-2:]
    step = pl.program_id(0)
    slot = step % 2
    tile = jnp.minimum(place_ref[2], owners - 1) * pl.num_programs(0) + step
    start, wait = place_copies(chunks, stage_ref, sems, split_places(outs, chunks), INNER)

    def put(side_ref, other_side_ref):
        product = jnp.dot(
            own_ref[...].T, side_ref[:, : CUTS[-1]], preferred_element_type=jnp.float32
        ) + jnp.dot(
            other_ref[...].T, other_side_ref[:, : CUTS[-1]], preferred_element_type=jnp.float32
        )
        stage_ref[slot, :, : CUTS[-1]] = product.astype(jnp.bfloat16)
        stage_ref[slot, :, CUTS[-1] :] = jnp.zeros((INNER, PADDED - CUTS[-1]), jnp.bfloat16)
        start(spots_of(0, place_ref), 0, step, step, slot)

    @pl.when(place_ref[2] < owners)
    def _():
        @pl.when(step >= 2)
        def _():
            wait(slot)

        @pl.when(tile < 3)
        def _():
            put(first_ref, other_first_ref)

        @pl.when(tile >= 3)
        def _():
            put(second_ref, other_second_ref)

        @pl.when(step == pl.num_programs(0) - 1)
        def _():
            wait(0)
            wait(1)


def attention_fill(chunks, arrays, own, other, sides):
    tokens = own.shape[0]
    unit_rows = unit_tiles(TILE) * TILE
    owners = 4 * INNER // unit_rows
    steps = unit_rows // INNER

    def column(i, place_ref):
        return 0, jnp.minimum(place_ref[2], owners - 1) * steps + i

    halves = [half_side(tokens, 0), half_side(tokens, 1)]
    anywhere = pl.BlockSpec(memory_space=pl.ANY)
    return pl.pallas_call(
        functools.partial(attention_fill_body, chunks, owners),
        grid_spec=pltpu.PrefetchScalarGridSpec(
            num_scalar_prefetch=1,
            grid=(steps,),
            in_specs=[pl.BlockSpec((tokens, INNER), column)] * 2
            + halves * 2
            + [anywhere] * len(arrays),
            out_specs=[anywhere] * len(arrays),
            scratch_shapes=[
                pltpu.VMEM((2, INNER, PADDED), jnp.bfloat16),
                pltpu.SemaphoreType.DMA((2, 5)),
            ],
        ),
        out_shape=[jax.ShapeDtypeStruct(array.shape, array.dtype) for array in arrays],
        input_output_aliases={7 + k: k for k in range(len(arrays))},
        compiler_params=pltpu.CompilerParams(vmem_limit_bytes=32 << 20),
        cost_estimate=pl.CostEstimate(
            flops=4 * unit_rows * tokens * CUTS[-1],
            bytes_accessed=4 * unit_rows * tokens + 2 * unit_rows * PADDED,
            transcendentals=0,
        ),
        name="attention_fill",
    )(place_of(TILE), own, other, sides[0], sides[0], sides[1], sides[1], *arrays)


def tied(first, second):
    return lax.optimization_barrier((first, second))


class Scatter:
    def __init__(self):
        self.waiting, self.flying, self.results = {}, {}, {}

    def push(self, name, route, kept, sends):
        self.waiting[name] = (route, kept, sends)

    def settle(self, values, *names):
        arrays, values = tied({name: self.flying[name][1:] for name in names}, values)
        moves = {}
        for name in names:
            route = self.flying.pop(name)[0]
            kept, moved = arrays[name]
            if not route:
                self.results[name] = kept.astype(jnp.float32) + sum(
                    part.astype(jnp.float32) for part in moved
                )
                continue
            total = total_of(kept, moved)
            total = total.reshape((lax.axis_size(route[0]), -1) + total.shape[-1:])
            sends = stage_sends(total, route[0], 0)
            moves[name] = (route, pick(total, lax.axis_index(route[0]), 0), sends)
        if moves and all(move[0] == ("z",) for move in moves.values()):
            kept = jnp.concatenate([move[1] for move in moves.values()], axis=-1)
            sends = [
                jnp.concatenate(parts, axis=-1) for parts in zip(*(m[2] for m in moves.values()))
            ]
            moves = {tuple(moves): (("z",), kept, sends)}
        arrays, values = tied({name: move[1:] for name, move in moves.items()}, values)
        for name, (route, *_) in moves.items():
            self.waiting[name] = (route,) + tuple(arrays[name])
        return values

    def start(self, values, *names):
        arrays, values = tied({name: self.waiting[name][1:] for name in names}, values)
        for name in names:
            route = self.waiting.pop(name)[0]
            kept, sends = arrays[name]
            self.flying[name] = (route[1:], kept, stage_moves(sends, route[0]))
        return values

    def step(self, values, *names):
        values = self.settle(values, *(name for name in names if name in self.flying))
        return self.start(values, *self.waiting) if self.waiting else values


def total_of(value, moved):
    total = value.astype(jnp.float32)
    for part in moved:
        total = total + part.astype(jnp.float32)
    return total.astype(jnp.bfloat16)


def fetch_rows(local_rows):
    return lax.all_gather(local_rows, DEVICES, axis=0, tiled=True)


def layer_forward(stream, gathered, gain_one, gain_two, gate_low, context):
    normed, inverse_one = rms_forward(stream, gain_one)
    normed_low = normed.astype(jnp.bfloat16)
    projected = times_rows(normed_low, gathered[: 3 * INNER]).astype(jnp.bfloat16)
    queries = projected[:, :INNER]
    parts = [projected[:, INNER:]]
    if gate_low is not None:
        parts.append(jnp.broadcast_to(gate_low[:, None], (stream.shape[0], BLOCK)))
    shared = with_neighbours(jnp.concatenate(parts, axis=1))
    attended, log_total = attend_forward(queries, shared, context)
    middle = stream + times_plain(attended, gathered[3 * INNER : 4 * INNER])
    normed_two, inverse_two = rms_forward(middle, gain_two)
    normed_two_low = normed_two.astype(jnp.bfloat16)
    result, up_gelu, up_linear = ffn_forward(normed_two_low, middle, gathered)
    kept = (
        stream,
        inverse_one,
        normed_low,
        queries,
        shared,
        attended,
        log_total,
        middle,
        inverse_two,
        normed_two_low,
        up_gelu,
        up_linear,
    )
    return (result, kept)


def layer_backward(grad_out, kept, gathered, gain_one, gain_two, context, before):
    (
        stream,
        inverse_one,
        normed_low,
        queries,
        shared,
        attended,
        log_total,
        middle,
        inverse_two,
        normed_two_low,
        up_gelu,
        up_linear,
    ) = kept
    tokens = queries.shape[0]
    branch_low = grad_out.astype(jnp.bfloat16)
    sides = jnp.concatenate([normed_two_low, branch_low], axis=0)
    sides = jnp.pad(sides, ((0, 0), (0, PADDED - sides.shape[1])))
    sides = (sides, shift(sides, "c", 1))
    grad_normed_two, own, sent = ffn_backward(
        branch_low, normed_two_low, up_gelu, up_linear, gathered
    )
    if before is not None:
        grad_normed_two, own, sent = before.settle((grad_normed_two, own, sent), 0, 1)
        grad_normed_two, own, sent = before.start((grad_normed_two, own, sent), 0, 1)
    other = shift(sent, "c", 1)
    grad_middle, grad_gain_two = rms_backward(middle, inverse_two, gain_two, grad_normed_two)
    grad_middle = grad_out + grad_middle
    middle_low = grad_middle.astype(jnp.bfloat16)
    late_sides = jnp.concatenate([normed_low, middle_low], axis=0)
    late_sides = jnp.pad(late_sides, ((0, 0), (0, PADDED - late_sides.shape[1])))
    late_sides = (late_sides, shift(late_sides, "c", 1))
    grad_mixed = times_rows(middle_low, gathered[3 * INNER : 4 * INNER]).astype(jnp.bfloat16)
    grad_query, grad_shared, grad_table = attend_backward(
        queries, grad_mixed, shared, log_total, context
    )
    if before is not None:
        grad_query, grad_shared = before.settle((grad_query, grad_shared), 0, 1)
    grad_shared, own = lax.optimization_barrier((grad_shared, own))
    moving = start_back(grad_shared, tokens)
    chunks = 2 if before is None else 4
    arrays = weight_grads(chunks, own, other, sides)
    arrays, moving = lax.optimization_barrier((arrays, moving))
    if before is not None:
        arrays, moving = before.start((arrays, moving), (0, 1))
    grad_own = finish_back(*moving)
    grad_gate = grad_own[:, 2 * INNER :]
    grad_input_low = jnp.concatenate(
        [grad_query, grad_own[:, : 2 * INNER].astype(jnp.bfloat16)], axis=1
    )
    late = jnp.concatenate([grad_input_low, attended], axis=1)
    arrays = attention_fill(chunks, arrays, late, shift(late, "c", 1), late_sides)
    scatter = Scatter()
    along_y, along_x, rest = split_places(arrays, chunks)
    for chunk in range(chunks):
        route = ("y", "x", "z") if chunk % 2 == 0 else ("x", "y", "z")
        ordered = [group[chunk // 2] for group in (along_y, along_x)[chunk % 2]]
        scatter.push(chunk, route, ordered[-1], ordered[:-1])
    grad_input_low, grad_gate = scatter.start((grad_input_low, grad_gate), 0, 1)
    if rest:
        grad_input_low, grad_gate, rest = lax.optimization_barrier(
            (grad_input_low, grad_gate, rest)
        )
        rest = lax.psum_scatter(rest[0], ("y", "x", "z"), scatter_dimension=0, tiled=True)
    grad_normed = times_plain(grad_input_low, gathered[: 3 * INNER])
    grad_stream, grad_gain_one = rms_backward(stream, inverse_one, gain_one, grad_normed)
    return (grad_middle + grad_stream, grad_table, grad_gate, grad_gain_one, grad_gain_two, scatter, rest)


def per_device(
    inputs, layer3_rows, layer4_rows, norm_gains, gate_weight, rel_bias, segment_ids, cotangent
):
    seqs_here, tokens_here, width = inputs.shape
    first_pos = lax.axis_index("z") * tokens_here
    context = attention_context(segment_ids[0], first_pos, tokens_here, rel_bias)
    stream = inputs.reshape(tokens_here, width)
    gathered_three = fetch_rows(layer3_rows)
    after_three, kept_three = layer_forward(
        stream, gathered_three, norm_gains[0], norm_gains[1], None, context
    )
    gate_inverse = lax.rsqrt(jnp.mean(after_three * after_three, axis=1, keepdims=True) + epsilon)
    gate_normed = after_three * gate_inverse
    gate_logit = jnp.sum(gate_normed * gate_weight, axis=1) + gate_offset
    sigmoid_value = 1.0 / (1.0 + jnp.exp(-gate_logit))
    gate_mask = gate_scale * sigmoid_value
    gate_low = gate_mask.astype(jnp.bfloat16)
    gathered_four = fetch_rows(layer4_rows)
    after_four, kept_four = layer_forward(
        after_three, gathered_four, norm_gains[2], norm_gains[3], gate_low, context
    )
    grad_three_out, table_four, grad_gate, gain_four_one, gain_four_two, before, rest = (
        layer_backward(
            cotangent.reshape(tokens_here, width),
            kept_four,
            gathered_four,
            norm_gains[2],
            norm_gains[3],
            context,
            None,
        )
    )
    grad_logit = grad_gate[:, 0] * gate_scale * sigmoid_value * (1.0 - sigmoid_value)
    grad_gate_weight = jnp.sum(grad_logit[:, None] * gate_normed, axis=0)
    gate_stream = stream_backward(after_three, gate_inverse, grad_logit[:, None] * gate_weight)
    grad_input, table_three, unused, gain_three_one, gain_three_two, scatter, _ = layer_backward(
        grad_three_out + gate_stream,
        kept_three,
        gathered_three,
        norm_gains[0],
        norm_gains[1],
        context,
        before,
    )
    table = jnp.pad((table_three + table_four).reshape(1, -1), ((0, 0), (0, width - 6 * BUCKETS)))
    small_sums = jnp.stack(
        [gain_three_one, gain_three_two, gain_four_one, gain_four_two, grad_gate_weight, table[0]]
    )
    small = hop(small_sums, "c")
    small, rest = before.settle((small, rest), (0, 1))
    small = scatter.settle(small, 0, 1)
    small = scatter.start(small, 0, 1)
    small = scatter.start(small, 2, 3)
    small = hop(small, "z", 1)
    small = scatter.step(small, 0, 1)
    for bit in range(2, lax.axis_size("z")):
        if bit & (bit - 1) == 0:
            small = hop(small, "z", bit)
    small = scatter.settle(small, (0, 1))
    small = scatter.step(small, 2, 3)
    small = scatter.step(small, 2, 3)
    small = hop(small, "x")
    for bit in range(1, lax.axis_size("y")):
        if bit & (bit - 1) == 0:
            small = hop(small, "y", bit)
    summed = scatter.settle(small, (2, 3))
    local_three = jnp.concatenate([scatter.results[pair] for pair in ((0, 1), (2, 3))], axis=1)
    local_four = jnp.concatenate([before.results[(0, 1)], rest.astype(jnp.float32)], axis=1)
    local_three, local_four = local_three[:, :width], local_four[:, :width]
    return (
        after_four.reshape(inputs.shape),
        gate_mask.reshape(seqs_here, tokens_here),
        grad_input.reshape(inputs.shape),
        local_three,
        local_four,
        summed[:4],
        summed[4],
        summed[5, : 6 * BUCKETS].reshape(BUCKETS, HEADS),
    )


def solution(mesh):
    outer, inner = mesh.devices.shape
    fine = Mesh(mesh.devices.reshape(outer // 4, 2, 2, inner), DEVICES)
    batch = ("y", "x", "c")
    tokens = P(batch, "z", None)
    rows = P(DEVICES, None)
    return jax.shard_map(
        per_device,
        mesh=fine,
        in_specs=(tokens, rows, rows, P(), P(), P(), P(batch, None), tokens),
        out_specs=(tokens, P(batch, "z"), tokens, rows, rows, P(), P(), P()),
        check_vma=False,
    )
```

```python
import functools

import jax
import jax.numpy as jnp
from jax import lax
from jax.experimental import pallas as pl
from jax.experimental.pallas import tpu as pltpu
from jax.sharding import Mesh
from jax.sharding import PartitionSpec as P

HEADS = 6
PAIRS = 3
BLOCK = 128
WIDE = 2 * BLOCK
INNER = 384
BUCKETS = 32
FF = 3584
REACH = 799
HALO = 896
TILE = 256
ATTENTION_TILES = 4 * INNER // TILE
OFFSETS = 5
PADDED = 1536
FORWARD_TILE = 512
CUTS = (0, 1472)
DEVICES = ("y", "x", "c", "z")
epsilon = 1e-06
gate_scale = -30.0
gate_offset = -3.5
masked_out = -1e30
limits = (12, 16, 23, 32, 46, 64, 91)
both_last = (((1,), (1,)), ((), ()))


def bucket_of(relative):
    magnitude = jnp.abs(relative)
    beyond = jnp.zeros_like(magnitude)
    for bound_value in limits:
        beyond = beyond + (magnitude >= bound_value).astype(jnp.int32)
    inside = jnp.where(magnitude < 8, magnitude, 8 + beyond)
    return inside + 16 * (relative > 0).astype(jnp.int32)


def near_buckets(offset):
    if offset < 0:
        return range(1, 16)
    if offset > 0:
        return range(17, 32)
    return range(0, 32)


def tile_buckets(offset, width):
    key_at = lax.broadcasted_iota(jnp.int32, (BLOCK, width), 0)
    query_at = lax.broadcasted_iota(jnp.int32, (BLOCK, width), 1) % BLOCK
    return bucket_of(offset * BLOCK + key_at - query_at)


def bias_body(table_ref, tiles_ref):
    head = pl.program_id(0)
    tiles_ref[0, 0] = jnp.full((BLOCK, BLOCK), table_ref[15, head], jnp.float32)
    tiles_ref[0, 4] = jnp.full((BLOCK, BLOCK), table_ref[31, head], jnp.float32)
    for offset in (-1, 0, 1):
        buckets = tile_buckets(offset, BLOCK)
        tile = jnp.zeros((BLOCK, BLOCK), jnp.float32)
        for bucket in near_buckets(offset):
            tile = jnp.where(buckets == bucket, table_ref[bucket, head], tile)
        tiles_ref[0, offset + 2] = tile


def bias_tiles(rel_bias):
    return pl.pallas_call(
        bias_body,
        grid=(HEADS,),
        in_specs=[pl.BlockSpec(memory_space=pltpu.SMEM)],
        out_specs=pl.BlockSpec((1, OFFSETS, BLOCK, BLOCK), lambda h: (h, 0, 0, 0)),
        out_shape=jax.ShapeDtypeStruct((HEADS, OFFSETS, BLOCK, BLOCK), jnp.float32),
        name="bias_tiles",
    )(rel_bias)


def lane_masks():
    lane = lax.broadcasted_iota(jnp.int32, (BLOCK, BLOCK), 1)
    low = jnp.where(lane < 64, 1.0, 0.0).astype(jnp.bfloat16)
    high = jnp.where(lane < 64, 0.0, 1.0).astype(jnp.bfloat16)
    return low, high


def stacked(block, masks):
    low, high = masks
    return jnp.concatenate([block * low, block * high], axis=0)


def pair_cols(pair):
    return slice(pair * BLOCK, (pair + 1) * BLOCK)


def value_cols(pair):
    return slice(INNER + pair * BLOCK, INNER + (pair + 1) * BLOCK)


def block_rows(block):
    return pl.ds(pl.multiple_of(block * BLOCK, BLOCK), BLOCK)


def wide_rows(block):
    return pl.ds(pl.multiple_of(block * WIDE, WIDE), WIDE)


def fold(values):
    return values.reshape(values.shape[0] // 8, 8, WIDE)


def shift_tile(gated, rows, own_segment, segment_ref, shared_ref):
    same = segment_ref[rows, :] == own_segment
    inside = shared_ref[rows, 2 * INNER :].astype(jnp.float32) if gated else 0.0
    shift = jnp.where(same, inside, masked_out)
    return jnp.concatenate([shift, shift], axis=1)


def used_blocks(low_ref, high_ref):
    last = pl.num_programs(0) - 1
    return low_ref[0] // 2 * 2, (high_ref[last] + 1) // 2 * 2


def tile_offsets(block, own_block):
    return [jnp.clip(2 * block + k - own_block, -2, 2) + 2 for k in range(2)]


def bias_pair(bias_ref, pair, offsets):
    halves = [
        jnp.concatenate([bias_ref[2 * pair, at], bias_ref[2 * pair + 1, at]], axis=1)
        for at in offsets
    ]
    return jnp.concatenate(halves, axis=0)


def pick_heads(wide):
    return jnp.concatenate([wide[:64, :BLOCK], wide[64:, BLOCK:]], axis=0)


def forward_body(gated, low_ref, high_ref, *refs):
    query_ref, shared_ref, own_ref, segment_ref, bias_ref = refs[:5]
    mixed_ref, total_ref, turned_ref, score_ref, sum_ref = refs[5:]
    step = pl.program_id(0)

    @pl.when(step == 0)
    def _():
        @pl.loop(*used_blocks(low_ref, high_ref))
        def _(block):
            rows = block_rows(block)
            turned_ref[:, rows] = shared_ref[rows, INNER : 2 * INNER].T

    first, last = low_ref[step] // 2, (high_ref[step] + 1) // 2
    own_block = HALO // BLOCK + step
    own_segment = own_ref[0]
    masks = lane_masks()
    queries = [stacked(query_ref[:, pair_cols(pair)], masks) for pair in range(PAIRS)]

    def scores(block, peaks):
        rows = wide_rows(block)
        shift = shift_tile(gated, rows, own_segment, segment_ref, shared_ref)
        offsets = tile_offsets(block, own_block)
        new_peaks = []
        for pair in range(PAIRS):
            score = lax.dot_general(
                shared_ref[rows, pair_cols(pair)],
                queries[pair],
                both_last,
                preferred_element_type=jnp.float32,
            )
            score = score + bias_pair(bias_ref, pair, offsets) + shift
            score_ref[pair, block] = score
            new_peaks.append(jnp.maximum(peaks[pair], jnp.max(fold(score), axis=0)))
        return tuple(new_peaks)

    start = jnp.full((8, WIDE), -3e38, jnp.float32)
    peaks = lax.fori_loop(first, last, scores, (start,) * PAIRS)
    peaks = [jnp.max(peak, axis=0, keepdims=True) for peak in peaks]
    sum_ref[...] = jnp.zeros_like(sum_ref)

    def mix(block, totals):
        new_totals = []
        for pair in range(PAIRS):
            weight = jnp.exp(score_ref[pair, block] - peaks[pair])
            new_totals.append(totals[pair] + jnp.sum(fold(weight), axis=0))
            sum_ref[pair] += jnp.dot(
                turned_ref[pair_cols(pair), wide_rows(block)],
                weight.astype(jnp.bfloat16),
                preferred_element_type=jnp.float32,
            )
        return tuple(new_totals)

    totals = lax.fori_loop(first, last, mix, (jnp.zeros((8, WIDE), jnp.float32),) * PAIRS)
    for pair in range(PAIRS):
        row_total = jnp.sum(totals[pair], axis=0, keepdims=True)
        mixed = pick_heads(sum_ref[pair] * (1.0 / row_total))
        mixed_ref[:, pair_cols(pair)] = mixed.T.astype(jnp.bfloat16)
        total_ref[0, pair : pair + 1, :] = peaks[pair] + jnp.log(row_total)


def whole(shape):
    return pl.BlockSpec(shape, lambda i, *_: (0,) * len(shape), pipeline_mode=pl.Buffered(1))


def rows_spec(width):
    return pl.BlockSpec((BLOCK, width), lambda i, *_: (i, 0))


def attend_forward(queries, shared, context):
    lows, highs, own_rows, segment_wide, tiles = context
    tokens, (length, width) = queries.shape[0], shared.shape
    steps, key_blocks = tokens // BLOCK, length // BLOCK
    return pl.pallas_call(
        functools.partial(forward_body, width > 2 * INNER),
        grid_spec=pltpu.PrefetchScalarGridSpec(
            num_scalar_prefetch=2,
            grid=(steps,),
            in_specs=[
                rows_spec(INNER),
                whole((length, width)),
                pl.BlockSpec((1, 1, BLOCK), lambda i, *_: (i, 0, 0)),
                whole((length, BLOCK)),
                whole(tiles.shape),
            ],
            out_specs=[
                rows_spec(INNER),
                pl.BlockSpec((1, 8, WIDE), lambda i, *_: (i, 0, 0)),
            ],
            scratch_shapes=[
                pltpu.VMEM((INNER, length), jnp.bfloat16),
                pltpu.VMEM((PAIRS, key_blocks // 2, WIDE, WIDE), jnp.float32),
                pltpu.VMEM((PAIRS, BLOCK, WIDE), jnp.float32),
            ],
        ),
        out_shape=[
            jax.ShapeDtypeStruct((tokens, INNER), jnp.bfloat16),
            jax.ShapeDtypeStruct((steps, 8, WIDE), jnp.float32),
        ],
        compiler_params=pltpu.CompilerParams(vmem_limit_bytes=40 << 20),
        cost_estimate=pl.CostEstimate(
            flops=tokens * length * INNER * 4,
            bytes_accessed=8 << 20,
            transcendentals=tokens * length * 3,
        ),
        name="attend_forward",
    )(lows, highs, queries, shared, own_rows, segment_wide, tiles)


def backward_body(gated, low_ref, high_ref, *refs):
    query_ref, grad_ref, shared_ref, own_ref, segment_ref, bias_ref, total_ref = refs[:7]
    grad_query_ref, grad_shared_ref, bucket_ref = refs[7:10]
    turned_ref, prob_ref, pull_ref, sum_ref, bias_sum_ref, turn_sum_ref = refs[10:]
    step = pl.program_id(0)

    @pl.when(step == 0)
    def _():
        bias_sum_ref[...] = jnp.zeros_like(bias_sum_ref)

        @pl.loop(*used_blocks(low_ref, high_ref))
        def _(block):
            rows = block_rows(block)
            turned_ref[:, rows] = shared_ref[rows, :INNER].T
            sum_ref[rows, :] = jnp.zeros((BLOCK, sum_ref.shape[1]), jnp.float32)

    first, last = low_ref[step] // 2, (high_ref[step] + 1) // 2
    own_block = HALO // BLOCK + step
    own_segment = own_ref[0]
    masks = lane_masks()
    queries = [stacked(query_ref[:, pair_cols(pair)], masks) for pair in range(PAIRS)]
    grads = [stacked(grad_ref[:, pair_cols(pair)], masks) for pair in range(PAIRS)]
    totals = [total_ref[0, pair : pair + 1, :] for pair in range(PAIRS)]

    def weights(block, deltas):
        rows = wide_rows(block)
        shift = shift_tile(gated, rows, own_segment, segment_ref, shared_ref)
        offsets = tile_offsets(block, own_block)
        new_deltas = []
        for pair in range(PAIRS):
            cols = pair_cols(pair)
            score = lax.dot_general(
                shared_ref[rows, cols], queries[pair], both_last, preferred_element_type=jnp.float32
            )
            pull = lax.dot_general(
                shared_ref[rows, value_cols(pair)],
                grads[pair],
                both_last,
                preferred_element_type=jnp.float32,
            )
            prob = jnp.exp(score + bias_pair(bias_ref, pair, offsets) + shift - totals[pair])
            prob_ref[pair, block] = prob
            pull_ref[pair, block] = pull
            sum_ref[rows, value_cols(pair)] += jnp.dot(
                prob.astype(jnp.bfloat16), grads[pair], preferred_element_type=jnp.float32
            )
            new_deltas.append(deltas[pair] + jnp.sum(fold(prob * pull), axis=0))
        return tuple(new_deltas)

    start = jnp.zeros((8, WIDE), jnp.float32)
    deltas = lax.fori_loop(first, last, weights, (start,) * PAIRS)
    deltas = [jnp.sum(delta, axis=0, keepdims=True) for delta in deltas]
    turn_sum_ref[...] = jnp.zeros_like(turn_sum_ref)

    @pl.loop(first, last)
    def _(block):
        rows = wide_rows(block)
        offsets = tile_offsets(block, own_block)
        gate_part = jnp.zeros((WIDE, BLOCK), jnp.float32)
        for pair in range(PAIRS):
            cols = pair_cols(pair)
            grad_score = prob_ref[pair, block] * (pull_ref[pair, block] - deltas[pair])
            bias_sum_ref[pair, offsets[0]] += grad_score[:BLOCK]
            bias_sum_ref[pair, offsets[1]] += grad_score[BLOCK:]
            if gated:
                gate_part = gate_part + (grad_score[:, :BLOCK] + grad_score[:, BLOCK:])
            score_low = grad_score.astype(jnp.bfloat16)
            sum_ref[rows, cols] += jnp.dot(
                score_low, queries[pair], preferred_element_type=jnp.float32
            )
            turn_sum_ref[pair] += jnp.dot(
                turned_ref[cols, rows], score_low, preferred_element_type=jnp.float32
            )
        if gated:
            sum_ref[rows, 2 * INNER :] += gate_part

    for pair in range(PAIRS):
        grad_query_ref[:, pair_cols(pair)] = pick_heads(turn_sum_ref[pair]).T.astype(jnp.bfloat16)

    @pl.when(step == pl.num_programs(0) - 1)
    def _():
        grad_shared_ref[...] = jnp.zeros_like(grad_shared_ref)

        @pl.loop(*used_blocks(low_ref, high_ref))
        def _(block):
            rows = block_rows(block)
            both = slice(0, 2 * INNER)
            grad_shared_ref[rows, both] = sum_ref[rows, both].astype(jnp.bfloat16)
            if gated:
                gate_total = jnp.sum(sum_ref[rows, 2 * INNER :], axis=1, keepdims=True)
                grad_shared_ref[rows, 2 * INNER :] = jnp.broadcast_to(
                    gate_total, (BLOCK, BLOCK)
                ).astype(jnp.bfloat16)

        tables = {offset: tile_buckets(offset, WIDE) for offset in (-1, 0, 1)}

        @pl.loop(0, PAIRS)
        def _(pair):
            for bucket in range(BUCKETS):
                part = jnp.zeros((8, WIDE), jnp.float32)
                for offset in (-1, 0, 1):
                    if bucket in near_buckets(offset):
                        chosen = jnp.where(
                            tables[offset] == bucket, bias_sum_ref[pair, offset + 2], 0.0
                        )
                        part = part + jnp.sum(fold(chosen), axis=0)
                if bucket == 15:
                    part = part + jnp.sum(fold(bias_sum_ref[pair, 0]), axis=0)
                if bucket == 31:
                    part = part + jnp.sum(fold(bias_sum_ref[pair, 4]), axis=0)
                bucket_ref[pair, bucket : bucket + 1, :] = jnp.sum(part, axis=0, keepdims=True)


def attend_backward(queries, grad_mixed, shared, log_total, context):
    lows, highs, own_rows, segment_wide, tiles = context
    tokens, (length, width) = queries.shape[0], shared.shape
    steps, key_blocks = tokens // BLOCK, length // BLOCK
    grad_query, grad_shared, bucket_sums = pl.pallas_call(
        functools.partial(backward_body, width > 2 * INNER),
        grid_spec=pltpu.PrefetchScalarGridSpec(
            num_scalar_prefetch=2,
            grid=(steps,),
            in_specs=[
                rows_spec(INNER),
                rows_spec(INNER),
                whole((length, width)),
                pl.BlockSpec((1, 1, BLOCK), lambda i, *_: (i, 0, 0)),
                whole((length, BLOCK)),
                whole(tiles.shape),
                pl.BlockSpec((1, 8, WIDE), lambda i, *_: (i, 0, 0)),
            ],
            out_specs=[
                rows_spec(INNER),
                whole((length, width)),
                whole((PAIRS, BUCKETS, WIDE)),
            ],
            scratch_shapes=[
                pltpu.VMEM((INNER, length), jnp.bfloat16),
                pltpu.VMEM((PAIRS, key_blocks // 2, WIDE, WIDE), jnp.float32),
                pltpu.VMEM((PAIRS, key_blocks // 2, WIDE, WIDE), jnp.float32),
                pltpu.VMEM((length, width), jnp.float32),
                pltpu.VMEM((PAIRS, OFFSETS, BLOCK, WIDE), jnp.float32),
                pltpu.VMEM((PAIRS, BLOCK, WIDE), jnp.float32),
            ],
        ),
        out_shape=[
            jax.ShapeDtypeStruct((tokens, INNER), jnp.bfloat16),
            jax.ShapeDtypeStruct((length, width), jnp.bfloat16),
            jax.ShapeDtypeStruct((PAIRS, BUCKETS, WIDE), jnp.float32),
        ],
        compiler_params=pltpu.CompilerParams(vmem_limit_bytes=48 << 20),
        cost_estimate=pl.CostEstimate(
            flops=tokens * length * INNER * 10,
            bytes_accessed=12 << 20,
            transcendentals=tokens * length * 3,
        ),
        name="attend_backward",
    )(lows, highs, queries, grad_mixed, shared, own_rows, segment_wide, tiles, log_total)
    table = jnp.sum(bucket_sums.reshape(PAIRS, BUCKETS, 2, BLOCK), axis=3)
    return grad_query, grad_shared, table.transpose(1, 0, 2).reshape(BUCKETS, HEADS)


def attention_context(segment_row, first_pos, tokens, rel_bias):
    steps = tokens // BLOCK
    padded = jnp.pad(segment_row, (HALO, 0), constant_values=-1)
    padded = jnp.pad(padded, (0, HALO), constant_values=1000)
    window = lax.dynamic_slice_in_dim(padded, first_pos, tokens + 2 * HALO, 0)
    own = window[HALO : HALO + tokens].reshape(steps, 1, BLOCK)
    lows = jnp.sum(window[None, :] < own[:, 0, :1], axis=1, dtype=jnp.int32) // BLOCK
    ends = jnp.sum(window[None, :] <= own[:, 0, BLOCK - 1 :], axis=1, dtype=jnp.int32)
    highs = (ends + BLOCK - 1) // BLOCK
    segment_wide = jnp.broadcast_to(window[:, None], (window.shape[0], BLOCK))
    return lows, highs, own, segment_wide, bias_tiles(rel_bias)


def rms_forward(stream, gain_row):
    inverse = lax.rsqrt(jnp.mean(stream * stream, axis=1, keepdims=True) + epsilon)
    return (stream * inverse * gain_row, inverse)


def stream_backward(stream, inverse, scaled):
    return inverse * scaled - stream * inverse**3 * jnp.mean(scaled * stream, axis=1, keepdims=True)


def rms_backward(stream, inverse, gain_row, grad_normed):
    grad_gain = jnp.sum(grad_normed * stream * inverse, axis=0)
    return (stream_backward(stream, inverse, gain_row * grad_normed), grad_gain)


def gelu_tanh(values):
    return 0.5 * values * (1.0 + jnp.tanh(0.7978845608028654 * (values + 0.044715 * values**3)))


def times_rows(left_side, weight):
    return lax.dot_general(
        left_side, weight, (((1,), (1,)), ((), ())), preferred_element_type=jnp.float32
    )


def times_plain(left_side, weight):
    return jnp.dot(left_side, weight, preferred_element_type=jnp.float32)


def outer_sum(left_side, right_side):
    return lax.dot_general(
        left_side, right_side, (((0,), (0,)), ((), ())), preferred_element_type=jnp.float32
    )


def shift(value, axis, amount):
    count = lax.axis_size(axis)
    return lax.ppermute(value, axis, [(i, (i + amount) % count) for i in range(count)])


def slide(value, amount):
    count = lax.axis_size("z")
    pairs = [(i, i + amount) for i in range(count) if 0 <= i + amount < count]
    return lax.ppermute(value, "z", pairs)


def far_pair(near_start, near_end, distance):
    count = lax.axis_size("z")
    first_half = lax.axis_index("z") < distance
    sent = jnp.where(first_half, near_end, near_start)
    pairs = [(i, (i + distance) % count) for i in range(count)]
    got = lax.ppermute(sent, "z", pairs)
    return got


def far_split(got, distance):
    first_half = lax.axis_index("z") < distance
    none = jnp.zeros_like(got)
    return jnp.where(first_half, none, got), jnp.where(first_half, got, none)


def halo_pieces(tokens):
    pieces = []
    distance, covered = 1, 0
    while covered < HALO:
        span = min(tokens, HALO - covered)
        needed = min(span, -(-(REACH - covered) // 16) * 16)
        pieces.append((distance, span, needed))
        distance, covered = distance + 1, covered + span
    return pieces


def with_neighbours(own):
    tokens = own.shape[0]
    before, after = [], []
    for distance, span, needed in halo_pieces(tokens):
        if distance < lax.axis_size("z"):
            if 2 * distance == lax.axis_size("z"):
                left, right = far_split(
                    far_pair(own[:needed], own[tokens - needed :], distance), distance
                )
            else:
                left = slide(own[tokens - needed :], distance)
                right = slide(own[:needed], -distance)
            before.append(jnp.pad(left, ((span - needed, 0), (0, 0))))
            after.append(jnp.pad(right, ((0, span - needed), (0, 0))))
        else:
            empty = jnp.zeros((span, own.shape[1]), own.dtype)
            before.append(empty)
            after.append(empty)
    return jnp.concatenate(before[::-1] + [own] + after, axis=0)


def start_back(window, tokens):
    moved = []
    covered = 0
    for distance, span, needed in halo_pieces(tokens):
        if distance < lax.axis_size("z"):
            left_end = HALO - covered
            right_start = HALO + tokens + covered
            left = window[left_end - needed : left_end]
            right = window[right_start : right_start + needed]
            if 2 * distance == lax.axis_size("z"):
                moved.append((far_pair(left, right, distance),))
            else:
                moved.append((slide(left, -distance), slide(right, distance)))
        covered += span
    return window[HALO : HALO + tokens], moved


def finish_back(own, moved):
    tokens = own.shape[0]
    total = own.astype(jnp.float32)
    for distance, pair in enumerate(moved, 1):
        if len(pair) == 1:
            ahead, back = far_split(pair[0], distance)
        else:
            back, ahead = pair
        needed = back.shape[0]
        total = total + jnp.pad(back.astype(jnp.float32), ((tokens - needed, 0), (0, 0)))
        total = total + jnp.pad(ahead.astype(jnp.float32), ((0, tokens - needed), (0, 0)))
    return total


def hop(value, axis, bit=1):
    pairs = [(i, i ^ bit) for i in range(lax.axis_size(axis))]
    return value + lax.ppermute(value, axis, pairs)


def pick(value, index, axis):
    return lax.dynamic_index_in_dim(value, index, axis, keepdims=False)


def stage_sends(value, axis_name, axis):
    count, here = lax.axis_size(axis_name), lax.axis_index(axis_name)
    return [pick(value, (here + k) % count, axis) for k in range(1, count)]


def stage_moves(sends, axis_name):
    return [shift(sent, axis_name, k + 1) for k, sent in enumerate(sends)]


def gelu_parts(values):
    squared = values * values
    slope = jnp.tanh(0.7978845608028654 * (values + 0.044715 * values * squared))
    active = 0.5 * values * (1.0 + slope)
    inner = 0.7978845608028654 * (1.0 + 3.0 * 0.044715 * squared)
    return active, 0.5 * (1.0 + slope) + 0.5 * values * (1.0 - slope * slope) * inner


def ffn_forward_body(normed_ref, middle_ref, gelu_ref, linear_ref, down_ref, *outs):
    result_ref, up_gelu_ref, up_linear_ref = outs

    @pl.when(pl.program_id(0) == 0)
    def _():
        result_ref[...] = middle_ref[...]

    up_gelu = times_rows(normed_ref[...], gelu_ref[...])
    up_linear = times_rows(normed_ref[...], linear_ref[...])
    up_gelu_ref[...] = up_gelu
    up_linear_ref[...] = up_linear
    hidden = (gelu_tanh(up_gelu) * up_linear).astype(jnp.bfloat16)
    result_ref[...] += times_plain(hidden, down_ref[...])


def resident(shape):
    return pl.BlockSpec(shape, lambda *_: (0,) * len(shape), pipeline_mode=pl.Buffered(1))


def ffn_forward(normed, middle, gathered):
    tokens, width = normed.shape
    steps = FF // FORWARD_TILE
    first = 4 * INNER // FORWARD_TILE

    def weight(kind):
        return pl.BlockSpec((FORWARD_TILE, width), lambda i: (first + kind * steps + i, 0))

    hidden = pl.BlockSpec((tokens, FORWARD_TILE), lambda i: (0, i))
    return pl.pallas_call(
        ffn_forward_body,
        grid=(steps,),
        in_specs=[
            resident((tokens, width)),
            resident((tokens, width)),
            weight(0),
            weight(1),
            weight(2),
        ],
        out_specs=[resident((tokens, width)), hidden, hidden],
        out_shape=[
            jax.ShapeDtypeStruct((tokens, width), jnp.float32),
            jax.ShapeDtypeStruct((tokens, FF), jnp.float32),
            jax.ShapeDtypeStruct((tokens, FF), jnp.float32),
        ],
        compiler_params=pltpu.CompilerParams(vmem_limit_bytes=48 << 20),
        cost_estimate=pl.CostEstimate(
            flops=6 * tokens * FF * width,
            bytes_accessed=6 * FF * width + 8 * tokens * FF,
            transcendentals=tokens * FF,
        ),
        name="ffn_forward",
    )(normed, middle, gathered, gathered, gathered)


def ffn_backward_body(core_ref, *refs):
    branch_ref, normed_ref, up_gelu_ref, up_linear_ref, gelu_ref, linear_ref, down_ref = refs[:7]
    grad_ref, kept_ref, sent_ref, stage_ref, sems = refs[7:]
    step = pl.program_id(0)
    slot = step % 2
    mine, unit = core_ref[0], core_ref[1]
    parts = FORWARD_TILE // TILE

    def copy(kind, part, place, at, where):
        spot = pl.ds(pl.multiple_of(at * TILE, TILE), TILE)
        source = stage_ref.at[where, kind, part * TILE : (part + 1) * TILE, :]
        return pltpu.make_async_copy(source, place.at[spot, :], sems.at[where, kind, part])

    def wait(where):
        for kind in range(3):
            for part in range(parts):
                copy(kind, part, kept_ref, 0, where).wait()

    def put(kind, turned):
        stage_ref[slot, kind] = turned
        for part in range(parts):
            target = ATTENTION_TILES + kind * (FF // TILE) + step * parts + part
            own = (target // unit) % 2 == mine
            at = (target // (2 * unit)) * unit + target % unit

            @pl.when(own)
            def _(part=part, at=at):
                copy(kind, part, kept_ref, at, slot).start()

            @pl.when(jnp.logical_not(own))
            def _(part=part, at=at):
                copy(kind, part, sent_ref, at, slot).start()

    @pl.when(step == 0)
    def _():
        grad_ref[...] = jnp.zeros_like(grad_ref)

    @pl.when(step >= 2)
    def _():
        wait(slot)

    grad_hidden = times_rows(branch_ref[...], down_ref[...])
    active, slope = gelu_parts(up_gelu_ref[...])
    linear = up_linear_ref[...]
    grad_gelu = (grad_hidden * linear * slope).astype(jnp.bfloat16)
    grad_linear = (grad_hidden * active).astype(jnp.bfloat16)
    put(2, (active * linear).astype(jnp.bfloat16).T)
    put(0, grad_gelu.T)
    put(1, grad_linear.T)
    grad_ref[...] += times_plain(grad_gelu, gelu_ref[...]) + times_plain(
        grad_linear, linear_ref[...]
    )

    @pl.when(step == pl.num_programs(0) - 1)
    def _():
        wait(0)
        wait(1)


def unit_tiles(tile):
    rows = 4 * INNER + 3 * FF
    return rows // tile // (2 * lax.axis_size("y") * lax.axis_size("x"))


def ffn_backward(branch, normed, up_gelu, up_linear, gathered):
    tokens, width = normed.shape
    rows = 4 * INNER + 3 * FF
    steps = FF // FORWARD_TILE
    core = jnp.stack([lax.axis_index("c").astype(jnp.int32), jnp.int32(unit_tiles(TILE))])

    def weight(kind):
        first = 4 * INNER // FORWARD_TILE + kind * steps
        return pl.BlockSpec((FORWARD_TILE, width), lambda i, *_: (first + i, 0))

    hidden = pl.BlockSpec((tokens, FORWARD_TILE), lambda i, *_: (0, i))
    side = resident((tokens, width))
    anywhere = pl.BlockSpec(memory_space=pl.ANY)
    return pl.pallas_call(
        ffn_backward_body,
        grid_spec=pltpu.PrefetchScalarGridSpec(
            num_scalar_prefetch=1,
            grid=(steps,),
            in_specs=[side, side, hidden, hidden, weight(0), weight(1), weight(2)],
            out_specs=[side, anywhere, anywhere],
            scratch_shapes=[
                pltpu.VMEM((2, 3, FORWARD_TILE, tokens), jnp.bfloat16),
                pltpu.SemaphoreType.DMA((2, 3, FORWARD_TILE // TILE)),
            ],
        ),
        out_shape=[jax.ShapeDtypeStruct((tokens, width), jnp.float32)]
        + [jax.ShapeDtypeStruct((rows // 2, tokens), jnp.bfloat16)] * 2,
        compiler_params=pltpu.CompilerParams(vmem_limit_bytes=56 << 20),
        cost_estimate=pl.CostEstimate(
            flops=6 * tokens * FF * width,
            bytes_accessed=6 * FF * width + 14 * tokens * FF,
            transcendentals=tokens * FF,
        ),
        name="ffn_backward",
    )(core, branch, normed, up_gelu, up_linear, gathered, gathered, gathered)


def spots_of(unit_at, place_ref):
    here_y, here_x, size_y, size_x = place_ref[0], place_ref[1], place_ref[4], place_ref[5]
    row, column = unit_at // size_x, unit_at % size_x
    return (
        ((row + 2 * size_y - here_y - 1) % size_y, column),
        ((column + 2 * size_x - here_x - 1) % size_x, row),
    )


def weight_grads_body(chunks, tile, place_ref, *refs):
    own_ref, other_ref, normed_ref, branch_ref, other_normed_ref, other_branch_ref = refs[:6]
    stage_ref, sems = refs[-2:]
    step = pl.program_id(0)
    unit = place_ref[3]
    at = (step // unit * 2 + place_ref[2]) * unit + step % unit
    first, second = 4 * INNER // tile, (4 * INNER + 2 * FF) // tile
    slot = step % 2
    places = split_places(refs[6:-2], chunks)
    start, wait = place_copies(chunks, stage_ref, sems, places, tile)

    def put(product):
        stage_ref[slot, :, : CUTS[-1]] = product.astype(jnp.bfloat16)
        start(spots_of(step // unit, place_ref), unit, step % unit, step, slot)

    def both(side_ref, other_side_ref):
        return jnp.dot(
            own_ref[...], side_ref[:, : CUTS[-1]], preferred_element_type=jnp.float32
        ) + jnp.dot(
            other_ref[...], other_side_ref[:, : CUTS[-1]], preferred_element_type=jnp.float32
        )

    @pl.when(step < 2)
    def _():
        stage_ref[slot, :, CUTS[-1] :] = jnp.zeros((tile, PADDED - CUTS[-1]), jnp.bfloat16)

    @pl.when(step >= 2)
    def _():
        wait(slot)

    @pl.when(at < first)
    def _():
        put(jnp.zeros((tile, CUTS[-1]), jnp.float32))

    @pl.when((at >= first) & (at < second))
    def _():
        put(both(normed_ref, other_normed_ref))

    @pl.when(at >= second)
    def _():
        put(both(branch_ref, other_branch_ref))

    @pl.when(step == pl.num_programs(0) - 1)
    def _():
        wait(0)
        wait(1)


def split_places(refs, chunks):
    size_y, size_x, per = lax.axis_size("y"), lax.axis_size("x"), chunks // 2
    refs = list(refs)
    along_y = [refs[per * k : per * (k + 1)] for k in range(size_y)]
    refs = refs[per * size_y :]
    along_x = [refs[per * k : per * (k + 1)] for k in range(size_x)]
    return along_y, along_x, refs[per * size_x :]


def array_shapes(chunks, rows):
    columns = chunk_width(chunks)
    shapes = [(rows // lax.axis_size("y"), columns)] * (chunks // 2 * lax.axis_size("y"))
    shapes += [(rows // lax.axis_size("x"), columns)] * (chunks // 2 * lax.axis_size("x"))
    if chunks < 4:
        shapes.append((rows, PADDED - chunks * columns))
    return [jax.ShapeDtypeStruct(shape, jnp.bfloat16) for shape in shapes]


def place_copies(chunks, stage_ref, sems, places, tile):
    along = places[:2]
    rest = places[2]

    def copy(lane, place, row, where):
        start = lane * chunk_width(chunks)
        end = PADDED if lane == chunks else start + chunk_width(chunks)
        spot = pl.ds(pl.multiple_of(row * tile, tile), tile)
        return pltpu.make_async_copy(
            stage_ref.at[where, :, start:end], place.at[spot, :], sems.at[where, lane]
        )

    def start(spots, unit, inside, row, where):
        for chunk in range(chunks):
            which, position = spots[chunk % 2]
            for k, group in enumerate(along[chunk % 2]):

                @pl.when(which == k)
                def _(chunk=chunk, place=group[chunk // 2], at=position * unit + inside):
                    copy(chunk, place, at, where).start()

        for place in rest:
            copy(chunks, place, row, where).start()

    def wait(where):
        for chunk in range(chunks):
            copy(chunk, along[chunk % 2][0][chunk // 2], 0, where).wait()
        for place in rest:
            copy(chunks, place, 0, where).wait()

    return start, wait


def place_of(tile):
    return jnp.stack(
        [
            lax.axis_index("y").astype(jnp.int32),
            lax.axis_index("x").astype(jnp.int32),
            lax.axis_index("c").astype(jnp.int32),
            jnp.int32(unit_tiles(tile)),
            jnp.int32(lax.axis_size("y")),
            jnp.int32(lax.axis_size("x")),
        ]
    )


def half_side(tokens, at):
    return pl.BlockSpec(
        (tokens, PADDED), lambda i, *_: (at, 0), pipeline_mode=pl.Buffered(1)
    )


def weight_grads(chunks, own, other, sides):
    rows, tokens = own.shape
    tile = 512 if unit_tiles(256) % 2 == 0 else 256
    source = pl.BlockSpec((tile, tokens), lambda i, *_: (i, 0))
    halves = [half_side(tokens, 0), half_side(tokens, 1)]
    out_shape = array_shapes(chunks, rows)
    return pl.pallas_call(
        functools.partial(weight_grads_body, chunks, tile),
        grid_spec=pltpu.PrefetchScalarGridSpec(
            num_scalar_prefetch=1,
            grid=(rows // tile,),
            in_specs=[source, source] + halves * 2,
            out_specs=[pl.BlockSpec(memory_space=pl.ANY)] * len(out_shape),
            scratch_shapes=[
                pltpu.VMEM((2, tile, PADDED), jnp.bfloat16),
                pltpu.SemaphoreType.DMA((2, 5)),
            ],
        ),
        out_shape=out_shape,
        compiler_params=pltpu.CompilerParams(vmem_limit_bytes=40 << 20),
        cost_estimate=pl.CostEstimate(
            flops=4 * rows * tokens * CUTS[-1],
            bytes_accessed=4 * rows * tokens + 2 * rows * PADDED,
            transcendentals=0,
        ),
        name="weight_grads",
    )(place_of(tile), own, other, sides[0], sides[0], sides[1], sides[1])


def attention_fill_body(chunks, owners, place_ref, *refs):
    own_ref, other_ref, first_ref, second_ref, other_first_ref, other_second_ref = refs[:6]
    outs = refs[6 + (len(refs) - 8) // 2 : -2]
    stage_ref, sems = refs[-2:]
    step = pl.program_id(0)
    slot = step % 2
    tile = jnp.minimum(place_ref[2], owners - 1) * pl.num_programs(0) + step
    start, wait = place_copies(chunks, stage_ref, sems, split_places(outs, chunks), INNER)

    def put(side_ref, other_side_ref):
        product = jnp.dot(
            own_ref[...].T, side_ref[:, : CUTS[-1]], preferred_element_type=jnp.float32
        ) + jnp.dot(
            other_ref[...].T, other_side_ref[:, : CUTS[-1]], preferred_element_type=jnp.float32
        )
        stage_ref[slot, :, : CUTS[-1]] = product.astype(jnp.bfloat16)
        stage_ref[slot, :, CUTS[-1] :] = jnp.zeros((INNER, PADDED - CUTS[-1]), jnp.bfloat16)
        start(spots_of(0, place_ref), 0, step, step, slot)

    @pl.when(place_ref[2] < owners)
    def _():
        @pl.when(step >= 2)
        def _():
            wait(slot)

        @pl.when(tile < 3)
        def _():
            put(first_ref, other_first_ref)

        @pl.when(tile >= 3)
        def _():
            put(second_ref, other_second_ref)

        @pl.when(step == pl.num_programs(0) - 1)
        def _():
            wait(0)
            wait(1)


def attention_fill(chunks, arrays, own, other, sides):
    tokens = own.shape[0]
    unit_rows = unit_tiles(TILE) * TILE
    owners = 4 * INNER // unit_rows
    steps = unit_rows // INNER

    def column(i, place_ref):
        return 0, jnp.minimum(place_ref[2], owners - 1) * steps + i

    halves = [half_side(tokens, 0), half_side(tokens, 1)]
    anywhere = pl.BlockSpec(memory_space=pl.ANY)
    return pl.pallas_call(
        functools.partial(attention_fill_body, chunks, owners),
        grid_spec=pltpu.PrefetchScalarGridSpec(
            num_scalar_prefetch=1,
            grid=(steps,),
            in_specs=[pl.BlockSpec((tokens, INNER), column)] * 2
            + halves * 2
            + [anywhere] * len(arrays),
            out_specs=[anywhere] * len(arrays),
            scratch_shapes=[
                pltpu.VMEM((2, INNER, PADDED), jnp.bfloat16),
                pltpu.SemaphoreType.DMA((2, 5)),
            ],
        ),
        out_shape=[jax.ShapeDtypeStruct(array.shape, array.dtype) for array in arrays],
        input_output_aliases={7 + k: k for k in range(len(arrays))},
        compiler_params=pltpu.CompilerParams(vmem_limit_bytes=32 << 20),
        cost_estimate=pl.CostEstimate(
            flops=4 * unit_rows * tokens * CUTS[-1],
            bytes_accessed=4 * unit_rows * tokens + 2 * unit_rows * PADDED,
            transcendentals=0,
        ),
        name="attention_fill",
    )(place_of(TILE), own, other, sides[0], sides[0], sides[1], sides[1], *arrays)


def tied(first, second):
    return lax.optimization_barrier((first, second))


def chunk_width(chunks):
    return PADDED // 4 if chunks == 4 else PADDED // 6


class Scatter:
    def __init__(self):
        self.waiting, self.flying, self.results = {}, {}, {}

    def push(self, name, route, kept, sends):
        self.waiting[name] = (route, kept, sends)

    def settle(self, values, *names):
        arrays, values = tied({name: self.flying[name][1:] for name in names}, values)
        moves = {}
        for name in names:
            route = self.flying.pop(name)[0]
            kept, moved = arrays[name]
            if not route:
                self.results[name] = kept.astype(jnp.float32) + sum(
                    part.astype(jnp.float32) for part in moved
                )
                continue
            total = total_of(kept, moved)
            total = total.reshape((lax.axis_size(route[0]), -1) + total.shape[-1:])
            sends = stage_sends(total, route[0], 0)
            moves[name] = (route, pick(total, lax.axis_index(route[0]), 0), sends)
        if moves and all(move[0] == ("z",) for move in moves.values()):
            kept = jnp.concatenate([move[1] for move in moves.values()], axis=-1)
            sends = [
                jnp.concatenate(parts, axis=-1) for parts in zip(*(m[2] for m in moves.values()))
            ]
            moves = {tuple(moves): (("z",), kept, sends)}
        arrays, values = tied({name: move[1:] for name, move in moves.items()}, values)
        for name, (route, *_) in moves.items():
            self.waiting[name] = (route,) + tuple(arrays[name])
        return values

    def start(self, values, *names):
        arrays, values = tied({name: self.waiting[name][1:] for name in names}, values)
        for name in names:
            route = self.waiting.pop(name)[0]
            kept, sends = arrays[name]
            self.flying[name] = (route[1:], kept, stage_moves(sends, route[0]))
        return values

    def step(self, values, *names):
        others = set(self.waiting)
        values = self.settle(values, *names)
        return self.start(values, *(name for name in self.waiting if name not in others))


def total_of(value, moved):
    total = value.astype(jnp.float32)
    for part in moved:
        total = total + part.astype(jnp.float32)
    return total.astype(jnp.bfloat16)


def fetch_rows(local_rows):
    return lax.all_gather(local_rows, DEVICES, axis=0, tiled=True)


def layer_forward(stream, gathered, gain_one, gain_two, gate_low, context):
    normed, inverse_one = rms_forward(stream, gain_one)
    normed_low = normed.astype(jnp.bfloat16)
    projected = times_rows(normed_low, gathered[: 3 * INNER]).astype(jnp.bfloat16)
    queries = projected[:, :INNER]
    parts = [projected[:, INNER:]]
    if gate_low is not None:
        parts.append(jnp.broadcast_to(gate_low[:, None], (stream.shape[0], BLOCK)))
    shared = with_neighbours(jnp.concatenate(parts, axis=1))
    attended, log_total = attend_forward(queries, shared, context)
    middle = stream + times_plain(attended, gathered[3 * INNER : 4 * INNER])
    normed_two, inverse_two = rms_forward(middle, gain_two)
    normed_two_low = normed_two.astype(jnp.bfloat16)
    result, up_gelu, up_linear = ffn_forward(normed_two_low, middle, gathered)
    kept = (
        stream,
        inverse_one,
        normed_low,
        queries,
        shared,
        attended,
        log_total,
        middle,
        inverse_two,
        normed_two_low,
        up_gelu,
        up_linear,
    )
    return (result, kept)


def layer_backward(grad_out, kept, gathered, gain_one, gain_two, context, before):
    (
        stream,
        inverse_one,
        normed_low,
        queries,
        shared,
        attended,
        log_total,
        middle,
        inverse_two,
        normed_two_low,
        up_gelu,
        up_linear,
    ) = kept
    tokens = queries.shape[0]
    branch_low = grad_out.astype(jnp.bfloat16)
    sides = jnp.concatenate([normed_two_low, branch_low], axis=0)
    sides = jnp.pad(sides, ((0, 0), (0, PADDED - sides.shape[1])))
    sides = (sides, shift(sides, "c", 1))
    grad_normed_two, own, sent = ffn_backward(
        branch_low, normed_two_low, up_gelu, up_linear, gathered
    )
    if before is not None:
        grad_normed_two, own, sent = before.step((grad_normed_two, own, sent), 0, 1)
    other = shift(sent, "c", 1)
    grad_middle, grad_gain_two = rms_backward(middle, inverse_two, gain_two, grad_normed_two)
    grad_middle = grad_out + grad_middle
    middle_low = grad_middle.astype(jnp.bfloat16)
    late_sides = jnp.concatenate([normed_low, middle_low], axis=0)
    late_sides = jnp.pad(late_sides, ((0, 0), (0, PADDED - late_sides.shape[1])))
    late_sides = (late_sides, shift(late_sides, "c", 1))
    grad_mixed = times_rows(middle_low, gathered[3 * INNER : 4 * INNER]).astype(jnp.bfloat16)
    grad_query, grad_shared, grad_table = attend_backward(
        queries, grad_mixed, shared, log_total, context
    )
    if before is not None:
        grad_query, grad_shared = before.settle((grad_query, grad_shared), 0, 1)
    grad_shared, own = lax.optimization_barrier((grad_shared, own))
    moving = start_back(grad_shared, tokens)
    chunks = 2 if before is None else 4
    arrays = weight_grads(chunks, own, other, sides)
    arrays, moving = lax.optimization_barrier((arrays, moving))
    if before is not None:
        arrays, moving = before.start((arrays, moving), (0, 1))
    grad_own = finish_back(*moving)
    grad_gate = grad_own[:, 2 * INNER :]
    grad_input_low = jnp.concatenate(
        [grad_query, grad_own[:, : 2 * INNER].astype(jnp.bfloat16)], axis=1
    )
    late = jnp.concatenate([grad_input_low, attended], axis=1)
    arrays = attention_fill(chunks, arrays, late, shift(late, "c", 1), late_sides)
    scatter = Scatter()
    along_y, along_x, rest = split_places(arrays, chunks)
    for chunk in range(chunks):
        route = ("y", "x", "z") if chunk % 2 == 0 else ("x", "y", "z")
        ordered = [group[chunk // 2] for group in (along_y, along_x)[chunk % 2]]
        scatter.push(chunk, route, ordered[-1], ordered[:-1])
    grad_input_low, grad_gate = scatter.start((grad_input_low, grad_gate), 0, 1)
    if rest:
        grad_input_low, grad_gate, rest = lax.optimization_barrier(
            (grad_input_low, grad_gate, rest)
        )
        rest = lax.psum_scatter(rest[0], ("y", "x", "z"), scatter_dimension=0, tiled=True)
    grad_normed = times_plain(grad_input_low, gathered[: 3 * INNER])
    grad_stream, grad_gain_one = rms_backward(stream, inverse_one, gain_one, grad_normed)
    return (grad_middle + grad_stream, grad_table, grad_gate, grad_gain_one, grad_gain_two, scatter, rest)


def per_device(
    inputs, layer3_rows, layer4_rows, norm_gains, gate_weight, rel_bias, segment_ids, cotangent
):
    seqs_here, tokens_here, width = inputs.shape
    first_pos = lax.axis_index("z") * tokens_here
    context = attention_context(segment_ids[0], first_pos, tokens_here, rel_bias)
    stream = inputs.reshape(tokens_here, width)
    gathered_three = fetch_rows(layer3_rows)
    after_three, kept_three = layer_forward(
        stream, gathered_three, norm_gains[0], norm_gains[1], None, context
    )
    gate_inverse = lax.rsqrt(jnp.mean(after_three * after_three, axis=1, keepdims=True) + epsilon)
    gate_normed = after_three * gate_inverse
    gate_logit = jnp.sum(gate_normed * gate_weight, axis=1) + gate_offset
    sigmoid_value = 1.0 / (1.0 + jnp.exp(-gate_logit))
    gate_mask = gate_scale * sigmoid_value
    gate_low = gate_mask.astype(jnp.bfloat16)
    gathered_four = fetch_rows(layer4_rows)
    after_four, kept_four = layer_forward(
        after_three, gathered_four, norm_gains[2], norm_gains[3], gate_low, context
    )
    grad_three_out, table_four, grad_gate, gain_four_one, gain_four_two, before, rest = (
        layer_backward(
            cotangent.reshape(tokens_here, width),
            kept_four,
            gathered_four,
            norm_gains[2],
            norm_gains[3],
            context,
            None,
        )
    )
    grad_logit = grad_gate[:, 0] * gate_scale * sigmoid_value * (1.0 - sigmoid_value)
    grad_gate_weight = jnp.sum(grad_logit[:, None] * gate_normed, axis=0)
    gate_stream = stream_backward(after_three, gate_inverse, grad_logit[:, None] * gate_weight)
    grad_input, table_three, unused, gain_three_one, gain_three_two, scatter, _ = layer_backward(
        grad_three_out + gate_stream,
        kept_three,
        gathered_three,
        norm_gains[0],
        norm_gains[1],
        context,
        before,
    )
    table = jnp.pad((table_three + table_four).reshape(1, -1), ((0, 0), (0, width - 6 * BUCKETS)))
    small_sums = jnp.stack(
        [gain_three_one, gain_three_two, gain_four_one, gain_four_two, grad_gate_weight, table[0]]
    )
    small = hop(small_sums, "c")
    small = before.settle(small, (0, 1))
    small = scatter.step(small, 0, 1)
    small = scatter.start(small, 2, 3)
    small = scatter.step(small, 0, 1)
    small, rest = scatter.settle((small, rest), (0, 1))
    for bit in range(1, lax.axis_size("z")):
        if bit & (bit - 1) == 0:
            small = hop(small, "z", bit)
    small = scatter.step(small, 2, 3)
    small = scatter.step(small, 2, 3)
    small = hop(small, "x")
    for bit in range(1, lax.axis_size("y")):
        if bit & (bit - 1) == 0:
            small = hop(small, "y", bit)
    summed = scatter.settle(small, (2, 3))
    local_three = jnp.concatenate([scatter.results[pair] for pair in ((0, 1), (2, 3))], axis=1)
    local_four = jnp.concatenate([before.results[(0, 1)], rest.astype(jnp.float32)], axis=1)
    local_three, local_four = local_three[:, :width], local_four[:, :width]
    return (
        after_four.reshape(inputs.shape),
        gate_mask.reshape(seqs_here, tokens_here),
        grad_input.reshape(inputs.shape),
        local_three,
        local_four,
        summed[:4],
        summed[4],
        summed[5, : 6 * BUCKETS].reshape(BUCKETS, HEADS),
    )


def solution(mesh):
    outer, inner = mesh.devices.shape
    fine = Mesh(mesh.devices.reshape(outer // 4, 2, 2, inner), DEVICES)
    batch = ("y", "x", "c")
    tokens = P(batch, "z", None)
    rows = P(DEVICES, None)
    return jax.shard_map(
        per_device,
        mesh=fine,
        in_specs=(tokens, rows, rows, P(), P(), P(), P(batch, None), tokens),
        out_specs=(tokens, P(batch, "z"), tokens, rows, rows, P(), P(), P()),
        check_vma=False,
    )
```

```python
import functools

import jax
import jax.numpy as jnp
from jax import lax
from jax.experimental import pallas as pl
from jax.experimental.pallas import tpu as pltpu
from jax.sharding import Mesh
from jax.sharding import PartitionSpec as P

HEADS = 6
PAIRS = 3
BLOCK = 128
WIDE = 2 * BLOCK
INNER = 384
BUCKETS = 32
FF = 3584
REACH = 799
HALO = 896
TILE = 256
ATTENTION_TILES = 4 * INNER // TILE
OFFSETS = 5
PADDED = 1536
FORWARD_TILE = 512
CUTS = (0, 1472)
DEVICES = ("y", "x", "c", "z")
epsilon = 1e-06
gate_scale = -30.0
gate_offset = -3.5
masked_out = -1e30
limits = (12, 16, 23, 32, 46, 64, 91)
both_last = (((1,), (1,)), ((), ()))


def bucket_of(relative):
    magnitude = jnp.abs(relative)
    beyond = jnp.zeros_like(magnitude)
    for bound_value in limits:
        beyond = beyond + (magnitude >= bound_value).astype(jnp.int32)
    inside = jnp.where(magnitude < 8, magnitude, 8 + beyond)
    return inside + 16 * (relative > 0).astype(jnp.int32)


def near_buckets(offset):
    if offset < 0:
        return range(1, 16)
    if offset > 0:
        return range(17, 32)
    return range(0, 32)


def tile_buckets(offset, width):
    key_at = lax.broadcasted_iota(jnp.int32, (BLOCK, width), 0)
    query_at = lax.broadcasted_iota(jnp.int32, (BLOCK, width), 1) % BLOCK
    return bucket_of(offset * BLOCK + key_at - query_at)


def bias_body(table_ref, tiles_ref):
    head = pl.program_id(0)
    tiles_ref[0, 0] = jnp.full((BLOCK, BLOCK), table_ref[15, head], jnp.float32)
    tiles_ref[0, 4] = jnp.full((BLOCK, BLOCK), table_ref[31, head], jnp.float32)
    for offset in (-1, 0, 1):
        buckets = tile_buckets(offset, BLOCK)
        tile = jnp.zeros((BLOCK, BLOCK), jnp.float32)
        for bucket in near_buckets(offset):
            tile = jnp.where(buckets == bucket, table_ref[bucket, head], tile)
        tiles_ref[0, offset + 2] = tile


def bias_tiles(rel_bias):
    return pl.pallas_call(
        bias_body,
        grid=(HEADS,),
        in_specs=[pl.BlockSpec(memory_space=pltpu.SMEM)],
        out_specs=pl.BlockSpec((1, OFFSETS, BLOCK, BLOCK), lambda h: (h, 0, 0, 0)),
        out_shape=jax.ShapeDtypeStruct((HEADS, OFFSETS, BLOCK, BLOCK), jnp.float32),
        name="bias_tiles",
    )(rel_bias)


def lane_masks():
    lane = lax.broadcasted_iota(jnp.int32, (BLOCK, BLOCK), 1)
    low = jnp.where(lane < 64, 1.0, 0.0).astype(jnp.bfloat16)
    high = jnp.where(lane < 64, 0.0, 1.0).astype(jnp.bfloat16)
    return low, high


def stacked(block, masks):
    low, high = masks
    return jnp.concatenate([block * low, block * high], axis=0)


def pair_cols(pair):
    return slice(pair * BLOCK, (pair + 1) * BLOCK)


def value_cols(pair):
    return slice(INNER + pair * BLOCK, INNER + (pair + 1) * BLOCK)


def block_rows(block):
    return pl.ds(pl.multiple_of(block * BLOCK, BLOCK), BLOCK)


def wide_rows(block):
    return pl.ds(pl.multiple_of(block * WIDE, WIDE), WIDE)


def fold(values):
    return values.reshape(values.shape[0] // 8, 8, WIDE)


def shift_tile(gated, rows, own_segment, segment_ref, shared_ref):
    same = segment_ref[rows, :] == own_segment
    inside = shared_ref[rows, 2 * INNER :].astype(jnp.float32) if gated else 0.0
    shift = jnp.where(same, inside, masked_out)
    return jnp.concatenate([shift, shift], axis=1)


def used_blocks(low_ref, high_ref):
    last = pl.num_programs(0) - 1
    return low_ref[0] // 2 * 2, (high_ref[last] + 1) // 2 * 2


def tile_offsets(block, own_block):
    return [jnp.clip(2 * block + k - own_block, -2, 2) + 2 for k in range(2)]


def bias_pair(bias_ref, pair, offsets):
    halves = [
        jnp.concatenate([bias_ref[2 * pair, at], bias_ref[2 * pair + 1, at]], axis=1)
        for at in offsets
    ]
    return jnp.concatenate(halves, axis=0)


def pick_heads(wide):
    return jnp.concatenate([wide[:64, :BLOCK], wide[64:, BLOCK:]], axis=0)


def forward_body(gated, low_ref, high_ref, *refs):
    query_ref, shared_ref, own_ref, segment_ref, bias_ref = refs[:5]
    mixed_ref, total_ref, turned_ref, score_ref, sum_ref = refs[5:]
    step = pl.program_id(0)

    @pl.when(step == 0)
    def _():
        @pl.loop(*used_blocks(low_ref, high_ref))
        def _(block):
            rows = block_rows(block)
            turned_ref[:, rows] = shared_ref[rows, INNER : 2 * INNER].T

    first, last = low_ref[step] // 2, (high_ref[step] + 1) // 2
    own_block = HALO // BLOCK + step
    own_segment = own_ref[0]
    masks = lane_masks()
    queries = [stacked(query_ref[:, pair_cols(pair)], masks) for pair in range(PAIRS)]

    def scores(block, peaks):
        rows = wide_rows(block)
        shift = shift_tile(gated, rows, own_segment, segment_ref, shared_ref)
        offsets = tile_offsets(block, own_block)
        new_peaks = []
        for pair in range(PAIRS):
            score = lax.dot_general(
                shared_ref[rows, pair_cols(pair)],
                queries[pair],
                both_last,
                preferred_element_type=jnp.float32,
            )
            score = score + bias_pair(bias_ref, pair, offsets) + shift
            score_ref[pair, block] = score
            new_peaks.append(jnp.maximum(peaks[pair], jnp.max(fold(score), axis=0)))
        return tuple(new_peaks)

    start = jnp.full((8, WIDE), -3e38, jnp.float32)
    peaks = lax.fori_loop(first, last, scores, (start,) * PAIRS)
    peaks = [jnp.max(peak, axis=0, keepdims=True) for peak in peaks]
    sum_ref[...] = jnp.zeros_like(sum_ref)

    def mix(block, totals):
        new_totals = []
        for pair in range(PAIRS):
            weight = jnp.exp(score_ref[pair, block] - peaks[pair])
            new_totals.append(totals[pair] + jnp.sum(fold(weight), axis=0))
            sum_ref[pair] += jnp.dot(
                turned_ref[pair_cols(pair), wide_rows(block)],
                weight.astype(jnp.bfloat16),
                preferred_element_type=jnp.float32,
            )
        return tuple(new_totals)

    totals = lax.fori_loop(first, last, mix, (jnp.zeros((8, WIDE), jnp.float32),) * PAIRS)
    for pair in range(PAIRS):
        row_total = jnp.sum(totals[pair], axis=0, keepdims=True)
        mixed = pick_heads(sum_ref[pair] * (1.0 / row_total))
        mixed_ref[:, pair_cols(pair)] = mixed.T.astype(jnp.bfloat16)
        total_ref[0, pair : pair + 1, :] = peaks[pair] + jnp.log(row_total)


def whole(shape):
    return pl.BlockSpec(shape, lambda i, *_: (0,) * len(shape), pipeline_mode=pl.Buffered(1))


def rows_spec(width):
    return pl.BlockSpec((BLOCK, width), lambda i, *_: (i, 0))


def attend_forward(queries, shared, context):
    lows, highs, own_rows, segment_wide, tiles = context
    tokens, (length, width) = queries.shape[0], shared.shape
    steps, key_blocks = tokens // BLOCK, length // BLOCK
    return pl.pallas_call(
        functools.partial(forward_body, width > 2 * INNER),
        grid_spec=pltpu.PrefetchScalarGridSpec(
            num_scalar_prefetch=2,
            grid=(steps,),
            in_specs=[
                rows_spec(INNER),
                whole((length, width)),
                pl.BlockSpec((1, 1, BLOCK), lambda i, *_: (i, 0, 0)),
                whole((length, BLOCK)),
                whole(tiles.shape),
            ],
            out_specs=[
                rows_spec(INNER),
                pl.BlockSpec((1, 8, WIDE), lambda i, *_: (i, 0, 0)),
            ],
            scratch_shapes=[
                pltpu.VMEM((INNER, length), jnp.bfloat16),
                pltpu.VMEM((PAIRS, key_blocks // 2, WIDE, WIDE), jnp.float32),
                pltpu.VMEM((PAIRS, BLOCK, WIDE), jnp.float32),
            ],
        ),
        out_shape=[
            jax.ShapeDtypeStruct((tokens, INNER), jnp.bfloat16),
            jax.ShapeDtypeStruct((steps, 8, WIDE), jnp.float32),
        ],
        compiler_params=pltpu.CompilerParams(vmem_limit_bytes=40 << 20),
        cost_estimate=pl.CostEstimate(
            flops=tokens * length * INNER * 4,
            bytes_accessed=8 << 20,
            transcendentals=tokens * length * 3,
        ),
        name="attend_forward",
    )(lows, highs, queries, shared, own_rows, segment_wide, tiles)


def backward_body(gated, low_ref, high_ref, *refs):
    query_ref, grad_ref, shared_ref, own_ref, segment_ref, bias_ref, total_ref = refs[:7]
    grad_query_ref, grad_shared_ref, bucket_ref = refs[7:10]
    turned_ref, prob_ref, pull_ref, sum_ref, bias_sum_ref, turn_sum_ref = refs[10:]
    step = pl.program_id(0)

    @pl.when(step == 0)
    def _():
        bias_sum_ref[...] = jnp.zeros_like(bias_sum_ref)

        @pl.loop(*used_blocks(low_ref, high_ref))
        def _(block):
            rows = block_rows(block)
            turned_ref[:, rows] = shared_ref[rows, :INNER].T
            sum_ref[rows, :] = jnp.zeros((BLOCK, sum_ref.shape[1]), jnp.float32)

    first, last = low_ref[step] // 2, (high_ref[step] + 1) // 2
    own_block = HALO // BLOCK + step
    own_segment = own_ref[0]
    masks = lane_masks()
    queries = [stacked(query_ref[:, pair_cols(pair)], masks) for pair in range(PAIRS)]
    grads = [stacked(grad_ref[:, pair_cols(pair)], masks) for pair in range(PAIRS)]
    totals = [total_ref[0, pair : pair + 1, :] for pair in range(PAIRS)]

    def weights(block, deltas):
        rows = wide_rows(block)
        shift = shift_tile(gated, rows, own_segment, segment_ref, shared_ref)
        offsets = tile_offsets(block, own_block)
        new_deltas = []
        for pair in range(PAIRS):
            cols = pair_cols(pair)
            score = lax.dot_general(
                shared_ref[rows, cols], queries[pair], both_last, preferred_element_type=jnp.float32
            )
            pull = lax.dot_general(
                shared_ref[rows, value_cols(pair)],
                grads[pair],
                both_last,
                preferred_element_type=jnp.float32,
            )
            prob = jnp.exp(score + bias_pair(bias_ref, pair, offsets) + shift - totals[pair])
            prob_ref[pair, block] = prob
            pull_ref[pair, block] = pull
            sum_ref[rows, value_cols(pair)] += jnp.dot(
                prob.astype(jnp.bfloat16), grads[pair], preferred_element_type=jnp.float32
            )
            new_deltas.append(deltas[pair] + jnp.sum(fold(prob * pull), axis=0))
        return tuple(new_deltas)

    start = jnp.zeros((8, WIDE), jnp.float32)
    deltas = lax.fori_loop(first, last, weights, (start,) * PAIRS)
    deltas = [jnp.sum(delta, axis=0, keepdims=True) for delta in deltas]
    turn_sum_ref[...] = jnp.zeros_like(turn_sum_ref)

    @pl.loop(first, last)
    def _(block):
        rows = wide_rows(block)
        offsets = tile_offsets(block, own_block)
        gate_part = jnp.zeros((WIDE, BLOCK), jnp.float32)
        for pair in range(PAIRS):
            cols = pair_cols(pair)
            grad_score = prob_ref[pair, block] * (pull_ref[pair, block] - deltas[pair])
            bias_sum_ref[pair, offsets[0]] += grad_score[:BLOCK]
            bias_sum_ref[pair, offsets[1]] += grad_score[BLOCK:]
            if gated:
                gate_part = gate_part + (grad_score[:, :BLOCK] + grad_score[:, BLOCK:])
            score_low = grad_score.astype(jnp.bfloat16)
            sum_ref[rows, cols] += jnp.dot(
                score_low, queries[pair], preferred_element_type=jnp.float32
            )
            turn_sum_ref[pair] += jnp.dot(
                turned_ref[cols, rows], score_low, preferred_element_type=jnp.float32
            )
        if gated:
            sum_ref[rows, 2 * INNER :] += gate_part

    for pair in range(PAIRS):
        grad_query_ref[:, pair_cols(pair)] = pick_heads(turn_sum_ref[pair]).T.astype(jnp.bfloat16)

    @pl.when(step == pl.num_programs(0) - 1)
    def _():
        grad_shared_ref[...] = jnp.zeros_like(grad_shared_ref)

        @pl.loop(*used_blocks(low_ref, high_ref))
        def _(block):
            rows = block_rows(block)
            both = slice(0, 2 * INNER)
            grad_shared_ref[rows, both] = sum_ref[rows, both].astype(jnp.bfloat16)
            if gated:
                gate_total = jnp.sum(sum_ref[rows, 2 * INNER :], axis=1, keepdims=True)
                grad_shared_ref[rows, 2 * INNER :] = jnp.broadcast_to(
                    gate_total, (BLOCK, BLOCK)
                ).astype(jnp.bfloat16)

        tables = {offset: tile_buckets(offset, WIDE) for offset in (-1, 0, 1)}

        @pl.loop(0, PAIRS)
        def _(pair):
            for bucket in range(BUCKETS):
                part = jnp.zeros((8, WIDE), jnp.float32)
                for offset in (-1, 0, 1):
                    if bucket in near_buckets(offset):
                        chosen = jnp.where(
                            tables[offset] == bucket, bias_sum_ref[pair, offset + 2], 0.0
                        )
                        part = part + jnp.sum(fold(chosen), axis=0)
                if bucket == 15:
                    part = part + jnp.sum(fold(bias_sum_ref[pair, 0]), axis=0)
                if bucket == 31:
                    part = part + jnp.sum(fold(bias_sum_ref[pair, 4]), axis=0)
                bucket_ref[pair, bucket : bucket + 1, :] = jnp.sum(part, axis=0, keepdims=True)


def attend_backward(queries, grad_mixed, shared, log_total, context):
    lows, highs, own_rows, segment_wide, tiles = context
    tokens, (length, width) = queries.shape[0], shared.shape
    steps, key_blocks = tokens // BLOCK, length // BLOCK
    grad_query, grad_shared, bucket_sums = pl.pallas_call(
        functools.partial(backward_body, width > 2 * INNER),
        grid_spec=pltpu.PrefetchScalarGridSpec(
            num_scalar_prefetch=2,
            grid=(steps,),
            in_specs=[
                rows_spec(INNER),
                rows_spec(INNER),
                whole((length, width)),
                pl.BlockSpec((1, 1, BLOCK), lambda i, *_: (i, 0, 0)),
                whole((length, BLOCK)),
                whole(tiles.shape),
                pl.BlockSpec((1, 8, WIDE), lambda i, *_: (i, 0, 0)),
            ],
            out_specs=[
                rows_spec(INNER),
                whole((length, width)),
                whole((PAIRS, BUCKETS, WIDE)),
            ],
            scratch_shapes=[
                pltpu.VMEM((INNER, length), jnp.bfloat16),
                pltpu.VMEM((PAIRS, key_blocks // 2, WIDE, WIDE), jnp.float32),
                pltpu.VMEM((PAIRS, key_blocks // 2, WIDE, WIDE), jnp.float32),
                pltpu.VMEM((length, width), jnp.float32),
                pltpu.VMEM((PAIRS, OFFSETS, BLOCK, WIDE), jnp.float32),
                pltpu.VMEM((PAIRS, BLOCK, WIDE), jnp.float32),
            ],
        ),
        out_shape=[
            jax.ShapeDtypeStruct((tokens, INNER), jnp.bfloat16),
            jax.ShapeDtypeStruct((length, width), jnp.bfloat16),
            jax.ShapeDtypeStruct((PAIRS, BUCKETS, WIDE), jnp.float32),
        ],
        compiler_params=pltpu.CompilerParams(vmem_limit_bytes=48 << 20),
        cost_estimate=pl.CostEstimate(
            flops=tokens * length * INNER * 10,
            bytes_accessed=12 << 20,
            transcendentals=tokens * length * 3,
        ),
        name="attend_backward",
    )(lows, highs, queries, grad_mixed, shared, own_rows, segment_wide, tiles, log_total)
    table = jnp.sum(bucket_sums.reshape(PAIRS, BUCKETS, 2, BLOCK), axis=3)
    return grad_query, grad_shared, table.transpose(1, 0, 2).reshape(BUCKETS, HEADS)


def attention_context(segment_row, first_pos, tokens, rel_bias):
    steps = tokens // BLOCK
    padded = jnp.pad(segment_row, (HALO, 0), constant_values=-1)
    padded = jnp.pad(padded, (0, HALO), constant_values=1000)
    window = lax.dynamic_slice_in_dim(padded, first_pos, tokens + 2 * HALO, 0)
    own = window[HALO : HALO + tokens].reshape(steps, 1, BLOCK)
    lows = jnp.sum(window[None, :] < own[:, 0, :1], axis=1, dtype=jnp.int32) // BLOCK
    ends = jnp.sum(window[None, :] <= own[:, 0, BLOCK - 1 :], axis=1, dtype=jnp.int32)
    highs = (ends + BLOCK - 1) // BLOCK
    segment_wide = jnp.broadcast_to(window[:, None], (window.shape[0], BLOCK))
    return lows, highs, own, segment_wide, bias_tiles(rel_bias)


def rms_forward(stream, gain_row):
    inverse = lax.rsqrt(jnp.mean(stream * stream, axis=1, keepdims=True) + epsilon)
    return (stream * inverse * gain_row, inverse)


def stream_backward(stream, inverse, scaled):
    return inverse * scaled - stream * inverse**3 * jnp.mean(scaled * stream, axis=1, keepdims=True)


def rms_backward(stream, inverse, gain_row, grad_normed):
    grad_gain = jnp.sum(grad_normed * stream * inverse, axis=0)
    return (stream_backward(stream, inverse, gain_row * grad_normed), grad_gain)


def gelu_tanh(values):
    return 0.5 * values * (1.0 + jnp.tanh(0.7978845608028654 * (values + 0.044715 * values**3)))


def times_rows(left_side, weight):
    return lax.dot_general(
        left_side, weight, (((1,), (1,)), ((), ())), preferred_element_type=jnp.float32
    )


def times_plain(left_side, weight):
    return jnp.dot(left_side, weight, preferred_element_type=jnp.float32)


def outer_sum(left_side, right_side):
    return lax.dot_general(
        left_side, right_side, (((0,), (0,)), ((), ())), preferred_element_type=jnp.float32
    )


def shift(value, axis, amount):
    count = lax.axis_size(axis)
    return lax.ppermute(value, axis, [(i, (i + amount) % count) for i in range(count)])


def slide(value, amount):
    count = lax.axis_size("z")
    pairs = [(i, i + amount) for i in range(count) if 0 <= i + amount < count]
    return lax.ppermute(value, "z", pairs)


def far_pair(near_start, near_end, distance):
    count = lax.axis_size("z")
    first_half = lax.axis_index("z") < distance
    sent = jnp.where(first_half, near_end, near_start)
    pairs = [(i, (i + distance) % count) for i in range(count)]
    got = lax.ppermute(sent, "z", pairs)
    return got


def far_split(got, distance):
    first_half = lax.axis_index("z") < distance
    none = jnp.zeros_like(got)
    return jnp.where(first_half, none, got), jnp.where(first_half, got, none)


def halo_pieces(tokens):
    pieces = []
    distance, covered = 1, 0
    while covered < HALO:
        span = min(tokens, HALO - covered)
        needed = min(span, -(-(REACH - covered) // 16) * 16)
        pieces.append((distance, span, needed))
        distance, covered = distance + 1, covered + span
    return pieces


def with_neighbours(own):
    tokens = own.shape[0]
    before, after = [], []
    for distance, span, needed in halo_pieces(tokens):
        if distance < lax.axis_size("z"):
            if 2 * distance == lax.axis_size("z"):
                left, right = far_split(
                    far_pair(own[:needed], own[tokens - needed :], distance), distance
                )
            else:
                left = slide(own[tokens - needed :], distance)
                right = slide(own[:needed], -distance)
            before.append(jnp.pad(left, ((span - needed, 0), (0, 0))))
            after.append(jnp.pad(right, ((0, span - needed), (0, 0))))
        else:
            empty = jnp.zeros((span, own.shape[1]), own.dtype)
            before.append(empty)
            after.append(empty)
    return jnp.concatenate(before[::-1] + [own] + after, axis=0)


def start_back(window, tokens):
    moved = []
    covered = 0
    for distance, span, needed in halo_pieces(tokens):
        if distance < lax.axis_size("z"):
            left_end = HALO - covered
            right_start = HALO + tokens + covered
            left = window[left_end - needed : left_end]
            right = window[right_start : right_start + needed]
            if 2 * distance == lax.axis_size("z"):
                moved.append((far_pair(left, right, distance),))
            else:
                moved.append((slide(left, -distance), slide(right, distance)))
        covered += span
    return window[HALO : HALO + tokens], moved


def finish_back(own, moved):
    tokens = own.shape[0]
    total = own.astype(jnp.float32)
    for distance, pair in enumerate(moved, 1):
        if len(pair) == 1:
            ahead, back = far_split(pair[0], distance)
        else:
            back, ahead = pair
        needed = back.shape[0]
        total = total + jnp.pad(back.astype(jnp.float32), ((tokens - needed, 0), (0, 0)))
        total = total + jnp.pad(ahead.astype(jnp.float32), ((0, tokens - needed), (0, 0)))
    return total


def hop(value, axis, bit=1):
    pairs = [(i, i ^ bit) for i in range(lax.axis_size(axis))]
    return value + lax.ppermute(value, axis, pairs)


def pick(value, index, axis):
    return lax.dynamic_index_in_dim(value, index, axis, keepdims=False)


def stage_sends(value, axis_name, axis):
    count, here = lax.axis_size(axis_name), lax.axis_index(axis_name)
    return [pick(value, (here + k) % count, axis) for k in range(1, count)]


def stage_moves(sends, axis_name):
    return [shift(sent, axis_name, k + 1) for k, sent in enumerate(sends)]


def gelu_parts(values):
    squared = values * values
    slope = jnp.tanh(0.7978845608028654 * (values + 0.044715 * values * squared))
    active = 0.5 * values * (1.0 + slope)
    inner = 0.7978845608028654 * (1.0 + 3.0 * 0.044715 * squared)
    return active, 0.5 * (1.0 + slope) + 0.5 * values * (1.0 - slope * slope) * inner


def turned_rows(core_ref, kept_ref, sent_ref, stage_ref, sems):
    mine, unit = core_ref[0], core_ref[1]
    parts = FORWARD_TILE // TILE

    def copy(lane, part, place, at, where):
        spot = pl.ds(pl.multiple_of(at * TILE, TILE), TILE)
        source = stage_ref.at[where, lane, part * TILE : (part + 1) * TILE, :]
        return pltpu.make_async_copy(source, place.at[spot, :], sems.at[where, lane, part])

    def put(lane, kind, step, turned):
        slot = step % 2
        stage_ref[slot, lane] = turned
        for part in range(parts):
            target = ATTENTION_TILES + kind * (FF // TILE) + step * parts + part
            own = (target // unit) % 2 == mine
            at = (target // (2 * unit)) * unit + target % unit

            @pl.when(own)
            def _(part=part, at=at):
                copy(lane, part, kept_ref, at, slot).start()

            @pl.when(jnp.logical_not(own))
            def _(part=part, at=at):
                copy(lane, part, sent_ref, at, slot).start()

    def wait(lanes, where):
        for lane in range(lanes):
            for part in range(parts):
                copy(lane, part, kept_ref, 0, where).wait()

    return put, wait


def ffn_forward_body(core_ref, *refs):
    normed_ref, middle_ref, gelu_ref, linear_ref, down_ref = refs[:5]
    result_ref, gelu_factor_ref, linear_factor_ref, kept_ref, sent_ref, stage_ref, sems = refs[5:]
    step = pl.program_id(0)
    put, wait = turned_rows(core_ref, kept_ref, sent_ref, stage_ref, sems)

    @pl.when(step == 0)
    def _():
        result_ref[...] = middle_ref[...]

    @pl.when(step >= 2)
    def _():
        wait(1, step % 2)

    active, slope = gelu_parts(times_rows(normed_ref[...], gelu_ref[...]))
    linear = times_rows(normed_ref[...], linear_ref[...])
    gelu_factor_ref[...] = slope * linear
    linear_factor_ref[...] = active
    hidden = (active * linear).astype(jnp.bfloat16)
    put(0, 2, step, hidden.T)
    result_ref[...] += times_plain(hidden, down_ref[...])

    @pl.when(step == pl.num_programs(0) - 1)
    def _():
        wait(1, 0)
        wait(1, 1)


def resident(shape):
    return pl.BlockSpec(shape, lambda *_: (0,) * len(shape), pipeline_mode=pl.Buffered(1))


def core_units():
    return jnp.stack([lax.axis_index("c").astype(jnp.int32), jnp.int32(unit_tiles(TILE))])


def hidden_weight(kind, width):
    first = (4 * INNER + kind * FF) // FORWARD_TILE
    return pl.BlockSpec((FORWARD_TILE, width), lambda i, *_: (first + i, 0))


def turned_scratch(lanes, tokens):
    return [
        pltpu.VMEM((2, lanes, FORWARD_TILE, tokens), jnp.bfloat16),
        pltpu.SemaphoreType.DMA((2, lanes, FORWARD_TILE // TILE)),
    ]


def ffn_forward(normed, middle, gathered):
    tokens, width = normed.shape
    half = (4 * INNER + 3 * FF) // 2
    hidden = pl.BlockSpec((tokens, FORWARD_TILE), lambda i, *_: (0, i))
    side = resident((tokens, width))
    anywhere = pl.BlockSpec(memory_space=pl.ANY)
    return pl.pallas_call(
        ffn_forward_body,
        grid_spec=pltpu.PrefetchScalarGridSpec(
            num_scalar_prefetch=1,
            grid=(FF // FORWARD_TILE,),
            in_specs=[side, side] + [hidden_weight(kind, width) for kind in range(3)],
            out_specs=[side, hidden, hidden, anywhere, anywhere],
            scratch_shapes=turned_scratch(1, tokens),
        ),
        out_shape=[
            jax.ShapeDtypeStruct((tokens, width), jnp.float32),
            jax.ShapeDtypeStruct((tokens, FF), jnp.float32),
            jax.ShapeDtypeStruct((tokens, FF), jnp.float32),
            jax.ShapeDtypeStruct((half, tokens), jnp.bfloat16),
            jax.ShapeDtypeStruct((half, tokens), jnp.bfloat16),
        ],
        compiler_params=pltpu.CompilerParams(vmem_limit_bytes=52 << 20),
        cost_estimate=pl.CostEstimate(
            flops=6 * tokens * FF * width,
            bytes_accessed=6 * FF * width + 10 * tokens * FF,
            transcendentals=tokens * FF,
        ),
        name="ffn_forward",
    )(core_units(), normed, middle, gathered, gathered, gathered)


def ffn_backward_body(core_ref, *refs):
    branch_ref, gelu_factor_ref, linear_factor_ref, gelu_ref, linear_ref, down_ref = refs[:6]
    grad_ref, kept_ref, sent_ref, stage_ref, sems = refs[8:]
    step = pl.program_id(0)
    put, wait = turned_rows(core_ref, kept_ref, sent_ref, stage_ref, sems)

    @pl.when(step == 0)
    def _():
        grad_ref[...] = jnp.zeros_like(grad_ref)

    @pl.when(step >= 2)
    def _():
        wait(2, step % 2)

    grad_hidden = times_rows(branch_ref[...], down_ref[...])
    grad_gelu = (grad_hidden * gelu_factor_ref[...]).astype(jnp.bfloat16)
    grad_linear = (grad_hidden * linear_factor_ref[...]).astype(jnp.bfloat16)
    put(0, 0, step, grad_gelu.T)
    put(1, 1, step, grad_linear.T)
    grad_ref[...] += times_plain(grad_gelu, gelu_ref[...]) + times_plain(
        grad_linear, linear_ref[...]
    )

    @pl.when(step == pl.num_programs(0) - 1)
    def _():
        wait(2, 0)
        wait(2, 1)


def unit_tiles(tile):
    rows = 4 * INNER + 3 * FF
    return rows // tile // (2 * lax.axis_size("y") * lax.axis_size("x"))


def ffn_backward(branch, gelu_factor, linear_factor, gathered, kept, sent):
    tokens, width = branch.shape
    hidden = pl.BlockSpec((tokens, FORWARD_TILE), lambda i, *_: (0, i))
    side = resident((tokens, width))
    anywhere = pl.BlockSpec(memory_space=pl.ANY)
    return pl.pallas_call(
        ffn_backward_body,
        grid_spec=pltpu.PrefetchScalarGridSpec(
            num_scalar_prefetch=1,
            grid=(FF // FORWARD_TILE,),
            in_specs=[side, hidden, hidden]
            + [hidden_weight(kind, width) for kind in range(3)]
            + [anywhere, anywhere],
            out_specs=[side, anywhere, anywhere],
            scratch_shapes=turned_scratch(2, tokens),
        ),
        out_shape=[
            jax.ShapeDtypeStruct((tokens, width), jnp.float32),
            jax.ShapeDtypeStruct(kept.shape, kept.dtype),
            jax.ShapeDtypeStruct(sent.shape, sent.dtype),
        ],
        input_output_aliases={7: 1, 8: 2},
        compiler_params=pltpu.CompilerParams(vmem_limit_bytes=52 << 20),
        cost_estimate=pl.CostEstimate(
            flops=6 * tokens * FF * width,
            bytes_accessed=6 * FF * width + 12 * tokens * FF,
            transcendentals=0,
        ),
        name="ffn_backward",
    )(core_units(), branch, gelu_factor, linear_factor, gathered, gathered, gathered, kept, sent)


def spots_of(unit_at, place_ref):
    here_y, here_x, size_y, size_x = place_ref[0], place_ref[1], place_ref[4], place_ref[5]
    row, column = unit_at // size_x, unit_at % size_x
    return (
        ((row + 2 * size_y - here_y - 1) % size_y, column),
        ((column + 2 * size_x - here_x - 1) % size_x, row),
    )


def weight_grads_body(chunks, tile, place_ref, *refs):
    own_ref, other_ref, normed_ref, branch_ref, other_normed_ref, other_branch_ref = refs[:6]
    stage_ref, sems = refs[-2:]
    step = pl.program_id(0)
    unit = place_ref[3]
    at = (step // unit * 2 + place_ref[2]) * unit + step % unit
    first, second = 4 * INNER // tile, (4 * INNER + 2 * FF) // tile
    slot = step % 2
    places = split_places(refs[6:-2], chunks)
    start, wait = place_copies(chunks, stage_ref, sems, places, tile)

    def put(product):
        stage_ref[slot, :, : CUTS[-1]] = product.astype(jnp.bfloat16)
        start(spots_of(step // unit, place_ref), unit, step % unit, step, slot)

    def both(side_ref, other_side_ref):
        return jnp.dot(
            own_ref[...], side_ref[:, : CUTS[-1]], preferred_element_type=jnp.float32
        ) + jnp.dot(
            other_ref[...], other_side_ref[:, : CUTS[-1]], preferred_element_type=jnp.float32
        )

    @pl.when(step < 2)
    def _():
        stage_ref[slot, :, CUTS[-1] :] = jnp.zeros((tile, PADDED - CUTS[-1]), jnp.bfloat16)

    @pl.when(step >= 2)
    def _():
        wait(slot)

    @pl.when(at < first)
    def _():
        put(jnp.zeros((tile, CUTS[-1]), jnp.float32))

    @pl.when((at >= first) & (at < second))
    def _():
        put(both(normed_ref, other_normed_ref))

    @pl.when(at >= second)
    def _():
        put(both(branch_ref, other_branch_ref))

    @pl.when(step == pl.num_programs(0) - 1)
    def _():
        wait(0)
        wait(1)


def split_places(refs, chunks):
    size_y, size_x, per = lax.axis_size("y"), lax.axis_size("x"), chunks // 2
    refs = list(refs)
    along_y = [refs[per * k : per * (k + 1)] for k in range(size_y)]
    refs = refs[per * size_y :]
    along_x = [refs[per * k : per * (k + 1)] for k in range(size_x)]
    return along_y, along_x, refs[per * size_x :]


def array_shapes(chunks, rows):
    columns = chunk_width(chunks)
    shapes = [(rows // lax.axis_size("y"), columns)] * (chunks // 2 * lax.axis_size("y"))
    shapes += [(rows // lax.axis_size("x"), columns)] * (chunks // 2 * lax.axis_size("x"))
    if chunks < 4:
        shapes.append((rows, PADDED - chunks * columns))
    return [jax.ShapeDtypeStruct(shape, jnp.bfloat16) for shape in shapes]


def place_copies(chunks, stage_ref, sems, places, tile):
    along = places[:2]
    rest = places[2]

    def copy(lane, place, row, where):
        start = lane * chunk_width(chunks)
        end = PADDED if lane == chunks else start + chunk_width(chunks)
        spot = pl.ds(pl.multiple_of(row * tile, tile), tile)
        return pltpu.make_async_copy(
            stage_ref.at[where, :, start:end], place.at[spot, :], sems.at[where, lane]
        )

    def start(spots, unit, inside, row, where):
        for chunk in range(chunks):
            which, position = spots[chunk % 2]
            for k, group in enumerate(along[chunk % 2]):

                @pl.when(which == k)
                def _(chunk=chunk, place=group[chunk // 2], at=position * unit + inside):
                    copy(chunk, place, at, where).start()

        for place in rest:
            copy(chunks, place, row, where).start()

    def wait(where):
        for chunk in range(chunks):
            copy(chunk, along[chunk % 2][0][chunk // 2], 0, where).wait()
        for place in rest:
            copy(chunks, place, 0, where).wait()

    return start, wait


def place_of(tile):
    return jnp.stack(
        [
            lax.axis_index("y").astype(jnp.int32),
            lax.axis_index("x").astype(jnp.int32),
            lax.axis_index("c").astype(jnp.int32),
            jnp.int32(unit_tiles(tile)),
            jnp.int32(lax.axis_size("y")),
            jnp.int32(lax.axis_size("x")),
        ]
    )


def half_side(tokens, at):
    return pl.BlockSpec(
        (tokens, PADDED), lambda i, *_: (at, 0), pipeline_mode=pl.Buffered(1)
    )


def weight_grads(chunks, own, other, sides):
    rows, tokens = own.shape
    tile = 512 if unit_tiles(256) % 2 == 0 else 256
    source = pl.BlockSpec((tile, tokens), lambda i, *_: (i, 0))
    halves = [half_side(tokens, 0), half_side(tokens, 1)]
    out_shape = array_shapes(chunks, rows)
    return pl.pallas_call(
        functools.partial(weight_grads_body, chunks, tile),
        grid_spec=pltpu.PrefetchScalarGridSpec(
            num_scalar_prefetch=1,
            grid=(rows // tile,),
            in_specs=[source, source] + halves * 2,
            out_specs=[pl.BlockSpec(memory_space=pl.ANY)] * len(out_shape),
            scratch_shapes=[
                pltpu.VMEM((2, tile, PADDED), jnp.bfloat16),
                pltpu.SemaphoreType.DMA((2, 5)),
            ],
        ),
        out_shape=out_shape,
        compiler_params=pltpu.CompilerParams(vmem_limit_bytes=40 << 20),
        cost_estimate=pl.CostEstimate(
            flops=4 * rows * tokens * CUTS[-1],
            bytes_accessed=4 * rows * tokens + 2 * rows * PADDED,
            transcendentals=0,
        ),
        name="weight_grads",
    )(place_of(tile), own, other, sides[0], sides[0], sides[1], sides[1])


def attention_fill_body(chunks, owners, place_ref, *refs):
    own_ref, other_ref, side_ref, other_side_ref = refs[:4]
    outs = refs[4 + (len(refs) - 6) // 2 : -2]
    stage_ref, sems = refs[-2:]
    step = pl.program_id(0)
    slot = step % 2
    start, wait = place_copies(chunks, stage_ref, sems, split_places(outs, chunks), INNER)

    def put():
        product = jnp.dot(
            own_ref[...].T, side_ref[:, : CUTS[-1]], preferred_element_type=jnp.float32
        ) + jnp.dot(
            other_ref[...].T, other_side_ref[:, : CUTS[-1]], preferred_element_type=jnp.float32
        )
        stage_ref[slot, :, : CUTS[-1]] = product.astype(jnp.bfloat16)
        stage_ref[slot, :, CUTS[-1] :] = jnp.zeros((INNER, PADDED - CUTS[-1]), jnp.bfloat16)
        start(spots_of(0, place_ref), 0, step, step, slot)

    @pl.when(place_ref[2] < owners)
    def _():
        @pl.when(step >= 2)
        def _():
            wait(slot)

        put()

        @pl.when(step == pl.num_programs(0) - 1)
        def _():
            wait(0)
            wait(1)


def attention_fill(chunks, arrays, own, other, sides):
    tokens = own.shape[0]
    unit_rows = unit_tiles(TILE) * TILE
    owners = 4 * INNER // unit_rows
    steps = unit_rows // INNER

    def column(i, place_ref):
        return 0, jnp.minimum(place_ref[2], owners - 1) * steps + i

    def half(i, place_ref):
        return jnp.where(column(i, place_ref)[1] < 3, 0, 1), 0

    anywhere = pl.BlockSpec(memory_space=pl.ANY)
    return pl.pallas_call(
        functools.partial(attention_fill_body, chunks, owners),
        grid_spec=pltpu.PrefetchScalarGridSpec(
            num_scalar_prefetch=1,
            grid=(steps,),
            in_specs=[pl.BlockSpec((tokens, INNER), column)] * 2
            + [pl.BlockSpec((tokens, PADDED), half)] * 2
            + [anywhere] * len(arrays),
            out_specs=[anywhere] * len(arrays),
            scratch_shapes=[
                pltpu.VMEM((2, INNER, PADDED), jnp.bfloat16),
                pltpu.SemaphoreType.DMA((2, 5)),
            ],
        ),
        out_shape=[jax.ShapeDtypeStruct(array.shape, array.dtype) for array in arrays],
        input_output_aliases={5 + k: k for k in range(len(arrays))},
        compiler_params=pltpu.CompilerParams(vmem_limit_bytes=32 << 20),
        cost_estimate=pl.CostEstimate(
            flops=4 * unit_rows * tokens * CUTS[-1],
            bytes_accessed=4 * unit_rows * tokens + 2 * unit_rows * PADDED,
            transcendentals=0,
        ),
        name="attention_fill",
    )(place_of(TILE), own, other, *sides, *arrays)


def tied(first, second):
    return lax.optimization_barrier((first, second))


def chunk_width(chunks):
    return PADDED // 4 if chunks == 4 else PADDED // 6


class Scatter:
    def __init__(self):
        self.waiting, self.flying, self.results = {}, {}, {}

    def push(self, name, route, kept, sends):
        self.waiting[name] = (route, kept, sends)

    def settle(self, values, *names):
        arrays, values = tied({name: self.flying[name][1:] for name in names}, values)
        moves = {}
        for name in names:
            route = self.flying.pop(name)[0]
            kept, moved = arrays[name]
            if not route:
                self.results[name] = kept.astype(jnp.float32) + sum(
                    part.astype(jnp.float32) for part in moved
                )
                continue
            total = total_of(kept, moved)
            total = total.reshape((lax.axis_size(route[0]), -1) + total.shape[-1:])
            sends = stage_sends(total, route[0], 0)
            moves[name] = (route, pick(total, lax.axis_index(route[0]), 0), sends)
        if moves and all(move[0] == ("z",) for move in moves.values()):
            kept = jnp.concatenate([move[1] for move in moves.values()], axis=-1)
            sends = [
                jnp.concatenate(parts, axis=-1) for parts in zip(*(m[2] for m in moves.values()))
            ]
            moves = {tuple(moves): (("z",), kept, sends)}
        arrays, values = tied({name: move[1:] for name, move in moves.items()}, values)
        for name, (route, *_) in moves.items():
            self.waiting[name] = (route,) + tuple(arrays[name])
        return values

    def start(self, values, *names):
        arrays, values = tied({name: self.waiting[name][1:] for name in names}, values)
        for name in names:
            route = self.waiting.pop(name)[0]
            kept, sends = arrays[name]
            self.flying[name] = (route[1:], kept, stage_moves(sends, route[0]))
        return values

    def step(self, values, *names):
        others = set(self.waiting)
        values = self.settle(values, *names)
        return self.start(values, *(name for name in self.waiting if name not in others))


def total_of(value, moved):
    total = value.astype(jnp.float32)
    for part in moved:
        total = total + part.astype(jnp.float32)
    return total.astype(jnp.bfloat16)


def fetch_rows(local_rows):
    return lax.all_gather(local_rows, DEVICES, axis=0, tiled=True)


def layer_forward(stream, gathered, gain_one, gain_two, gate_low, context):
    normed, inverse_one = rms_forward(stream, gain_one)
    normed_low = normed.astype(jnp.bfloat16)
    projected = times_rows(normed_low, gathered[: 3 * INNER]).astype(jnp.bfloat16)
    queries = projected[:, :INNER]
    parts = [projected[:, INNER:]]
    if gate_low is not None:
        parts.append(jnp.broadcast_to(gate_low[:, None], (stream.shape[0], BLOCK)))
    shared = with_neighbours(jnp.concatenate(parts, axis=1))
    attended, log_total = attend_forward(queries, shared, context)
    middle = stream + times_plain(attended, gathered[3 * INNER : 4 * INNER])
    normed_two, inverse_two = rms_forward(middle, gain_two)
    normed_two_low = normed_two.astype(jnp.bfloat16)
    result, *factors = ffn_forward(normed_two_low, middle, gathered)
    kept = (
        stream,
        inverse_one,
        normed_low,
        queries,
        shared,
        attended,
        log_total,
        middle,
        inverse_two,
        normed_two_low,
        factors,
    )
    return (result, kept)


def layer_backward(grad_out, kept, gathered, gain_one, gain_two, context, before):
    (
        stream,
        inverse_one,
        normed_low,
        queries,
        shared,
        attended,
        log_total,
        middle,
        inverse_two,
        normed_two_low,
        factors,
    ) = kept
    tokens = queries.shape[0]
    branch_low = grad_out.astype(jnp.bfloat16)
    sides = jnp.concatenate([normed_two_low, branch_low], axis=0)
    sides = jnp.pad(sides, ((0, 0), (0, PADDED - sides.shape[1])))
    sides = (sides, shift(sides, "c", 1))
    grad_normed_two, own, sent = ffn_backward(
        branch_low, factors[0], factors[1], gathered, factors[2], factors[3]
    )
    if before is not None:
        grad_normed_two, own, sent = before.step((grad_normed_two, own, sent), 0, 1)
    other = shift(sent, "c", 1)
    grad_middle, grad_gain_two = rms_backward(middle, inverse_two, gain_two, grad_normed_two)
    grad_middle = grad_out + grad_middle
    middle_low = grad_middle.astype(jnp.bfloat16)
    late_sides = jnp.concatenate([normed_low, middle_low], axis=0)
    late_sides = jnp.pad(late_sides, ((0, 0), (0, PADDED - late_sides.shape[1])))
    late_sides = (late_sides, shift(late_sides, "c", 1))
    grad_mixed = times_rows(middle_low, gathered[3 * INNER : 4 * INNER]).astype(jnp.bfloat16)
    grad_query, grad_shared, grad_table = attend_backward(
        queries, grad_mixed, shared, log_total, context
    )
    if before is not None:
        grad_query, grad_shared = before.settle((grad_query, grad_shared), 0, 1)
    grad_shared, own = lax.optimization_barrier((grad_shared, own))
    moving = start_back(grad_shared, tokens)
    chunks = 2 if before is None else 4
    arrays = weight_grads(chunks, own, other, sides)
    arrays, moving = lax.optimization_barrier((arrays, moving))
    if before is not None:
        arrays, moving = before.start((arrays, moving), (0, 1))
    grad_own = finish_back(*moving)
    grad_gate = grad_own[:, 2 * INNER :]
    grad_input_low = jnp.concatenate(
        [grad_query, grad_own[:, : 2 * INNER].astype(jnp.bfloat16)], axis=1
    )
    late = jnp.concatenate([grad_input_low, attended], axis=1)
    arrays = attention_fill(chunks, arrays, late, shift(late, "c", 1), late_sides)
    scatter = Scatter()
    along_y, along_x, rest = split_places(arrays, chunks)
    for chunk in range(chunks):
        route = ("y", "x", "z") if chunk % 2 == 0 else ("x", "y", "z")
        ordered = [group[chunk // 2] for group in (along_y, along_x)[chunk % 2]]
        scatter.push(chunk, route, ordered[-1], ordered[:-1])
    grad_input_low, grad_gate = scatter.start((grad_input_low, grad_gate), 0, 1)
    if rest:
        grad_input_low, grad_gate, rest = lax.optimization_barrier(
            (grad_input_low, grad_gate, rest)
        )
        rest = lax.psum_scatter(rest[0], ("y", "x", "z"), scatter_dimension=0, tiled=True)
    grad_normed = times_plain(grad_input_low, gathered[: 3 * INNER])
    grad_stream, grad_gain_one = rms_backward(stream, inverse_one, gain_one, grad_normed)
    return (grad_middle + grad_stream, grad_table, grad_gate, grad_gain_one, grad_gain_two, scatter, rest)


def per_device(
    inputs, layer3_rows, layer4_rows, norm_gains, gate_weight, rel_bias, segment_ids, cotangent
):
    seqs_here, tokens_here, width = inputs.shape
    first_pos = lax.axis_index("z") * tokens_here
    context = attention_context(segment_ids[0], first_pos, tokens_here, rel_bias)
    stream = inputs.reshape(tokens_here, width)
    gathered_three = fetch_rows(layer3_rows)
    after_three, kept_three = layer_forward(
        stream, gathered_three, norm_gains[0], norm_gains[1], None, context
    )
    gate_inverse = lax.rsqrt(jnp.mean(after_three * after_three, axis=1, keepdims=True) + epsilon)
    gate_normed = after_three * gate_inverse
    gate_logit = jnp.sum(gate_normed * gate_weight, axis=1) + gate_offset
    sigmoid_value = 1.0 / (1.0 + jnp.exp(-gate_logit))
    gate_mask = gate_scale * sigmoid_value
    gate_low = gate_mask.astype(jnp.bfloat16)
    gathered_four = fetch_rows(layer4_rows)
    after_four, kept_four = layer_forward(
        after_three, gathered_four, norm_gains[2], norm_gains[3], gate_low, context
    )
    grad_three_out, table_four, grad_gate, gain_four_one, gain_four_two, before, rest = (
        layer_backward(
            cotangent.reshape(tokens_here, width),
            kept_four,
            gathered_four,
            norm_gains[2],
            norm_gains[3],
            context,
            None,
        )
    )
    grad_logit = grad_gate[:, 0] * gate_scale * sigmoid_value * (1.0 - sigmoid_value)
    grad_gate_weight = jnp.sum(grad_logit[:, None] * gate_normed, axis=0)
    gate_stream = stream_backward(after_three, gate_inverse, grad_logit[:, None] * gate_weight)
    grad_input, table_three, unused, gain_three_one, gain_three_two, scatter, _ = layer_backward(
        grad_three_out + gate_stream,
        kept_three,
        gathered_three,
        norm_gains[0],
        norm_gains[1],
        context,
        before,
    )
    table = jnp.pad((table_three + table_four).reshape(1, -1), ((0, 0), (0, width - 6 * BUCKETS)))
    small_sums = jnp.stack(
        [gain_three_one, gain_three_two, gain_four_one, gain_four_two, grad_gate_weight, table[0]]
    )
    small = hop(small_sums, "c")
    small = before.settle(small, (0, 1))
    small = scatter.step(small, 0, 1)
    small = scatter.start(small, 2, 3)
    small = scatter.step(small, 0, 1)
    small, rest = scatter.settle((small, rest), (0, 1))
    small = scatter.step(small, 2, 3)
    for bit in range(1, lax.axis_size("z")):
        if bit & (bit - 1) == 0:
            small = hop(small, "z", bit)
    small = scatter.step(small, 2, 3)
    small = hop(small, "x")
    for bit in range(1, lax.axis_size("y")):
        if bit & (bit - 1) == 0:
            small = hop(small, "y", bit)
    summed = scatter.settle(small, (2, 3))
    local_three = jnp.concatenate([scatter.results[pair] for pair in ((0, 1), (2, 3))], axis=1)
    local_four = jnp.concatenate([before.results[(0, 1)], rest.astype(jnp.float32)], axis=1)
    local_three, local_four = local_three[:, :width], local_four[:, :width]
    return (
        after_four.reshape(inputs.shape),
        gate_mask.reshape(seqs_here, tokens_here),
        grad_input.reshape(inputs.shape),
        local_three,
        local_four,
        summed[:4],
        summed[4],
        summed[5, : 6 * BUCKETS].reshape(BUCKETS, HEADS),
    )


def solution(mesh):
    outer, inner = mesh.devices.shape
    fine = Mesh(mesh.devices.reshape(outer // 4, 2, 2, inner), DEVICES)
    batch = ("y", "x", "c")
    tokens = P(batch, "z", None)
    rows = P(DEVICES, None)
    return jax.shard_map(
        per_device,
        mesh=fine,
        in_specs=(tokens, rows, rows, P(), P(), P(), P(batch, None), tokens),
        out_specs=(tokens, P(batch, "z"), tokens, rows, rows, P(), P(), P()),
        check_vma=False,
    )
```

```python
import functools

import jax
import jax.numpy as jnp
from jax import lax
from jax.experimental import pallas as pl
from jax.experimental.pallas import tpu as pltpu
from jax.sharding import Mesh
from jax.sharding import PartitionSpec as P

HEADS = 6
PAIRS = 3
BLOCK = 128
WIDE = 2 * BLOCK
INNER = 384
BUCKETS = 32
FF = 3584
REACH = 799
HALO = 896
TILE = 256
ATTENTION_TILES = 4 * INNER // TILE
OFFSETS = 5
PADDED = 1536
FORWARD_TILE = 512
CUTS = (0, 1472)
DEVICES = ("y", "x", "c", "z")
epsilon = 1e-06
gate_scale = -30.0
gate_offset = -3.5
masked_out = -1e30
limits = (12, 16, 23, 32, 46, 64, 91)
both_last = (((1,), (1,)), ((), ()))


def bucket_of(relative):
    magnitude = jnp.abs(relative)
    beyond = jnp.zeros_like(magnitude)
    for bound_value in limits:
        beyond = beyond + (magnitude >= bound_value).astype(jnp.int32)
    inside = jnp.where(magnitude < 8, magnitude, 8 + beyond)
    return inside + 16 * (relative > 0).astype(jnp.int32)


def near_buckets(offset):
    if offset < 0:
        return range(1, 16)
    if offset > 0:
        return range(17, 32)
    return range(0, 32)


def tile_buckets(offset, width):
    key_at = lax.broadcasted_iota(jnp.int32, (BLOCK, width), 0)
    query_at = lax.broadcasted_iota(jnp.int32, (BLOCK, width), 1) % BLOCK
    return bucket_of(offset * BLOCK + key_at - query_at)


def bias_body(table_ref, tiles_ref):
    head = pl.program_id(0)
    tiles_ref[0, 0] = jnp.full((BLOCK, BLOCK), table_ref[15, head], jnp.float32)
    tiles_ref[0, 4] = jnp.full((BLOCK, BLOCK), table_ref[31, head], jnp.float32)
    for offset in (-1, 0, 1):
        buckets = tile_buckets(offset, BLOCK)
        tile = jnp.zeros((BLOCK, BLOCK), jnp.float32)
        for bucket in near_buckets(offset):
            tile = jnp.where(buckets == bucket, table_ref[bucket, head], tile)
        tiles_ref[0, offset + 2] = tile


def bias_tiles(rel_bias):
    return pl.pallas_call(
        bias_body,
        grid=(HEADS,),
        in_specs=[pl.BlockSpec(memory_space=pltpu.SMEM)],
        out_specs=pl.BlockSpec((1, OFFSETS, BLOCK, BLOCK), lambda h: (h, 0, 0, 0)),
        out_shape=jax.ShapeDtypeStruct((HEADS, OFFSETS, BLOCK, BLOCK), jnp.float32),
        name="bias_tiles",
    )(rel_bias)


def lane_masks():
    lane = lax.broadcasted_iota(jnp.int32, (BLOCK, BLOCK), 1)
    low = jnp.where(lane < 64, 1.0, 0.0).astype(jnp.bfloat16)
    high = jnp.where(lane < 64, 0.0, 1.0).astype(jnp.bfloat16)
    return low, high


def stacked(block, masks):
    low, high = masks
    return jnp.concatenate([block * low, block * high], axis=0)


def pair_cols(pair):
    return slice(pair * BLOCK, (pair + 1) * BLOCK)


def value_cols(pair):
    return slice(INNER + pair * BLOCK, INNER + (pair + 1) * BLOCK)


def block_rows(block):
    return pl.ds(pl.multiple_of(block * BLOCK, BLOCK), BLOCK)


def wide_rows(block):
    return pl.ds(pl.multiple_of(block * WIDE, WIDE), WIDE)


def fold(values):
    return values.reshape(values.shape[0] // 8, 8, WIDE)


def shift_tile(gated, rows, own_segment, segment_ref, shared_ref):
    same = segment_ref[rows, :] == own_segment
    inside = shared_ref[rows, 2 * INNER :].astype(jnp.float32) if gated else 0.0
    shift = jnp.where(same, inside, masked_out)
    return jnp.concatenate([shift, shift], axis=1)


def used_blocks(low_ref, high_ref):
    last = pl.num_programs(0) - 1
    return low_ref[0] // 2 * 2, (high_ref[last] + 1) // 2 * 2


def tile_offsets(block, own_block):
    return [jnp.clip(2 * block + k - own_block, -2, 2) + 2 for k in range(2)]


def bias_pair(bias_ref, pair, offsets):
    halves = [
        jnp.concatenate([bias_ref[2 * pair, at], bias_ref[2 * pair + 1, at]], axis=1)
        for at in offsets
    ]
    return jnp.concatenate(halves, axis=0)


def pick_heads(wide):
    return jnp.concatenate([wide[:64, :BLOCK], wide[64:, BLOCK:]], axis=0)


def forward_body(gated, low_ref, high_ref, *refs):
    query_ref, shared_ref, own_ref, segment_ref, bias_ref = refs[:5]
    mixed_ref, full_ref, total_ref, turned_ref, score_ref, sum_ref = refs[5:]
    step = pl.program_id(0)

    @pl.when(step == 0)
    def _():
        @pl.loop(*used_blocks(low_ref, high_ref))
        def _(block):
            rows = block_rows(block)
            turned_ref[:, rows] = shared_ref[rows, INNER : 2 * INNER].T

    first, last = low_ref[step] // 2, (high_ref[step] + 1) // 2
    own_block = HALO // BLOCK + step
    own_segment = own_ref[0]
    masks = lane_masks()
    queries = [stacked(query_ref[:, pair_cols(pair)], masks) for pair in range(PAIRS)]

    def scores(block, peaks):
        rows = wide_rows(block)
        shift = shift_tile(gated, rows, own_segment, segment_ref, shared_ref)
        offsets = tile_offsets(block, own_block)
        new_peaks = []
        for pair in range(PAIRS):
            score = lax.dot_general(
                shared_ref[rows, pair_cols(pair)],
                queries[pair],
                both_last,
                preferred_element_type=jnp.float32,
            )
            score = score + bias_pair(bias_ref, pair, offsets) + shift
            score_ref[pair, block] = score
            new_peaks.append(jnp.maximum(peaks[pair], jnp.max(fold(score), axis=0)))
        return tuple(new_peaks)

    start = jnp.full((8, WIDE), -3e38, jnp.float32)
    peaks = lax.fori_loop(first, last, scores, (start,) * PAIRS)
    peaks = [jnp.max(peak, axis=0, keepdims=True) for peak in peaks]
    sum_ref[...] = jnp.zeros_like(sum_ref)

    def mix(block, totals):
        new_totals = []
        for pair in range(PAIRS):
            weight = jnp.exp(score_ref[pair, block] - peaks[pair])
            new_totals.append(totals[pair] + jnp.sum(fold(weight), axis=0))
            sum_ref[pair] += jnp.dot(
                turned_ref[pair_cols(pair), wide_rows(block)],
                weight.astype(jnp.bfloat16),
                preferred_element_type=jnp.float32,
            )
        return tuple(new_totals)

    totals = lax.fori_loop(first, last, mix, (jnp.zeros((8, WIDE), jnp.float32),) * PAIRS)
    for pair in range(PAIRS):
        row_total = jnp.sum(totals[pair], axis=0, keepdims=True)
        mixed = pick_heads(sum_ref[pair] * (1.0 / row_total))
        full_ref[:, pair_cols(pair)] = mixed.T
        mixed_ref[:, pair_cols(pair)] = full_ref[:, pair_cols(pair)].astype(jnp.bfloat16)
        total_ref[0, pair : pair + 1, :] = peaks[pair] + jnp.log(row_total)


def whole(shape):
    return pl.BlockSpec(shape, lambda i, *_: (0,) * len(shape), pipeline_mode=pl.Buffered(1))


def rows_spec(width):
    return pl.BlockSpec((BLOCK, width), lambda i, *_: (i, 0))


def attend_forward(queries, shared, context):
    lows, highs, own_rows, segment_wide, tiles = context
    tokens, (length, width) = queries.shape[0], shared.shape
    steps, key_blocks = tokens // BLOCK, length // BLOCK
    return pl.pallas_call(
        functools.partial(forward_body, width > 2 * INNER),
        grid_spec=pltpu.PrefetchScalarGridSpec(
            num_scalar_prefetch=2,
            grid=(steps,),
            in_specs=[
                rows_spec(INNER),
                whole((length, width)),
                pl.BlockSpec((1, 1, BLOCK), lambda i, *_: (i, 0, 0)),
                whole((length, BLOCK)),
                whole(tiles.shape),
            ],
            out_specs=[
                rows_spec(INNER),
                rows_spec(INNER),
                pl.BlockSpec((1, 8, WIDE), lambda i, *_: (i, 0, 0)),
            ],
            scratch_shapes=[
                pltpu.VMEM((INNER, length), jnp.bfloat16),
                pltpu.VMEM((PAIRS, key_blocks // 2, WIDE, WIDE), jnp.float32),
                pltpu.VMEM((PAIRS, BLOCK, WIDE), jnp.float32),
            ],
        ),
        out_shape=[
            jax.ShapeDtypeStruct((tokens, INNER), jnp.bfloat16),
            jax.ShapeDtypeStruct((tokens, INNER), jnp.float32),
            jax.ShapeDtypeStruct((steps, 8, WIDE), jnp.float32),
        ],
        compiler_params=pltpu.CompilerParams(vmem_limit_bytes=40 << 20),
        cost_estimate=pl.CostEstimate(
            flops=tokens * length * INNER * 4,
            bytes_accessed=8 << 20,
            transcendentals=tokens * length * 3,
        ),
        name="attend_forward",
    )(lows, highs, queries, shared, own_rows, segment_wide, tiles)


def backward_body(gated, low_ref, high_ref, *refs):
    query_ref, grad_ref, full_ref, shared_ref, own_ref, segment_ref, bias_ref, total_ref = refs[:8]
    grad_query_ref, grad_shared_ref, bucket_ref = refs[8:11]
    turned_ref, sum_ref, bias_sum_ref, turn_sum_ref = refs[11:]
    step = pl.program_id(0)

    @pl.when(step == 0)
    def _():
        bias_sum_ref[...] = jnp.zeros_like(bias_sum_ref)

        @pl.loop(*used_blocks(low_ref, high_ref))
        def _(block):
            rows = block_rows(block)
            turned_ref[:, rows] = shared_ref[rows, :INNER].T
            sum_ref[rows, :] = jnp.zeros((BLOCK, sum_ref.shape[1]), jnp.float32)

    first, last = low_ref[step] // 2, (high_ref[step] + 1) // 2
    own_block = HALO // BLOCK + step
    own_segment = own_ref[0]
    masks = lane_masks()
    queries = [stacked(query_ref[:, pair_cols(pair)], masks) for pair in range(PAIRS)]
    grads = [stacked(grad_ref[:, pair_cols(pair)], masks) for pair in range(PAIRS)]
    totals = [total_ref[0, pair : pair + 1, :] for pair in range(PAIRS)]

    deltas = []
    for pair in range(PAIRS):
        cols = pair_cols(pair)
        product = (grad_ref[:, cols].astype(jnp.float32) * full_ref[:, cols]).T
        halves = [jnp.sum(half, axis=0, keepdims=True) for half in (product[:64], product[64:])]
        deltas.append(jnp.concatenate(halves, axis=1))
    turn_sum_ref[...] = jnp.zeros_like(turn_sum_ref)

    @pl.loop(first, last)
    def _(block):
        rows = wide_rows(block)
        shift = shift_tile(gated, rows, own_segment, segment_ref, shared_ref)
        offsets = tile_offsets(block, own_block)
        gate_part = jnp.zeros((WIDE, BLOCK), jnp.float32)
        for pair in range(PAIRS):
            cols = pair_cols(pair)
            score = lax.dot_general(
                shared_ref[rows, cols], queries[pair], both_last, preferred_element_type=jnp.float32
            )
            pull = lax.dot_general(
                shared_ref[rows, value_cols(pair)],
                grads[pair],
                both_last,
                preferred_element_type=jnp.float32,
            )
            prob = jnp.exp(score + bias_pair(bias_ref, pair, offsets) + shift - totals[pair])
            sum_ref[rows, value_cols(pair)] += jnp.dot(
                prob.astype(jnp.bfloat16), grads[pair], preferred_element_type=jnp.float32
            )
            grad_score = prob * (pull - deltas[pair])
            bias_sum_ref[pair, offsets[0]] += grad_score[:BLOCK]
            bias_sum_ref[pair, offsets[1]] += grad_score[BLOCK:]
            if gated:
                gate_part = gate_part + (grad_score[:, :BLOCK] + grad_score[:, BLOCK:])
            score_low = grad_score.astype(jnp.bfloat16)
            sum_ref[rows, cols] += jnp.dot(
                score_low, queries[pair], preferred_element_type=jnp.float32
            )
            turn_sum_ref[pair] += jnp.dot(
                turned_ref[cols, rows], score_low, preferred_element_type=jnp.float32
            )
        if gated:
            sum_ref[rows, 2 * INNER :] += gate_part

    for pair in range(PAIRS):
        grad_query_ref[:, pair_cols(pair)] = pick_heads(turn_sum_ref[pair]).T.astype(jnp.bfloat16)

    @pl.when(step == pl.num_programs(0) - 1)
    def _():
        grad_shared_ref[...] = jnp.zeros_like(grad_shared_ref)

        @pl.loop(*used_blocks(low_ref, high_ref))
        def _(block):
            rows = block_rows(block)
            both = slice(0, 2 * INNER)
            grad_shared_ref[rows, both] = sum_ref[rows, both].astype(jnp.bfloat16)
            if gated:
                gate_total = jnp.sum(sum_ref[rows, 2 * INNER :], axis=1, keepdims=True)
                grad_shared_ref[rows, 2 * INNER :] = jnp.broadcast_to(
                    gate_total, (BLOCK, BLOCK)
                ).astype(jnp.bfloat16)

        tables = {offset: tile_buckets(offset, WIDE) for offset in (-1, 0, 1)}

        @pl.loop(0, PAIRS)
        def _(pair):
            for bucket in range(BUCKETS):
                part = jnp.zeros((8, WIDE), jnp.float32)
                for offset in (-1, 0, 1):
                    if bucket in near_buckets(offset):
                        chosen = jnp.where(
                            tables[offset] == bucket, bias_sum_ref[pair, offset + 2], 0.0
                        )
                        part = part + jnp.sum(fold(chosen), axis=0)
                if bucket == 15:
                    part = part + jnp.sum(fold(bias_sum_ref[pair, 0]), axis=0)
                if bucket == 31:
                    part = part + jnp.sum(fold(bias_sum_ref[pair, 4]), axis=0)
                bucket_ref[pair, bucket : bucket + 1, :] = jnp.sum(part, axis=0, keepdims=True)


def attend_backward(queries, grad_mixed, full, shared, log_total, context):
    lows, highs, own_rows, segment_wide, tiles = context
    tokens, (length, width) = queries.shape[0], shared.shape
    steps = tokens // BLOCK
    grad_query, grad_shared, bucket_sums = pl.pallas_call(
        functools.partial(backward_body, width > 2 * INNER),
        grid_spec=pltpu.PrefetchScalarGridSpec(
            num_scalar_prefetch=2,
            grid=(steps,),
            in_specs=[
                rows_spec(INNER),
                rows_spec(INNER),
                rows_spec(INNER),
                whole((length, width)),
                pl.BlockSpec((1, 1, BLOCK), lambda i, *_: (i, 0, 0)),
                whole((length, BLOCK)),
                whole(tiles.shape),
                pl.BlockSpec((1, 8, WIDE), lambda i, *_: (i, 0, 0)),
            ],
            out_specs=[
                rows_spec(INNER),
                whole((length, width)),
                whole((PAIRS, BUCKETS, WIDE)),
            ],
            scratch_shapes=[
                pltpu.VMEM((INNER, length), jnp.bfloat16),
                pltpu.VMEM((length, width), jnp.float32),
                pltpu.VMEM((PAIRS, OFFSETS, BLOCK, WIDE), jnp.float32),
                pltpu.VMEM((PAIRS, BLOCK, WIDE), jnp.float32),
            ],
        ),
        out_shape=[
            jax.ShapeDtypeStruct((tokens, INNER), jnp.bfloat16),
            jax.ShapeDtypeStruct((length, width), jnp.bfloat16),
            jax.ShapeDtypeStruct((PAIRS, BUCKETS, WIDE), jnp.float32),
        ],
        compiler_params=pltpu.CompilerParams(vmem_limit_bytes=48 << 20),
        cost_estimate=pl.CostEstimate(
            flops=tokens * length * INNER * 10,
            bytes_accessed=12 << 20,
            transcendentals=tokens * length * 3,
        ),
        name="attend_backward",
    )(lows, highs, queries, grad_mixed, full, shared, own_rows, segment_wide, tiles, log_total)
    table = jnp.sum(bucket_sums.reshape(PAIRS, BUCKETS, 2, BLOCK), axis=3)
    return grad_query, grad_shared, table.transpose(1, 0, 2).reshape(BUCKETS, HEADS)


def attention_context(segment_row, first_pos, tokens, rel_bias):
    steps = tokens // BLOCK
    padded = jnp.pad(segment_row, (HALO, 0), constant_values=-1)
    padded = jnp.pad(padded, (0, HALO), constant_values=1000)
    window = lax.dynamic_slice_in_dim(padded, first_pos, tokens + 2 * HALO, 0)
    own = window[HALO : HALO + tokens].reshape(steps, 1, BLOCK)
    lows = jnp.sum(window[None, :] < own[:, 0, :1], axis=1, dtype=jnp.int32) // BLOCK
    ends = jnp.sum(window[None, :] <= own[:, 0, BLOCK - 1 :], axis=1, dtype=jnp.int32)
    highs = (ends + BLOCK - 1) // BLOCK
    segment_wide = jnp.broadcast_to(window[:, None], (window.shape[0], BLOCK))
    return lows, highs, own, segment_wide, bias_tiles(rel_bias)


def rms_forward(stream, gain_row):
    inverse = lax.rsqrt(jnp.mean(stream * stream, axis=1, keepdims=True) + epsilon)
    return (stream * inverse * gain_row, inverse)


def stream_backward(stream, inverse, scaled):
    return inverse * scaled - stream * inverse**3 * jnp.mean(scaled * stream, axis=1, keepdims=True)


def rms_backward(stream, inverse, gain_row, grad_normed):
    grad_gain = jnp.sum(grad_normed * stream * inverse, axis=0)
    return (stream_backward(stream, inverse, gain_row * grad_normed), grad_gain)


def gelu_tanh(values):
    return 0.5 * values * (1.0 + jnp.tanh(0.7978845608028654 * (values + 0.044715 * values**3)))


def times_rows(left_side, weight):
    return lax.dot_general(
        left_side, weight, (((1,), (1,)), ((), ())), preferred_element_type=jnp.float32
    )


def times_plain(left_side, weight):
    return jnp.dot(left_side, weight, preferred_element_type=jnp.float32)


def outer_sum(left_side, right_side):
    return lax.dot_general(
        left_side, right_side, (((0,), (0,)), ((), ())), preferred_element_type=jnp.float32
    )


def shift(value, axis, amount):
    count = lax.axis_size(axis)
    return lax.ppermute(value, axis, [(i, (i + amount) % count) for i in range(count)])


def slide(value, amount):
    count = lax.axis_size("z")
    pairs = [(i, i + amount) for i in range(count) if 0 <= i + amount < count]
    return lax.ppermute(value, "z", pairs)


def far_pair(near_start, near_end, distance):
    count = lax.axis_size("z")
    first_half = lax.axis_index("z") < distance
    sent = jnp.where(first_half, near_end, near_start)
    pairs = [(i, (i + distance) % count) for i in range(count)]
    got = lax.ppermute(sent, "z", pairs)
    return got


def far_split(got, distance):
    first_half = lax.axis_index("z") < distance
    none = jnp.zeros_like(got)
    return jnp.where(first_half, none, got), jnp.where(first_half, got, none)


def halo_pieces(tokens):
    pieces = []
    distance, covered = 1, 0
    while covered < HALO:
        span = min(tokens, HALO - covered)
        needed = min(span, -(-(REACH - covered) // 16) * 16)
        pieces.append((distance, span, needed))
        distance, covered = distance + 1, covered + span
    return pieces


def with_neighbours(own):
    tokens = own.shape[0]
    before, after = [], []
    for distance, span, needed in halo_pieces(tokens):
        if distance < lax.axis_size("z"):
            if 2 * distance == lax.axis_size("z"):
                left, right = far_split(
                    far_pair(own[:needed], own[tokens - needed :], distance), distance
                )
            else:
                left = slide(own[tokens - needed :], distance)
                right = slide(own[:needed], -distance)
            before.append(jnp.pad(left, ((span - needed, 0), (0, 0))))
            after.append(jnp.pad(right, ((0, span - needed), (0, 0))))
        else:
            empty = jnp.zeros((span, own.shape[1]), own.dtype)
            before.append(empty)
            after.append(empty)
    return jnp.concatenate(before[::-1] + [own] + after, axis=0)


def start_back(window, tokens):
    moved = []
    covered = 0
    for distance, span, needed in halo_pieces(tokens):
        if distance < lax.axis_size("z"):
            left_end = HALO - covered
            right_start = HALO + tokens + covered
            left = window[left_end - needed : left_end]
            right = window[right_start : right_start + needed]
            if 2 * distance == lax.axis_size("z"):
                moved.append((far_pair(left, right, distance),))
            else:
                moved.append((slide(left, -distance), slide(right, distance)))
        covered += span
    return window[HALO : HALO + tokens], moved


def finish_back(own, moved):
    tokens = own.shape[0]
    total = own.astype(jnp.float32)
    for distance, pair in enumerate(moved, 1):
        if len(pair) == 1:
            ahead, back = far_split(pair[0], distance)
        else:
            back, ahead = pair
        needed = back.shape[0]
        total = total + jnp.pad(back.astype(jnp.float32), ((tokens - needed, 0), (0, 0)))
        total = total + jnp.pad(ahead.astype(jnp.float32), ((0, tokens - needed), (0, 0)))
    return total


def hop(value, axis, bit=1):
    pairs = [(i, i ^ bit) for i in range(lax.axis_size(axis))]
    return value + lax.ppermute(value, axis, pairs)


def pick(value, index, axis):
    return lax.dynamic_index_in_dim(value, index, axis, keepdims=False)


def stage_sends(value, axis_name, axis):
    count, here = lax.axis_size(axis_name), lax.axis_index(axis_name)
    return [pick(value, (here + k) % count, axis) for k in range(1, count)]


def stage_moves(sends, axis_name):
    return [shift(sent, axis_name, k + 1) for k, sent in enumerate(sends)]


def gelu_parts(values):
    squared = values * values
    slope = jnp.tanh(0.7978845608028654 * (values + 0.044715 * values * squared))
    active = 0.5 * values * (1.0 + slope)
    inner = 0.7978845608028654 * (1.0 + 3.0 * 0.044715 * squared)
    return active, 0.5 * (1.0 + slope) + 0.5 * values * (1.0 - slope * slope) * inner


def turned_rows(core_ref, kept_ref, sent_ref, stage_ref, sems):
    mine, unit = core_ref[0], core_ref[1]
    parts = FORWARD_TILE // TILE

    def copy(lane, part, place, at, where):
        spot = pl.ds(pl.multiple_of(at * TILE, TILE), TILE)
        source = stage_ref.at[where, lane, part * TILE : (part + 1) * TILE, :]
        return pltpu.make_async_copy(source, place.at[spot, :], sems.at[where, lane, part])

    def put(lane, kind, step, turned):
        slot = step % 2
        stage_ref[slot, lane] = turned
        for part in range(parts):
            target = ATTENTION_TILES + kind * (FF // TILE) + step * parts + part
            own = (target // unit) % 2 == mine
            at = (target // (2 * unit)) * unit + target % unit

            @pl.when(own)
            def _(part=part, at=at):
                copy(lane, part, kept_ref, at, slot).start()

            @pl.when(jnp.logical_not(own))
            def _(part=part, at=at):
                copy(lane, part, sent_ref, at, slot).start()

    def wait(lanes, where):
        for lane in range(lanes):
            for part in range(parts):
                copy(lane, part, kept_ref, 0, where).wait()

    return put, wait


def ffn_forward_body(core_ref, *refs):
    normed_ref, middle_ref, gelu_ref, linear_ref, down_ref = refs[:5]
    result_ref, gelu_factor_ref, linear_factor_ref, kept_ref, sent_ref, stage_ref, sems = refs[5:]
    step = pl.program_id(0)
    put, wait = turned_rows(core_ref, kept_ref, sent_ref, stage_ref, sems)

    @pl.when(step == 0)
    def _():
        result_ref[...] = middle_ref[...]

    @pl.when(step >= 2)
    def _():
        wait(1, step % 2)

    active, slope = gelu_parts(times_rows(normed_ref[...], gelu_ref[...]))
    linear = times_rows(normed_ref[...], linear_ref[...])
    gelu_factor_ref[...] = slope * linear
    linear_factor_ref[...] = active
    hidden = (active * linear).astype(jnp.bfloat16)
    put(0, 2, step, hidden.T)
    result_ref[...] += times_plain(hidden, down_ref[...])

    @pl.when(step == pl.num_programs(0) - 1)
    def _():
        wait(1, 0)
        wait(1, 1)


def resident(shape):
    return pl.BlockSpec(shape, lambda *_: (0,) * len(shape), pipeline_mode=pl.Buffered(1))


def core_units():
    return jnp.stack([lax.axis_index("c").astype(jnp.int32), jnp.int32(unit_tiles(TILE))])


def hidden_weight(kind, width):
    first = (4 * INNER + kind * FF) // FORWARD_TILE
    return pl.BlockSpec((FORWARD_TILE, width), lambda i, *_: (first + i, 0))


def turned_scratch(lanes, tokens):
    return [
        pltpu.VMEM((2, lanes, FORWARD_TILE, tokens), jnp.bfloat16),
        pltpu.SemaphoreType.DMA((2, lanes, FORWARD_TILE // TILE)),
    ]


def ffn_forward(normed, middle, gathered):
    tokens, width = normed.shape
    half = (4 * INNER + 3 * FF) // 2
    hidden = pl.BlockSpec((tokens, FORWARD_TILE), lambda i, *_: (0, i))
    side = resident((tokens, width))
    anywhere = pl.BlockSpec(memory_space=pl.ANY)
    return pl.pallas_call(
        ffn_forward_body,
        grid_spec=pltpu.PrefetchScalarGridSpec(
            num_scalar_prefetch=1,
            grid=(FF // FORWARD_TILE,),
            in_specs=[side, side] + [hidden_weight(kind, width) for kind in range(3)],
            out_specs=[side, hidden, hidden, anywhere, anywhere],
            scratch_shapes=turned_scratch(1, tokens),
        ),
        out_shape=[
            jax.ShapeDtypeStruct((tokens, width), jnp.float32),
            jax.ShapeDtypeStruct((tokens, FF), jnp.float32),
            jax.ShapeDtypeStruct((tokens, FF), jnp.float32),
            jax.ShapeDtypeStruct((half, tokens), jnp.bfloat16),
            jax.ShapeDtypeStruct((half, tokens), jnp.bfloat16),
        ],
        compiler_params=pltpu.CompilerParams(vmem_limit_bytes=52 << 20),
        cost_estimate=pl.CostEstimate(
            flops=6 * tokens * FF * width,
            bytes_accessed=6 * FF * width + 10 * tokens * FF,
            transcendentals=tokens * FF,
        ),
        name="ffn_forward",
    )(core_units(), normed, middle, gathered, gathered, gathered)


def ffn_backward_body(core_ref, *refs):
    branch_ref, gelu_factor_ref, linear_factor_ref, gelu_ref, linear_ref, down_ref = refs[:6]
    grad_ref, kept_ref, sent_ref, stage_ref, sems = refs[8:]
    step = pl.program_id(0)
    put, wait = turned_rows(core_ref, kept_ref, sent_ref, stage_ref, sems)

    @pl.when(step == 0)
    def _():
        grad_ref[...] = jnp.zeros_like(grad_ref)

    @pl.when(step >= 2)
    def _():
        wait(2, step % 2)

    grad_hidden = times_rows(branch_ref[...], down_ref[...])
    grad_gelu = (grad_hidden * gelu_factor_ref[...]).astype(jnp.bfloat16)
    grad_linear = (grad_hidden * linear_factor_ref[...]).astype(jnp.bfloat16)
    put(0, 0, step, grad_gelu.T)
    put(1, 1, step, grad_linear.T)
    grad_ref[...] += times_plain(grad_gelu, gelu_ref[...]) + times_plain(
        grad_linear, linear_ref[...]
    )

    @pl.when(step == pl.num_programs(0) - 1)
    def _():
        wait(2, 0)
        wait(2, 1)


def unit_tiles(tile):
    rows = 4 * INNER + 3 * FF
    return rows // tile // (2 * lax.axis_size("y") * lax.axis_size("x"))


def ffn_backward(branch, gelu_factor, linear_factor, gathered, kept, sent):
    tokens, width = branch.shape
    hidden = pl.BlockSpec((tokens, FORWARD_TILE), lambda i, *_: (0, i))
    side = resident((tokens, width))
    anywhere = pl.BlockSpec(memory_space=pl.ANY)
    return pl.pallas_call(
        ffn_backward_body,
        grid_spec=pltpu.PrefetchScalarGridSpec(
            num_scalar_prefetch=1,
            grid=(FF // FORWARD_TILE,),
            in_specs=[side, hidden, hidden]
            + [hidden_weight(kind, width) for kind in range(3)]
            + [anywhere, anywhere],
            out_specs=[side, anywhere, anywhere],
            scratch_shapes=turned_scratch(2, tokens),
        ),
        out_shape=[
            jax.ShapeDtypeStruct((tokens, width), jnp.float32),
            jax.ShapeDtypeStruct(kept.shape, kept.dtype),
            jax.ShapeDtypeStruct(sent.shape, sent.dtype),
        ],
        input_output_aliases={7: 1, 8: 2},
        compiler_params=pltpu.CompilerParams(vmem_limit_bytes=52 << 20),
        cost_estimate=pl.CostEstimate(
            flops=6 * tokens * FF * width,
            bytes_accessed=6 * FF * width + 12 * tokens * FF,
            transcendentals=0,
        ),
        name="ffn_backward",
    )(core_units(), branch, gelu_factor, linear_factor, gathered, gathered, gathered, kept, sent)


def spots_of(unit_at, place_ref):
    here_y, here_x, size_y, size_x = place_ref[0], place_ref[1], place_ref[4], place_ref[5]
    row, column = unit_at // size_x, unit_at % size_x
    return (
        ((row + 2 * size_y - here_y - 1) % size_y, column),
        ((column + 2 * size_x - here_x - 1) % size_x, row),
    )


def weight_grads_body(chunks, tile, place_ref, *refs):
    own_ref, other_ref, normed_ref, branch_ref, other_normed_ref, other_branch_ref = refs[:6]
    stage_ref, sems = refs[-2:]
    step = pl.program_id(0)
    unit = place_ref[3]
    at = (step // unit * 2 + place_ref[2]) * unit + step % unit
    first, second = 4 * INNER // tile, (4 * INNER + 2 * FF) // tile
    slot = step % 2
    places = split_places(refs[6:-2], chunks)
    start, wait = place_copies(chunks, stage_ref, sems, places, tile)

    def put(product):
        stage_ref[slot, :, : CUTS[-1]] = product.astype(jnp.bfloat16)
        start(spots_of(step // unit, place_ref), unit, step % unit, step, slot)

    def both(side_ref, other_side_ref):
        return jnp.dot(
            own_ref[...], side_ref[:, : CUTS[-1]], preferred_element_type=jnp.float32
        ) + jnp.dot(
            other_ref[...], other_side_ref[:, : CUTS[-1]], preferred_element_type=jnp.float32
        )

    @pl.when(step < 2)
    def _():
        stage_ref[slot, :, CUTS[-1] :] = jnp.zeros((tile, PADDED - CUTS[-1]), jnp.bfloat16)

    @pl.when(step >= 2)
    def _():
        wait(slot)

    @pl.when(at < first)
    def _():
        put(jnp.zeros((tile, CUTS[-1]), jnp.float32))

    @pl.when((at >= first) & (at < second))
    def _():
        put(both(normed_ref, other_normed_ref))

    @pl.when(at >= second)
    def _():
        put(both(branch_ref, other_branch_ref))

    @pl.when(step == pl.num_programs(0) - 1)
    def _():
        wait(0)
        wait(1)


def split_places(refs, chunks):
    size_y, size_x, per = lax.axis_size("y"), lax.axis_size("x"), chunks // 2
    refs = list(refs)
    along_y = [refs[per * k : per * (k + 1)] for k in range(size_y)]
    refs = refs[per * size_y :]
    along_x = [refs[per * k : per * (k + 1)] for k in range(size_x)]
    return along_y, along_x, refs[per * size_x :]


def array_shapes(chunks, rows):
    columns = chunk_width(chunks)
    shapes = [(rows // lax.axis_size("y"), columns)] * (chunks // 2 * lax.axis_size("y"))
    shapes += [(rows // lax.axis_size("x"), columns)] * (chunks // 2 * lax.axis_size("x"))
    if chunks < 4:
        shapes.append((rows, PADDED - chunks * columns))
    return [jax.ShapeDtypeStruct(shape, jnp.bfloat16) for shape in shapes]


def place_copies(chunks, stage_ref, sems, places, tile):
    along = places[:2]
    rest = places[2]

    def copy(lane, place, row, where):
        start = lane * chunk_width(chunks)
        end = PADDED if lane == chunks else start + chunk_width(chunks)
        spot = pl.ds(pl.multiple_of(row * tile, tile), tile)
        return pltpu.make_async_copy(
            stage_ref.at[where, :, start:end], place.at[spot, :], sems.at[where, lane]
        )

    def start(spots, unit, inside, row, where):
        for chunk in range(chunks):
            which, position = spots[chunk % 2]
            for k, group in enumerate(along[chunk % 2]):

                @pl.when(which == k)
                def _(chunk=chunk, place=group[chunk // 2], at=position * unit + inside):
                    copy(chunk, place, at, where).start()

        for place in rest:
            copy(chunks, place, row, where).start()

    def wait(where):
        for chunk in range(chunks):
            copy(chunk, along[chunk % 2][0][chunk // 2], 0, where).wait()
        for place in rest:
            copy(chunks, place, 0, where).wait()

    return start, wait


def place_of(tile):
    return jnp.stack(
        [
            lax.axis_index("y").astype(jnp.int32),
            lax.axis_index("x").astype(jnp.int32),
            lax.axis_index("c").astype(jnp.int32),
            jnp.int32(unit_tiles(tile)),
            jnp.int32(lax.axis_size("y")),
            jnp.int32(lax.axis_size("x")),
        ]
    )


def half_side(tokens, at):
    return pl.BlockSpec(
        (tokens, PADDED), lambda i, *_: (at, 0), pipeline_mode=pl.Buffered(1)
    )


def weight_grads(chunks, own, other, sides):
    rows, tokens = own.shape
    tile = 512 if unit_tiles(256) % 2 == 0 else 256
    source = pl.BlockSpec((tile, tokens), lambda i, *_: (i, 0))
    halves = [half_side(tokens, 0), half_side(tokens, 1)]
    out_shape = array_shapes(chunks, rows)
    return pl.pallas_call(
        functools.partial(weight_grads_body, chunks, tile),
        grid_spec=pltpu.PrefetchScalarGridSpec(
            num_scalar_prefetch=1,
            grid=(rows // tile,),
            in_specs=[source, source] + halves * 2,
            out_specs=[pl.BlockSpec(memory_space=pl.ANY)] * len(out_shape),
            scratch_shapes=[
                pltpu.VMEM((2, tile, PADDED), jnp.bfloat16),
                pltpu.SemaphoreType.DMA((2, 5)),
            ],
        ),
        out_shape=out_shape,
        compiler_params=pltpu.CompilerParams(vmem_limit_bytes=40 << 20),
        cost_estimate=pl.CostEstimate(
            flops=4 * rows * tokens * CUTS[-1],
            bytes_accessed=4 * rows * tokens + 2 * rows * PADDED,
            transcendentals=0,
        ),
        name="weight_grads",
    )(place_of(tile), own, other, sides[0], sides[0], sides[1], sides[1])


def attention_fill_body(chunks, owners, place_ref, *refs):
    own_ref, other_ref, side_ref, other_side_ref = refs[:4]
    outs = refs[4 + (len(refs) - 6) // 2 : -2]
    stage_ref, sems = refs[-2:]
    step = pl.program_id(0)
    slot = step % 2
    start, wait = place_copies(chunks, stage_ref, sems, split_places(outs, chunks), INNER)

    def put():
        product = jnp.dot(
            own_ref[...].T, side_ref[:, : CUTS[-1]], preferred_element_type=jnp.float32
        ) + jnp.dot(
            other_ref[...].T, other_side_ref[:, : CUTS[-1]], preferred_element_type=jnp.float32
        )
        stage_ref[slot, :, : CUTS[-1]] = product.astype(jnp.bfloat16)
        stage_ref[slot, :, CUTS[-1] :] = jnp.zeros((INNER, PADDED - CUTS[-1]), jnp.bfloat16)
        start(spots_of(0, place_ref), 0, step, step, slot)

    @pl.when(place_ref[2] < owners)
    def _():
        @pl.when(step >= 2)
        def _():
            wait(slot)

        put()

        @pl.when(step == pl.num_programs(0) - 1)
        def _():
            wait(0)
            wait(1)


def attention_fill(chunks, arrays, own, other, sides):
    tokens = own.shape[0]
    unit_rows = unit_tiles(TILE) * TILE
    owners = 4 * INNER // unit_rows
    steps = unit_rows // INNER

    def column(i, place_ref):
        return 0, jnp.minimum(place_ref[2], owners - 1) * steps + i

    def half(i, place_ref):
        return jnp.where(column(i, place_ref)[1] < 3, 0, 1), 0

    anywhere = pl.BlockSpec(memory_space=pl.ANY)
    return pl.pallas_call(
        functools.partial(attention_fill_body, chunks, owners),
        grid_spec=pltpu.PrefetchScalarGridSpec(
            num_scalar_prefetch=1,
            grid=(steps,),
            in_specs=[pl.BlockSpec((tokens, INNER), column)] * 2
            + [pl.BlockSpec((tokens, PADDED), half)] * 2
            + [anywhere] * len(arrays),
            out_specs=[anywhere] * len(arrays),
            scratch_shapes=[
                pltpu.VMEM((2, INNER, PADDED), jnp.bfloat16),
                pltpu.SemaphoreType.DMA((2, 5)),
            ],
        ),
        out_shape=[jax.ShapeDtypeStruct(array.shape, array.dtype) for array in arrays],
        input_output_aliases={5 + k: k for k in range(len(arrays))},
        compiler_params=pltpu.CompilerParams(vmem_limit_bytes=32 << 20),
        cost_estimate=pl.CostEstimate(
            flops=4 * unit_rows * tokens * CUTS[-1],
            bytes_accessed=4 * unit_rows * tokens + 2 * unit_rows * PADDED,
            transcendentals=0,
        ),
        name="attention_fill",
    )(place_of(TILE), own, other, *sides, *arrays)


def tied(first, second):
    return lax.optimization_barrier((first, second))


def chunk_width(chunks):
    return PADDED // 4 if chunks == 4 else PADDED // 6


class Scatter:
    def __init__(self):
        self.waiting, self.flying, self.results = {}, {}, {}

    def push(self, name, route, kept, sends):
        self.waiting[name] = (route, kept, sends)

    def settle(self, values, *names):
        arrays, values = tied({name: self.flying[name][1:] for name in names}, values)
        moves = {}
        for name in names:
            route = self.flying.pop(name)[0]
            kept, moved = arrays[name]
            if not route:
                self.results[name] = kept.astype(jnp.float32) + sum(
                    part.astype(jnp.float32) for part in moved
                )
                continue
            total = total_of(kept, moved)
            total = total.reshape((lax.axis_size(route[0]), -1) + total.shape[-1:])
            sends = stage_sends(total, route[0], 0)
            moves[name] = (route, pick(total, lax.axis_index(route[0]), 0), sends)
        if moves and all(move[0] == ("z",) for move in moves.values()):
            kept = jnp.concatenate([move[1] for move in moves.values()], axis=-1)
            sends = [
                jnp.concatenate(parts, axis=-1) for parts in zip(*(m[2] for m in moves.values()))
            ]
            moves = {tuple(moves): (("z",), kept, sends)}
        arrays, values = tied({name: move[1:] for name, move in moves.items()}, values)
        for name, (route, *_) in moves.items():
            self.waiting[name] = (route,) + tuple(arrays[name])
        return values

    def start(self, values, *names):
        arrays, values = tied({name: self.waiting[name][1:] for name in names}, values)
        for name in names:
            route = self.waiting.pop(name)[0]
            kept, sends = arrays[name]
            self.flying[name] = (route[1:], kept, stage_moves(sends, route[0]))
        return values

    def step(self, values, *names):
        others = set(self.waiting)
        values = self.settle(values, *names)
        return self.start(values, *(name for name in self.waiting if name not in others))


def total_of(value, moved):
    total = value.astype(jnp.float32)
    for part in moved:
        total = total + part.astype(jnp.float32)
    return total.astype(jnp.bfloat16)


def fetch_rows(local_rows):
    return lax.all_gather(local_rows, DEVICES, axis=0, tiled=True)


def layer_forward(stream, gathered, gain_one, gain_two, gate_low, context):
    normed, inverse_one = rms_forward(stream, gain_one)
    normed_low = normed.astype(jnp.bfloat16)
    projected = times_rows(normed_low, gathered[: 3 * INNER]).astype(jnp.bfloat16)
    queries = projected[:, :INNER]
    parts = [projected[:, INNER:]]
    if gate_low is not None:
        parts.append(jnp.broadcast_to(gate_low[:, None], (stream.shape[0], BLOCK)))
    shared = with_neighbours(jnp.concatenate(parts, axis=1))
    attended, full, log_total = attend_forward(queries, shared, context)
    middle = stream + times_plain(attended, gathered[3 * INNER : 4 * INNER])
    normed_two, inverse_two = rms_forward(middle, gain_two)
    normed_two_low = normed_two.astype(jnp.bfloat16)
    result, *factors = ffn_forward(normed_two_low, middle, gathered)
    kept = (
        stream,
        inverse_one,
        normed_low,
        queries,
        shared,
        attended,
        full,
        log_total,
        middle,
        inverse_two,
        normed_two_low,
        factors,
    )
    return (result, kept)


def layer_backward(grad_out, kept, gathered, gain_one, gain_two, context, before):
    (
        stream,
        inverse_one,
        normed_low,
        queries,
        shared,
        attended,
        full,
        log_total,
        middle,
        inverse_two,
        normed_two_low,
        factors,
    ) = kept
    tokens = queries.shape[0]
    branch_low = grad_out.astype(jnp.bfloat16)
    sides = jnp.concatenate([normed_two_low, branch_low], axis=0)
    sides = jnp.pad(sides, ((0, 0), (0, PADDED - sides.shape[1])))
    sides = (sides, shift(sides, "c", 1))
    grad_normed_two, own, sent = ffn_backward(
        branch_low, factors[0], factors[1], gathered, factors[2], factors[3]
    )
    if before is not None:
        grad_normed_two, own, sent = before.step((grad_normed_two, own, sent), 0, 1)
    other = shift(sent, "c", 1)
    grad_middle, grad_gain_two = rms_backward(middle, inverse_two, gain_two, grad_normed_two)
    grad_middle = grad_out + grad_middle
    middle_low = grad_middle.astype(jnp.bfloat16)
    late_sides = jnp.concatenate([normed_low, middle_low], axis=0)
    late_sides = jnp.pad(late_sides, ((0, 0), (0, PADDED - late_sides.shape[1])))
    late_sides = (late_sides, shift(late_sides, "c", 1))
    grad_mixed = times_rows(middle_low, gathered[3 * INNER : 4 * INNER]).astype(jnp.bfloat16)
    grad_query, grad_shared, grad_table = attend_backward(
        queries, grad_mixed, full, shared, log_total, context
    )
    if before is not None:
        grad_query, grad_shared = before.settle((grad_query, grad_shared), 0, 1)
    grad_shared, own = lax.optimization_barrier((grad_shared, own))
    moving = start_back(grad_shared, tokens)
    chunks = 2 if before is None else 4
    arrays = weight_grads(chunks, own, other, sides)
    arrays, moving = lax.optimization_barrier((arrays, moving))
    if before is not None:
        arrays, moving = before.start((arrays, moving), (0, 1))
    grad_own = finish_back(*moving)
    grad_gate = grad_own[:, 2 * INNER :]
    grad_input_low = jnp.concatenate(
        [grad_query, grad_own[:, : 2 * INNER].astype(jnp.bfloat16)], axis=1
    )
    late = jnp.concatenate([grad_input_low, attended], axis=1)
    arrays = attention_fill(chunks, arrays, late, shift(late, "c", 1), late_sides)
    scatter = Scatter()
    along_y, along_x, rest = split_places(arrays, chunks)
    for chunk in range(chunks):
        route = ("y", "x", "z") if chunk % 2 == 0 else ("x", "y", "z")
        ordered = [group[chunk // 2] for group in (along_y, along_x)[chunk % 2]]
        scatter.push(chunk, route, ordered[-1], ordered[:-1])
    grad_input_low, grad_gate = scatter.start((grad_input_low, grad_gate), 0, 1)
    if rest:
        grad_input_low, grad_gate, rest = lax.optimization_barrier(
            (grad_input_low, grad_gate, rest)
        )
        rest = lax.psum_scatter(rest[0], ("y", "x", "z"), scatter_dimension=0, tiled=True)
    grad_normed = times_plain(grad_input_low, gathered[: 3 * INNER])
    grad_stream, grad_gain_one = rms_backward(stream, inverse_one, gain_one, grad_normed)
    return (grad_middle + grad_stream, grad_table, grad_gate, grad_gain_one, grad_gain_two, scatter, rest)


def per_device(
    inputs, layer3_rows, layer4_rows, norm_gains, gate_weight, rel_bias, segment_ids, cotangent
):
    seqs_here, tokens_here, width = inputs.shape
    first_pos = lax.axis_index("z") * tokens_here
    context = attention_context(segment_ids[0], first_pos, tokens_here, rel_bias)
    stream = inputs.reshape(tokens_here, width)
    gathered_three = fetch_rows(layer3_rows)
    after_three, kept_three = layer_forward(
        stream, gathered_three, norm_gains[0], norm_gains[1], None, context
    )
    gate_inverse = lax.rsqrt(jnp.mean(after_three * after_three, axis=1, keepdims=True) + epsilon)
    gate_normed = after_three * gate_inverse
    gate_logit = jnp.sum(gate_normed * gate_weight, axis=1) + gate_offset
    sigmoid_value = 1.0 / (1.0 + jnp.exp(-gate_logit))
    gate_mask = gate_scale * sigmoid_value
    gate_low = gate_mask.astype(jnp.bfloat16)
    gathered_four = fetch_rows(layer4_rows)
    after_four, kept_four = layer_forward(
        after_three, gathered_four, norm_gains[2], norm_gains[3], gate_low, context
    )
    grad_three_out, table_four, grad_gate, gain_four_one, gain_four_two, before, rest = (
        layer_backward(
            cotangent.reshape(tokens_here, width),
            kept_four,
            gathered_four,
            norm_gains[2],
            norm_gains[3],
            context,
            None,
        )
    )
    grad_logit = grad_gate[:, 0] * gate_scale * sigmoid_value * (1.0 - sigmoid_value)
    grad_gate_weight = jnp.sum(grad_logit[:, None] * gate_normed, axis=0)
    gate_stream = stream_backward(after_three, gate_inverse, grad_logit[:, None] * gate_weight)
    grad_input, table_three, unused, gain_three_one, gain_three_two, scatter, _ = layer_backward(
        grad_three_out + gate_stream,
        kept_three,
        gathered_three,
        norm_gains[0],
        norm_gains[1],
        context,
        before,
    )
    table = jnp.pad((table_three + table_four).reshape(1, -1), ((0, 0), (0, width - 6 * BUCKETS)))
    small_sums = jnp.stack(
        [gain_three_one, gain_three_two, gain_four_one, gain_four_two, grad_gate_weight, table[0]]
    )
    small = hop(small_sums, "c")
    small = before.settle(small, (0, 1))
    small = scatter.step(small, 0, 1)
    small = scatter.start(small, 2, 3)
    small = scatter.step(small, 0, 1)
    small, rest = scatter.settle((small, rest), (0, 1))
    small = scatter.step(small, 2, 3)
    for bit in range(1, lax.axis_size("z")):
        if bit & (bit - 1) == 0:
            small = hop(small, "z", bit)
    small = scatter.step(small, 2, 3)
    small = hop(small, "x")
    for bit in range(1, lax.axis_size("y")):
        if bit & (bit - 1) == 0:
            small = hop(small, "y", bit)
    summed = scatter.settle(small, (2, 3))
    local_three = jnp.concatenate([scatter.results[pair] for pair in ((0, 1), (2, 3))], axis=1)
    local_four = jnp.concatenate([before.results[(0, 1)], rest.astype(jnp.float32)], axis=1)
    local_three, local_four = local_three[:, :width], local_four[:, :width]
    return (
        after_four.reshape(inputs.shape),
        gate_mask.reshape(seqs_here, tokens_here),
        grad_input.reshape(inputs.shape),
        local_three,
        local_four,
        summed[:4],
        summed[4],
        summed[5, : 6 * BUCKETS].reshape(BUCKETS, HEADS),
    )


def solution(mesh):
    outer, inner = mesh.devices.shape
    fine = Mesh(mesh.devices.reshape(outer // 4, 2, 2, inner), DEVICES)
    batch = ("y", "x", "c")
    tokens = P(batch, "z", None)
    rows = P(DEVICES, None)
    return jax.shard_map(
        per_device,
        mesh=fine,
        in_specs=(tokens, rows, rows, P(), P(), P(), P(batch, None), tokens),
        out_specs=(tokens, P(batch, "z"), tokens, rows, rows, P(), P(), P()),
        check_vma=False,
    )
```

```python
import functools

import jax
import jax.numpy as jnp
from jax import lax
from jax.experimental import pallas as pl
from jax.experimental.pallas import tpu as pltpu
from jax.sharding import Mesh
from jax.sharding import PartitionSpec as P

HEADS = 6
PAIRS = 3
BLOCK = 128
WIDE = 2 * BLOCK
INNER = 384
BUCKETS = 32
FF = 3584
REACH = 799
HALO = 896
TILE = 256
ATTENTION_TILES = 4 * INNER // TILE
OFFSETS = 5
PADDED = 1536
FORWARD_TILE = 512
CUTS = (0, 1472)
DEVICES = ("y", "x", "c", "z")
epsilon = 1e-06
gate_scale = -30.0
gate_offset = -3.5
masked_out = -1e30
limits = (12, 16, 23, 32, 46, 64, 91)
both_last = (((1,), (1,)), ((), ()))


def bucket_of(relative):
    magnitude = jnp.abs(relative)
    beyond = jnp.zeros_like(magnitude)
    for bound_value in limits:
        beyond = beyond + (magnitude >= bound_value).astype(jnp.int32)
    inside = jnp.where(magnitude < 8, magnitude, 8 + beyond)
    return inside + 16 * (relative > 0).astype(jnp.int32)


def near_buckets(offset):
    if offset < 0:
        return range(1, 16)
    if offset > 0:
        return range(17, 32)
    return range(0, 32)


def tile_buckets(offset, width):
    key_at = lax.broadcasted_iota(jnp.int32, (BLOCK, width), 0)
    query_at = lax.broadcasted_iota(jnp.int32, (BLOCK, width), 1) % BLOCK
    return bucket_of(offset * BLOCK + key_at - query_at)


def bias_body(table_ref, tiles_ref):
    head = pl.program_id(0)
    tiles_ref[0, 0] = jnp.full((BLOCK, BLOCK), table_ref[15, head], jnp.float32)
    tiles_ref[0, 4] = jnp.full((BLOCK, BLOCK), table_ref[31, head], jnp.float32)
    for offset in (-1, 0, 1):
        buckets = tile_buckets(offset, BLOCK)
        tile = jnp.zeros((BLOCK, BLOCK), jnp.float32)
        for bucket in near_buckets(offset):
            tile = jnp.where(buckets == bucket, table_ref[bucket, head], tile)
        tiles_ref[0, offset + 2] = tile


def bias_tiles(rel_bias):
    return pl.pallas_call(
        bias_body,
        grid=(HEADS,),
        in_specs=[pl.BlockSpec(memory_space=pltpu.SMEM)],
        out_specs=pl.BlockSpec((1, OFFSETS, BLOCK, BLOCK), lambda h: (h, 0, 0, 0)),
        out_shape=jax.ShapeDtypeStruct((HEADS, OFFSETS, BLOCK, BLOCK), jnp.float32),
        name="bias_tiles",
    )(rel_bias)


def lane_masks():
    lane = lax.broadcasted_iota(jnp.int32, (BLOCK, BLOCK), 1)
    low = jnp.where(lane < 64, 1.0, 0.0).astype(jnp.bfloat16)
    high = jnp.where(lane < 64, 0.0, 1.0).astype(jnp.bfloat16)
    return low, high


def stacked(block, masks):
    low, high = masks
    return jnp.concatenate([block * low, block * high], axis=0)


def pair_cols(pair):
    return slice(pair * BLOCK, (pair + 1) * BLOCK)


def value_cols(pair):
    return slice(INNER + pair * BLOCK, INNER + (pair + 1) * BLOCK)


def block_rows(block):
    return pl.ds(pl.multiple_of(block * BLOCK, BLOCK), BLOCK)


def wide_rows(block):
    return pl.ds(pl.multiple_of(block * WIDE, WIDE), WIDE)


def fold(values):
    return values.reshape(values.shape[0] // 8, 8, WIDE)


def shift_tile(gated, rows, own_segment, segment_ref, shared_ref):
    same = segment_ref[rows, :] == own_segment
    inside = shared_ref[rows, 2 * INNER :].astype(jnp.float32) if gated else 0.0
    shift = jnp.where(same, inside, masked_out)
    return jnp.concatenate([shift, shift], axis=1)


def used_blocks(low_ref, high_ref):
    last = pl.num_programs(0) - 1
    return low_ref[0] // 2 * 2, (high_ref[last] + 1) // 2 * 2


def tile_offsets(block, own_block):
    return [jnp.clip(2 * block + k - own_block, -2, 2) + 2 for k in range(2)]


def bias_pair(bias_ref, pair, offsets):
    halves = [
        jnp.concatenate([bias_ref[2 * pair, at], bias_ref[2 * pair + 1, at]], axis=1)
        for at in offsets
    ]
    return jnp.concatenate(halves, axis=0)


def pick_heads(wide):
    return jnp.concatenate([wide[:64, :BLOCK], wide[64:, BLOCK:]], axis=0)


def forward_body(gated, low_ref, high_ref, *refs):
    query_ref, shared_ref, own_ref, segment_ref, bias_ref = refs[:5]
    mixed_ref, full_ref, total_ref, turned_ref, score_ref, sum_ref = refs[5:]
    step = pl.program_id(0)

    @pl.when(step == 0)
    def _():
        @pl.loop(*used_blocks(low_ref, high_ref))
        def _(block):
            rows = block_rows(block)
            turned_ref[:, rows] = shared_ref[rows, INNER : 2 * INNER].T

    first, last = low_ref[step] // 2, (high_ref[step] + 1) // 2
    own_block = HALO // BLOCK + step
    own_segment = own_ref[0]
    masks = lane_masks()
    queries = [stacked(query_ref[:, pair_cols(pair)], masks) for pair in range(PAIRS)]

    def scores(block, peaks):
        rows = wide_rows(block)
        shift = shift_tile(gated, rows, own_segment, segment_ref, shared_ref)
        offsets = tile_offsets(block, own_block)
        new_peaks = []
        for pair in range(PAIRS):
            score = lax.dot_general(
                shared_ref[rows, pair_cols(pair)],
                queries[pair],
                both_last,
                preferred_element_type=jnp.float32,
            )
            score = score + bias_pair(bias_ref, pair, offsets) + shift
            score_ref[pair, block] = score
            new_peaks.append(jnp.maximum(peaks[pair], jnp.max(fold(score), axis=0)))
        return tuple(new_peaks)

    start = jnp.full((8, WIDE), -3e38, jnp.float32)
    peaks = lax.fori_loop(first, last, scores, (start,) * PAIRS)
    peaks = [jnp.max(peak, axis=0, keepdims=True) for peak in peaks]
    sum_ref[...] = jnp.zeros_like(sum_ref)

    def mix(block, totals):
        new_totals = []
        for pair in range(PAIRS):
            weight = jnp.exp(score_ref[pair, block] - peaks[pair])
            new_totals.append(totals[pair] + jnp.sum(fold(weight), axis=0))
            sum_ref[pair] += jnp.dot(
                turned_ref[pair_cols(pair), wide_rows(block)],
                weight.astype(jnp.bfloat16),
                preferred_element_type=jnp.float32,
            )
        return tuple(new_totals)

    totals = lax.fori_loop(first, last, mix, (jnp.zeros((8, WIDE), jnp.float32),) * PAIRS)
    for pair in range(PAIRS):
        row_total = jnp.sum(totals[pair], axis=0, keepdims=True)
        mixed = pick_heads(sum_ref[pair] * (1.0 / row_total))
        full_ref[:, pair_cols(pair)] = mixed.T
        mixed_ref[:, pair_cols(pair)] = full_ref[:, pair_cols(pair)].astype(jnp.bfloat16)
        total_ref[0, pair : pair + 1, :] = peaks[pair] + jnp.log(row_total)


def whole(shape):
    return pl.BlockSpec(shape, lambda i, *_: (0,) * len(shape), pipeline_mode=pl.Buffered(1))


def rows_spec(width):
    return pl.BlockSpec((BLOCK, width), lambda i, *_: (i, 0))


def attend_forward(queries, shared, context):
    lows, highs, own_rows, segment_wide, tiles = context
    tokens, (length, width) = queries.shape[0], shared.shape
    steps, key_blocks = tokens // BLOCK, length // BLOCK
    return pl.pallas_call(
        functools.partial(forward_body, width > 2 * INNER),
        grid_spec=pltpu.PrefetchScalarGridSpec(
            num_scalar_prefetch=2,
            grid=(steps,),
            in_specs=[
                rows_spec(INNER),
                whole((length, width)),
                pl.BlockSpec((1, 1, BLOCK), lambda i, *_: (i, 0, 0)),
                whole((length, BLOCK)),
                whole(tiles.shape),
            ],
            out_specs=[
                rows_spec(INNER),
                rows_spec(INNER),
                pl.BlockSpec((1, 8, WIDE), lambda i, *_: (i, 0, 0)),
            ],
            scratch_shapes=[
                pltpu.VMEM((INNER, length), jnp.bfloat16),
                pltpu.VMEM((PAIRS, key_blocks // 2, WIDE, WIDE), jnp.float32),
                pltpu.VMEM((PAIRS, BLOCK, WIDE), jnp.float32),
            ],
        ),
        out_shape=[
            jax.ShapeDtypeStruct((tokens, INNER), jnp.bfloat16),
            jax.ShapeDtypeStruct((tokens, INNER), jnp.float32),
            jax.ShapeDtypeStruct((steps, 8, WIDE), jnp.float32),
        ],
        compiler_params=pltpu.CompilerParams(vmem_limit_bytes=40 << 20),
        cost_estimate=pl.CostEstimate(
            flops=tokens * length * INNER * 4,
            bytes_accessed=8 << 20,
            transcendentals=tokens * length * 3,
        ),
        name="attend_forward",
    )(lows, highs, queries, shared, own_rows, segment_wide, tiles)


def backward_body(gated, low_ref, high_ref, *refs):
    query_ref, grad_ref, full_ref, shared_ref, own_ref, segment_ref, bias_ref, total_ref = refs[:8]
    grad_query_ref, grad_shared_ref, bucket_ref = refs[8:11]
    turned_ref, sum_ref, bias_sum_ref, turn_sum_ref = refs[11:]
    step = pl.program_id(0)

    @pl.when(step == 0)
    def _():
        bias_sum_ref[...] = jnp.zeros_like(bias_sum_ref)

        @pl.loop(*used_blocks(low_ref, high_ref))
        def _(block):
            rows = block_rows(block)
            turned_ref[:, rows] = shared_ref[rows, :INNER].T
            sum_ref[rows, :] = jnp.zeros((BLOCK, sum_ref.shape[1]), jnp.float32)

    first, last = low_ref[step] // 2, (high_ref[step] + 1) // 2
    own_block = HALO // BLOCK + step
    own_segment = own_ref[0]
    masks = lane_masks()
    queries = [stacked(query_ref[:, pair_cols(pair)], masks) for pair in range(PAIRS)]
    grads = [stacked(grad_ref[:, pair_cols(pair)], masks) for pair in range(PAIRS)]
    totals = [total_ref[0, pair : pair + 1, :] for pair in range(PAIRS)]

    deltas = []
    for pair in range(PAIRS):
        cols = pair_cols(pair)
        product = (grad_ref[:, cols].astype(jnp.float32) * full_ref[:, cols]).T
        halves = [jnp.sum(half, axis=0, keepdims=True) for half in (product[:64], product[64:])]
        deltas.append(jnp.concatenate(halves, axis=1))
    turn_sum_ref[...] = jnp.zeros_like(turn_sum_ref)

    @pl.loop(first, last)
    def _(block):
        rows = wide_rows(block)
        shift = shift_tile(gated, rows, own_segment, segment_ref, shared_ref)
        offsets = tile_offsets(block, own_block)
        gate_part = jnp.zeros((WIDE, BLOCK), jnp.float32)
        for pair in range(PAIRS):
            cols = pair_cols(pair)
            score = lax.dot_general(
                shared_ref[rows, cols], queries[pair], both_last, preferred_element_type=jnp.float32
            )
            pull = lax.dot_general(
                shared_ref[rows, value_cols(pair)],
                grads[pair],
                both_last,
                preferred_element_type=jnp.float32,
            )
            prob = jnp.exp(score + bias_pair(bias_ref, pair, offsets) + shift - totals[pair])
            sum_ref[rows, value_cols(pair)] += jnp.dot(
                prob.astype(jnp.bfloat16), grads[pair], preferred_element_type=jnp.float32
            )
            grad_score = prob * (pull - deltas[pair])
            bias_sum_ref[pair, offsets[0]] += grad_score[:BLOCK]
            bias_sum_ref[pair, offsets[1]] += grad_score[BLOCK:]
            if gated:
                gate_part = gate_part + (grad_score[:, :BLOCK] + grad_score[:, BLOCK:])
            score_low = grad_score.astype(jnp.bfloat16)
            sum_ref[rows, cols] += jnp.dot(
                score_low, queries[pair], preferred_element_type=jnp.float32
            )
            turn_sum_ref[pair] += jnp.dot(
                turned_ref[cols, rows], score_low, preferred_element_type=jnp.float32
            )
        if gated:
            sum_ref[rows, 2 * INNER :] += gate_part

    for pair in range(PAIRS):
        grad_query_ref[:, pair_cols(pair)] = pick_heads(turn_sum_ref[pair]).T.astype(jnp.bfloat16)

    @pl.when(step == pl.num_programs(0) - 1)
    def _():
        grad_shared_ref[...] = jnp.zeros_like(grad_shared_ref)

        @pl.loop(*used_blocks(low_ref, high_ref))
        def _(block):
            rows = block_rows(block)
            both = slice(0, 2 * INNER)
            grad_shared_ref[rows, both] = sum_ref[rows, both].astype(jnp.bfloat16)
            if gated:
                gate_total = jnp.sum(sum_ref[rows, 2 * INNER :], axis=1, keepdims=True)
                grad_shared_ref[rows, 2 * INNER :] = jnp.broadcast_to(
                    gate_total, (BLOCK, BLOCK)
                ).astype(jnp.bfloat16)

        tables = {offset: tile_buckets(offset, WIDE) for offset in (-1, 0, 1)}

        @pl.loop(0, PAIRS)
        def _(pair):
            for bucket in range(BUCKETS):
                part = jnp.zeros((8, WIDE), jnp.float32)
                for offset in (-1, 0, 1):
                    if bucket in near_buckets(offset):
                        chosen = jnp.where(
                            tables[offset] == bucket, bias_sum_ref[pair, offset + 2], 0.0
                        )
                        part = part + jnp.sum(fold(chosen), axis=0)
                if bucket == 15:
                    part = part + jnp.sum(fold(bias_sum_ref[pair, 0]), axis=0)
                if bucket == 31:
                    part = part + jnp.sum(fold(bias_sum_ref[pair, 4]), axis=0)
                bucket_ref[pair, bucket : bucket + 1, :] = jnp.sum(part, axis=0, keepdims=True)


def attend_backward(queries, grad_mixed, full, shared, log_total, context):
    lows, highs, own_rows, segment_wide, tiles = context
    tokens, (length, width) = queries.shape[0], shared.shape
    steps = tokens // BLOCK
    grad_query, grad_shared, bucket_sums = pl.pallas_call(
        functools.partial(backward_body, width > 2 * INNER),
        grid_spec=pltpu.PrefetchScalarGridSpec(
            num_scalar_prefetch=2,
            grid=(steps,),
            in_specs=[
                rows_spec(INNER),
                rows_spec(INNER),
                rows_spec(INNER),
                whole((length, width)),
                pl.BlockSpec((1, 1, BLOCK), lambda i, *_: (i, 0, 0)),
                whole((length, BLOCK)),
                whole(tiles.shape),
                pl.BlockSpec((1, 8, WIDE), lambda i, *_: (i, 0, 0)),
            ],
            out_specs=[
                rows_spec(INNER),
                whole((length, width)),
                whole((PAIRS, BUCKETS, WIDE)),
            ],
            scratch_shapes=[
                pltpu.VMEM((INNER, length), jnp.bfloat16),
                pltpu.VMEM((length, width), jnp.float32),
                pltpu.VMEM((PAIRS, OFFSETS, BLOCK, WIDE), jnp.float32),
                pltpu.VMEM((PAIRS, BLOCK, WIDE), jnp.float32),
            ],
        ),
        out_shape=[
            jax.ShapeDtypeStruct((tokens, INNER), jnp.bfloat16),
            jax.ShapeDtypeStruct((length, width), jnp.bfloat16),
            jax.ShapeDtypeStruct((PAIRS, BUCKETS, WIDE), jnp.float32),
        ],
        compiler_params=pltpu.CompilerParams(vmem_limit_bytes=48 << 20),
        cost_estimate=pl.CostEstimate(
            flops=tokens * length * INNER * 10,
            bytes_accessed=12 << 20,
            transcendentals=tokens * length * 3,
        ),
        name="attend_backward",
    )(lows, highs, queries, grad_mixed, full, shared, own_rows, segment_wide, tiles, log_total)
    table = jnp.sum(bucket_sums.reshape(PAIRS, BUCKETS, 2, BLOCK), axis=3)
    return grad_query, grad_shared, table.transpose(1, 0, 2).reshape(BUCKETS, HEADS)


def attention_context(segment_row, first_pos, tokens, rel_bias):
    steps = tokens // BLOCK
    padded = jnp.pad(segment_row, (HALO, 0), constant_values=-1)
    padded = jnp.pad(padded, (0, HALO), constant_values=1000)
    window = lax.dynamic_slice_in_dim(padded, first_pos, tokens + 2 * HALO, 0)
    own = window[HALO : HALO + tokens].reshape(steps, 1, BLOCK)
    lows = jnp.sum(window[None, :] < own[:, 0, :1], axis=1, dtype=jnp.int32) // BLOCK
    ends = jnp.sum(window[None, :] <= own[:, 0, BLOCK - 1 :], axis=1, dtype=jnp.int32)
    highs = (ends + BLOCK - 1) // BLOCK
    segment_wide = jnp.broadcast_to(window[:, None], (window.shape[0], BLOCK))
    return lows, highs, own, segment_wide, bias_tiles(rel_bias)


def rms_forward(stream, gain_row):
    inverse = lax.rsqrt(jnp.mean(stream * stream, axis=1, keepdims=True) + epsilon)
    return (stream * inverse * gain_row, inverse)


def stream_backward(stream, inverse, scaled):
    return inverse * scaled - stream * inverse**3 * jnp.mean(scaled * stream, axis=1, keepdims=True)


def rms_backward(stream, inverse, gain_row, grad_normed):
    grad_gain = jnp.sum(grad_normed * stream * inverse, axis=0)
    return (stream_backward(stream, inverse, gain_row * grad_normed), grad_gain)


def gelu_tanh(values):
    return 0.5 * values * (1.0 + jnp.tanh(0.7978845608028654 * (values + 0.044715 * values**3)))


def times_rows(left_side, weight):
    return lax.dot_general(
        left_side, weight, (((1,), (1,)), ((), ())), preferred_element_type=jnp.float32
    )


def times_plain(left_side, weight):
    return jnp.dot(left_side, weight, preferred_element_type=jnp.float32)


def outer_sum(left_side, right_side):
    return lax.dot_general(
        left_side, right_side, (((0,), (0,)), ((), ())), preferred_element_type=jnp.float32
    )


def shift(value, axis, amount):
    count = lax.axis_size(axis)
    return lax.ppermute(value, axis, [(i, (i + amount) % count) for i in range(count)])


def slide(value, amount):
    count = lax.axis_size("z")
    pairs = [(i, i + amount) for i in range(count) if 0 <= i + amount < count]
    return lax.ppermute(value, "z", pairs)


def far_pair(near_start, near_end, distance):
    count = lax.axis_size("z")
    first_half = lax.axis_index("z") < distance
    sent = jnp.where(first_half, near_end, near_start)
    pairs = [(i, (i + distance) % count) for i in range(count)]
    got = lax.ppermute(sent, "z", pairs)
    return got


def far_split(got, distance):
    first_half = lax.axis_index("z") < distance
    none = jnp.zeros_like(got)
    return jnp.where(first_half, none, got), jnp.where(first_half, got, none)


def halo_pieces(tokens):
    pieces = []
    distance, covered = 1, 0
    while covered < HALO:
        span = min(tokens, HALO - covered)
        needed = min(span, -(-(REACH - covered) // 16) * 16)
        pieces.append((distance, span, needed))
        distance, covered = distance + 1, covered + span
    return pieces


def with_neighbours(own):
    tokens = own.shape[0]
    before, after = [], []
    for distance, span, needed in halo_pieces(tokens):
        if distance < lax.axis_size("z"):
            if 2 * distance == lax.axis_size("z"):
                left, right = far_split(
                    far_pair(own[:needed], own[tokens - needed :], distance), distance
                )
            else:
                left = slide(own[tokens - needed :], distance)
                right = slide(own[:needed], -distance)
            before.append(jnp.pad(left, ((span - needed, 0), (0, 0))))
            after.append(jnp.pad(right, ((0, span - needed), (0, 0))))
        else:
            empty = jnp.zeros((span, own.shape[1]), own.dtype)
            before.append(empty)
            after.append(empty)
    return jnp.concatenate(before[::-1] + [own] + after, axis=0)


def start_back(window, tokens):
    moved = []
    covered = 0
    for distance, span, needed in halo_pieces(tokens):
        if distance < lax.axis_size("z"):
            left_end = HALO - covered
            right_start = HALO + tokens + covered
            left = window[left_end - needed : left_end]
            right = window[right_start : right_start + needed]
            if 2 * distance == lax.axis_size("z"):
                moved.append((far_pair(left, right, distance),))
            else:
                moved.append((slide(left, -distance), slide(right, distance)))
        covered += span
    return window[HALO : HALO + tokens], moved


def finish_back(own, moved):
    tokens = own.shape[0]
    total = own.astype(jnp.float32)
    for distance, pair in enumerate(moved, 1):
        if len(pair) == 1:
            ahead, back = far_split(pair[0], distance)
        else:
            back, ahead = pair
        needed = back.shape[0]
        total = total + jnp.pad(back.astype(jnp.float32), ((tokens - needed, 0), (0, 0)))
        total = total + jnp.pad(ahead.astype(jnp.float32), ((0, tokens - needed), (0, 0)))
    return total


def hop(value, axis, bit=1):
    pairs = [(i, i ^ bit) for i in range(lax.axis_size(axis))]
    return value + lax.ppermute(value, axis, pairs)


def pick(value, index, axis):
    return lax.dynamic_index_in_dim(value, index, axis, keepdims=False)


def stage_sends(value, axis_name, axis):
    count, here = lax.axis_size(axis_name), lax.axis_index(axis_name)
    return [pick(value, (here + k) % count, axis) for k in range(1, count)]


def stage_moves(sends, axis_name):
    return [shift(sent, axis_name, k + 1) for k, sent in enumerate(sends)]


def gelu_parts(values):
    squared = values * values
    slope = jnp.tanh(0.7978845608028654 * (values + 0.044715 * values * squared))
    active = 0.5 * values * (1.0 + slope)
    inner = 0.7978845608028654 * (1.0 + 3.0 * 0.044715 * squared)
    return active, 0.5 * (1.0 + slope) + 0.5 * values * (1.0 - slope * slope) * inner


def turned_rows(core_ref, kept_ref, sent_ref, stage_ref, sems):
    mine, unit = core_ref[0], core_ref[1]
    parts = FORWARD_TILE // TILE

    def copy(lane, part, place, at, where):
        spot = pl.ds(pl.multiple_of(at * TILE, TILE), TILE)
        source = stage_ref.at[where, lane, part * TILE : (part + 1) * TILE, :]
        return pltpu.make_async_copy(source, place.at[spot, :], sems.at[where, lane, part])

    def put(lane, kind, step, turned):
        slot = step % 2
        stage_ref[slot, lane] = turned
        for part in range(parts):
            target = ATTENTION_TILES + kind * (FF // TILE) + step * parts + part
            own = (target // unit) % 2 == mine
            at = (target // (2 * unit)) * unit + target % unit

            @pl.when(own)
            def _(part=part, at=at):
                copy(lane, part, kept_ref, at, slot).start()

            @pl.when(jnp.logical_not(own))
            def _(part=part, at=at):
                copy(lane, part, sent_ref, at, slot).start()

    def wait(lanes, where):
        for lane in range(lanes):
            for part in range(parts):
                copy(lane, part, kept_ref, 0, where).wait()

    return put, wait


def ffn_forward_body(core_ref, *refs):
    normed_ref, middle_ref, gelu_ref, linear_ref, down_ref = refs[:5]
    result_ref, gelu_factor_ref, linear_factor_ref, kept_ref, sent_ref, stage_ref, sems = refs[5:]
    step = pl.program_id(0)
    put, wait = turned_rows(core_ref, kept_ref, sent_ref, stage_ref, sems)

    @pl.when(step == 0)
    def _():
        result_ref[...] = middle_ref[...]

    @pl.when(step >= 2)
    def _():
        wait(1, step % 2)

    active, slope = gelu_parts(times_rows(normed_ref[...], gelu_ref[...]))
    linear = times_rows(normed_ref[...], linear_ref[...])
    gelu_factor_ref[...] = slope * linear
    linear_factor_ref[...] = active
    hidden = (active * linear).astype(jnp.bfloat16)
    put(0, 2, step, hidden.T)
    result_ref[...] += times_plain(hidden, down_ref[...])

    @pl.when(step == pl.num_programs(0) - 1)
    def _():
        wait(1, 0)
        wait(1, 1)


def resident(shape):
    return pl.BlockSpec(shape, lambda *_: (0,) * len(shape), pipeline_mode=pl.Buffered(1))


def core_units():
    return jnp.stack([lax.axis_index("c").astype(jnp.int32), jnp.int32(unit_tiles(TILE))])


def hidden_weight(kind, width):
    first = (4 * INNER + kind * FF) // FORWARD_TILE
    return pl.BlockSpec((FORWARD_TILE, width), lambda i, *_: (first + i, 0))


def turned_scratch(lanes, tokens):
    return [
        pltpu.VMEM((2, lanes, FORWARD_TILE, tokens), jnp.bfloat16),
        pltpu.SemaphoreType.DMA((2, lanes, FORWARD_TILE // TILE)),
    ]


def ffn_forward(normed, middle, gathered):
    tokens, width = normed.shape
    half = (4 * INNER + 3 * FF) // 2
    hidden = pl.BlockSpec((tokens, FORWARD_TILE), lambda i, *_: (0, i))
    side = resident((tokens, width))
    anywhere = pl.BlockSpec(memory_space=pl.ANY)
    return pl.pallas_call(
        ffn_forward_body,
        grid_spec=pltpu.PrefetchScalarGridSpec(
            num_scalar_prefetch=1,
            grid=(FF // FORWARD_TILE,),
            in_specs=[side, side] + [hidden_weight(kind, width) for kind in range(3)],
            out_specs=[side, hidden, hidden, anywhere, anywhere],
            scratch_shapes=turned_scratch(1, tokens),
        ),
        out_shape=[
            jax.ShapeDtypeStruct((tokens, width), jnp.float32),
            jax.ShapeDtypeStruct((tokens, FF), jnp.float32),
            jax.ShapeDtypeStruct((tokens, FF), jnp.float32),
            jax.ShapeDtypeStruct((half, tokens), jnp.bfloat16),
            jax.ShapeDtypeStruct((half, tokens), jnp.bfloat16),
        ],
        compiler_params=pltpu.CompilerParams(vmem_limit_bytes=52 << 20),
        cost_estimate=pl.CostEstimate(
            flops=6 * tokens * FF * width,
            bytes_accessed=6 * FF * width + 10 * tokens * FF,
            transcendentals=tokens * FF,
        ),
        name="ffn_forward",
    )(core_units(), normed, middle, gathered, gathered, gathered)


def ffn_backward_body(core_ref, *refs):
    branch_ref, gelu_factor_ref, linear_factor_ref, gelu_ref, linear_ref, down_ref = refs[:6]
    grad_ref, kept_ref, sent_ref, stage_ref, sems = refs[8:]
    step = pl.program_id(0)
    put, wait = turned_rows(core_ref, kept_ref, sent_ref, stage_ref, sems)

    @pl.when(step == 0)
    def _():
        grad_ref[...] = jnp.zeros_like(grad_ref)

    @pl.when(step >= 2)
    def _():
        wait(2, step % 2)

    grad_hidden = times_rows(branch_ref[...], down_ref[...])
    grad_gelu = (grad_hidden * gelu_factor_ref[...]).astype(jnp.bfloat16)
    grad_linear = (grad_hidden * linear_factor_ref[...]).astype(jnp.bfloat16)
    put(0, 0, step, grad_gelu.T)
    put(1, 1, step, grad_linear.T)
    grad_ref[...] += times_plain(grad_gelu, gelu_ref[...]) + times_plain(
        grad_linear, linear_ref[...]
    )

    @pl.when(step == pl.num_programs(0) - 1)
    def _():
        wait(2, 0)
        wait(2, 1)


def unit_tiles(tile):
    rows = 4 * INNER + 3 * FF
    return rows // tile // (2 * lax.axis_size("y") * lax.axis_size("x"))


def ffn_backward(branch, gelu_factor, linear_factor, gathered, kept, sent):
    tokens, width = branch.shape
    hidden = pl.BlockSpec((tokens, FORWARD_TILE), lambda i, *_: (0, i))
    side = resident((tokens, width))
    anywhere = pl.BlockSpec(memory_space=pl.ANY)
    return pl.pallas_call(
        ffn_backward_body,
        grid_spec=pltpu.PrefetchScalarGridSpec(
            num_scalar_prefetch=1,
            grid=(FF // FORWARD_TILE,),
            in_specs=[side, hidden, hidden]
            + [hidden_weight(kind, width) for kind in range(3)]
            + [anywhere, anywhere],
            out_specs=[side, anywhere, anywhere],
            scratch_shapes=turned_scratch(2, tokens),
        ),
        out_shape=[
            jax.ShapeDtypeStruct((tokens, width), jnp.float32),
            jax.ShapeDtypeStruct(kept.shape, kept.dtype),
            jax.ShapeDtypeStruct(sent.shape, sent.dtype),
        ],
        input_output_aliases={7: 1, 8: 2},
        compiler_params=pltpu.CompilerParams(vmem_limit_bytes=52 << 20),
        cost_estimate=pl.CostEstimate(
            flops=6 * tokens * FF * width,
            bytes_accessed=6 * FF * width + 12 * tokens * FF,
            transcendentals=0,
        ),
        name="ffn_backward",
    )(core_units(), branch, gelu_factor, linear_factor, gathered, gathered, gathered, kept, sent)


def spots_of(unit_at, place_ref):
    here_y, here_x, size_y, size_x = place_ref[0], place_ref[1], place_ref[4], place_ref[5]
    row, column = unit_at // size_x, unit_at % size_x
    return (
        ((row + 2 * size_y - here_y - 1) % size_y, column),
        ((column + 2 * size_x - here_x - 1) % size_x, row),
    )


def weight_grads_body(chunks, tile, place_ref, *refs):
    own_ref, other_ref, normed_ref, branch_ref, other_normed_ref, other_branch_ref = refs[:6]
    stage_ref, sems = refs[-2:]
    step = pl.program_id(0)
    unit = place_ref[3]
    at = (step // unit * 2 + place_ref[2]) * unit + step % unit
    first, second = 4 * INNER // tile, (4 * INNER + 2 * FF) // tile
    slot = step % 2
    places = split_places(refs[6:-2], chunks)
    start, wait = place_copies(chunks, stage_ref, sems, places, tile)

    def put(product):
        stage_ref[slot, :, : CUTS[-1]] = product.astype(jnp.bfloat16)
        start(spots_of(step // unit, place_ref), unit, step % unit, step, slot)

    def both(side_ref, other_side_ref):
        return jnp.dot(
            own_ref[...], side_ref[:, : CUTS[-1]], preferred_element_type=jnp.float32
        ) + jnp.dot(
            other_ref[...], other_side_ref[:, : CUTS[-1]], preferred_element_type=jnp.float32
        )

    @pl.when(step < 2)
    def _():
        stage_ref[slot, :, CUTS[-1] :] = jnp.zeros((tile, PADDED - CUTS[-1]), jnp.bfloat16)

    @pl.when(step >= 2)
    def _():
        wait(slot)

    @pl.when(at < first)
    def _():
        put(jnp.zeros((tile, CUTS[-1]), jnp.float32))

    @pl.when((at >= first) & (at < second))
    def _():
        put(both(normed_ref, other_normed_ref))

    @pl.when(at >= second)
    def _():
        put(both(branch_ref, other_branch_ref))

    @pl.when(step == pl.num_programs(0) - 1)
    def _():
        wait(0)
        wait(1)


def split_places(refs, chunks):
    size_y, size_x, per = lax.axis_size("y"), lax.axis_size("x"), chunks // 2
    refs = list(refs)
    along_y = [refs[per * k : per * (k + 1)] for k in range(size_y)]
    refs = refs[per * size_y :]
    along_x = [refs[per * k : per * (k + 1)] for k in range(size_x)]
    return along_y, along_x, refs[per * size_x :]


def array_shapes(chunks, rows):
    columns = chunk_width(chunks)
    shapes = [(rows // lax.axis_size("y"), columns)] * (chunks // 2 * lax.axis_size("y"))
    shapes += [(rows // lax.axis_size("x"), columns)] * (chunks // 2 * lax.axis_size("x"))
    if chunks < 4:
        shapes.append((rows, PADDED - chunks * columns))
    return [jax.ShapeDtypeStruct(shape, jnp.bfloat16) for shape in shapes]


def place_copies(chunks, stage_ref, sems, places, tile):
    along = places[:2]
    rest = places[2]

    def copy(lane, place, row, where):
        start = lane * chunk_width(chunks)
        end = PADDED if lane == chunks else start + chunk_width(chunks)
        spot = pl.ds(pl.multiple_of(row * tile, tile), tile)
        return pltpu.make_async_copy(
            stage_ref.at[where, :, start:end], place.at[spot, :], sems.at[where, lane]
        )

    def start(spots, unit, inside, row, where):
        for chunk in range(chunks):
            which, position = spots[chunk % 2]
            for k, group in enumerate(along[chunk % 2]):

                @pl.when(which == k)
                def _(chunk=chunk, place=group[chunk // 2], at=position * unit + inside):
                    copy(chunk, place, at, where).start()

        for place in rest:
            copy(chunks, place, row, where).start()

    def wait(where):
        for chunk in range(chunks):
            copy(chunk, along[chunk % 2][0][chunk // 2], 0, where).wait()
        for place in rest:
            copy(chunks, place, 0, where).wait()

    return start, wait


def place_of(tile):
    return jnp.stack(
        [
            lax.axis_index("y").astype(jnp.int32),
            lax.axis_index("x").astype(jnp.int32),
            lax.axis_index("c").astype(jnp.int32),
            jnp.int32(unit_tiles(tile)),
            jnp.int32(lax.axis_size("y")),
            jnp.int32(lax.axis_size("x")),
        ]
    )


def half_side(tokens, at):
    return pl.BlockSpec(
        (tokens, PADDED), lambda i, *_: (at, 0), pipeline_mode=pl.Buffered(1)
    )


def weight_grads(chunks, own, other, sides):
    rows, tokens = own.shape
    tile = 512 if unit_tiles(256) % 2 == 0 else 256
    source = pl.BlockSpec((tile, tokens), lambda i, *_: (i, 0))
    halves = [half_side(tokens, 0), half_side(tokens, 1)]
    out_shape = array_shapes(chunks, rows)
    return pl.pallas_call(
        functools.partial(weight_grads_body, chunks, tile),
        grid_spec=pltpu.PrefetchScalarGridSpec(
            num_scalar_prefetch=1,
            grid=(rows // tile,),
            in_specs=[source, source] + halves * 2,
            out_specs=[pl.BlockSpec(memory_space=pl.ANY)] * len(out_shape),
            scratch_shapes=[
                pltpu.VMEM((2, tile, PADDED), jnp.bfloat16),
                pltpu.SemaphoreType.DMA((2, 5)),
            ],
        ),
        out_shape=out_shape,
        compiler_params=pltpu.CompilerParams(vmem_limit_bytes=40 << 20),
        cost_estimate=pl.CostEstimate(
            flops=4 * rows * tokens * CUTS[-1],
            bytes_accessed=4 * rows * tokens + 2 * rows * PADDED,
            transcendentals=0,
        ),
        name="weight_grads",
    )(place_of(tile), own, other, sides[0], sides[0], sides[1], sides[1])


def attention_fill_body(chunks, owners, tiles, place_ref, *refs):
    own_ref, other_ref, side_ref, other_side_ref = refs[:4]
    outs = refs[4 + (len(refs) - 6) // 2 : -2]
    stage_ref, sems = refs[-2:]
    step = pl.program_id(0)
    start, wait = place_copies(chunks, stage_ref, sems, split_places(outs, chunks), INNER)

    def mine(tile):
        return place_ref[2] == (0 if owners == 1 else tile // 2)

    for at, tile in enumerate(tiles):

        @pl.when((step == at) & mine(tile))
        def _(at=at, row=tile % (4 // owners)):
            product = jnp.dot(
                own_ref[...].T, side_ref[:, : CUTS[-1]], preferred_element_type=jnp.float32
            ) + jnp.dot(
                other_ref[...].T, other_side_ref[:, : CUTS[-1]], preferred_element_type=jnp.float32
            )
            stage_ref[at, :, : CUTS[-1]] = product.astype(jnp.bfloat16)
            stage_ref[at, :, CUTS[-1] :] = jnp.zeros((INNER, PADDED - CUTS[-1]), jnp.bfloat16)
            start(spots_of(0, place_ref), 0, row, row, at)

    for at, tile in enumerate(tiles):

        @pl.when((step == len(tiles) - 1) & mine(tile))
        def _(at=at):
            wait(at)


def attention_fill(chunks, arrays, own, other, sides, tiles):
    tokens = own.shape[0]
    unit_rows = unit_tiles(TILE) * TILE
    owners = 4 * INNER // unit_rows

    def half(i, *_):
        picked = 1 if tiles[0] == 3 else 0
        for at, tile in enumerate(tiles[1:], 1):
            picked = jnp.where(i >= at, 1 if tile == 3 else 0, picked)
        return picked, 0

    anywhere = pl.BlockSpec(memory_space=pl.ANY)
    return pl.pallas_call(
        functools.partial(attention_fill_body, chunks, owners, tiles),
        grid_spec=pltpu.PrefetchScalarGridSpec(
            num_scalar_prefetch=1,
            grid=(len(tiles),),
            in_specs=[pl.BlockSpec((tokens, INNER), lambda i, *_: (0, i))] * 2
            + [pl.BlockSpec((tokens, PADDED), half)] * 2
            + [anywhere] * len(arrays),
            out_specs=[anywhere] * len(arrays),
            scratch_shapes=[
                pltpu.VMEM((len(tiles), INNER, PADDED), jnp.bfloat16),
                pltpu.SemaphoreType.DMA((len(tiles), 5)),
            ],
        ),
        out_shape=[jax.ShapeDtypeStruct(array.shape, array.dtype) for array in arrays],
        input_output_aliases={5 + k: k for k in range(len(arrays))},
        compiler_params=pltpu.CompilerParams(vmem_limit_bytes=32 << 20),
        cost_estimate=pl.CostEstimate(
            flops=4 * len(tiles) * INNER * tokens * CUTS[-1],
            bytes_accessed=4 * len(tiles) * INNER * (tokens + PADDED),
            transcendentals=0,
        ),
        name="attention_fill",
    )(place_of(TILE), own, other, *sides, *arrays)


def tied(first, second):
    return lax.optimization_barrier((first, second))


def chunk_width(chunks):
    return PADDED // 4 if chunks == 4 else PADDED // 6


class Scatter:
    def __init__(self):
        self.waiting, self.flying, self.results = {}, {}, {}

    def push(self, name, route, kept, sends):
        self.waiting[name] = (route, kept, sends)

    def settle(self, values, *names):
        arrays, values = tied({name: self.flying[name][1:] for name in names}, values)
        moves = {}
        for name in names:
            route = self.flying.pop(name)[0]
            kept, moved = arrays[name]
            if not route:
                self.results[name] = kept.astype(jnp.float32) + sum(
                    part.astype(jnp.float32) for part in moved
                )
                continue
            total = total_of(kept, moved)
            total = total.reshape((lax.axis_size(route[0]), -1) + total.shape[-1:])
            sends = stage_sends(total, route[0], 0)
            moves[name] = (route, pick(total, lax.axis_index(route[0]), 0), sends)
        if moves and all(move[0] == ("z",) for move in moves.values()):
            kept = jnp.concatenate([move[1] for move in moves.values()], axis=-1)
            sends = [
                jnp.concatenate(parts, axis=-1) for parts in zip(*(m[2] for m in moves.values()))
            ]
            moves = {tuple(moves): (("z",), kept, sends)}
        arrays, values = tied({name: move[1:] for name, move in moves.items()}, values)
        for name, (route, *_) in moves.items():
            self.waiting[name] = (route,) + tuple(arrays[name])
        return values

    def start(self, values, *names):
        arrays, values = tied({name: self.waiting[name][1:] for name in names}, values)
        for name in names:
            route = self.waiting.pop(name)[0]
            kept, sends = arrays[name]
            self.flying[name] = (route[1:], kept, stage_moves(sends, route[0]))
        return values

    def step(self, values, *names):
        others = set(self.waiting)
        values = self.settle(values, *names)
        return self.start(values, *(name for name in self.waiting if name not in others))


def total_of(value, moved):
    total = value.astype(jnp.float32)
    for part in moved:
        total = total + part.astype(jnp.float32)
    return total.astype(jnp.bfloat16)


def fetch_rows(local_rows):
    return lax.all_gather(local_rows, DEVICES, axis=0, tiled=True)


def layer_forward(stream, gathered, gain_one, gain_two, gate_low, context):
    normed, inverse_one = rms_forward(stream, gain_one)
    normed_low = normed.astype(jnp.bfloat16)
    projected = times_rows(normed_low, gathered[: 3 * INNER]).astype(jnp.bfloat16)
    queries = projected[:, :INNER]
    parts = [projected[:, INNER:]]
    if gate_low is not None:
        parts.append(jnp.broadcast_to(gate_low[:, None], (stream.shape[0], BLOCK)))
    shared = with_neighbours(jnp.concatenate(parts, axis=1))
    attended, full, log_total = attend_forward(queries, shared, context)
    middle = stream + times_plain(attended, gathered[3 * INNER : 4 * INNER])
    normed_two, inverse_two = rms_forward(middle, gain_two)
    normed_two_low = normed_two.astype(jnp.bfloat16)
    result, *factors = ffn_forward(normed_two_low, middle, gathered)
    kept = (
        stream,
        inverse_one,
        normed_low,
        queries,
        shared,
        attended,
        full,
        log_total,
        middle,
        inverse_two,
        normed_two_low,
        factors,
    )
    return (result, kept)


def layer_backward(grad_out, kept, gathered, gain_one, gain_two, context, before):
    (
        stream,
        inverse_one,
        normed_low,
        queries,
        shared,
        attended,
        full,
        log_total,
        middle,
        inverse_two,
        normed_two_low,
        factors,
    ) = kept
    tokens = queries.shape[0]
    branch_low = grad_out.astype(jnp.bfloat16)
    sides = jnp.concatenate([normed_two_low, branch_low], axis=0)
    sides = jnp.pad(sides, ((0, 0), (0, PADDED - sides.shape[1])))
    sides = (sides, shift(sides, "c", 1))
    grad_normed_two, own, sent = ffn_backward(
        branch_low, factors[0], factors[1], gathered, factors[2], factors[3]
    )
    if before is not None:
        grad_normed_two, own, sent = before.step((grad_normed_two, own, sent), 0, 1)
    other = shift(sent, "c", 1)
    grad_middle, grad_gain_two = rms_backward(middle, inverse_two, gain_two, grad_normed_two)
    grad_middle = grad_out + grad_middle
    middle_low = grad_middle.astype(jnp.bfloat16)
    late_sides = jnp.concatenate([normed_low, middle_low], axis=0)
    late_sides = jnp.pad(late_sides, ((0, 0), (0, PADDED - late_sides.shape[1])))
    late_sides = (late_sides, shift(late_sides, "c", 1))
    grad_mixed = times_rows(middle_low, gathered[3 * INNER : 4 * INNER]).astype(jnp.bfloat16)
    grad_query, grad_shared, grad_table = attend_backward(
        queries, grad_mixed, full, shared, log_total, context
    )
    if before is not None:
        grad_query, grad_shared = before.settle((grad_query, grad_shared), 0, 1)
    grad_shared, own = lax.optimization_barrier((grad_shared, own))
    moving = start_back(grad_shared, tokens)
    chunks = 2 if before is None else 4
    arrays = weight_grads(chunks, own, other, sides)
    early = jnp.concatenate([grad_query, attended], axis=1)
    arrays = attention_fill(chunks, arrays, early, shift(early, "c", 1), late_sides, (0, 3))
    arrays, moving = lax.optimization_barrier((arrays, moving))
    if before is not None:
        arrays, moving = before.start((arrays, moving), (0, 1))
    grad_own = finish_back(*moving)
    grad_gate = grad_own[:, 2 * INNER :]
    grad_input_low = jnp.concatenate(
        [grad_query, grad_own[:, : 2 * INNER].astype(jnp.bfloat16)], axis=1
    )
    late = grad_input_low[:, INNER:]
    arrays = attention_fill(chunks, arrays, late, shift(late, "c", 1), late_sides, (1, 2))
    scatter = Scatter()
    along_y, along_x, rest = split_places(arrays, chunks)
    for chunk in range(chunks):
        route = ("y", "x", "z") if chunk % 2 == 0 else ("x", "y", "z")
        ordered = [group[chunk // 2] for group in (along_y, along_x)[chunk % 2]]
        scatter.push(chunk, route, ordered[-1], ordered[:-1])
    grad_input_low, grad_gate = scatter.start((grad_input_low, grad_gate), 0, 1)
    if rest:
        grad_input_low, grad_gate, rest = lax.optimization_barrier(
            (grad_input_low, grad_gate, rest)
        )
        rest = lax.psum_scatter(rest[0], ("y", "x", "z"), scatter_dimension=0, tiled=True)
    grad_normed = times_plain(grad_input_low, gathered[: 3 * INNER])
    grad_stream, grad_gain_one = rms_backward(stream, inverse_one, gain_one, grad_normed)
    return (grad_middle + grad_stream, grad_table, grad_gate, grad_gain_one, grad_gain_two, scatter, rest)


def per_device(
    inputs, layer3_rows, layer4_rows, norm_gains, gate_weight, rel_bias, segment_ids, cotangent
):
    seqs_here, tokens_here, width = inputs.shape
    first_pos = lax.axis_index("z") * tokens_here
    context = attention_context(segment_ids[0], first_pos, tokens_here, rel_bias)
    stream = inputs.reshape(tokens_here, width)
    gathered_three = fetch_rows(layer3_rows)
    after_three, kept_three = layer_forward(
        stream, gathered_three, norm_gains[0], norm_gains[1], None, context
    )
    gate_inverse = lax.rsqrt(jnp.mean(after_three * after_three, axis=1, keepdims=True) + epsilon)
    gate_normed = after_three * gate_inverse
    gate_logit = jnp.sum(gate_normed * gate_weight, axis=1) + gate_offset
    sigmoid_value = 1.0 / (1.0 + jnp.exp(-gate_logit))
    gate_mask = gate_scale * sigmoid_value
    gate_low = gate_mask.astype(jnp.bfloat16)
    gathered_four = fetch_rows(layer4_rows)
    after_four, kept_four = layer_forward(
        after_three, gathered_four, norm_gains[2], norm_gains[3], gate_low, context
    )
    grad_three_out, table_four, grad_gate, gain_four_one, gain_four_two, before, rest = (
        layer_backward(
            cotangent.reshape(tokens_here, width),
            kept_four,
            gathered_four,
            norm_gains[2],
            norm_gains[3],
            context,
            None,
        )
    )
    grad_logit = grad_gate[:, 0] * gate_scale * sigmoid_value * (1.0 - sigmoid_value)
    grad_gate_weight = jnp.sum(grad_logit[:, None] * gate_normed, axis=0)
    gate_stream = stream_backward(after_three, gate_inverse, grad_logit[:, None] * gate_weight)
    grad_input, table_three, unused, gain_three_one, gain_three_two, scatter, _ = layer_backward(
        grad_three_out + gate_stream,
        kept_three,
        gathered_three,
        norm_gains[0],
        norm_gains[1],
        context,
        before,
    )
    table = jnp.pad((table_three + table_four).reshape(1, -1), ((0, 0), (0, width - 6 * BUCKETS)))
    small_sums = jnp.stack(
        [gain_three_one, gain_three_two, gain_four_one, gain_four_two, grad_gate_weight, table[0]]
    )
    small = hop(small_sums, "c")
    small = before.settle(small, (0, 1))
    small = scatter.step(small, 0, 1)
    small = scatter.start(small, 2, 3)
    small = scatter.step(small, 0, 1)
    small, rest = scatter.settle((small, rest), (0, 1))
    small = scatter.step(small, 2, 3)
    for bit in range(1, lax.axis_size("z")):
        if bit & (bit - 1) == 0:
            small = hop(small, "z", bit)
    small = scatter.step(small, 2, 3)
    small = hop(small, "x")
    for bit in range(1, lax.axis_size("y")):
        if bit & (bit - 1) == 0:
            small = hop(small, "y", bit)
    summed = scatter.settle(small, (2, 3))
    local_three = jnp.concatenate([scatter.results[pair] for pair in ((0, 1), (2, 3))], axis=1)
    local_four = jnp.concatenate([before.results[(0, 1)], rest.astype(jnp.float32)], axis=1)
    local_three, local_four = local_three[:, :width], local_four[:, :width]
    return (
        after_four.reshape(inputs.shape),
        gate_mask.reshape(seqs_here, tokens_here),
        grad_input.reshape(inputs.shape),
        local_three,
        local_four,
        summed[:4],
        summed[4],
        summed[5, : 6 * BUCKETS].reshape(BUCKETS, HEADS),
    )


def solution(mesh):
    outer, inner = mesh.devices.shape
    fine = Mesh(mesh.devices.reshape(outer // 4, 2, 2, inner), DEVICES)
    batch = ("y", "x", "c")
    tokens = P(batch, "z", None)
    rows = P(DEVICES, None)
    return jax.shard_map(
        per_device,
        mesh=fine,
        in_specs=(tokens, rows, rows, P(), P(), P(), P(batch, None), tokens),
        out_specs=(tokens, P(batch, "z"), tokens, rows, rows, P(), P(), P()),
        check_vma=False,
    )
```

```python
import functools

import jax
import jax.numpy as jnp
from jax import lax
from jax.experimental import pallas as pl
from jax.experimental.pallas import tpu as pltpu
from jax.sharding import Mesh
from jax.sharding import PartitionSpec as P

HEADS = 6
PAIRS = 3
BLOCK = 128
WIDE = 2 * BLOCK
INNER = 384
BUCKETS = 32
FF = 3584
REACH = 799
HALO = 896
TILE = 256
ATTENTION_TILES = 4 * INNER // TILE
OFFSETS = 5
PADDED = 1536
FORWARD_TILE = 512
CUTS = (0, 1472)
DEVICES = ("y", "x", "c", "z")
epsilon = 1e-06
gate_scale = -30.0
gate_offset = -3.5
masked_out = -1e30
limits = (12, 16, 23, 32, 46, 64, 91)
both_last = (((1,), (1,)), ((), ()))


def bucket_of(relative):
    magnitude = jnp.abs(relative)
    beyond = jnp.zeros_like(magnitude)
    for bound_value in limits:
        beyond = beyond + (magnitude >= bound_value).astype(jnp.int32)
    inside = jnp.where(magnitude < 8, magnitude, 8 + beyond)
    return inside + 16 * (relative > 0).astype(jnp.int32)


def near_buckets(offset):
    if offset < 0:
        return range(1, 16)
    if offset > 0:
        return range(17, 32)
    return range(0, 32)


def tile_buckets(offset, width):
    key_at = lax.broadcasted_iota(jnp.int32, (BLOCK, width), 0)
    query_at = lax.broadcasted_iota(jnp.int32, (BLOCK, width), 1) % BLOCK
    return bucket_of(offset * BLOCK + key_at - query_at)


def bias_body(table_ref, tiles_ref):
    head = pl.program_id(0)
    tiles_ref[0, 0] = jnp.full((BLOCK, BLOCK), table_ref[15, head], jnp.float32)
    tiles_ref[0, 4] = jnp.full((BLOCK, BLOCK), table_ref[31, head], jnp.float32)
    for offset in (-1, 0, 1):
        buckets = tile_buckets(offset, BLOCK)
        tile = jnp.zeros((BLOCK, BLOCK), jnp.float32)
        for bucket in near_buckets(offset):
            tile = jnp.where(buckets == bucket, table_ref[bucket, head], tile)
        tiles_ref[0, offset + 2] = tile


def bias_tiles(rel_bias):
    return pl.pallas_call(
        bias_body,
        grid=(HEADS,),
        in_specs=[pl.BlockSpec(memory_space=pltpu.SMEM)],
        out_specs=pl.BlockSpec((1, OFFSETS, BLOCK, BLOCK), lambda h: (h, 0, 0, 0)),
        out_shape=jax.ShapeDtypeStruct((HEADS, OFFSETS, BLOCK, BLOCK), jnp.float32),
        name="bias_tiles",
    )(rel_bias)


def lane_masks():
    lane = lax.broadcasted_iota(jnp.int32, (BLOCK, BLOCK), 1)
    low = jnp.where(lane < 64, 1.0, 0.0).astype(jnp.bfloat16)
    high = jnp.where(lane < 64, 0.0, 1.0).astype(jnp.bfloat16)
    return low, high


def stacked(block, masks):
    low, high = masks
    return jnp.concatenate([block * low, block * high], axis=0)


def pair_cols(pair):
    return slice(pair * BLOCK, (pair + 1) * BLOCK)


def value_cols(pair):
    return slice(INNER + pair * BLOCK, INNER + (pair + 1) * BLOCK)


def block_rows(block):
    return pl.ds(pl.multiple_of(block * BLOCK, BLOCK), BLOCK)


def wide_rows(block):
    return pl.ds(pl.multiple_of(block * WIDE, WIDE), WIDE)


def fold(values):
    return values.reshape(values.shape[0] // 8, 8, WIDE)


def shift_tile(gated, rows, own_segment, segment_ref, shared_ref):
    same = segment_ref[rows, :] == own_segment
    inside = shared_ref[rows, 2 * INNER :].astype(jnp.float32) if gated else 0.0
    shift = jnp.where(same, inside, masked_out)
    return jnp.concatenate([shift, shift], axis=1)


def used_blocks(low_ref, high_ref):
    last = pl.num_programs(0) - 1
    return low_ref[0] // 2 * 2, (high_ref[last] + 1) // 2 * 2


def tile_offsets(block, own_block):
    return [jnp.clip(2 * block + k - own_block, -2, 2) + 2 for k in range(2)]


def bias_pair(bias_ref, pair, offsets):
    halves = [
        jnp.concatenate([bias_ref[2 * pair, at], bias_ref[2 * pair + 1, at]], axis=1)
        for at in offsets
    ]
    return jnp.concatenate(halves, axis=0)


def pick_heads(wide):
    return jnp.concatenate([wide[:64, :BLOCK], wide[64:, BLOCK:]], axis=0)


def forward_body(gated, low_ref, high_ref, *refs):
    query_ref, shared_ref, own_ref, segment_ref, bias_ref = refs[:5]
    mixed_ref, full_ref, total_ref, turned_ref, score_ref, sum_ref = refs[5:]
    step = pl.program_id(0)

    @pl.when(step == 0)
    def _():
        @pl.loop(*used_blocks(low_ref, high_ref))
        def _(block):
            rows = block_rows(block)
            turned_ref[:, rows] = shared_ref[rows, INNER : 2 * INNER].T

    first, last = low_ref[step] // 2, (high_ref[step] + 1) // 2
    own_block = HALO // BLOCK + step
    own_segment = own_ref[0]
    masks = lane_masks()
    queries = [stacked(query_ref[:, pair_cols(pair)], masks) for pair in range(PAIRS)]

    def scores(block, peaks):
        rows = wide_rows(block)
        shift = shift_tile(gated, rows, own_segment, segment_ref, shared_ref)
        offsets = tile_offsets(block, own_block)
        new_peaks = []
        for pair in range(PAIRS):
            score = lax.dot_general(
                shared_ref[rows, pair_cols(pair)],
                queries[pair],
                both_last,
                preferred_element_type=jnp.float32,
            )
            score = score + bias_pair(bias_ref, pair, offsets) + shift
            score_ref[pair, block] = score
            new_peaks.append(jnp.maximum(peaks[pair], jnp.max(fold(score), axis=0)))
        return tuple(new_peaks)

    start = jnp.full((8, WIDE), -3e38, jnp.float32)
    peaks = lax.fori_loop(first, last, scores, (start,) * PAIRS)
    peaks = [jnp.max(peak, axis=0, keepdims=True) for peak in peaks]
    sum_ref[...] = jnp.zeros_like(sum_ref)

    def mix(block, totals):
        new_totals = []
        for pair in range(PAIRS):
            weight = jnp.exp(score_ref[pair, block] - peaks[pair])
            new_totals.append(totals[pair] + jnp.sum(fold(weight), axis=0))
            sum_ref[pair] += jnp.dot(
                turned_ref[pair_cols(pair), wide_rows(block)],
                weight.astype(jnp.bfloat16),
                preferred_element_type=jnp.float32,
            )
        return tuple(new_totals)

    totals = lax.fori_loop(first, last, mix, (jnp.zeros((8, WIDE), jnp.float32),) * PAIRS)
    for pair in range(PAIRS):
        row_total = jnp.sum(totals[pair], axis=0, keepdims=True)
        mixed = pick_heads(sum_ref[pair] * (1.0 / row_total))
        full_ref[:, pair_cols(pair)] = mixed.T
        mixed_ref[:, pair_cols(pair)] = full_ref[:, pair_cols(pair)].astype(jnp.bfloat16)
        total_ref[0, pair : pair + 1, :] = peaks[pair] + jnp.log(row_total)


def whole(shape):
    return pl.BlockSpec(shape, lambda i, *_: (0,) * len(shape), pipeline_mode=pl.Buffered(1))


def rows_spec(width):
    return pl.BlockSpec((BLOCK, width), lambda i, *_: (i, 0))


def attend_forward(queries, shared, context):
    lows, highs, own_rows, segment_wide, tiles = context
    tokens, (length, width) = queries.shape[0], shared.shape
    steps, key_blocks = tokens // BLOCK, length // BLOCK
    return pl.pallas_call(
        functools.partial(forward_body, width > 2 * INNER),
        grid_spec=pltpu.PrefetchScalarGridSpec(
            num_scalar_prefetch=2,
            grid=(steps,),
            in_specs=[
                rows_spec(INNER),
                whole((length, width)),
                pl.BlockSpec((1, 1, BLOCK), lambda i, *_: (i, 0, 0)),
                whole((length, BLOCK)),
                whole(tiles.shape),
            ],
            out_specs=[
                rows_spec(INNER),
                rows_spec(INNER),
                pl.BlockSpec((1, 8, WIDE), lambda i, *_: (i, 0, 0)),
            ],
            scratch_shapes=[
                pltpu.VMEM((INNER, length), jnp.bfloat16),
                pltpu.VMEM((PAIRS, key_blocks // 2, WIDE, WIDE), jnp.float32),
                pltpu.VMEM((PAIRS, BLOCK, WIDE), jnp.float32),
            ],
        ),
        out_shape=[
            jax.ShapeDtypeStruct((tokens, INNER), jnp.bfloat16),
            jax.ShapeDtypeStruct((tokens, INNER), jnp.float32),
            jax.ShapeDtypeStruct((steps, 8, WIDE), jnp.float32),
        ],
        compiler_params=pltpu.CompilerParams(vmem_limit_bytes=40 << 20),
        cost_estimate=pl.CostEstimate(
            flops=tokens * length * INNER * 4,
            bytes_accessed=8 << 20,
            transcendentals=tokens * length * 3,
        ),
        name="attend_forward",
    )(lows, highs, queries, shared, own_rows, segment_wide, tiles)


def backward_body(gated, low_ref, high_ref, *refs):
    query_ref, grad_ref, full_ref, shared_ref, own_ref, segment_ref, bias_ref, total_ref = refs[:8]
    grad_query_ref, grad_shared_ref, bucket_ref = refs[8:11]
    turned_ref, sum_ref, bias_sum_ref, turn_sum_ref = refs[11:]
    step = pl.program_id(0)

    @pl.when(step == 0)
    def _():
        bias_sum_ref[...] = jnp.zeros_like(bias_sum_ref)

        @pl.loop(*used_blocks(low_ref, high_ref))
        def _(block):
            rows = block_rows(block)
            turned_ref[:, rows] = shared_ref[rows, :INNER].T
            sum_ref[rows, :] = jnp.zeros((BLOCK, sum_ref.shape[1]), jnp.float32)

    first, last = low_ref[step] // 2, (high_ref[step] + 1) // 2
    own_block = HALO // BLOCK + step
    own_segment = own_ref[0]
    masks = lane_masks()
    queries = [stacked(query_ref[:, pair_cols(pair)], masks) for pair in range(PAIRS)]
    grads = [stacked(grad_ref[:, pair_cols(pair)], masks) for pair in range(PAIRS)]
    totals = [total_ref[0, pair : pair + 1, :] for pair in range(PAIRS)]

    deltas = []
    for pair in range(PAIRS):
        cols = pair_cols(pair)
        product = (grad_ref[:, cols].astype(jnp.float32) * full_ref[:, cols]).T
        halves = [jnp.sum(half, axis=0, keepdims=True) for half in (product[:64], product[64:])]
        deltas.append(jnp.concatenate(halves, axis=1))
    turn_sum_ref[...] = jnp.zeros_like(turn_sum_ref)

    @pl.loop(first, last)
    def _(block):
        rows = wide_rows(block)
        shift = shift_tile(gated, rows, own_segment, segment_ref, shared_ref)
        offsets = tile_offsets(block, own_block)
        gate_part = jnp.zeros((WIDE, BLOCK), jnp.float32)
        for pair in range(PAIRS):
            cols = pair_cols(pair)
            score = lax.dot_general(
                shared_ref[rows, cols], queries[pair], both_last, preferred_element_type=jnp.float32
            )
            pull = lax.dot_general(
                shared_ref[rows, value_cols(pair)],
                grads[pair],
                both_last,
                preferred_element_type=jnp.float32,
            )
            prob = jnp.exp(score + bias_pair(bias_ref, pair, offsets) + shift - totals[pair])
            sum_ref[rows, value_cols(pair)] += jnp.dot(
                prob.astype(jnp.bfloat16), grads[pair], preferred_element_type=jnp.float32
            )
            grad_score = prob * (pull - deltas[pair])
            bias_sum_ref[pair, offsets[0]] += grad_score[:BLOCK]
            bias_sum_ref[pair, offsets[1]] += grad_score[BLOCK:]
            if gated:
                gate_part = gate_part + (grad_score[:, :BLOCK] + grad_score[:, BLOCK:])
            score_low = grad_score.astype(jnp.bfloat16)
            sum_ref[rows, cols] += jnp.dot(
                score_low, queries[pair], preferred_element_type=jnp.float32
            )
            turn_sum_ref[pair] += jnp.dot(
                turned_ref[cols, rows], score_low, preferred_element_type=jnp.float32
            )
        if gated:
            sum_ref[rows, 2 * INNER :] += gate_part

    for pair in range(PAIRS):
        grad_query_ref[:, pair_cols(pair)] = pick_heads(turn_sum_ref[pair]).T.astype(jnp.bfloat16)

    @pl.when(step == pl.num_programs(0) - 1)
    def _():
        grad_shared_ref[...] = jnp.zeros_like(grad_shared_ref)

        @pl.loop(*used_blocks(low_ref, high_ref))
        def _(block):
            rows = block_rows(block)
            both = slice(0, 2 * INNER)
            grad_shared_ref[rows, both] = sum_ref[rows, both].astype(jnp.bfloat16)
            if gated:
                gate_total = jnp.sum(sum_ref[rows, 2 * INNER :], axis=1, keepdims=True)
                grad_shared_ref[rows, 2 * INNER :] = jnp.broadcast_to(
                    gate_total, (BLOCK, BLOCK)
                ).astype(jnp.bfloat16)

        tables = {offset: tile_buckets(offset, WIDE) for offset in (-1, 0, 1)}

        @pl.loop(0, PAIRS)
        def _(pair):
            for bucket in range(BUCKETS):
                part = jnp.zeros((8, WIDE), jnp.float32)
                for offset in (-1, 0, 1):
                    if bucket in near_buckets(offset):
                        chosen = jnp.where(
                            tables[offset] == bucket, bias_sum_ref[pair, offset + 2], 0.0
                        )
                        part = part + jnp.sum(fold(chosen), axis=0)
                if bucket == 15:
                    part = part + jnp.sum(fold(bias_sum_ref[pair, 0]), axis=0)
                if bucket == 31:
                    part = part + jnp.sum(fold(bias_sum_ref[pair, 4]), axis=0)
                bucket_ref[pair, bucket : bucket + 1, :] = jnp.sum(part, axis=0, keepdims=True)


def attend_backward(queries, grad_mixed, full, shared, log_total, context):
    lows, highs, own_rows, segment_wide, tiles = context
    tokens, (length, width) = queries.shape[0], shared.shape
    steps = tokens // BLOCK
    grad_query, grad_shared, bucket_sums = pl.pallas_call(
        functools.partial(backward_body, width > 2 * INNER),
        grid_spec=pltpu.PrefetchScalarGridSpec(
            num_scalar_prefetch=2,
            grid=(steps,),
            in_specs=[
                rows_spec(INNER),
                rows_spec(INNER),
                rows_spec(INNER),
                whole((length, width)),
                pl.BlockSpec((1, 1, BLOCK), lambda i, *_: (i, 0, 0)),
                whole((length, BLOCK)),
                whole(tiles.shape),
                pl.BlockSpec((1, 8, WIDE), lambda i, *_: (i, 0, 0)),
            ],
            out_specs=[
                rows_spec(INNER),
                whole((length, width)),
                whole((PAIRS, BUCKETS, WIDE)),
            ],
            scratch_shapes=[
                pltpu.VMEM((INNER, length), jnp.bfloat16),
                pltpu.VMEM((length, width), jnp.float32),
                pltpu.VMEM((PAIRS, OFFSETS, BLOCK, WIDE), jnp.float32),
                pltpu.VMEM((PAIRS, BLOCK, WIDE), jnp.float32),
            ],
        ),
        out_shape=[
            jax.ShapeDtypeStruct((tokens, INNER), jnp.bfloat16),
            jax.ShapeDtypeStruct((length, width), jnp.bfloat16),
            jax.ShapeDtypeStruct((PAIRS, BUCKETS, WIDE), jnp.float32),
        ],
        compiler_params=pltpu.CompilerParams(vmem_limit_bytes=48 << 20),
        cost_estimate=pl.CostEstimate(
            flops=tokens * length * INNER * 10,
            bytes_accessed=12 << 20,
            transcendentals=tokens * length * 3,
        ),
        name="attend_backward",
    )(lows, highs, queries, grad_mixed, full, shared, own_rows, segment_wide, tiles, log_total)
    table = jnp.sum(bucket_sums.reshape(PAIRS, BUCKETS, 2, BLOCK), axis=3)
    return grad_query, grad_shared, table.transpose(1, 0, 2).reshape(BUCKETS, HEADS)


def attention_context(segment_row, first_pos, tokens, rel_bias):
    steps = tokens // BLOCK
    padded = jnp.pad(segment_row, (HALO, 0), constant_values=-1)
    padded = jnp.pad(padded, (0, HALO), constant_values=1000)
    window = lax.dynamic_slice_in_dim(padded, first_pos, tokens + 2 * HALO, 0)
    own = window[HALO : HALO + tokens].reshape(steps, 1, BLOCK)
    lows = jnp.sum(window[None, :] < own[:, 0, :1], axis=1, dtype=jnp.int32) // BLOCK
    ends = jnp.sum(window[None, :] <= own[:, 0, BLOCK - 1 :], axis=1, dtype=jnp.int32)
    highs = (ends + BLOCK - 1) // BLOCK
    segment_wide = jnp.broadcast_to(window[:, None], (window.shape[0], BLOCK))
    return lows, highs, own, segment_wide, bias_tiles(rel_bias)


def rms_forward(stream, gain_row):
    inverse = lax.rsqrt(jnp.mean(stream * stream, axis=1, keepdims=True) + epsilon)
    return (stream * inverse * gain_row, inverse)


def stream_backward(stream, inverse, scaled):
    return inverse * scaled - stream * inverse**3 * jnp.mean(scaled * stream, axis=1, keepdims=True)


def rms_backward(stream, inverse, gain_row, grad_normed):
    grad_gain = jnp.sum(grad_normed * stream * inverse, axis=0)
    return (stream_backward(stream, inverse, gain_row * grad_normed), grad_gain)


def gelu_tanh(values):
    return 0.5 * values * (1.0 + jnp.tanh(0.7978845608028654 * (values + 0.044715 * values**3)))


def times_rows(left_side, weight):
    return lax.dot_general(
        left_side, weight, (((1,), (1,)), ((), ())), preferred_element_type=jnp.float32
    )


def times_plain(left_side, weight):
    return jnp.dot(left_side, weight, preferred_element_type=jnp.float32)


def outer_sum(left_side, right_side):
    return lax.dot_general(
        left_side, right_side, (((0,), (0,)), ((), ())), preferred_element_type=jnp.float32
    )


def shift(value, axis, amount):
    count = lax.axis_size(axis)
    return lax.ppermute(value, axis, [(i, (i + amount) % count) for i in range(count)])


def slide(value, amount):
    count = lax.axis_size("z")
    pairs = [(i, i + amount) for i in range(count) if 0 <= i + amount < count]
    return lax.ppermute(value, "z", pairs)


def far_pair(near_start, near_end, distance):
    count = lax.axis_size("z")
    first_half = lax.axis_index("z") < distance
    sent = jnp.where(first_half, near_end, near_start)
    pairs = [(i, (i + distance) % count) for i in range(count)]
    got = lax.ppermute(sent, "z", pairs)
    return got


def far_split(got, distance):
    first_half = lax.axis_index("z") < distance
    none = jnp.zeros_like(got)
    return jnp.where(first_half, none, got), jnp.where(first_half, got, none)


def halo_pieces(tokens):
    pieces = []
    distance, covered = 1, 0
    while covered < HALO:
        span = min(tokens, HALO - covered)
        needed = min(span, -(-(REACH - covered) // 16) * 16)
        pieces.append((distance, span, needed))
        distance, covered = distance + 1, covered + span
    return pieces


def with_neighbours(own):
    tokens = own.shape[0]
    before, after = [], []
    for distance, span, needed in halo_pieces(tokens):
        if distance < lax.axis_size("z"):
            if 2 * distance == lax.axis_size("z"):
                left, right = far_split(
                    far_pair(own[:needed], own[tokens - needed :], distance), distance
                )
            else:
                left = slide(own[tokens - needed :], distance)
                right = slide(own[:needed], -distance)
            before.append(jnp.pad(left, ((span - needed, 0), (0, 0))))
            after.append(jnp.pad(right, ((0, span - needed), (0, 0))))
        else:
            empty = jnp.zeros((span, own.shape[1]), own.dtype)
            before.append(empty)
            after.append(empty)
    return jnp.concatenate(before[::-1] + [own] + after, axis=0)


def start_back(window, tokens):
    moved = []
    covered = 0
    for distance, span, needed in halo_pieces(tokens):
        if distance < lax.axis_size("z"):
            left_end = HALO - covered
            right_start = HALO + tokens + covered
            left = window[left_end - needed : left_end]
            right = window[right_start : right_start + needed]
            if 2 * distance == lax.axis_size("z"):
                moved.append((far_pair(left, right, distance),))
            else:
                moved.append((slide(left, -distance), slide(right, distance)))
        covered += span
    return window[HALO : HALO + tokens], moved


def finish_back(own, moved):
    tokens = own.shape[0]
    total = own.astype(jnp.float32)
    for distance, pair in enumerate(moved, 1):
        if len(pair) == 1:
            ahead, back = far_split(pair[0], distance)
        else:
            back, ahead = pair
        needed = back.shape[0]
        total = total + jnp.pad(back.astype(jnp.float32), ((tokens - needed, 0), (0, 0)))
        total = total + jnp.pad(ahead.astype(jnp.float32), ((0, tokens - needed), (0, 0)))
    return total


def hop(value, axis, bit=1):
    pairs = [(i, i ^ bit) for i in range(lax.axis_size(axis))]
    return value + lax.ppermute(value, axis, pairs)


def pick(value, index, axis):
    return lax.dynamic_index_in_dim(value, index, axis, keepdims=False)


def stage_sends(value, axis_name, axis):
    count, here = lax.axis_size(axis_name), lax.axis_index(axis_name)
    return [pick(value, (here + k) % count, axis) for k in range(1, count)]


def stage_moves(sends, axis_name):
    return [shift(sent, axis_name, k + 1) for k, sent in enumerate(sends)]


def gelu_parts(values):
    squared = values * values
    slope = jnp.tanh(0.7978845608028654 * (values + 0.044715 * values * squared))
    active = 0.5 * values * (1.0 + slope)
    inner = 0.7978845608028654 * (1.0 + 3.0 * 0.044715 * squared)
    return active, 0.5 * (1.0 + slope) + 0.5 * values * (1.0 - slope * slope) * inner


def turned_rows(core_ref, kept_ref, sent_ref, stage_ref, sems):
    mine, unit = core_ref[0], core_ref[1]
    parts = FORWARD_TILE // TILE

    def copy(lane, part, place, at, where):
        spot = pl.ds(pl.multiple_of(at * TILE, TILE), TILE)
        source = stage_ref.at[where, lane, part * TILE : (part + 1) * TILE, :]
        return pltpu.make_async_copy(source, place.at[spot, :], sems.at[where, lane, part])

    def put(lane, kind, step, turned):
        slot = step % 2
        stage_ref[slot, lane] = turned
        for part in range(parts):
            target = ATTENTION_TILES + kind * (FF // TILE) + step * parts + part
            own = (target // unit) % 2 == mine
            at = (target // (2 * unit)) * unit + target % unit

            @pl.when(own)
            def _(part=part, at=at):
                copy(lane, part, kept_ref, at, slot).start()

            @pl.when(jnp.logical_not(own))
            def _(part=part, at=at):
                copy(lane, part, sent_ref, at, slot).start()

    def wait(lanes, where):
        for lane in range(lanes):
            for part in range(parts):
                copy(lane, part, kept_ref, 0, where).wait()

    return put, wait


def ffn_forward_body(whole_layer, core_ref, *refs):
    normed_ref, gelu_ref, linear_ref = refs[:3]
    if whole_layer:
        middle_ref, down_ref, result_ref = refs[3:6]
    else:
        hidden_ref = refs[3]
    gelu_factor_ref, linear_factor_ref, kept_ref, sent_ref, stage_ref, sems = refs[-6:]
    step = pl.program_id(0)
    put, wait = turned_rows(core_ref, kept_ref, sent_ref, stage_ref, sems)

    if whole_layer:

        @pl.when(step == 0)
        def _():
            result_ref[...] = middle_ref[...]

    @pl.when(step >= 2)
    def _():
        wait(1, step % 2)

    active, slope = gelu_parts(times_rows(normed_ref[...], gelu_ref[...]))
    linear = times_rows(normed_ref[...], linear_ref[...])
    gelu_factor_ref[...] = slope * linear
    linear_factor_ref[...] = active
    hidden = (active * linear).astype(jnp.bfloat16)
    put(0, 2, step, hidden.T)
    if whole_layer:
        result_ref[...] += times_plain(hidden, down_ref[...])
    else:
        hidden_ref[...] = hidden

    @pl.when(step == pl.num_programs(0) - 1)
    def _():
        wait(1, 0)
        wait(1, 1)


def resident(shape):
    return pl.BlockSpec(shape, lambda *_: (0,) * len(shape), pipeline_mode=pl.Buffered(1))


def core_units():
    return jnp.stack([lax.axis_index("c").astype(jnp.int32), jnp.int32(unit_tiles(TILE))])


def hidden_weight(kind, width):
    first = (4 * INNER + kind * FF) // FORWARD_TILE
    return pl.BlockSpec((FORWARD_TILE, width), lambda i, *_: (first + i, 0))


def turned_scratch(lanes, tokens):
    return [
        pltpu.VMEM((2, lanes, FORWARD_TILE, tokens), jnp.bfloat16),
        pltpu.SemaphoreType.DMA((2, lanes, FORWARD_TILE // TILE)),
    ]


def ffn_forward(normed, middle, gathered):
    tokens, width = normed.shape
    half = (4 * INNER + 3 * FF) // 2
    hidden = pl.BlockSpec((tokens, FORWARD_TILE), lambda i, *_: (0, i))
    side = resident((tokens, width))
    anywhere = pl.BlockSpec(memory_space=pl.ANY)
    operands = [normed, gathered, gathered]
    in_specs = [side, hidden_weight(0, width), hidden_weight(1, width)]
    first_spec, first_shape = hidden, jax.ShapeDtypeStruct((tokens, FF), jnp.bfloat16)
    if middle is not None:
        operands += [middle, gathered]
        in_specs += [side, hidden_weight(2, width)]
        first_spec, first_shape = side, jax.ShapeDtypeStruct((tokens, width), jnp.float32)
    return pl.pallas_call(
        functools.partial(ffn_forward_body, middle is not None),
        grid_spec=pltpu.PrefetchScalarGridSpec(
            num_scalar_prefetch=1,
            grid=(FF // FORWARD_TILE,),
            in_specs=in_specs,
            out_specs=[first_spec, hidden, hidden, anywhere, anywhere],
            scratch_shapes=turned_scratch(1, tokens),
        ),
        out_shape=[
            first_shape,
            jax.ShapeDtypeStruct((tokens, FF), jnp.float32),
            jax.ShapeDtypeStruct((tokens, FF), jnp.float32),
            jax.ShapeDtypeStruct((half, tokens), jnp.bfloat16),
            jax.ShapeDtypeStruct((half, tokens), jnp.bfloat16),
        ],
        compiler_params=pltpu.CompilerParams(vmem_limit_bytes=52 << 20),
        cost_estimate=pl.CostEstimate(
            flops=6 * tokens * FF * width,
            bytes_accessed=6 * FF * width + 10 * tokens * FF,
            transcendentals=tokens * FF,
        ),
        name="ffn_forward",
    )(core_units(), *operands)


def ffn_backward_body(core_ref, *refs):
    branch_ref, gelu_factor_ref, linear_factor_ref, gelu_ref, linear_ref, down_ref = refs[:6]
    grad_ref, kept_ref, sent_ref, stage_ref, sems = refs[8:]
    step = pl.program_id(0)
    put, wait = turned_rows(core_ref, kept_ref, sent_ref, stage_ref, sems)

    @pl.when(step == 0)
    def _():
        grad_ref[...] = jnp.zeros_like(grad_ref)

    @pl.when(step >= 2)
    def _():
        wait(2, step % 2)

    grad_hidden = times_rows(branch_ref[...], down_ref[...])
    grad_gelu = (grad_hidden * gelu_factor_ref[...]).astype(jnp.bfloat16)
    grad_linear = (grad_hidden * linear_factor_ref[...]).astype(jnp.bfloat16)
    put(0, 0, step, grad_gelu.T)
    put(1, 1, step, grad_linear.T)
    grad_ref[...] += times_plain(grad_gelu, gelu_ref[...]) + times_plain(
        grad_linear, linear_ref[...]
    )

    @pl.when(step == pl.num_programs(0) - 1)
    def _():
        wait(2, 0)
        wait(2, 1)


def unit_tiles(tile):
    rows = 4 * INNER + 3 * FF
    return rows // tile // (2 * lax.axis_size("y") * lax.axis_size("x"))


def ffn_backward(branch, gelu_factor, linear_factor, gathered, kept, sent):
    tokens, width = branch.shape
    hidden = pl.BlockSpec((tokens, FORWARD_TILE), lambda i, *_: (0, i))
    side = resident((tokens, width))
    anywhere = pl.BlockSpec(memory_space=pl.ANY)
    return pl.pallas_call(
        ffn_backward_body,
        grid_spec=pltpu.PrefetchScalarGridSpec(
            num_scalar_prefetch=1,
            grid=(FF // FORWARD_TILE,),
            in_specs=[side, hidden, hidden]
            + [hidden_weight(kind, width) for kind in range(3)]
            + [anywhere, anywhere],
            out_specs=[side, anywhere, anywhere],
            scratch_shapes=turned_scratch(2, tokens),
        ),
        out_shape=[
            jax.ShapeDtypeStruct((tokens, width), jnp.float32),
            jax.ShapeDtypeStruct(kept.shape, kept.dtype),
            jax.ShapeDtypeStruct(sent.shape, sent.dtype),
        ],
        input_output_aliases={7: 1, 8: 2},
        compiler_params=pltpu.CompilerParams(vmem_limit_bytes=52 << 20),
        cost_estimate=pl.CostEstimate(
            flops=6 * tokens * FF * width,
            bytes_accessed=6 * FF * width + 12 * tokens * FF,
            transcendentals=0,
        ),
        name="ffn_backward",
    )(core_units(), branch, gelu_factor, linear_factor, gathered, gathered, gathered, kept, sent)


def spots_of(unit_at, place_ref):
    here_y, here_x, size_y, size_x = place_ref[0], place_ref[1], place_ref[4], place_ref[5]
    row, column = unit_at // size_x, unit_at % size_x
    return (
        ((row + 2 * size_y - here_y - 1) % size_y, column),
        ((column + 2 * size_x - here_x - 1) % size_x, row),
    )


def weight_grads_body(chunks, tile, place_ref, *refs):
    own_ref, other_ref, normed_ref, branch_ref, other_normed_ref, other_branch_ref = refs[:6]
    stage_ref, sems = refs[-2:]
    step = pl.program_id(0)
    unit = place_ref[3]
    at = (step // unit * 2 + place_ref[2]) * unit + step % unit
    first, second = 4 * INNER // tile, (4 * INNER + 2 * FF) // tile
    slot = step % 2
    places = split_places(refs[6:-2], chunks)
    start, wait = place_copies(chunks, stage_ref, sems, places, tile)

    def put(product):
        stage_ref[slot, :, : CUTS[-1]] = product.astype(jnp.bfloat16)
        start(spots_of(step // unit, place_ref), unit, step % unit, step, slot)

    def both(side_ref, other_side_ref):
        return jnp.dot(
            own_ref[...], side_ref[:, : CUTS[-1]], preferred_element_type=jnp.float32
        ) + jnp.dot(
            other_ref[...], other_side_ref[:, : CUTS[-1]], preferred_element_type=jnp.float32
        )

    @pl.when(step < 2)
    def _():
        stage_ref[slot, :, CUTS[-1] :] = jnp.zeros((tile, PADDED - CUTS[-1]), jnp.bfloat16)

    @pl.when(step >= 2)
    def _():
        wait(slot)

    @pl.when(at < first)
    def _():
        put(jnp.zeros((tile, CUTS[-1]), jnp.float32))

    @pl.when((at >= first) & (at < second))
    def _():
        put(both(normed_ref, other_normed_ref))

    @pl.when(at >= second)
    def _():
        put(both(branch_ref, other_branch_ref))

    @pl.when(step == pl.num_programs(0) - 1)
    def _():
        wait(0)
        wait(1)


def split_places(refs, chunks):
    size_y, size_x, per = lax.axis_size("y"), lax.axis_size("x"), chunks // 2
    refs = list(refs)
    along_y = [refs[per * k : per * (k + 1)] for k in range(size_y)]
    refs = refs[per * size_y :]
    along_x = [refs[per * k : per * (k + 1)] for k in range(size_x)]
    return along_y, along_x, refs[per * size_x :]


def array_shapes(chunks, rows):
    columns = chunk_width(chunks)
    shapes = [(rows // lax.axis_size("y"), columns)] * (chunks // 2 * lax.axis_size("y"))
    shapes += [(rows // lax.axis_size("x"), columns)] * (chunks // 2 * lax.axis_size("x"))
    if chunks < 4:
        shapes.append((rows, PADDED - chunks * columns))
    return [jax.ShapeDtypeStruct(shape, jnp.bfloat16) for shape in shapes]


def place_copies(chunks, stage_ref, sems, places, tile):
    along = places[:2]
    rest = places[2]

    def copy(lane, place, row, where):
        start = lane * chunk_width(chunks)
        end = PADDED if lane == chunks else start + chunk_width(chunks)
        spot = pl.ds(pl.multiple_of(row * tile, tile), tile)
        return pltpu.make_async_copy(
            stage_ref.at[where, :, start:end], place.at[spot, :], sems.at[where, lane]
        )

    def start(spots, unit, inside, row, where):
        for chunk in range(chunks):
            which, position = spots[chunk % 2]
            for k, group in enumerate(along[chunk % 2]):

                @pl.when(which == k)
                def _(chunk=chunk, place=group[chunk // 2], at=position * unit + inside):
                    copy(chunk, place, at, where).start()

        for place in rest:
            copy(chunks, place, row, where).start()

    def wait(where):
        for chunk in range(chunks):
            copy(chunk, along[chunk % 2][0][chunk // 2], 0, where).wait()
        for place in rest:
            copy(chunks, place, 0, where).wait()

    return start, wait


def place_of(tile):
    return jnp.stack(
        [
            lax.axis_index("y").astype(jnp.int32),
            lax.axis_index("x").astype(jnp.int32),
            lax.axis_index("c").astype(jnp.int32),
            jnp.int32(unit_tiles(tile)),
            jnp.int32(lax.axis_size("y")),
            jnp.int32(lax.axis_size("x")),
        ]
    )


def half_side(tokens, at):
    return pl.BlockSpec(
        (tokens, PADDED), lambda i, *_: (at, 0), pipeline_mode=pl.Buffered(1)
    )


def weight_grads(chunks, own, other, sides):
    rows, tokens = own.shape
    tile = 512 if unit_tiles(256) % 2 == 0 else 256
    source = pl.BlockSpec((tile, tokens), lambda i, *_: (i, 0))
    halves = [half_side(tokens, 0), half_side(tokens, 1)]
    out_shape = array_shapes(chunks, rows)
    return pl.pallas_call(
        functools.partial(weight_grads_body, chunks, tile),
        grid_spec=pltpu.PrefetchScalarGridSpec(
            num_scalar_prefetch=1,
            grid=(rows // tile,),
            in_specs=[source, source] + halves * 2,
            out_specs=[pl.BlockSpec(memory_space=pl.ANY)] * len(out_shape),
            scratch_shapes=[
                pltpu.VMEM((2, tile, PADDED), jnp.bfloat16),
                pltpu.SemaphoreType.DMA((2, 5)),
            ],
        ),
        out_shape=out_shape,
        compiler_params=pltpu.CompilerParams(vmem_limit_bytes=40 << 20),
        cost_estimate=pl.CostEstimate(
            flops=4 * rows * tokens * CUTS[-1],
            bytes_accessed=4 * rows * tokens + 2 * rows * PADDED,
            transcendentals=0,
        ),
        name="weight_grads",
    )(place_of(tile), own, other, sides[0], sides[0], sides[1], sides[1])


def attention_fill_body(chunks, owners, place_ref, *refs):
    own_ref, other_ref, side_ref, other_side_ref = refs[:4]
    outs = refs[4 + (len(refs) - 6) // 2 : -2]
    stage_ref, sems = refs[-2:]
    step = pl.program_id(0)
    slot = step % 2
    start, wait = place_copies(chunks, stage_ref, sems, split_places(outs, chunks), INNER)

    def put():
        product = jnp.dot(
            own_ref[...].T, side_ref[:, : CUTS[-1]], preferred_element_type=jnp.float32
        ) + jnp.dot(
            other_ref[...].T, other_side_ref[:, : CUTS[-1]], preferred_element_type=jnp.float32
        )
        stage_ref[slot, :, : CUTS[-1]] = product.astype(jnp.bfloat16)
        stage_ref[slot, :, CUTS[-1] :] = jnp.zeros((INNER, PADDED - CUTS[-1]), jnp.bfloat16)
        start(spots_of(0, place_ref), 0, step, step, slot)

    @pl.when(place_ref[2] < owners)
    def _():
        @pl.when(step >= 2)
        def _():
            wait(slot)

        put()

        @pl.when(step == pl.num_programs(0) - 1)
        def _():
            wait(0)
            wait(1)


def attention_fill(chunks, arrays, own, other, sides):
    tokens = own.shape[0]
    unit_rows = unit_tiles(TILE) * TILE
    owners = 4 * INNER // unit_rows
    steps = unit_rows // INNER

    def column(i, place_ref):
        return 0, jnp.minimum(place_ref[2], owners - 1) * steps + i

    def half(i, place_ref):
        return jnp.where(column(i, place_ref)[1] < 3, 0, 1), 0

    anywhere = pl.BlockSpec(memory_space=pl.ANY)
    return pl.pallas_call(
        functools.partial(attention_fill_body, chunks, owners),
        grid_spec=pltpu.PrefetchScalarGridSpec(
            num_scalar_prefetch=1,
            grid=(steps,),
            in_specs=[pl.BlockSpec((tokens, INNER), column)] * 2
            + [pl.BlockSpec((tokens, PADDED), half)] * 2
            + [anywhere] * len(arrays),
            out_specs=[anywhere] * len(arrays),
            scratch_shapes=[
                pltpu.VMEM((2, INNER, PADDED), jnp.bfloat16),
                pltpu.SemaphoreType.DMA((2, 5)),
            ],
        ),
        out_shape=[jax.ShapeDtypeStruct(array.shape, array.dtype) for array in arrays],
        input_output_aliases={5 + k: k for k in range(len(arrays))},
        compiler_params=pltpu.CompilerParams(vmem_limit_bytes=32 << 20),
        cost_estimate=pl.CostEstimate(
            flops=4 * unit_rows * tokens * CUTS[-1],
            bytes_accessed=4 * unit_rows * tokens + 2 * unit_rows * PADDED,
            transcendentals=0,
        ),
        name="attention_fill",
    )(place_of(TILE), own, other, *sides, *arrays)


def tied(first, second):
    return lax.optimization_barrier((first, second))


def chunk_width(chunks):
    return PADDED // 4 if chunks == 4 else PADDED // 6


class Scatter:
    def __init__(self):
        self.waiting, self.flying, self.results = {}, {}, {}

    def push(self, name, route, kept, sends):
        self.waiting[name] = (route, kept, sends)

    def settle(self, values, *names):
        arrays, values = tied({name: self.flying[name][1:] for name in names}, values)
        moves = {}
        for name in names:
            route = self.flying.pop(name)[0]
            kept, moved = arrays[name]
            if not route:
                self.results[name] = kept.astype(jnp.float32) + sum(
                    part.astype(jnp.float32) for part in moved
                )
                continue
            total = total_of(kept, moved)
            total = total.reshape((lax.axis_size(route[0]), -1) + total.shape[-1:])
            sends = stage_sends(total, route[0], 0)
            moves[name] = (route, pick(total, lax.axis_index(route[0]), 0), sends)
        if moves and all(move[0] == ("z",) for move in moves.values()):
            kept = jnp.concatenate([move[1] for move in moves.values()], axis=-1)
            sends = [
                jnp.concatenate(parts, axis=-1) for parts in zip(*(m[2] for m in moves.values()))
            ]
            moves = {tuple(moves): (("z",), kept, sends)}
        arrays, values = tied({name: move[1:] for name, move in moves.items()}, values)
        for name, (route, *_) in moves.items():
            self.waiting[name] = (route,) + tuple(arrays[name])
        return values

    def start(self, values, *names):
        arrays, values = tied({name: self.waiting[name][1:] for name in names}, values)
        for name in names:
            route = self.waiting.pop(name)[0]
            kept, sends = arrays[name]
            self.flying[name] = (route[1:], kept, stage_moves(sends, route[0]))
        return values

    def step(self, values, *names):
        others = set(self.waiting)
        values = self.settle(values, *names)
        return self.start(values, *(name for name in self.waiting if name not in others))


def total_of(value, moved):
    total = value.astype(jnp.float32)
    for part in moved:
        total = total + part.astype(jnp.float32)
    return total.astype(jnp.bfloat16)


def fetch_rows(local_rows):
    return lax.all_gather(local_rows, DEVICES, axis=0, tiled=True)


def layer_forward(stream, gathered, gain_one, gain_two, gate_low, context):
    normed, inverse_one = rms_forward(stream, gain_one)
    normed_low = normed.astype(jnp.bfloat16)
    projected = times_rows(normed_low, gathered[: 3 * INNER]).astype(jnp.bfloat16)
    queries = projected[:, :INNER]
    parts = [projected[:, INNER:]]
    if gate_low is not None:
        parts.append(jnp.broadcast_to(gate_low[:, None], (stream.shape[0], BLOCK)))
    shared = with_neighbours(jnp.concatenate(parts, axis=1))
    attended, full, log_total = attend_forward(queries, shared, context)
    middle = stream + times_plain(attended, gathered[3 * INNER : 4 * INNER])
    normed_two, inverse_two = rms_forward(middle, gain_two)
    normed_two_low = normed_two.astype(jnp.bfloat16)
    last = gate_low is not None
    result, *factors = ffn_forward(normed_two_low, None if last else middle, gathered)
    kept = (
        stream,
        inverse_one,
        normed_low,
        queries,
        shared,
        attended,
        full,
        log_total,
        middle,
        inverse_two,
        normed_two_low,
        factors,
    )
    return (result, kept)


def layer_backward(grad_out, kept, gathered, gain_one, gain_two, context, before):
    (
        stream,
        inverse_one,
        normed_low,
        queries,
        shared,
        attended,
        full,
        log_total,
        middle,
        inverse_two,
        normed_two_low,
        factors,
    ) = kept
    tokens = queries.shape[0]
    branch_low = grad_out.astype(jnp.bfloat16)
    sides = jnp.concatenate([normed_two_low, branch_low], axis=0)
    sides = jnp.pad(sides, ((0, 0), (0, PADDED - sides.shape[1])))
    sides = (sides, shift(sides, "c", 1))
    grad_normed_two, own, sent = ffn_backward(
        branch_low, factors[0], factors[1], gathered, factors[2], factors[3]
    )
    if before is not None:
        grad_normed_two, own, sent = before.step((grad_normed_two, own, sent), 0, 1)
    other = shift(sent, "c", 1)
    grad_middle, grad_gain_two = rms_backward(middle, inverse_two, gain_two, grad_normed_two)
    grad_middle = grad_out + grad_middle
    middle_low = grad_middle.astype(jnp.bfloat16)
    late_sides = jnp.concatenate([normed_low, middle_low], axis=0)
    late_sides = jnp.pad(late_sides, ((0, 0), (0, PADDED - late_sides.shape[1])))
    late_sides = (late_sides, shift(late_sides, "c", 1))
    grad_mixed = times_rows(middle_low, gathered[3 * INNER : 4 * INNER]).astype(jnp.bfloat16)
    grad_query, grad_shared, grad_table = attend_backward(
        queries, grad_mixed, full, shared, log_total, context
    )
    if before is not None:
        grad_query, grad_shared = before.settle((grad_query, grad_shared), 0, 1)
    grad_shared, own = lax.optimization_barrier((grad_shared, own))
    moving = start_back(grad_shared, tokens)
    chunks = 2 if before is None else 4
    arrays = weight_grads(chunks, own, other, sides)
    arrays, moving = lax.optimization_barrier((arrays, moving))
    if before is not None:
        arrays, moving = before.start((arrays, moving), (0, 1))
    grad_own = finish_back(*moving)
    grad_gate = grad_own[:, 2 * INNER :]
    grad_input_low = jnp.concatenate(
        [grad_query, grad_own[:, : 2 * INNER].astype(jnp.bfloat16)], axis=1
    )
    late = jnp.concatenate([grad_input_low, attended], axis=1)
    arrays = attention_fill(chunks, arrays, late, shift(late, "c", 1), late_sides)
    scatter = Scatter()
    along_y, along_x, rest = split_places(arrays, chunks)
    for chunk in range(chunks):
        route = ("y", "x", "z") if chunk % 2 == 0 else ("x", "y", "z")
        ordered = [group[chunk // 2] for group in (along_y, along_x)[chunk % 2]]
        scatter.push(chunk, route, ordered[-1], ordered[:-1])
    grad_input_low, grad_gate = scatter.start((grad_input_low, grad_gate), 0, 1)
    if rest:
        grad_input_low, grad_gate, rest = lax.optimization_barrier(
            (grad_input_low, grad_gate, rest)
        )
        rest = lax.psum_scatter(rest[0], ("y", "x", "z"), scatter_dimension=0, tiled=True)
    grad_normed = times_plain(grad_input_low, gathered[: 3 * INNER])
    grad_stream, grad_gain_one = rms_backward(stream, inverse_one, gain_one, grad_normed)
    return (grad_middle + grad_stream, grad_table, grad_gate, grad_gain_one, grad_gain_two, scatter, rest)


def per_device(
    inputs, layer3_rows, layer4_rows, norm_gains, gate_weight, rel_bias, segment_ids, cotangent
):
    seqs_here, tokens_here, width = inputs.shape
    first_pos = lax.axis_index("z") * tokens_here
    context = attention_context(segment_ids[0], first_pos, tokens_here, rel_bias)
    stream = inputs.reshape(tokens_here, width)
    gathered_three = fetch_rows(layer3_rows)
    after_three, kept_three = layer_forward(
        stream, gathered_three, norm_gains[0], norm_gains[1], None, context
    )
    gate_inverse = lax.rsqrt(jnp.mean(after_three * after_three, axis=1, keepdims=True) + epsilon)
    gate_normed = after_three * gate_inverse
    gate_logit = jnp.sum(gate_normed * gate_weight, axis=1) + gate_offset
    sigmoid_value = 1.0 / (1.0 + jnp.exp(-gate_logit))
    gate_mask = gate_scale * sigmoid_value
    gate_low = gate_mask.astype(jnp.bfloat16)
    gathered_four = fetch_rows(layer4_rows)
    hidden_four, kept_four = layer_forward(
        after_three, gathered_four, norm_gains[2], norm_gains[3], gate_low, context
    )
    grad_three_out, table_four, grad_gate, gain_four_one, gain_four_two, before, rest = (
        layer_backward(
            cotangent.reshape(tokens_here, width),
            kept_four,
            gathered_four,
            norm_gains[2],
            norm_gains[3],
            context,
            None,
        )
    )
    grad_logit = grad_gate[:, 0] * gate_scale * sigmoid_value * (1.0 - sigmoid_value)
    grad_gate_weight = jnp.sum(grad_logit[:, None] * gate_normed, axis=0)
    gate_stream = stream_backward(after_three, gate_inverse, grad_logit[:, None] * gate_weight)
    grad_input, table_three, unused, gain_three_one, gain_three_two, scatter, _ = layer_backward(
        grad_three_out + gate_stream,
        kept_three,
        gathered_three,
        norm_gains[0],
        norm_gains[1],
        context,
        before,
    )
    table = jnp.pad((table_three + table_four).reshape(1, -1), ((0, 0), (0, width - 6 * BUCKETS)))
    small_sums = jnp.stack(
        [gain_three_one, gain_three_two, gain_four_one, gain_four_two, grad_gate_weight, table[0]]
    )
    small = hop(small_sums, "c")
    small = before.settle(small, (0, 1))
    small = scatter.step(small, 0, 1)
    small = scatter.start(small, 2, 3)
    small, hidden_four = tied(small, hidden_four)
    after_four = kept_four[8] + times_plain(hidden_four, gathered_four[4 * INNER + 2 * FF :])
    small, after_four = scatter.step((small, after_four), 0, 1)
    small, rest = scatter.settle((small, rest), (0, 1))
    small = scatter.step(small, 2, 3)
    for bit in range(1, lax.axis_size("z")):
        if bit & (bit - 1) == 0:
            small = hop(small, "z", bit)
    small = scatter.step(small, 2, 3)
    small = hop(small, "x")
    for bit in range(1, lax.axis_size("y")):
        if bit & (bit - 1) == 0:
            small = hop(small, "y", bit)
    summed = scatter.settle(small, (2, 3))
    local_three = jnp.concatenate([scatter.results[pair] for pair in ((0, 1), (2, 3))], axis=1)
    local_four = jnp.concatenate([before.results[(0, 1)], rest.astype(jnp.float32)], axis=1)
    local_three, local_four = local_three[:, :width], local_four[:, :width]
    return (
        after_four.reshape(inputs.shape),
        gate_mask.reshape(seqs_here, tokens_here),
        grad_input.reshape(inputs.shape),
        local_three,
        local_four,
        summed[:4],
        summed[4],
        summed[5, : 6 * BUCKETS].reshape(BUCKETS, HEADS),
    )


def solution(mesh):
    outer, inner = mesh.devices.shape
    fine = Mesh(mesh.devices.reshape(outer // 4, 2, 2, inner), DEVICES)
    batch = ("y", "x", "c")
    tokens = P(batch, "z", None)
    rows = P(DEVICES, None)
    return jax.shard_map(
        per_device,
        mesh=fine,
        in_specs=(tokens, rows, rows, P(), P(), P(), P(batch, None), tokens),
        out_specs=(tokens, P(batch, "z"), tokens, rows, rows, P(), P(), P()),
        check_vma=False,
    )
```

```python
import functools

import jax
import jax.numpy as jnp
from jax import lax
from jax.experimental import pallas as pl
from jax.experimental.pallas import tpu as pltpu
from jax.sharding import Mesh
from jax.sharding import PartitionSpec as P

HEADS = 6
PAIRS = 3
BLOCK = 128
WIDE = 2 * BLOCK
INNER = 384
BUCKETS = 32
FF = 3584
REACH = 799
HALO = 896
TILE = 256
ATTENTION_TILES = 4 * INNER // TILE
OFFSETS = 5
PADDED = 1536
FORWARD_TILE = 512
CUTS = (0, 1472)
DEVICES = ("y", "x", "c", "z")
epsilon = 1e-06
gate_scale = -30.0
gate_offset = -3.5
masked_out = -1e30
limits = (12, 16, 23, 32, 46, 64, 91)
both_last = (((1,), (1,)), ((), ()))


def bucket_of(relative):
    magnitude = jnp.abs(relative)
    beyond = jnp.zeros_like(magnitude)
    for bound_value in limits:
        beyond = beyond + (magnitude >= bound_value).astype(jnp.int32)
    inside = jnp.where(magnitude < 8, magnitude, 8 + beyond)
    return inside + 16 * (relative > 0).astype(jnp.int32)


def near_buckets(offset):
    if offset < 0:
        return range(1, 16)
    if offset > 0:
        return range(17, 32)
    return range(0, 32)


def tile_buckets(offset, width):
    key_at = lax.broadcasted_iota(jnp.int32, (BLOCK, width), 0)
    query_at = lax.broadcasted_iota(jnp.int32, (BLOCK, width), 1) % BLOCK
    return bucket_of(offset * BLOCK + key_at - query_at)


def bias_body(table_ref, tiles_ref):
    head = pl.program_id(0)
    tiles_ref[0, 0] = jnp.full((BLOCK, BLOCK), table_ref[15, head], jnp.float32)
    tiles_ref[0, 4] = jnp.full((BLOCK, BLOCK), table_ref[31, head], jnp.float32)
    for offset in (-1, 0, 1):
        buckets = tile_buckets(offset, BLOCK)
        tile = jnp.zeros((BLOCK, BLOCK), jnp.float32)
        for bucket in near_buckets(offset):
            tile = jnp.where(buckets == bucket, table_ref[bucket, head], tile)
        tiles_ref[0, offset + 2] = tile


def bias_tiles(rel_bias):
    return pl.pallas_call(
        bias_body,
        grid=(HEADS,),
        in_specs=[pl.BlockSpec(memory_space=pltpu.SMEM)],
        out_specs=pl.BlockSpec((1, OFFSETS, BLOCK, BLOCK), lambda h: (h, 0, 0, 0)),
        out_shape=jax.ShapeDtypeStruct((HEADS, OFFSETS, BLOCK, BLOCK), jnp.float32),
        name="bias_tiles",
    )(rel_bias)


def lane_masks():
    lane = lax.broadcasted_iota(jnp.int32, (BLOCK, BLOCK), 1)
    low = jnp.where(lane < 64, 1.0, 0.0).astype(jnp.bfloat16)
    high = jnp.where(lane < 64, 0.0, 1.0).astype(jnp.bfloat16)
    return low, high


def stacked(block, masks):
    low, high = masks
    return jnp.concatenate([block * low, block * high], axis=0)


def pair_cols(pair):
    return slice(pair * BLOCK, (pair + 1) * BLOCK)


def value_cols(pair):
    return slice(INNER + pair * BLOCK, INNER + (pair + 1) * BLOCK)


def block_rows(block):
    return pl.ds(pl.multiple_of(block * BLOCK, BLOCK), BLOCK)


def wide_rows(block):
    return pl.ds(pl.multiple_of(block * WIDE, WIDE), WIDE)


def fold(values):
    return values.reshape(values.shape[0] // 8, 8, WIDE)


def shift_tile(gated, rows, own_segment, segment_ref, shared_ref):
    same = segment_ref[rows, :] == own_segment
    inside = shared_ref[rows, 2 * INNER :].astype(jnp.float32) if gated else 0.0
    shift = jnp.where(same, inside, masked_out)
    return jnp.concatenate([shift, shift], axis=1)


def used_blocks(low_ref, high_ref):
    last = pl.num_programs(0) - 1
    return low_ref[0] // 2 * 2, (high_ref[last] + 1) // 2 * 2


def tile_offsets(block, own_block):
    return [jnp.clip(2 * block + k - own_block, -2, 2) + 2 for k in range(2)]


def bias_pair(bias_ref, pair, offsets):
    halves = [
        jnp.concatenate([bias_ref[2 * pair, at], bias_ref[2 * pair + 1, at]], axis=1)
        for at in offsets
    ]
    return jnp.concatenate(halves, axis=0)


def pick_heads(wide):
    return jnp.concatenate([wide[:64, :BLOCK], wide[64:, BLOCK:]], axis=0)


def forward_body(gated, low_ref, high_ref, *refs):
    query_ref, shared_ref, own_ref, segment_ref, bias_ref = refs[:5]
    mixed_ref, full_ref, total_ref, turned_ref, score_ref, sum_ref = refs[5:]
    step = pl.program_id(0)

    @pl.when(step == 0)
    def _():
        @pl.loop(*used_blocks(low_ref, high_ref))
        def _(block):
            rows = block_rows(block)
            turned_ref[:, rows] = shared_ref[rows, INNER : 2 * INNER].T

    first, last = low_ref[step] // 2, (high_ref[step] + 1) // 2
    own_block = HALO // BLOCK + step
    own_segment = own_ref[0]
    masks = lane_masks()
    queries = [stacked(query_ref[:, pair_cols(pair)], masks) for pair in range(PAIRS)]

    def scores(block, peaks):
        rows = wide_rows(block)
        shift = shift_tile(gated, rows, own_segment, segment_ref, shared_ref)
        offsets = tile_offsets(block, own_block)
        new_peaks = []
        for pair in range(PAIRS):
            score = lax.dot_general(
                shared_ref[rows, pair_cols(pair)],
                queries[pair],
                both_last,
                preferred_element_type=jnp.float32,
            )
            score = score + bias_pair(bias_ref, pair, offsets) + shift
            score_ref[pair, block] = score
            new_peaks.append(jnp.maximum(peaks[pair], jnp.max(fold(score), axis=0)))
        return tuple(new_peaks)

    start = jnp.full((8, WIDE), -3e38, jnp.float32)
    peaks = lax.fori_loop(first, last, scores, (start,) * PAIRS)
    peaks = [jnp.max(peak, axis=0, keepdims=True) for peak in peaks]
    sum_ref[...] = jnp.zeros_like(sum_ref)

    def mix(block, totals):
        new_totals = []
        for pair in range(PAIRS):
            weight = jnp.exp(score_ref[pair, block] - peaks[pair])
            new_totals.append(totals[pair] + jnp.sum(fold(weight), axis=0))
            sum_ref[pair] += jnp.dot(
                turned_ref[pair_cols(pair), wide_rows(block)],
                weight.astype(jnp.bfloat16),
                preferred_element_type=jnp.float32,
            )
        return tuple(new_totals)

    totals = lax.fori_loop(first, last, mix, (jnp.zeros((8, WIDE), jnp.float32),) * PAIRS)
    for pair in range(PAIRS):
        row_total = jnp.sum(totals[pair], axis=0, keepdims=True)
        mixed = pick_heads(sum_ref[pair] * (1.0 / row_total))
        full_ref[:, pair_cols(pair)] = mixed.T
        mixed_ref[:, pair_cols(pair)] = full_ref[:, pair_cols(pair)].astype(jnp.bfloat16)
        total_ref[0, pair : pair + 1, :] = peaks[pair] + jnp.log(row_total)


def whole(shape):
    return pl.BlockSpec(shape, lambda i, *_: (0,) * len(shape), pipeline_mode=pl.Buffered(1))


def rows_spec(width):
    return pl.BlockSpec((BLOCK, width), lambda i, *_: (i, 0))


def attend_forward(queries, shared, context):
    lows, highs, own_rows, segment_wide, tiles = context
    tokens, (length, width) = queries.shape[0], shared.shape
    steps, key_blocks = tokens // BLOCK, length // BLOCK
    return pl.pallas_call(
        functools.partial(forward_body, width > 2 * INNER),
        grid_spec=pltpu.PrefetchScalarGridSpec(
            num_scalar_prefetch=2,
            grid=(steps,),
            in_specs=[
                rows_spec(INNER),
                whole((length, width)),
                pl.BlockSpec((1, 1, BLOCK), lambda i, *_: (i, 0, 0)),
                whole((length, BLOCK)),
                whole(tiles.shape),
            ],
            out_specs=[
                rows_spec(INNER),
                rows_spec(INNER),
                pl.BlockSpec((1, 8, WIDE), lambda i, *_: (i, 0, 0)),
            ],
            scratch_shapes=[
                pltpu.VMEM((INNER, length), jnp.bfloat16),
                pltpu.VMEM((PAIRS, key_blocks // 2, WIDE, WIDE), jnp.float32),
                pltpu.VMEM((PAIRS, BLOCK, WIDE), jnp.float32),
            ],
        ),
        out_shape=[
            jax.ShapeDtypeStruct((tokens, INNER), jnp.bfloat16),
            jax.ShapeDtypeStruct((tokens, INNER), jnp.float32),
            jax.ShapeDtypeStruct((steps, 8, WIDE), jnp.float32),
        ],
        compiler_params=pltpu.CompilerParams(vmem_limit_bytes=40 << 20),
        cost_estimate=pl.CostEstimate(
            flops=tokens * length * INNER * 4,
            bytes_accessed=8 << 20,
            transcendentals=tokens * length * 3,
        ),
        name="attend_forward",
    )(lows, highs, queries, shared, own_rows, segment_wide, tiles)


def backward_body(gated, low_ref, high_ref, *refs):
    query_ref, grad_ref, full_ref, shared_ref, own_ref, segment_ref, bias_ref, total_ref = refs[:8]
    grad_query_ref, grad_shared_ref, bucket_ref = refs[8:11]
    turned_ref, sum_ref, bias_sum_ref, turn_sum_ref = refs[11:]
    step = pl.program_id(0)

    @pl.when(step == 0)
    def _():
        bias_sum_ref[...] = jnp.zeros_like(bias_sum_ref)

        @pl.loop(*used_blocks(low_ref, high_ref))
        def _(block):
            rows = block_rows(block)
            turned_ref[:, rows] = shared_ref[rows, :INNER].T
            sum_ref[rows, :] = jnp.zeros((BLOCK, sum_ref.shape[1]), jnp.float32)

    first, last = low_ref[step] // 2, (high_ref[step] + 1) // 2
    own_block = HALO // BLOCK + step
    own_segment = own_ref[0]
    masks = lane_masks()
    queries = [stacked(query_ref[:, pair_cols(pair)], masks) for pair in range(PAIRS)]
    grads = [stacked(grad_ref[:, pair_cols(pair)], masks) for pair in range(PAIRS)]
    totals = [total_ref[0, pair : pair + 1, :] for pair in range(PAIRS)]

    deltas = []
    for pair in range(PAIRS):
        cols = pair_cols(pair)
        product = (grad_ref[:, cols].astype(jnp.float32) * full_ref[:, cols]).T
        halves = [jnp.sum(half, axis=0, keepdims=True) for half in (product[:64], product[64:])]
        deltas.append(jnp.concatenate(halves, axis=1))
    turn_sum_ref[...] = jnp.zeros_like(turn_sum_ref)

    @pl.loop(first, last)
    def _(block):
        rows = wide_rows(block)
        shift = shift_tile(gated, rows, own_segment, segment_ref, shared_ref)
        offsets = tile_offsets(block, own_block)
        gate_part = jnp.zeros((WIDE, BLOCK), jnp.float32)
        for pair in range(PAIRS):
            cols = pair_cols(pair)
            score = lax.dot_general(
                shared_ref[rows, cols], queries[pair], both_last, preferred_element_type=jnp.float32
            )
            pull = lax.dot_general(
                shared_ref[rows, value_cols(pair)],
                grads[pair],
                both_last,
                preferred_element_type=jnp.float32,
            )
            prob = jnp.exp(score + bias_pair(bias_ref, pair, offsets) + shift - totals[pair])
            sum_ref[rows, value_cols(pair)] += jnp.dot(
                prob.astype(jnp.bfloat16), grads[pair], preferred_element_type=jnp.float32
            )
            grad_score = prob * (pull - deltas[pair])
            bias_sum_ref[pair, offsets[0]] += grad_score[:BLOCK]
            bias_sum_ref[pair, offsets[1]] += grad_score[BLOCK:]
            if gated:
                gate_part = gate_part + (grad_score[:, :BLOCK] + grad_score[:, BLOCK:])
            score_low = grad_score.astype(jnp.bfloat16)
            sum_ref[rows, cols] += jnp.dot(
                score_low, queries[pair], preferred_element_type=jnp.float32
            )
            turn_sum_ref[pair] += jnp.dot(
                turned_ref[cols, rows], score_low, preferred_element_type=jnp.float32
            )
        if gated:
            sum_ref[rows, 2 * INNER :] += gate_part

    for pair in range(PAIRS):
        grad_query_ref[:, pair_cols(pair)] = pick_heads(turn_sum_ref[pair]).T.astype(jnp.bfloat16)

    @pl.when(step == pl.num_programs(0) - 1)
    def _():
        grad_shared_ref[...] = jnp.zeros_like(grad_shared_ref)

        @pl.loop(*used_blocks(low_ref, high_ref))
        def _(block):
            rows = block_rows(block)
            both = slice(0, 2 * INNER)
            grad_shared_ref[rows, both] = sum_ref[rows, both].astype(jnp.bfloat16)
            if gated:
                gate_total = jnp.sum(sum_ref[rows, 2 * INNER :], axis=1, keepdims=True)
                grad_shared_ref[rows, 2 * INNER :] = jnp.broadcast_to(
                    gate_total, (BLOCK, BLOCK)
                ).astype(jnp.bfloat16)

        tables = {offset: tile_buckets(offset, WIDE) for offset in (-1, 0, 1)}

        @pl.loop(0, PAIRS)
        def _(pair):
            for bucket in range(BUCKETS):
                part = jnp.zeros((8, WIDE), jnp.float32)
                for offset in (-1, 0, 1):
                    if bucket in near_buckets(offset):
                        chosen = jnp.where(
                            tables[offset] == bucket, bias_sum_ref[pair, offset + 2], 0.0
                        )
                        part = part + jnp.sum(fold(chosen), axis=0)
                if bucket == 15:
                    part = part + jnp.sum(fold(bias_sum_ref[pair, 0]), axis=0)
                if bucket == 31:
                    part = part + jnp.sum(fold(bias_sum_ref[pair, 4]), axis=0)
                bucket_ref[pair, bucket : bucket + 1, :] = jnp.sum(part, axis=0, keepdims=True)


def attend_backward(queries, grad_mixed, full, shared, log_total, context):
    lows, highs, own_rows, segment_wide, tiles = context
    tokens, (length, width) = queries.shape[0], shared.shape
    steps = tokens // BLOCK
    grad_query, grad_shared, bucket_sums = pl.pallas_call(
        functools.partial(backward_body, width > 2 * INNER),
        grid_spec=pltpu.PrefetchScalarGridSpec(
            num_scalar_prefetch=2,
            grid=(steps,),
            in_specs=[
                rows_spec(INNER),
                rows_spec(INNER),
                rows_spec(INNER),
                whole((length, width)),
                pl.BlockSpec((1, 1, BLOCK), lambda i, *_: (i, 0, 0)),
                whole((length, BLOCK)),
                whole(tiles.shape),
                pl.BlockSpec((1, 8, WIDE), lambda i, *_: (i, 0, 0)),
            ],
            out_specs=[
                rows_spec(INNER),
                whole((length, width)),
                whole((PAIRS, BUCKETS, WIDE)),
            ],
            scratch_shapes=[
                pltpu.VMEM((INNER, length), jnp.bfloat16),
                pltpu.VMEM((length, width), jnp.float32),
                pltpu.VMEM((PAIRS, OFFSETS, BLOCK, WIDE), jnp.float32),
                pltpu.VMEM((PAIRS, BLOCK, WIDE), jnp.float32),
            ],
        ),
        out_shape=[
            jax.ShapeDtypeStruct((tokens, INNER), jnp.bfloat16),
            jax.ShapeDtypeStruct((length, width), jnp.bfloat16),
            jax.ShapeDtypeStruct((PAIRS, BUCKETS, WIDE), jnp.float32),
        ],
        compiler_params=pltpu.CompilerParams(vmem_limit_bytes=48 << 20),
        cost_estimate=pl.CostEstimate(
            flops=tokens * length * INNER * 10,
            bytes_accessed=12 << 20,
            transcendentals=tokens * length * 3,
        ),
        name="attend_backward",
    )(lows, highs, queries, grad_mixed, full, shared, own_rows, segment_wide, tiles, log_total)
    table = jnp.sum(bucket_sums.reshape(PAIRS, BUCKETS, 2, BLOCK), axis=3)
    return grad_query, grad_shared, table.transpose(1, 0, 2).reshape(BUCKETS, HEADS)


def attention_context(segment_row, first_pos, tokens, rel_bias):
    steps = tokens // BLOCK
    padded = jnp.pad(segment_row, (HALO, 0), constant_values=-1)
    padded = jnp.pad(padded, (0, HALO), constant_values=1000)
    window = lax.dynamic_slice_in_dim(padded, first_pos, tokens + 2 * HALO, 0)
    own = window[HALO : HALO + tokens].reshape(steps, 1, BLOCK)
    lows = jnp.sum(window[None, :] < own[:, 0, :1], axis=1, dtype=jnp.int32) // BLOCK
    ends = jnp.sum(window[None, :] <= own[:, 0, BLOCK - 1 :], axis=1, dtype=jnp.int32)
    highs = (ends + BLOCK - 1) // BLOCK
    segment_wide = jnp.broadcast_to(window[:, None], (window.shape[0], BLOCK))
    return lows, highs, own, segment_wide, bias_tiles(rel_bias)


def rms_forward(stream, gain_row):
    inverse = lax.rsqrt(jnp.mean(stream * stream, axis=1, keepdims=True) + epsilon)
    return (stream * inverse * gain_row, inverse)


def stream_backward(stream, inverse, scaled):
    return inverse * scaled - stream * inverse**3 * jnp.mean(scaled * stream, axis=1, keepdims=True)


def rms_backward(stream, inverse, gain_row, grad_normed):
    grad_gain = jnp.sum(grad_normed * stream * inverse, axis=0)
    return (stream_backward(stream, inverse, gain_row * grad_normed), grad_gain)


def gelu_tanh(values):
    return 0.5 * values * (1.0 + jnp.tanh(0.7978845608028654 * (values + 0.044715 * values**3)))


def times_rows(left_side, weight):
    return lax.dot_general(
        left_side, weight, (((1,), (1,)), ((), ())), preferred_element_type=jnp.float32
    )


def times_plain(left_side, weight):
    return jnp.dot(left_side, weight, preferred_element_type=jnp.float32)


def outer_sum(left_side, right_side):
    return lax.dot_general(
        left_side, right_side, (((0,), (0,)), ((), ())), preferred_element_type=jnp.float32
    )


def shift(value, axis, amount):
    count = lax.axis_size(axis)
    return lax.ppermute(value, axis, [(i, (i + amount) % count) for i in range(count)])


def slide(value, amount):
    count = lax.axis_size("z")
    pairs = [(i, i + amount) for i in range(count) if 0 <= i + amount < count]
    return lax.ppermute(value, "z", pairs)


def far_pair(near_start, near_end, distance):
    count = lax.axis_size("z")
    first_half = lax.axis_index("z") < distance
    sent = jnp.where(first_half, near_end, near_start)
    pairs = [(i, (i + distance) % count) for i in range(count)]
    got = lax.ppermute(sent, "z", pairs)
    return got


def far_split(got, distance):
    first_half = lax.axis_index("z") < distance
    none = jnp.zeros_like(got)
    return jnp.where(first_half, none, got), jnp.where(first_half, got, none)


def halo_pieces(tokens):
    pieces = []
    distance, covered = 1, 0
    while covered < HALO:
        span = min(tokens, HALO - covered)
        needed = min(span, -(-(REACH - covered) // 16) * 16)
        pieces.append((distance, span, needed))
        distance, covered = distance + 1, covered + span
    return pieces


def with_neighbours(own):
    tokens = own.shape[0]
    before, after = [], []
    for distance, span, needed in halo_pieces(tokens):
        if distance < lax.axis_size("z"):
            if 2 * distance == lax.axis_size("z"):
                left, right = far_split(
                    far_pair(own[:needed], own[tokens - needed :], distance), distance
                )
            else:
                left = slide(own[tokens - needed :], distance)
                right = slide(own[:needed], -distance)
            before.append(jnp.pad(left, ((span - needed, 0), (0, 0))))
            after.append(jnp.pad(right, ((0, span - needed), (0, 0))))
        else:
            empty = jnp.zeros((span, own.shape[1]), own.dtype)
            before.append(empty)
            after.append(empty)
    return jnp.concatenate(before[::-1] + [own] + after, axis=0)


def start_back(window, tokens):
    moved = []
    covered = 0
    for distance, span, needed in halo_pieces(tokens):
        if distance < lax.axis_size("z"):
            left_end = HALO - covered
            right_start = HALO + tokens + covered
            left = window[left_end - needed : left_end]
            right = window[right_start : right_start + needed]
            if 2 * distance == lax.axis_size("z"):
                moved.append((far_pair(left, right, distance),))
            else:
                moved.append((slide(left, -distance), slide(right, distance)))
        covered += span
    return window[HALO : HALO + tokens], moved


def finish_back(own, moved):
    tokens = own.shape[0]
    total = own.astype(jnp.float32)
    for distance, pair in enumerate(moved, 1):
        if len(pair) == 1:
            ahead, back = far_split(pair[0], distance)
        else:
            back, ahead = pair
        needed = back.shape[0]
        total = total + jnp.pad(back.astype(jnp.float32), ((tokens - needed, 0), (0, 0)))
        total = total + jnp.pad(ahead.astype(jnp.float32), ((0, tokens - needed), (0, 0)))
    return total


def hop(value, axis, bit=1):
    pairs = [(i, i ^ bit) for i in range(lax.axis_size(axis))]
    return value + lax.ppermute(value, axis, pairs)


def pick(value, index, axis):
    return lax.dynamic_index_in_dim(value, index, axis, keepdims=False)


def stage_sends(value, axis_name, axis):
    count, here = lax.axis_size(axis_name), lax.axis_index(axis_name)
    return [pick(value, (here + k) % count, axis) for k in range(1, count)]


def stage_moves(sends, axis_name):
    return [shift(sent, axis_name, k + 1) for k, sent in enumerate(sends)]


def gelu_parts(values):
    squared = values * values
    slope = jnp.tanh(0.7978845608028654 * (values + 0.044715 * values * squared))
    active = 0.5 * values * (1.0 + slope)
    inner = 0.7978845608028654 * (1.0 + 3.0 * 0.044715 * squared)
    return active, 0.5 * (1.0 + slope) + 0.5 * values * (1.0 - slope * slope) * inner


def turned_rows(core_ref, kept_ref, sent_ref, stage_ref, sems):
    mine, unit = core_ref[0], core_ref[1]
    parts = FORWARD_TILE // TILE

    def copy(lane, part, place, at, where):
        spot = pl.ds(pl.multiple_of(at * TILE, TILE), TILE)
        source = stage_ref.at[where, lane, part * TILE : (part + 1) * TILE, :]
        return pltpu.make_async_copy(source, place.at[spot, :], sems.at[where, lane, part])

    def put(lane, kind, step, turned):
        slot = step % 2
        stage_ref[slot, lane] = turned
        for part in range(parts):
            target = ATTENTION_TILES + kind * (FF // TILE) + step * parts + part
            own = (target // unit) % 2 == mine
            at = (target // (2 * unit)) * unit + target % unit

            @pl.when(own)
            def _(part=part, at=at):
                copy(lane, part, kept_ref, at, slot).start()

            @pl.when(jnp.logical_not(own))
            def _(part=part, at=at):
                copy(lane, part, sent_ref, at, slot).start()

    def wait(lanes, where):
        for lane in range(lanes):
            for part in range(parts):
                copy(lane, part, kept_ref, 0, where).wait()

    return put, wait


def ffn_forward_body(whole_layer, core_ref, *refs):
    normed_ref, gelu_ref, linear_ref = refs[:3]
    if whole_layer:
        middle_ref, down_ref, result_ref = refs[3:6]
    else:
        hidden_ref = refs[3]
    gelu_factor_ref, linear_factor_ref, kept_ref, sent_ref, stage_ref, sems = refs[-6:]
    step = pl.program_id(0)
    put, wait = turned_rows(core_ref, kept_ref, sent_ref, stage_ref, sems)

    if whole_layer:

        @pl.when(step == 0)
        def _():
            result_ref[...] = middle_ref[...]

    @pl.when(step >= 2)
    def _():
        wait(1, step % 2)

    active, slope = gelu_parts(times_rows(normed_ref[...], gelu_ref[...]))
    linear = times_rows(normed_ref[...], linear_ref[...])
    gelu_factor_ref[...] = slope * linear
    linear_factor_ref[...] = active
    hidden = (active * linear).astype(jnp.bfloat16)
    put(0, 2, step, hidden.T)
    if whole_layer:
        result_ref[...] += times_plain(hidden, down_ref[...])
    else:
        hidden_ref[...] = hidden

    @pl.when(step == pl.num_programs(0) - 1)
    def _():
        wait(1, 0)
        wait(1, 1)


def resident(shape):
    return pl.BlockSpec(shape, lambda *_: (0,) * len(shape), pipeline_mode=pl.Buffered(1))


def core_units():
    return jnp.stack([lax.axis_index("c").astype(jnp.int32), jnp.int32(unit_tiles(TILE))])


def hidden_weight(kind, width):
    first = (4 * INNER + kind * FF) // FORWARD_TILE
    return pl.BlockSpec((FORWARD_TILE, width), lambda i, *_: (first + i, 0))


def turned_scratch(lanes, tokens):
    return [
        pltpu.VMEM((2, lanes, FORWARD_TILE, tokens), jnp.bfloat16),
        pltpu.SemaphoreType.DMA((2, lanes, FORWARD_TILE // TILE)),
    ]


def ffn_forward(normed, middle, gathered):
    tokens, width = normed.shape
    half = (4 * INNER + 3 * FF) // 2
    hidden = pl.BlockSpec((tokens, FORWARD_TILE), lambda i, *_: (0, i))
    side = resident((tokens, width))
    anywhere = pl.BlockSpec(memory_space=pl.ANY)
    operands = [normed, gathered, gathered]
    in_specs = [side, hidden_weight(0, width), hidden_weight(1, width)]
    first_spec, first_shape = hidden, jax.ShapeDtypeStruct((tokens, FF), jnp.bfloat16)
    if middle is not None:
        operands += [middle, gathered]
        in_specs += [side, hidden_weight(2, width)]
        first_spec, first_shape = side, jax.ShapeDtypeStruct((tokens, width), jnp.float32)
    return pl.pallas_call(
        functools.partial(ffn_forward_body, middle is not None),
        grid_spec=pltpu.PrefetchScalarGridSpec(
            num_scalar_prefetch=1,
            grid=(FF // FORWARD_TILE,),
            in_specs=in_specs,
            out_specs=[first_spec, hidden, hidden, anywhere, anywhere],
            scratch_shapes=turned_scratch(1, tokens),
        ),
        out_shape=[
            first_shape,
            jax.ShapeDtypeStruct((tokens, FF), jnp.float32),
            jax.ShapeDtypeStruct((tokens, FF), jnp.float32),
            jax.ShapeDtypeStruct((half, tokens), jnp.bfloat16),
            jax.ShapeDtypeStruct((half, tokens), jnp.bfloat16),
        ],
        compiler_params=pltpu.CompilerParams(vmem_limit_bytes=52 << 20),
        cost_estimate=pl.CostEstimate(
            flops=6 * tokens * FF * width,
            bytes_accessed=6 * FF * width + 10 * tokens * FF,
            transcendentals=tokens * FF,
        ),
        name="ffn_forward",
    )(core_units(), *operands)


def ffn_backward_body(core_ref, *refs):
    branch_ref, gelu_factor_ref, linear_factor_ref, gelu_ref, linear_ref, down_ref = refs[:6]
    grad_ref, kept_ref, sent_ref, stage_ref, sems = refs[8:]
    step = pl.program_id(0)
    put, wait = turned_rows(core_ref, kept_ref, sent_ref, stage_ref, sems)

    @pl.when(step == 0)
    def _():
        grad_ref[...] = jnp.zeros_like(grad_ref)

    @pl.when(step >= 2)
    def _():
        wait(2, step % 2)

    grad_hidden = times_rows(branch_ref[...], down_ref[...])
    grad_gelu = (grad_hidden * gelu_factor_ref[...]).astype(jnp.bfloat16)
    grad_linear = (grad_hidden * linear_factor_ref[...]).astype(jnp.bfloat16)
    put(0, 0, step, grad_gelu.T)
    put(1, 1, step, grad_linear.T)
    grad_ref[...] += times_plain(grad_gelu, gelu_ref[...]) + times_plain(
        grad_linear, linear_ref[...]
    )

    @pl.when(step == pl.num_programs(0) - 1)
    def _():
        wait(2, 0)
        wait(2, 1)


def unit_tiles(tile):
    rows = 4 * INNER + 3 * FF
    return rows // tile // (2 * lax.axis_size("y") * lax.axis_size("x"))


def ffn_backward(branch, gelu_factor, linear_factor, gathered, kept, sent):
    tokens, width = branch.shape
    hidden = pl.BlockSpec((tokens, FORWARD_TILE), lambda i, *_: (0, i))
    side = resident((tokens, width))
    anywhere = pl.BlockSpec(memory_space=pl.ANY)
    return pl.pallas_call(
        ffn_backward_body,
        grid_spec=pltpu.PrefetchScalarGridSpec(
            num_scalar_prefetch=1,
            grid=(FF // FORWARD_TILE,),
            in_specs=[side, hidden, hidden]
            + [hidden_weight(kind, width) for kind in range(3)]
            + [anywhere, anywhere],
            out_specs=[side, anywhere, anywhere],
            scratch_shapes=turned_scratch(2, tokens),
        ),
        out_shape=[
            jax.ShapeDtypeStruct((tokens, width), jnp.float32),
            jax.ShapeDtypeStruct(kept.shape, kept.dtype),
            jax.ShapeDtypeStruct(sent.shape, sent.dtype),
        ],
        input_output_aliases={7: 1, 8: 2},
        compiler_params=pltpu.CompilerParams(vmem_limit_bytes=52 << 20),
        cost_estimate=pl.CostEstimate(
            flops=6 * tokens * FF * width,
            bytes_accessed=6 * FF * width + 12 * tokens * FF,
            transcendentals=0,
        ),
        name="ffn_backward",
    )(core_units(), branch, gelu_factor, linear_factor, gathered, gathered, gathered, kept, sent)


def spots_of(unit_at, place_ref):
    here_y, here_x, size_y, size_x = place_ref[0], place_ref[1], place_ref[4], place_ref[5]
    row, column = unit_at // size_x, unit_at % size_x
    return (
        ((row + 2 * size_y - here_y - 1) % size_y, column),
        ((column + 2 * size_x - here_x - 1) % size_x, row),
    )


def weight_grads_body(chunks, tile, place_ref, *refs):
    own_ref, other_ref, normed_ref, branch_ref, other_normed_ref, other_branch_ref = refs[:6]
    stage_ref, sems = refs[-2:]
    step = pl.program_id(0)
    unit = place_ref[3]
    at = (step // unit * 2 + place_ref[2]) * unit + step % unit
    first, second = 4 * INNER // tile, (4 * INNER + 2 * FF) // tile
    slot = step % 2
    places = split_places(refs[6:-2], chunks)
    start, wait = place_copies(chunks, stage_ref, sems, places, tile)

    def put(product):
        stage_ref[slot, :, : CUTS[-1]] = product.astype(jnp.bfloat16)
        start(spots_of(step // unit, place_ref), unit, step % unit, step, slot)

    def both(side_ref, other_side_ref):
        return jnp.dot(
            own_ref[...], side_ref[:, : CUTS[-1]], preferred_element_type=jnp.float32
        ) + jnp.dot(
            other_ref[...], other_side_ref[:, : CUTS[-1]], preferred_element_type=jnp.float32
        )

    @pl.when(step < 2)
    def _():
        stage_ref[slot, :, CUTS[-1] :] = jnp.zeros((tile, PADDED - CUTS[-1]), jnp.bfloat16)

    @pl.when(step >= 2)
    def _():
        wait(slot)

    @pl.when(at < first)
    def _():
        put(jnp.zeros((tile, CUTS[-1]), jnp.float32))

    @pl.when((at >= first) & (at < second))
    def _():
        put(both(normed_ref, other_normed_ref))

    @pl.when(at >= second)
    def _():
        put(both(branch_ref, other_branch_ref))

    @pl.when(step == pl.num_programs(0) - 1)
    def _():
        wait(0)
        wait(1)


def split_places(refs, chunks):
    size_y, size_x, per = lax.axis_size("y"), lax.axis_size("x"), chunks // 2
    refs = list(refs)
    along_y = [refs[per * k : per * (k + 1)] for k in range(size_y)]
    refs = refs[per * size_y :]
    along_x = [refs[per * k : per * (k + 1)] for k in range(size_x)]
    return along_y, along_x, refs[per * size_x :]


def array_shapes(chunks, rows):
    columns = chunk_width(chunks)
    shapes = [(rows // lax.axis_size("y"), columns)] * (chunks // 2 * lax.axis_size("y"))
    shapes += [(rows // lax.axis_size("x"), columns)] * (chunks // 2 * lax.axis_size("x"))
    if chunks < 4:
        shapes.append((rows, PADDED - chunks * columns))
    return [jax.ShapeDtypeStruct(shape, jnp.bfloat16) for shape in shapes]


def place_copies(chunks, stage_ref, sems, places, tile):
    along = places[:2]
    rest = places[2]

    def copy(lane, place, row, where):
        start = lane * chunk_width(chunks)
        end = PADDED if lane == chunks else start + chunk_width(chunks)
        spot = pl.ds(pl.multiple_of(row * tile, tile), tile)
        return pltpu.make_async_copy(
            stage_ref.at[where, :, start:end], place.at[spot, :], sems.at[where, lane]
        )

    def start(spots, unit, inside, row, where):
        for chunk in range(chunks):
            which, position = spots[chunk % 2]
            for k, group in enumerate(along[chunk % 2]):

                @pl.when(which == k)
                def _(chunk=chunk, place=group[chunk // 2], at=position * unit + inside):
                    copy(chunk, place, at, where).start()

        for place in rest:
            copy(chunks, place, row, where).start()

    def wait(where):
        for chunk in range(chunks):
            copy(chunk, along[chunk % 2][0][chunk // 2], 0, where).wait()
        for place in rest:
            copy(chunks, place, 0, where).wait()

    return start, wait


def place_of(tile):
    return jnp.stack(
        [
            lax.axis_index("y").astype(jnp.int32),
            lax.axis_index("x").astype(jnp.int32),
            lax.axis_index("c").astype(jnp.int32),
            jnp.int32(unit_tiles(tile)),
            jnp.int32(lax.axis_size("y")),
            jnp.int32(lax.axis_size("x")),
        ]
    )


def half_side(tokens, at):
    return pl.BlockSpec(
        (tokens, PADDED), lambda i, *_: (at, 0), pipeline_mode=pl.Buffered(1)
    )


def weight_grads(chunks, own, other, sides):
    rows, tokens = own.shape
    tile = 512 if unit_tiles(256) % 2 == 0 else 256
    source = pl.BlockSpec((tile, tokens), lambda i, *_: (i, 0))
    halves = [half_side(tokens, 0), half_side(tokens, 1)]
    out_shape = array_shapes(chunks, rows)
    return pl.pallas_call(
        functools.partial(weight_grads_body, chunks, tile),
        grid_spec=pltpu.PrefetchScalarGridSpec(
            num_scalar_prefetch=1,
            grid=(rows // tile,),
            in_specs=[source, source] + halves * 2,
            out_specs=[pl.BlockSpec(memory_space=pl.ANY)] * len(out_shape),
            scratch_shapes=[
                pltpu.VMEM((2, tile, PADDED), jnp.bfloat16),
                pltpu.SemaphoreType.DMA((2, 5)),
            ],
        ),
        out_shape=out_shape,
        compiler_params=pltpu.CompilerParams(vmem_limit_bytes=40 << 20),
        cost_estimate=pl.CostEstimate(
            flops=4 * rows * tokens * CUTS[-1],
            bytes_accessed=4 * rows * tokens + 2 * rows * PADDED,
            transcendentals=0,
        ),
        name="weight_grads",
    )(place_of(tile), own, other, sides[0], sides[0], sides[1], sides[1])


def attention_fill_body(chunks, owners, place_ref, *refs):
    own_ref, other_ref, side_ref, other_side_ref = refs[:4]
    outs = refs[4 + (len(refs) - 6) // 2 : -2]
    stage_ref, sems = refs[-2:]
    step = pl.program_id(0)
    slot = step % 2
    start, wait = place_copies(chunks, stage_ref, sems, split_places(outs, chunks), INNER)

    def put():
        product = jnp.dot(
            own_ref[...].T, side_ref[:, : CUTS[-1]], preferred_element_type=jnp.float32
        ) + jnp.dot(
            other_ref[...].T, other_side_ref[:, : CUTS[-1]], preferred_element_type=jnp.float32
        )
        stage_ref[slot, :, : CUTS[-1]] = product.astype(jnp.bfloat16)
        stage_ref[slot, :, CUTS[-1] :] = jnp.zeros((INNER, PADDED - CUTS[-1]), jnp.bfloat16)
        start(spots_of(0, place_ref), 0, step, step, slot)

    @pl.when(place_ref[2] < owners)
    def _():
        @pl.when(step >= 2)
        def _():
            wait(slot)

        put()

        @pl.when(step == pl.num_programs(0) - 1)
        def _():
            wait(0)
            wait(1)


def attention_fill(chunks, arrays, own, other, sides):
    tokens = own.shape[0]
    unit_rows = unit_tiles(TILE) * TILE
    owners = 4 * INNER // unit_rows
    steps = unit_rows // INNER

    def column(i, place_ref):
        return 0, jnp.minimum(place_ref[2], owners - 1) * steps + i

    def half(i, place_ref):
        return jnp.where(column(i, place_ref)[1] < 3, 0, 1), 0

    anywhere = pl.BlockSpec(memory_space=pl.ANY)
    return pl.pallas_call(
        functools.partial(attention_fill_body, chunks, owners),
        grid_spec=pltpu.PrefetchScalarGridSpec(
            num_scalar_prefetch=1,
            grid=(steps,),
            in_specs=[pl.BlockSpec((tokens, INNER), column)] * 2
            + [pl.BlockSpec((tokens, PADDED), half)] * 2
            + [anywhere] * len(arrays),
            out_specs=[anywhere] * len(arrays),
            scratch_shapes=[
                pltpu.VMEM((2, INNER, PADDED), jnp.bfloat16),
                pltpu.SemaphoreType.DMA((2, 5)),
            ],
        ),
        out_shape=[jax.ShapeDtypeStruct(array.shape, array.dtype) for array in arrays],
        input_output_aliases={5 + k: k for k in range(len(arrays))},
        compiler_params=pltpu.CompilerParams(vmem_limit_bytes=32 << 20),
        cost_estimate=pl.CostEstimate(
            flops=4 * unit_rows * tokens * CUTS[-1],
            bytes_accessed=4 * unit_rows * tokens + 2 * unit_rows * PADDED,
            transcendentals=0,
        ),
        name="attention_fill",
    )(place_of(TILE), own, other, *sides, *arrays)


def tied(first, second):
    return lax.optimization_barrier((first, second))


def chunk_width(chunks):
    return PADDED // 4 if chunks == 4 else PADDED // 6


class Scatter:
    def __init__(self):
        self.waiting, self.flying, self.results = {}, {}, {}

    def push(self, name, route, kept, sends):
        self.waiting[name] = (route, kept, sends)

    def settle(self, values, *names):
        arrays, values = tied({name: self.flying[name][1:] for name in names}, values)
        moves = {}
        for name in names:
            route = self.flying.pop(name)[0]
            kept, moved = arrays[name]
            if not route:
                self.results[name] = kept.astype(jnp.float32) + sum(
                    part.astype(jnp.float32) for part in moved
                )
                continue
            total = total_of(kept, moved)
            total = total.reshape((lax.axis_size(route[0]), -1) + total.shape[-1:])
            sends = stage_sends(total, route[0], 0)
            moves[name] = (route, pick(total, lax.axis_index(route[0]), 0), sends)
        if moves and all(move[0] == ("z",) for move in moves.values()):
            kept = jnp.concatenate([move[1] for move in moves.values()], axis=-1)
            sends = [
                jnp.concatenate(parts, axis=-1) for parts in zip(*(m[2] for m in moves.values()))
            ]
            moves = {tuple(moves): (("z",), kept, sends)}
        arrays, values = tied({name: move[1:] for name, move in moves.items()}, values)
        for name, (route, *_) in moves.items():
            self.waiting[name] = (route,) + tuple(arrays[name])
        return values

    def start(self, values, *names):
        arrays, values = tied({name: self.waiting[name][1:] for name in names}, values)
        for name in names:
            route = self.waiting.pop(name)[0]
            kept, sends = arrays[name]
            self.flying[name] = (route[1:], kept, stage_moves(sends, route[0]))
        return values

    def step(self, values, *names):
        others = set(self.waiting)
        values = self.settle(values, *names)
        return self.start(values, *(name for name in self.waiting if name not in others))


def total_of(value, moved):
    total = value.astype(jnp.float32)
    for part in moved:
        total = total + part.astype(jnp.float32)
    return total.astype(jnp.bfloat16)


def fetch_rows(local_rows):
    return lax.all_gather(local_rows, DEVICES, axis=0, tiled=True)


def layer_forward(stream, gathered, gain_one, gain_two, gate_low, context):
    normed, inverse_one = rms_forward(stream, gain_one)
    normed_low = normed.astype(jnp.bfloat16)
    parts = [times_rows(normed_low, gathered[INNER : 3 * INNER]).astype(jnp.bfloat16)]
    queries = times_rows(normed_low, gathered[:INNER]).astype(jnp.bfloat16)
    if gate_low is not None:
        parts.append(jnp.broadcast_to(gate_low[:, None], (stream.shape[0], BLOCK)))
    shared = with_neighbours(jnp.concatenate(parts, axis=1))
    attended, full, log_total = attend_forward(queries, shared, context)
    middle = stream + times_plain(attended, gathered[3 * INNER : 4 * INNER])
    normed_two, inverse_two = rms_forward(middle, gain_two)
    normed_two_low = normed_two.astype(jnp.bfloat16)
    last = gate_low is not None
    result, *factors = ffn_forward(normed_two_low, None if last else middle, gathered)
    kept = (
        stream,
        inverse_one,
        normed_low,
        queries,
        shared,
        attended,
        full,
        log_total,
        middle,
        inverse_two,
        normed_two_low,
        factors,
    )
    return (result, kept)


def layer_backward(grad_out, kept, gathered, gain_one, gain_two, context, before):
    (
        stream,
        inverse_one,
        normed_low,
        queries,
        shared,
        attended,
        full,
        log_total,
        middle,
        inverse_two,
        normed_two_low,
        factors,
    ) = kept
    tokens = queries.shape[0]
    branch_low = grad_out.astype(jnp.bfloat16)
    sides = jnp.concatenate([normed_two_low, branch_low], axis=0)
    sides = jnp.pad(sides, ((0, 0), (0, PADDED - sides.shape[1])))
    sides = (sides, shift(sides, "c", 1))
    grad_normed_two, own, sent = ffn_backward(
        branch_low, factors[0], factors[1], gathered, factors[2], factors[3]
    )
    if before is not None:
        grad_normed_two, own, sent = before.step((grad_normed_two, own, sent), 0, 1)
    other = shift(sent, "c", 1)
    grad_middle, grad_gain_two = rms_backward(middle, inverse_two, gain_two, grad_normed_two)
    grad_middle = grad_out + grad_middle
    middle_low = grad_middle.astype(jnp.bfloat16)
    late_sides = jnp.concatenate([normed_low, middle_low], axis=0)
    late_sides = jnp.pad(late_sides, ((0, 0), (0, PADDED - late_sides.shape[1])))
    late_sides = (late_sides, shift(late_sides, "c", 1))
    grad_mixed = times_rows(middle_low, gathered[3 * INNER : 4 * INNER]).astype(jnp.bfloat16)
    grad_query, grad_shared, grad_table = attend_backward(
        queries, grad_mixed, full, shared, log_total, context
    )
    if before is not None:
        grad_query, grad_shared = before.settle((grad_query, grad_shared), 0, 1)
    grad_shared, own = lax.optimization_barrier((grad_shared, own))
    moving = start_back(grad_shared, tokens)
    chunks = 2 if before is None else 4
    arrays = weight_grads(chunks, own, other, sides)
    arrays, moving = lax.optimization_barrier((arrays, moving))
    if before is not None:
        arrays, moving = before.start((arrays, moving), (0, 1))
    grad_own = finish_back(*moving)
    grad_gate = grad_own[:, 2 * INNER :]
    grad_input_low = jnp.concatenate(
        [grad_query, grad_own[:, : 2 * INNER].astype(jnp.bfloat16)], axis=1
    )
    late = jnp.concatenate([grad_input_low, attended], axis=1)
    arrays = attention_fill(chunks, arrays, late, shift(late, "c", 1), late_sides)
    scatter = Scatter()
    along_y, along_x, rest = split_places(arrays, chunks)
    for chunk in range(chunks):
        route = ("y", "x", "z") if chunk % 2 == 0 else ("x", "y", "z")
        ordered = [group[chunk // 2] for group in (along_y, along_x)[chunk % 2]]
        scatter.push(chunk, route, ordered[-1], ordered[:-1])
    grad_input_low, grad_gate = scatter.start((grad_input_low, grad_gate), 0, 1)
    if rest:
        grad_input_low, grad_gate, rest = lax.optimization_barrier(
            (grad_input_low, grad_gate, rest)
        )
        rest = lax.psum_scatter(rest[0], ("y", "x", "z"), scatter_dimension=0, tiled=True)
    grad_normed = times_plain(grad_input_low, gathered[: 3 * INNER])
    grad_stream, grad_gain_one = rms_backward(stream, inverse_one, gain_one, grad_normed)
    return (grad_middle + grad_stream, grad_table, grad_gate, grad_gain_one, grad_gain_two, scatter, rest)


def per_device(
    inputs, layer3_rows, layer4_rows, norm_gains, gate_weight, rel_bias, segment_ids, cotangent
):
    seqs_here, tokens_here, width = inputs.shape
    first_pos = lax.axis_index("z") * tokens_here
    context = attention_context(segment_ids[0], first_pos, tokens_here, rel_bias)
    stream = inputs.reshape(tokens_here, width)
    gathered_three = fetch_rows(layer3_rows)
    after_three, kept_three = layer_forward(
        stream, gathered_three, norm_gains[0], norm_gains[1], None, context
    )
    gate_inverse = lax.rsqrt(jnp.mean(after_three * after_three, axis=1, keepdims=True) + epsilon)
    gate_normed = after_three * gate_inverse
    gate_logit = jnp.sum(gate_normed * gate_weight, axis=1) + gate_offset
    sigmoid_value = 1.0 / (1.0 + jnp.exp(-gate_logit))
    gate_mask = gate_scale * sigmoid_value
    gate_low = gate_mask.astype(jnp.bfloat16)
    gathered_four = fetch_rows(layer4_rows)
    hidden_four, kept_four = layer_forward(
        after_three, gathered_four, norm_gains[2], norm_gains[3], gate_low, context
    )
    grad_three_out, table_four, grad_gate, gain_four_one, gain_four_two, before, rest = (
        layer_backward(
            cotangent.reshape(tokens_here, width),
            kept_four,
            gathered_four,
            norm_gains[2],
            norm_gains[3],
            context,
            None,
        )
    )
    grad_logit = grad_gate[:, 0] * gate_scale * sigmoid_value * (1.0 - sigmoid_value)
    grad_gate_weight = jnp.sum(grad_logit[:, None] * gate_normed, axis=0)
    gate_stream = stream_backward(after_three, gate_inverse, grad_logit[:, None] * gate_weight)
    grad_input, table_three, unused, gain_three_one, gain_three_two, scatter, _ = layer_backward(
        grad_three_out + gate_stream,
        kept_three,
        gathered_three,
        norm_gains[0],
        norm_gains[1],
        context,
        before,
    )
    table = jnp.pad((table_three + table_four).reshape(1, -1), ((0, 0), (0, width - 6 * BUCKETS)))
    small_sums = jnp.stack(
        [gain_three_one, gain_three_two, gain_four_one, gain_four_two, grad_gate_weight, table[0]]
    )
    small = hop(small_sums, "c")
    small = before.settle(small, (0, 1))
    small = scatter.step(small, 0, 1)
    small = scatter.start(small, 2, 3)
    small, hidden_four = tied(small, hidden_four)
    after_four = kept_four[8] + times_plain(hidden_four, gathered_four[4 * INNER + 2 * FF :])
    small, after_four = scatter.step((small, after_four), 0, 1)
    small, rest = scatter.settle((small, rest), (0, 1))
    small = scatter.step(small, 2, 3)
    for bit in range(1, lax.axis_size("z")):
        if bit & (bit - 1) == 0:
            small = hop(small, "z", bit)
    small = scatter.step(small, 2, 3)
    small = hop(small, "x")
    for bit in range(1, lax.axis_size("y")):
        if bit & (bit - 1) == 0:
            small = hop(small, "y", bit)
    summed = scatter.settle(small, (2, 3))
    local_three = jnp.concatenate([scatter.results[pair] for pair in ((0, 1), (2, 3))], axis=1)
    local_four = jnp.concatenate([before.results[(0, 1)], rest.astype(jnp.float32)], axis=1)
    local_three, local_four = local_three[:, :width], local_four[:, :width]
    return (
        after_four.reshape(inputs.shape),
        gate_mask.reshape(seqs_here, tokens_here),
        grad_input.reshape(inputs.shape),
        local_three,
        local_four,
        summed[:4],
        summed[4],
        summed[5, : 6 * BUCKETS].reshape(BUCKETS, HEADS),
    )


def solution(mesh):
    outer, inner = mesh.devices.shape
    fine = Mesh(mesh.devices.reshape(outer // 4, 2, 2, inner), DEVICES)
    batch = ("y", "x", "c")
    tokens = P(batch, "z", None)
    rows = P(DEVICES, None)
    return jax.shard_map(
        per_device,
        mesh=fine,
        in_specs=(tokens, rows, rows, P(), P(), P(), P(batch, None), tokens),
        out_specs=(tokens, P(batch, "z"), tokens, rows, rows, P(), P(), P()),
        check_vma=False,
    )
```
